32 devices in a mesh: wide: 8 (over z, y), narrow: 4 (over x, core).
Axes of the slice: x: 2, y: 2, z: 4, core: 2. Of those that a mesh axis runs over, the one named last changes fastest.
Arguments:
- layer_input: bfloat16 [16384, 768], P(('wide', 'narrow')), may hold values from -9 to 9
- layer_cotangent: bfloat16 [16384, 768], P(('wide', 'narrow')), may hold values from -13 to 13
- attend_weight: float32 [3, 768, 768], P(None, 'wide', 'narrow'), may hold values from -0.21875 to 0.21875
- attend_first: float32 [3, 768, 768], P(None, 'wide', 'narrow'), may hold values from -16 to 16
- attend_second: float32 [3, 768, 768], P(None, 'wide', 'narrow'), may hold values from 7.86432 to 31.1296
- output_weight: float32 [768, 768], P('narrow', 'wide'), may hold values from -1.75 to 1.75
- output_first: float32 [768, 768], P('narrow', 'wide'), may hold values from -6 to 6
- output_second: float32 [768, 768], P('narrow', 'wide'), may hold values from 0.147456 to 0.589824
- gated_weight: float32 [2, 768, 2048], P(None, 'wide', 'narrow'), may hold values from -0.21875 to 0.21875
- gated_first: float32 [2, 768, 2048], P(None, 'wide', 'narrow'), may hold values from -6 to 6
- gated_second: float32 [2, 768, 2048], P(None, 'wide', 'narrow'), may hold values from 4.194304 to 16.384
- down_weight: float32 [2048, 768], P('narrow', 'wide'), may hold values from -0.125 to 0.125
- down_first: float32 [2048, 768], P('narrow', 'wide'), may hold values from -16 to 16
- down_second: float32 [2048, 768], P('narrow', 'wide'), may hold values from 7.86432 to 31.1296
- norm_gains: float32 [2, 768], P(None, 'wide'), may hold values from 0.5 to 1.5
- gains_first: float32 [2, 768], P(None, 'wide'), may hold values from -48 to 48
- gains_second: float32 [2, 768], P(None, 'wide'), may hold values from 58.9824 to 235.9296
Outputs:
- layer_output: bfloat16 [16384, 768], P(('wide', 'narrow'))
- input_grad: float32 [16384, 768], P(('wide', 'narrow'))
- grad_norm: float32 [], replicated
- new_attend: float32 [3, 768, 768], P(None, 'wide', 'narrow')
- new_attend_first: float32 [3, 768, 768], P(None, 'wide', 'narrow')
- new_attend_second: float32 [3, 768, 768], P(None, 'wide', 'narrow')
- new_output: float32 [768, 768], P('narrow', 'wide')
- new_output_first: float32 [768, 768], P('narrow', 'wide')
- new_output_second: float32 [768, 768], P('narrow', 'wide')
- new_gated: float32 [2, 768, 2048], P(None, 'wide', 'narrow')
- new_gated_first: float32 [2, 768, 2048], P(None, 'wide', 'narrow')
- new_gated_second: float32 [2, 768, 2048], P(None, 'wide', 'narrow')
- new_down: float32 [2048, 768], P('narrow', 'wide')
- new_down_first: float32 [2048, 768], P('narrow', 'wide')
- new_down_second: float32 [2048, 768], P('narrow', 'wide')
- new_gains: float32 [2, 768], P(None, 'wide')
- new_gains_first: float32 [2, 768], P(None, 'wide')
- new_gains_second: float32 [2, 768], P(None, 'wide')
The draws below stay inside these ranges and needn't reach their ends.
All inputs are finite; a program needn't handle non-finite values.
Results may differ from the reference program's by a relative error of at most 0.012.
The reference program's roundings to bfloat16 on the way count: a program that leaves them out, or rounds other values in their place, can miss the bound.
Values may be sent and summed in bfloat16 or wider, within the bound.
No kernel may reach another device: no remote copies, remote signals or barrier semaphores. Data moves between devices by JAX's collectives and lax.ppermute only.
A program may use at most 128 MiB of HBM per device.

```python
import math
import jax
import jax.numpy as jnp
from jax import lax

D = 768
HEADS = 12
HD = 64
FF = 2048
L = 1024
ADAM_STEP = 5
BATCH = 16
TOKENS = 16384


def column_fraction():
    return jnp.arange(D).astype(jnp.float32) / max(D - 1, 1)


def draw_layer_input(key, part):
    columns = column_fraction()
    base = jnp.clip(jax.random.normal(key, (TOKENS, D), jnp.float32), -5.0, 5.0)
    ramp = 0.5 + 1.2 * columns
    return (base * ramp[None, :]).astype(jnp.bfloat16)


def draw_layer_cotangent(key, part):
    sequence = (jnp.arange(TOKENS) // L).astype(jnp.float32)
    fraction = sequence / max(BATCH - 1, 1)
    columns = column_fraction()
    base = jnp.clip(jax.random.normal(key, (TOKENS, D), jnp.float32), -4.0, 4.0)
    ramp = 0.6 + 1.2 * fraction
    spread = 0.5 + 1.2 * columns
    return (base * ramp[:, None] * spread[None, :]).astype(jnp.bfloat16)


def steps_of(rng, shape, split, smallest, largest):
    loudness, own = 1.0, jax.random.fold_in(rng, 6)
    for position, blocks in split:
        draws = jnp.exp(jax.random.uniform(jax.random.fold_in(own, position), (blocks,), jnp.float32, smallest / len(split), largest / len(split)))
        loudness = loudness * jnp.repeat(draws, shape[position] // blocks).reshape([-1 if axis == position else 1 for axis in range(len(shape))])
    return loudness


def gaussian(own_key, extent, scale, most, cuts=(), held_as=jnp.bfloat16):
    loudness = steps_of(own_key, extent, cuts, -0.22, 0.18) if cuts else 1.0
    array = jax.random.normal(own_key, extent, jnp.float32) * scale * loudness
    return jnp.minimum(jnp.maximum(array, -most), most).astype(held_as)


def setup_inputs(seed: int = 0) -> dict:
    streams_of = jax.random.split(jax.random.key(seed), 18)
    return {
        "layer_input": draw_layer_input(jax.random.fold_in(streams_of[17], 71), 0),
        "layer_cotangent": draw_layer_cotangent(jax.random.fold_in(streams_of[17], 71), 0),
        "attend_weight": gaussian(streams_of[2], (3, D, D), D ** -0.5, 0.21875, ((1, 8), (2, 4)), jnp.float32),
        "attend_first": gaussian(streams_of[3], (3, D, D), (0.022 * TOKENS ** 0.5), 16.0, ((1, 8), (2, 4)), jnp.float32),
        "attend_second": jnp.clip(jnp.exp(math.log(31.1296) - 1.3758231 * jax.random.uniform(streams_of[4], (3, D, D), jnp.float32) ** steps_of(streams_of[4], (3, D, D), ((1, 8), (2, 4)), -0.2, 0.2)), 7.86432, 31.1296),
        "output_weight": gaussian(streams_of[5], (D, D), (max(D // 64, 1)) ** -0.5, 1.75, ((0, 4), (1, 8)), jnp.float32),
        "output_first": gaussian(streams_of[6], (D, D), (0.003 * TOKENS ** 0.5), 6.0, ((0, 4), (1, 8)), jnp.float32),
        "output_second": jnp.clip(jnp.exp(math.log(0.589824) - 1.3862944 * jax.random.uniform(streams_of[7], (D, D), jnp.float32) ** steps_of(streams_of[7], (D, D), ((0, 4), (1, 8)), -0.2, 0.2)), 0.147456, 0.589824),
        "gated_weight": gaussian(streams_of[8], (2, D, FF), D ** -0.5, 0.21875, ((1, 8), (2, 4)), jnp.float32),
        "gated_first": gaussian(streams_of[9], (2, D, FF), (0.016 * TOKENS ** 0.5), 6.0, ((1, 8), (2, 4)), jnp.float32),
        "gated_second": jnp.clip(jnp.exp(math.log(16.384) - 1.3625779 * jax.random.uniform(streams_of[10], (2, D, FF), jnp.float32) ** steps_of(streams_of[10], (2, D, FF), ((1, 8), (2, 4)), -0.2, 0.2)), 4.194304, 16.384),
        "down_weight": gaussian(streams_of[11], (FF, D), FF ** -0.5, 0.125, ((0, 4), (1, 8)), jnp.float32),
        "down_first": gaussian(streams_of[12], (FF, D), (0.022 * TOKENS ** 0.5), 16.0, ((0, 4), (1, 8)), jnp.float32),
        "down_second": jnp.clip(jnp.exp(math.log(31.1296) - 1.3758231 * jax.random.uniform(streams_of[13], (FF, D), jnp.float32) ** steps_of(streams_of[13], (FF, D), ((0, 4), (1, 8)), -0.2, 0.2)), 7.86432, 31.1296),
        "norm_gains": jnp.clip(1.0 + 0.1 * jax.random.normal(streams_of[14], (2, D), jnp.float32), 0.5, 1.5),
        "gains_first": gaussian(streams_of[15], (2, D), (0.06 * TOKENS ** 0.5), 48.0, ((1, 8),), jnp.float32),
        "gains_second": jnp.clip(jnp.exp(math.log(235.9296) - 1.3862944 * jax.random.uniform(streams_of[16], (2, D), jnp.float32) ** steps_of(streams_of[16], (2, D), ((1, 8),), -0.2, 0.2)), 58.9824, 235.9296),
    }


EPSILON = 1e-05
WEIGHT_DECAY = 0.1
AVERAGING = 0.5
HIGHEST = lax.Precision.HIGHEST

@jax.custom_vjp
def low(v):
    return lax.optimization_barrier(v.astype(jnp.bfloat16)).astype(jnp.float32)

@jax.custom_vjp
def low_back(v):
    return v

def low_keep(v):
    return (low(v), None)

def low_pass(kept, grad):
    return (grad,)

def back_keep(v):
    return (v, None)

def back_low(kept, grad):
    return (low(grad),)
low.defvjp(low_keep, low_pass)
low_back.defvjp(back_keep, back_low)

def rope_tables(length, width):
    half = width // 2
    freq = jnp.exp(-jnp.log(10000.0) * jnp.arange(half, dtype=jnp.float32) / half)
    angle = jnp.arange(length, dtype=jnp.float32)[:, None] * freq[None, :]
    return (jnp.cos(angle), jnp.sin(angle))

def rotate(vector, cosine, sine):
    half = vector.shape[-1] // 2
    first = vector[..., :half]
    second = vector[..., half:]
    cos_view = cosine[:, None, :]
    sin_view = sine[:, None, :]
    return jnp.concatenate([first * cos_view - second * sin_view, second * cos_view + first * sin_view], axis=-1)

def matmul(left, right):
    return jnp.dot(left, right, precision=HIGHEST, preferred_element_type=jnp.float32)

def attend(block):
    query, key, value = block
    length = query.shape[0]
    causal = jnp.arange(length)[:, None] >= jnp.arange(length)[None, :]
    scores = low_back(jnp.einsum('qhd,khd->hqk', query, key, precision=HIGHEST) * query.shape[2] ** (-0.5))
    scores = jnp.where(causal[None], scores, -1e+30)
    peak = lax.optimization_barrier(jnp.max(scores, axis=2, keepdims=True))
    weights = jnp.exp(scores - peak)
    probs = low(weights / lax.optimization_barrier(jnp.sum(weights, axis=2, keepdims=True)))
    return jnp.einsum('hqk,khd->qhd', probs, value, precision=HIGHEST)

def rms_scale(residual):
    return lax.rsqrt(lax.optimization_barrier(jnp.mean(residual * residual, axis=1, keepdims=True)) + EPSILON)

def layer(inputs, attend_w, output_w, gated_w, down_w, gains):
    attend_low = low(attend_w)
    output_low = low(output_w)
    gated_low = low(gated_w)
    down_low = low(down_w)
    gains_low = low(gains)
    batch = inputs.shape[0] // L
    cosine, sine = rope_tables(L, HD)

    def view(vector):
        return vector.reshape(batch, L, HEADS, HD)
    query = low(rotate(view(low_back(matmul(inputs, attend_low[0]))), cosine, sine))
    key = low(rotate(view(low_back(matmul(inputs, attend_low[1]))), cosine, sine))
    value = low(low_back(view(matmul(inputs, attend_low[2]))))
    context = lax.map(jax.checkpoint(attend), (query, key, value))
    context = low(low_back(context.reshape(batch * L, D)))
    attn_out = low_back(matmul(context, output_low))
    residual_one = inputs + attn_out
    hidden_state = residual_one * rms_scale(residual_one) * gains_low[0]
    hidden_low = low(hidden_state)
    gate = low_back(matmul(hidden_low, gated_low[0]))
    up = low_back(matmul(hidden_low, gated_low[1]))
    activated = low(jax.nn.silu(gate) * up)
    ffn_out = low_back(matmul(activated, down_low))
    residual_two = hidden_state + ffn_out
    return residual_two * rms_scale(residual_two) * gains_low[1]

def adam_update(weight, first, second, grad, ratio, rate, decay):
    clipped = grad * ratio
    first_new = AVERAGING * first + (1.0 - AVERAGING) * clipped
    second_new = AVERAGING * second + (1.0 - AVERAGING) * clipped * clipped
    correction = 1.0 - AVERAGING ** ADAM_STEP
    step = first_new / correction / (jnp.sqrt(second_new / correction) + 1e-08)
    return (weight - rate * (step + decay * weight), first_new, second_new)

def reference(layer_input, layer_cotangent, attend_weight, attend_first, attend_second, output_weight, output_first, output_second, gated_weight, gated_first, gated_second, down_weight, down_first, down_second, norm_gains, gains_first, gains_second):
    inputs = layer_input.astype(jnp.float32)
    result, pullback = jax.vjp(layer, inputs, attend_weight, output_weight, gated_weight, down_weight, norm_gains)
    grads = pullback(layer_cotangent.astype(jnp.float32))
    input_grad = grads[0]
    attend_grad, output_grad, gated_grad, down_grad, gains_grad = grads[1:]
    total = jnp.sum(attend_grad * attend_grad) + jnp.sum(output_grad * output_grad)
    total = total + jnp.sum(gated_grad * gated_grad) + jnp.sum(down_grad * down_grad)
    total = total + jnp.sum(gains_grad * gains_grad)
    grad_norm = jnp.sqrt(total)
    clip = 0.02 * math.sqrt(TOKENS * (4 * D * D + 3 * D * FF + 2 * D))
    ratio = clip / jnp.maximum(grad_norm, clip)
    new_attend = adam_update(attend_weight, attend_first, attend_second, attend_grad, ratio, D ** (-0.5), WEIGHT_DECAY)
    new_output = adam_update(output_weight, output_first, output_second, output_grad, ratio, max(D // 64, 1) ** (-0.5), WEIGHT_DECAY)
    new_gated = adam_update(gated_weight, gated_first, gated_second, gated_grad, ratio, D ** (-0.5), WEIGHT_DECAY)
    new_down = adam_update(down_weight, down_first, down_second, down_grad, ratio, FF ** (-0.5), WEIGHT_DECAY)
    new_gains = adam_update(norm_gains, gains_first, gains_second, gains_grad, ratio, 0.4, 0.0)
    return (result.astype(jnp.bfloat16), input_grad, grad_norm, new_attend[0], new_attend[1], new_attend[2], new_output[0], new_output[1], new_output[2], new_gated[0], new_gated[1], new_gated[2], new_down[0], new_down[1], new_down[2], new_gains[0], new_gains[1], new_gains[2])
```

```python
import functools
import math

import jax
import jax.numpy as jnp
from jax import lax
from jax.experimental import pallas as pl
from jax.experimental.pallas import tpu as pltpu
from jax.sharding import PartitionSpec as P

D = 768
HD = 64
FF = 2048
L = 1024
ADAM_STEP = 5

EPSILON = 1e-05
WEIGHT_DECAY = 0.1
AVERAGING = 0.5

LOW = jnp.bfloat16
FULL = jnp.float32
QB = 256
MASKED = -1e30


def swap(value, axis, bit):
    size = lax.axis_size(axis)
    return lax.ppermute(value, axis, [(i, i ^ bit) for i in range(size)])


def wide_bits():
    top = lax.axis_size("wide").bit_length() - 1
    return [1 << b for b in range(top - 1, -1, -1)]


def block_masks():
    masks = [0]
    for bit in wide_bits():
        masks = masks + [m ^ bit for m in masks]
    return masks


def gather_pieces(shard, x_last):
    held = shard
    for bit in wide_bits()[:-1]:
        held = jnp.concatenate([held, swap(held, "wide", bit)], axis=0)
    across_y = swap(held, "wide", 1)
    across_x = swap(held, "narrow", 2)
    if x_last:
        corner = swap(across_y, "narrow", 2)
    else:
        corner = swap(across_x, "wide", 1)
    return [[held, across_y], [across_x, corner]]


def add(kept, received):
    return kept.astype(FULL) + received.astype(FULL)


def scatter_pieces(pieces, x_first):
    (own, across_y), (across_x, corner) = pieces
    if x_first:
        own = add(own, swap(across_x, "narrow", 2))
        other = add(across_y, swap(corner, "narrow", 2))
        held = add(own, swap(other.astype(LOW), "wide", 1))
    else:
        own = add(own, swap(across_y, "wide", 1))
        other = add(across_x, swap(corner, "wide", 1))
        held = add(own, swap(other.astype(LOW), "narrow", 2))
    for bit in wide_bits()[:-1][::-1]:
        half = held.shape[0] // 2
        held = add(held[:half], swap(held[half:].astype(LOW), "wide", bit))
    return held


def tree_sum(value, axis):
    bits = [1 << b for b in range(lax.axis_size(axis).bit_length() - 1)]
    for start in range(0, len(bits), 3):
        group = bits[start : start + 3]
        masks = [0]
        for bit in group:
            masks = masks + [m ^ bit for m in masks]
        parts = [value if m == 0 else swap(value, axis, m) for m in masks]
        while len(parts) > 1:
            parts = [parts[i] + parts[i + 1] for i in range(0, len(parts), 2)]
        value = parts[0]
    return value


def turn(value, cosine, sine, sign):
    width = value.shape[1]
    lane = lax.broadcasted_iota(jnp.int32, value.shape, 1) % HD
    other = jnp.where(
        lane < HD // 2,
        pltpu.roll(value, width - HD // 2, 1),
        pltpu.roll(value, HD // 2, 1),
    )
    reps = width // 128
    return value * jnp.concatenate([cosine] * reps, axis=1) + sign * other * jnp.concatenate(
        [sine] * reps, axis=1
    )


def nn(a, b):
    return lax.dot_general(a, b, (((1,), (0,)), ((), ())), preferred_element_type=FULL)


def nt(a, b):
    return lax.dot_general(a, b, (((1,), (1,)), ((), ())), preferred_element_type=FULL)


def diagonal(scores):
    key = lax.broadcasted_iota(jnp.int32, scores.shape, 0)
    query = lax.broadcasted_iota(jnp.int32, scores.shape, 1)
    return jnp.where(key <= query, scores, MASKED)


def flip(value):
    return value.astype(FULL).T


def attend_kernel(
    rows_ref, qka_ref, qkb_ref, voa_ref, vob_ref, cos_ref, sin_ref,
    q_ref, k_ref, v_ref, ctx_ref, lse_ref, hold,
):
    heads = q_ref.shape[0]
    width = heads * HD
    half = qka_ref.shape[0]

    def project(i, carry):
        rows = pl.ds(pl.multiple_of(i * QB, QB), QB)
        first, second = rows_ref[rows, :half], rows_ref[rows, half:]
        pair = nn(first, qka_ref[...]) + nn(second, qkb_ref[...])
        pair = turn(pair, cos_ref[rows, :], sin_ref[rows, :], 1.0)
        value = nn(first, voa_ref[:, :width]) + nn(second, vob_ref[:, :width])
        for h in range(heads):
            q_ref[h, rows, :] = (pair[:, h * HD : (h + 1) * HD] * (HD**-0.5)).astype(LOW)
            k_ref[h, rows, :] = pair[:, width + h * HD : width + (h + 1) * HD].astype(LOW)
            v_ref[h, rows, :] = value[:, h * HD : (h + 1) * HD].astype(LOW)
        return carry

    lax.fori_loop(0, L // QB, project, 0)

    def head(h, carry):
        turned = flip(v_ref[h]).astype(LOW)
        for i in range(L // QB):
            lo, hi = i * QB, (i + 1) * QB
            query = q_ref[h, lo:hi, :]
            diag = diagonal(nt(k_ref[h, lo:hi, :], query))
            peak = jnp.max(diag, axis=0, keepdims=True)
            if i:
                body = nt(k_ref[h, :lo, :], query)
                peak = jnp.maximum(peak, jnp.max(body, axis=0, keepdims=True))
            weight = jnp.exp(diag - peak)
            total = jnp.sum(weight, axis=0, keepdims=True)
            out = nn(turned[:, lo:hi], weight.astype(LOW))
            if i:
                weight = jnp.exp(body - peak)
                total = total + jnp.sum(weight, axis=0, keepdims=True)
                out = out + nn(turned[:, :lo], weight.astype(LOW))
            lse_ref[h, :, lo:hi] = peak + jnp.log(total)
            hold[h, lo:hi, :] = (out / total).T.astype(LOW)
        return carry

    lax.fori_loop(0, heads, head, 0)
    for h in range(heads):
        ctx_ref[:, h * HD : (h + 1) * HD] = hold[h]


def attend_forward(rows, qk, vo, cosine, sine):
    heads = qk[0].shape[1] // 2 // HD
    headed = jax.ShapeDtypeStruct((heads, L, HD), LOW)
    return pl.pallas_call(
        attend_kernel,
        out_shape=(
            headed, headed, headed,
            jax.ShapeDtypeStruct((L, heads * HD), LOW),
            jax.ShapeDtypeStruct((heads, 1, L), FULL),
        ),
        scratch_shapes=[pltpu.VMEM((heads, L, HD), LOW)],
        compiler_params=pltpu.CompilerParams(vmem_limit_bytes=40 << 20),
        name="attend_forward",
    )(rows, qk[0], qk[1], vo[0], vo[1], cosine, sine)


def attend_back_kernel(
    q_ref, k_ref, v_ref, lse_ref, dctx_ref, cos_ref, sin_ref,
    dqk_ref, dv_ref, dctx, dqk, dk_sum, dv_sum,
):
    heads = q_ref.shape[0]
    width = heads * HD
    for h in range(heads):
        dctx[h] = dctx_ref[:, h * HD : (h + 1) * HD]

    def head(h, carry):
        turned = flip(k_ref[h]).astype(LOW)
        for i in range(L // QB):
            lo, hi = i * QB, (i + 1) * QB
            query, back = q_ref[h, lo:hi, :], dctx[h, lo:hi, :]
            lse = lse_ref[h, :, lo:hi]
            prob = jnp.exp(diagonal(nt(k_ref[h, lo:hi, :], query)) - lse)
            grad = nt(v_ref[h, lo:hi, :], back)
            inner = jnp.sum(prob * grad, axis=0, keepdims=True)
            if i:
                prob_body = jnp.exp(nt(k_ref[h, :lo, :], query) - lse)
                grad_body = nt(v_ref[h, :lo, :], back)
                inner = inner + jnp.sum(prob_body * grad_body, axis=0, keepdims=True)
            score = (prob * (grad - inner)).astype(LOW)
            dv_sum[h, lo:hi, :] = nn(prob.astype(LOW), back)
            dk_sum[h, lo:hi, :] = nn(score, query)
            dquery = nn(turned[:, lo:hi], score)
            if i:
                score = (prob_body * (grad_body - inner)).astype(LOW)
                dv_sum[h, :lo, :] += nn(prob_body.astype(LOW), back)
                dk_sum[h, :lo, :] += nn(score, query)
                dquery = dquery + nn(turned[:, :lo], score)
            dqk[h, lo:hi, :] = (dquery * (HD**-0.5)).T
        return carry

    lax.fori_loop(0, heads, head, 0)

    def finish(i, carry):
        rows = pl.ds(pl.multiple_of(i * QB, QB), QB)
        pair = jnp.concatenate(
            [dqk[h, rows, :] for h in range(heads)] + [dk_sum[h, rows, :] for h in range(heads)],
            axis=1,
        )
        dqk_ref[rows, :] = turn(pair, cos_ref[rows, :], sin_ref[rows, :], -1.0).astype(LOW)
        dv_ref[rows, :] = jnp.concatenate(
            [dv_sum[h, rows, :] for h in range(heads)], axis=1
        ).astype(LOW)
        return carry

    lax.fori_loop(0, L // QB, finish, 0)


def attend_backward(q, k, v, lse, dctx, cosine, sine):
    heads = q.shape[0]
    return pl.pallas_call(
        attend_back_kernel,
        out_shape=(
            jax.ShapeDtypeStruct((L, 2 * heads * HD), LOW),
            jax.ShapeDtypeStruct((L, heads * HD), LOW),
        ),
        scratch_shapes=[
            pltpu.VMEM((heads, L, HD), LOW),
            pltpu.VMEM((heads, L, HD), FULL),
            pltpu.VMEM((heads, L, HD), FULL),
            pltpu.VMEM((heads, L, HD), FULL),
        ],
        compiler_params=pltpu.CompilerParams(vmem_limit_bytes=40 << 20),
        name="attend_backward",
    )(q, k, v, lse, dctx, cosine, sine)


def rope_tables():
    half = HD // 2
    lane = jnp.arange(128) % HD
    freq = jnp.exp(-jnp.log(10000.0) * (lane % half).astype(FULL) / half)
    angle = jnp.arange(L, dtype=FULL)[:, None] * freq[None, :]
    return jnp.cos(angle), jnp.where(lane < half, -1.0, 1.0)[None, :] * jnp.sin(angle)


def rms_scale(residual):
    return lax.rsqrt(jnp.mean(residual * residual, axis=1, keepdims=True) + EPSILON)


def adam_update(weight, first, second, grad, ratio, rate, decay):
    clipped = grad * ratio
    first_new = AVERAGING * first + (1.0 - AVERAGING) * clipped
    second_new = AVERAGING * second + (1.0 - AVERAGING) * clipped * clipped
    correction = 1.0 - AVERAGING**ADAM_STEP
    step = first_new / correction / (jnp.sqrt(second_new / correction) + 1e-08)
    return (weight - rate * (step + decay * weight), first_new, second_new)


def norm_back(scaled, normed, inv):
    return inv * (scaled - normed * jnp.mean(scaled * normed, axis=1, keepdims=True))


def weight_grad(rows, grads):
    whole = lax.dot_general(rows, grads, (((0,), (0,)), ((), ())), preferred_element_type=FULL)
    whole = whole.astype(LOW)
    half = whole.shape[0] // 2
    return [whole[:half], whole[half:]]


def per_device(
    layer_input, layer_cotangent,
    attend_weight, attend_first, attend_second,
    output_weight, output_first, output_second,
    gated_weight, gated_first, gated_second,
    down_weight, down_first, down_second,
    norm_gains, gains_first, gains_second,
):
    rows = layer_input.shape[0]
    wide = lax.axis_size("wide")
    block = D // wide
    me = lax.axis_index("wide")
    narrow = lax.axis_index("narrow")
    core = narrow % 2
    cols = attend_weight.shape[2]

    attend_low = attend_weight.astype(LOW)
    qk_shard = jnp.concatenate([attend_low[0], attend_low[1]], axis=1)
    vo_shard = jnp.concatenate([attend_low[2], output_weight.T.astype(LOW)], axis=1)
    gu_shard = jnp.concatenate([gated_weight[0], gated_weight[1]], axis=1).astype(LOW)
    down_shard = down_weight.T.astype(LOW)
    qk = gather_pieces(qk_shard, True)
    vo = gather_pieces(vo_shard, False)
    gu = gather_pieces(gu_shard, True)
    down = gather_pieces(down_shard, False)
    gains = norm_gains.astype(LOW).astype(FULL)[None]
    for bit in wide_bits():
        gains = jnp.concatenate([gains, swap(gains, "wide", bit)], axis=0)
    gains = gains.transpose(1, 0, 2).reshape(2, 1, D)

    order = me ^ jnp.array(block_masks(), jnp.int32)
    source = (order[:, None] * block + jnp.arange(block)[None, :]).reshape(1, D)
    mover = (lax.broadcasted_iota(jnp.int32, (D, D), 0) == source).astype(LOW)

    def whole_sequence(own):
        moved = jnp.dot(own, mover, preferred_element_type=FULL).astype(LOW)
        received = swap(moved, "narrow", 1)
        return jnp.where(
            core == 0,
            jnp.concatenate([moved, received], axis=0),
            jnp.concatenate([received, moved], axis=0),
        )

    def own_rows(value):
        return lax.dynamic_slice_in_dim(value, core * rows, rows, axis=0)

    def both_cores(partial):
        low = partial.astype(LOW)
        return low.astype(FULL) + swap(low, "narrow", 1).astype(FULL)

    inputs = whole_sequence(layer_input)
    upstream = whole_sequence(layer_cotangent).astype(FULL)
    cosine, sine = rope_tables()

    saved = [attend_forward(inputs, qk[x], vo[x], cosine, sine) for x in range(2)]
    context = [s[3] for s in saved]
    out_t = [jnp.concatenate([p[:, cols:] for p in vo[x]], axis=0) for x in range(2)]
    attn_out = both_cores(nt(context[0], out_t[0]) + nt(context[1], out_t[1]))
    residual_one = inputs.astype(FULL) + attn_out
    inv_one = rms_scale(residual_one)
    normed_one = residual_one * inv_one
    hidden = normed_one * gains[0]
    hidden_low = hidden.astype(LOW)
    gu_full = [jnp.concatenate(p, axis=0) for p in gu]
    down_full = [jnp.concatenate(p, axis=0) for p in down]
    hid = down_shard.shape[1]
    gates, ups, acts = [], [], []
    for x in range(2):
        both = nn(hidden_low, gu_full[x])
        gates.append(both[:, :hid])
        ups.append(both[:, hid:])
        acts.append((gates[x] * jax.nn.sigmoid(gates[x]) * ups[x]).astype(LOW))
    ffn_out = both_cores(nt(acts[0], down_full[0]) + nt(acts[1], down_full[1]))
    residual_two = hidden + ffn_out
    inv_two = rms_scale(residual_two)
    normed_two = residual_two * inv_two
    layer_output = own_rows((normed_two * gains[1]).astype(LOW))
    layer_output = nt(layer_output, mover).astype(LOW)

    gain_two_grad = jnp.sum(upstream * normed_two, axis=0)
    grad_two = norm_back(upstream * gains[1], normed_two, inv_two)
    grad_two_low = grad_two.astype(LOW)
    gu_grads = []
    for x in range(2):
        act_grad = nn(grad_two_low, down_full[x])
        sig = jax.nn.sigmoid(gates[x])
        gate_grad = act_grad * ups[x] * (sig * (1.0 + gates[x] * (1.0 - sig)))
        up_grad = act_grad * (gates[x] * sig)
        gu_grads.append(jnp.concatenate([gate_grad, up_grad], axis=1).astype(LOW))
    mid_grad = both_cores(nt(gu_grads[0], gu_full[0]) + nt(gu_grads[1], gu_full[1]))
    down_red = scatter_pieces([weight_grad(grad_two_low, acts[x]) for x in range(2)], False)
    gu_red = scatter_pieces([weight_grad(hidden_low, gu_grads[x]) for x in range(2)], True)

    hidden_grad = grad_two + mid_grad
    gain_one_grad = jnp.sum(hidden_grad * normed_one, axis=0)
    grad_one = norm_back(hidden_grad * gains[0], normed_one, inv_one)
    grad_one_low = grad_one.astype(LOW)
    gain_red = jnp.stack([gain_one_grad, gain_two_grad]).reshape(2, wide, block)
    gain_red = gain_red.transpose(1, 0, 2)
    gain_red = gain_red + swap(gain_red, "narrow", 2)
    for bit in wide_bits()[::-1]:
        half = gain_red.shape[0] // 2
        gain_red = gain_red[:half] + swap(gain_red[half:], "wide", bit)
    gain_red = gain_red[0]

    qk_grads, vo_grads, input_part = [], [], 0.0
    for x in range(2):
        context_grad = nn(grad_one_low, out_t[x]).astype(LOW)
        q, k, v, _, lse = saved[x]
        dqk, dv = attend_backward(q, k, v, lse, context_grad, cosine, sine)
        qk_grads.append(weight_grad(inputs, dqk))
        d_value = weight_grad(inputs, dv)
        d_out = weight_grad(grad_one_low, context[x])
        vo_grads.append([jnp.concatenate(p, axis=1) for p in zip(d_value, d_out)])
        qk_full = jnp.concatenate(qk[x], axis=0)
        v_full = jnp.concatenate([p[:, :cols] for p in vo[x]], axis=0)
        input_part = input_part + nt(dqk, qk_full) + nt(dv, v_full)
    qk_red = scatter_pieces(qk_grads, True)
    vo_red = scatter_pieces(vo_grads, False)

    theirs = lax.dynamic_slice_in_dim(input_part, (1 - core) * rows, rows, axis=0).astype(LOW)
    input_grad = own_rows(grad_one) + own_rows(input_part) + swap(theirs, "narrow", 1).astype(FULL)
    input_grad = lax.dot_general(
        input_grad, mover.astype(FULL), (((1,), (1,)), ((), ())),
        precision=lax.Precision.HIGHEST, preferred_element_type=FULL,
    )

    square = sum(jnp.sum(g * g) for g in (qk_red, vo_red, gu_red, down_red))
    square = square + jnp.where(narrow == 0, jnp.sum(gain_red * gain_red), 0.0)
    total = tree_sum(jnp.full((1, 128), square, FULL), "narrow")
    total = tree_sum(total, "wide")[0, 0]
    grad_norm = jnp.sqrt(total)
    all_tokens = rows * wide * lax.axis_size("narrow")
    clip = 0.02 * math.sqrt(all_tokens * (4 * D * D + 3 * D * FF + 2 * D))
    ratio = clip / jnp.maximum(grad_norm, clip)
    attend_red = jnp.stack([qk_red[:, :cols], qk_red[:, cols:], vo_red[:, :cols]])
    output_red = vo_red[:, cols:].T
    gated_red = jnp.stack([gu_red[:, :hid], gu_red[:, hid:]])
    new_attend = adam_update(
        attend_weight, attend_first, attend_second, attend_red, ratio, D ** (-0.5), WEIGHT_DECAY
    )
    new_output = adam_update(
        output_weight, output_first, output_second, output_red, ratio,
        max(D // 64, 1) ** (-0.5), WEIGHT_DECAY,
    )
    new_gated = adam_update(
        gated_weight, gated_first, gated_second, gated_red, ratio, D ** (-0.5), WEIGHT_DECAY
    )
    new_down = adam_update(
        down_weight, down_first, down_second, down_red.T, ratio, FF ** (-0.5), WEIGHT_DECAY
    )
    new_gains = adam_update(norm_gains, gains_first, gains_second, gain_red, ratio, 0.4, 0.0)
    return (
        layer_output, input_grad, grad_norm,
        *new_attend, *new_output, *new_gated, *new_down, *new_gains,
    )


def solution(mesh):
    rows = P(("wide", "narrow"), None)
    stacked = P(None, "wide", "narrow")
    turned = P("narrow", "wide")
    gains = P(None, "wide")
    params = (stacked,) * 3 + (turned,) * 3 + (stacked,) * 3 + (turned,) * 3 + (gains,) * 3
    return jax.shard_map(
        per_device,
        mesh=mesh,
        in_specs=(rows, rows) + params,
        out_specs=(rows, rows, P()) + params,
        check_vma=False,
    )
```

```python
import functools
import math

import jax
import jax.numpy as jnp
from jax import lax
from jax.experimental import pallas as pl
from jax.experimental.pallas import tpu as pltpu
from jax.sharding import PartitionSpec as P

D = 768
HD = 64
FF = 2048
L = 1024
ADAM_STEP = 5

EPSILON = 1e-05
WEIGHT_DECAY = 0.1
AVERAGING = 0.5

LOW = jnp.bfloat16
FULL = jnp.float32
QB = 256
MASKED = -1e30


def swap(value, axis, bit):
    size = lax.axis_size(axis)
    return lax.ppermute(value, axis, [(i, i ^ bit) for i in range(size)])


def wide_bits():
    top = lax.axis_size("wide").bit_length() - 1
    return [1 << b for b in range(top - 1, -1, -1)]


def block_masks():
    masks = [0]
    for bit in wide_bits():
        masks = masks + [m ^ bit for m in masks]
    return masks


def after(value, *done):
    return lax.optimization_barrier((value, done))[0]


def widen(held, bits):
    for bit in bits:
        held = jnp.concatenate([held, swap(held, "wide", bit)], axis=0)
    return held


def add(kept, received):
    return kept.astype(FULL) + received.astype(FULL)


def narrow_down(held, bits):
    for bit in bits:
        half = held.shape[0] // 2
        held = add(held[:half], swap(held[half:].astype(LOW), "wide", bit))
    return held


def tree_sum(value, axis):
    bits = [1 << b for b in range(lax.axis_size(axis).bit_length() - 1)]
    for bit in bits:
        value = value + swap(value, axis, bit)
    return value


def turn(value, cosine, sine, sign):
    width = value.shape[1]
    lane = lax.broadcasted_iota(jnp.int32, value.shape, 1) % HD
    other = jnp.where(
        lane < HD // 2,
        pltpu.roll(value, width - HD // 2, 1),
        pltpu.roll(value, HD // 2, 1),
    )
    reps = width // 128
    return value * jnp.concatenate([cosine] * reps, axis=1) + sign * other * jnp.concatenate(
        [sine] * reps, axis=1
    )


def nn(a, b):
    return lax.dot_general(a, b, (((1,), (0,)), ((), ())), preferred_element_type=FULL)


def nt(a, b):
    return lax.dot_general(a, b, (((1,), (1,)), ((), ())), preferred_element_type=FULL)


def diagonal(scores):
    key = lax.broadcasted_iota(jnp.int32, scores.shape, 0)
    query = lax.broadcasted_iota(jnp.int32, scores.shape, 1)
    return jnp.where(key <= query, scores, MASKED)


def flip(value):
    return value.astype(FULL).T


def attend_kernel(
    rows_ref, qka_ref, qkb_ref, voa_ref, vob_ref, cos_ref, sin_ref,
    q_ref, k_ref, v_ref, ctx_ref, lse_ref, hold,
):
    heads = q_ref.shape[0]
    width = heads * HD
    half = qka_ref.shape[0]

    def project(i, carry):
        rows = pl.ds(pl.multiple_of(i * QB, QB), QB)
        first, second = rows_ref[rows, :half], rows_ref[rows, half:]
        pair = nn(first, qka_ref[...]) + nn(second, qkb_ref[...])
        pair = turn(pair, cos_ref[rows, :], sin_ref[rows, :], 1.0)
        value = nn(first, voa_ref[:, :width]) + nn(second, vob_ref[:, :width])
        for h in range(heads):
            q_ref[h, rows, :] = (pair[:, h * HD : (h + 1) * HD] * (HD**-0.5)).astype(LOW)
            k_ref[h, rows, :] = pair[:, width + h * HD : width + (h + 1) * HD].astype(LOW)
            v_ref[h, rows, :] = value[:, h * HD : (h + 1) * HD].astype(LOW)
        return carry

    lax.fori_loop(0, L // QB, project, 0)

    def head(h, carry):
        turned = flip(v_ref[h]).astype(LOW)
        for i in range(L // QB):
            lo, hi = i * QB, (i + 1) * QB
            query = q_ref[h, lo:hi, :]
            diag = diagonal(nt(k_ref[h, lo:hi, :], query))
            peak = jnp.max(diag, axis=0, keepdims=True)
            if i:
                body = nt(k_ref[h, :lo, :], query)
                peak = jnp.maximum(peak, jnp.max(body, axis=0, keepdims=True))
            weight = jnp.exp(diag - peak)
            total = jnp.sum(weight, axis=0, keepdims=True)
            out = nn(turned[:, lo:hi], weight.astype(LOW))
            if i:
                weight = jnp.exp(body - peak)
                total = total + jnp.sum(weight, axis=0, keepdims=True)
                out = out + nn(turned[:, :lo], weight.astype(LOW))
            lse_ref[h, :, lo:hi] = peak + jnp.log(total)
            hold[h, lo:hi, :] = (out / total).T.astype(LOW)
        return carry

    lax.fori_loop(0, heads, head, 0)
    for h in range(heads):
        ctx_ref[:, h * HD : (h + 1) * HD] = hold[h]


def whole(array):
    zero = (0,) * array.ndim
    return pl.BlockSpec(array.shape, lambda *_: zero)


def columns(piece):
    if not isinstance(piece, tuple):
        return piece, whole(piece)
    array, width, j = piece
    return array, pl.BlockSpec((array.shape[0], width), lambda *_: (0, j))


def width_of(piece):
    return piece[1] if isinstance(piece, tuple) else piece.shape[1]


def attend_forward(rows, qk, vo, cosine, sine):
    heads = width_of(qk[0]) // 2 // HD
    headed = jax.ShapeDtypeStruct((heads, L, HD), LOW)
    outs = (
        headed, headed, headed,
        jax.ShapeDtypeStruct((L, heads * HD), LOW),
        jax.ShapeDtypeStruct((heads, 1, L), FULL),
    )
    args, specs = zip(*[columns(p) for p in (rows, *qk, *vo, cosine, sine)])
    return pl.pallas_call(
        attend_kernel,
        grid=(1,),
        in_specs=list(specs),
        out_specs=[whole(o) for o in outs],
        out_shape=outs,
        scratch_shapes=[pltpu.VMEM((heads, L, HD), LOW)],
        compiler_params=pltpu.CompilerParams(vmem_limit_bytes=40 << 20),
        cost_estimate=pl.CostEstimate(
            flops=8 * 10**9, bytes_accessed=8 << 20, transcendentals=2 << 20
        ),
        name="attend_forward",
    )(*args)


def attend_back_kernel(
    q_ref, k_ref, v_ref, lse_ref, dctx_ref, cos_ref, sin_ref,
    dqk_ref, dv_ref, dctx, dqk, dk_sum, dv_sum,
):
    heads = q_ref.shape[0]
    width = heads * HD
    for h in range(heads):
        dctx[h] = dctx_ref[:, h * HD : (h + 1) * HD]

    def head(h, carry):
        turned = flip(k_ref[h]).astype(LOW)
        for i in range(L // QB):
            lo, hi = i * QB, (i + 1) * QB
            query, back = q_ref[h, lo:hi, :], dctx[h, lo:hi, :]
            lse = lse_ref[h, :, lo:hi]
            prob = jnp.exp(diagonal(nt(k_ref[h, lo:hi, :], query)) - lse)
            grad = nt(v_ref[h, lo:hi, :], back)
            inner = jnp.sum(prob * grad, axis=0, keepdims=True)
            if i:
                prob_body = jnp.exp(nt(k_ref[h, :lo, :], query) - lse)
                grad_body = nt(v_ref[h, :lo, :], back)
                inner = inner + jnp.sum(prob_body * grad_body, axis=0, keepdims=True)
            score = (prob * (grad - inner)).astype(LOW)
            dv_sum[h, lo:hi, :] = nn(prob.astype(LOW), back)
            dk_sum[h, lo:hi, :] = nn(score, query)
            dquery = nn(turned[:, lo:hi], score)
            if i:
                score = (prob_body * (grad_body - inner)).astype(LOW)
                dv_sum[h, :lo, :] += nn(prob_body.astype(LOW), back)
                dk_sum[h, :lo, :] += nn(score, query)
                dquery = dquery + nn(turned[:, :lo], score)
            dqk[h, lo:hi, :] = (dquery * (HD**-0.5)).T
        return carry

    lax.fori_loop(0, heads, head, 0)

    def finish(i, carry):
        rows = pl.ds(pl.multiple_of(i * QB, QB), QB)
        pair = jnp.concatenate(
            [dqk[h, rows, :] for h in range(heads)] + [dk_sum[h, rows, :] for h in range(heads)],
            axis=1,
        )
        dqk_ref[rows, :] = turn(pair, cos_ref[rows, :], sin_ref[rows, :], -1.0).astype(LOW)
        dv_ref[rows, :] = jnp.concatenate(
            [dv_sum[h, rows, :] for h in range(heads)], axis=1
        ).astype(LOW)
        return carry

    lax.fori_loop(0, L // QB, finish, 0)


def attend_backward(q, k, v, lse, dctx, cosine, sine):
    heads = q.shape[0]
    return pl.pallas_call(
        attend_back_kernel,
        out_shape=(
            jax.ShapeDtypeStruct((L, 2 * heads * HD), LOW),
            jax.ShapeDtypeStruct((L, heads * HD), LOW),
        ),
        scratch_shapes=[
            pltpu.VMEM((heads, L, HD), LOW),
            pltpu.VMEM((heads, L, HD), FULL),
            pltpu.VMEM((heads, L, HD), FULL),
            pltpu.VMEM((heads, L, HD), FULL),
        ],
        compiler_params=pltpu.CompilerParams(vmem_limit_bytes=40 << 20),
        cost_estimate=pl.CostEstimate(
            flops=9 * 10**9, bytes_accessed=8 << 20, transcendentals=2 << 20
        ),
        name="attend_backward",
    )(q, k, v, lse, dctx, cosine, sine)


def by_rows(kernel, name, flops, row_args, fixed, outs, sums=0):
    specs = [pl.BlockSpec((QB, r.shape[1]), lambda i: (i, 0)) for r in row_args]
    held, held_specs = zip(*[columns(p) for p in fixed])
    shapes = [jax.ShapeDtypeStruct((L, w), t) for w, t in outs]
    out_specs = [pl.BlockSpec((QB, w), lambda i: (i, 0)) for w, _ in outs]
    shapes += [jax.ShapeDtypeStruct((1, D), FULL)] * sums
    out_specs += [pl.BlockSpec((1, D), lambda i: (0, 0))] * sums
    return pl.pallas_call(
        kernel,
        grid=(L // QB,),
        in_specs=specs + list(held_specs),
        out_specs=out_specs,
        out_shape=shapes,
        compiler_params=pltpu.CompilerParams(vmem_limit_bytes=48 << 20),
        cost_estimate=pl.CostEstimate(
            flops=int(flops), bytes_accessed=16 << 20, transcendentals=1 << 20
        ),
        name=name,
    )(*row_args, *held)


def rms_scale(residual):
    return lax.rsqrt(jnp.mean(residual * residual, axis=1, keepdims=True) + EPSILON)


def norm_back(scaled, normed, inv):
    return inv * (scaled - normed * jnp.mean(scaled * normed, axis=1, keepdims=True))


def column_sum(sum_ref, value):
    @pl.when(pl.program_id(0) == 0)
    def _():
        sum_ref[...] = jnp.zeros_like(sum_ref)

    sum_ref[...] += jnp.sum(value, axis=0, keepdims=True)


def project_kernel(one_ref, two_ref, voa_ref, vob_ref, voc_ref, vod_ref, out_ref):
    width = one_ref.shape[1]
    half = voa_ref.shape[0]
    one, two = one_ref[...], two_ref[...]
    out_ref[:, :half] = (nt(one, voa_ref[:, width:]) + nt(two, voc_ref[:, width:])).astype(LOW)
    out_ref[:, half:] = (nt(one, vob_ref[:, width:]) + nt(two, vod_ref[:, width:])).astype(LOW)


def gate_up(hidden, ga_ref, gb_ref, ua_ref, ub_ref, gate_ref, up_ref, act_ref):
    half = ga_ref.shape[0]
    first, second = hidden[:, :half], hidden[:, half:]
    gate = nn(first, ga_ref[...]) + nn(second, gb_ref[...])
    up = nn(first, ua_ref[...]) + nn(second, ub_ref[...])
    gate_ref[...] = gate
    up_ref[...] = up
    act_ref[...] = (gate * jax.nn.sigmoid(gate) * up).astype(LOW)


def enter_kernel(
    rows_ref, mine_ref, theirs_ref, gain_ref, ga_ref, gb_ref, ua_ref, ub_ref,
    normed_ref, inv_ref, hidden_ref, gate_ref, up_ref, act_ref,
):
    residual = rows_ref[...].astype(FULL) + add(mine_ref[...], theirs_ref[...])
    inv = rms_scale(residual)
    normed = residual * inv
    hidden = (normed * gain_ref[...]).astype(LOW)
    normed_ref[...] = normed
    inv_ref[...] = inv
    hidden_ref[...] = hidden
    gate_up(hidden, ga_ref, gb_ref, ua_ref, ub_ref, gate_ref, up_ref, act_ref)


def more_kernel(hidden_ref, ga_ref, gb_ref, ua_ref, ub_ref, gate_ref, up_ref, act_ref):
    gate_up(hidden_ref[...], ga_ref, gb_ref, ua_ref, ub_ref, gate_ref, up_ref, act_ref)


def down_kernel(one_ref, two_ref, da_ref, db_ref, dc_ref, dd_ref, out_ref):
    half = da_ref.shape[0]
    one, two = one_ref[...], two_ref[...]
    out_ref[:, :half] = (nt(one, da_ref[...]) + nt(two, dc_ref[...])).astype(LOW)
    out_ref[:, half:] = (nt(one, db_ref[...]) + nt(two, dd_ref[...])).astype(LOW)


def back_kernel(
    normed_ref, mine_ref, theirs_ref, up_rows_ref, gate1_ref, up1_ref, gate2_ref, up2_ref,
    gain1_ref, gain2_ref, da_ref, db_ref, dc_ref, dd_ref,
    ga_ref, gb_ref, ua_ref, ub_ref, gc_ref, gd_ref, uc_ref, ud_ref,
    out_ref, grad_ref, low_ref, gg1_ref, ug1_ref, gg2_ref, ug2_ref, mid_ref, sum_ref,
):
    half = da_ref.shape[0]
    residual = normed_ref[...] * gain1_ref[...] + add(mine_ref[...], theirs_ref[...])
    inv = rms_scale(residual)
    normed = residual * inv
    gain = gain2_ref[...]
    out_ref[...] = (normed * gain).astype(LOW)
    upstream = up_rows_ref[...].astype(FULL)
    column_sum(sum_ref, upstream * normed)
    grad = norm_back(upstream * gain, normed, inv)
    low = grad.astype(LOW)
    grad_ref[...] = grad
    low_ref[...] = low
    first, second = low[:, :half], low[:, half:]

    def hidden_grads(da_ref, db_ref, gate_ref, up_ref, gg_ref, ug_ref):
        act_grad = nn(first, da_ref[...]) + nn(second, db_ref[...])
        gate = gate_ref[...]
        sig = jax.nn.sigmoid(gate)
        gg = (act_grad * up_ref[...] * (sig * (1.0 + gate * (1.0 - sig)))).astype(LOW)
        ug = (act_grad * (gate * sig)).astype(LOW)
        gg_ref[...] = gg
        ug_ref[...] = ug
        return gg, ug

    gg1, ug1 = hidden_grads(da_ref, db_ref, gate1_ref, up1_ref, gg1_ref, ug1_ref)
    gg2, ug2 = hidden_grads(dc_ref, dd_ref, gate2_ref, up2_ref, gg2_ref, ug2_ref)
    mid_ref[:, :half] = (
        nt(gg1, ga_ref[...]) + nt(ug1, ua_ref[...]) + nt(gg2, gc_ref[...]) + nt(ug2, uc_ref[...])
    ).astype(LOW)
    mid_ref[:, half:] = (
        nt(gg1, gb_ref[...]) + nt(ug1, ub_ref[...]) + nt(gg2, gd_ref[...]) + nt(ug2, ud_ref[...])
    ).astype(LOW)


def leave_kernel(
    grad_two_ref, mine_ref, theirs_ref, normed_ref, inv_ref,
    gain_ref, voa_ref, vob_ref, voc_ref, vod_ref,
    grad_ref, low_ref, ctx1_ref, ctx2_ref, sum_ref,
):
    half = voa_ref.shape[0]
    width = ctx1_ref.shape[1]
    hidden_grad = grad_two_ref[...] + add(mine_ref[...], theirs_ref[...])
    normed = normed_ref[...]
    column_sum(sum_ref, hidden_grad * normed)
    grad = norm_back(hidden_grad * gain_ref[...], normed, inv_ref[...])
    low = grad.astype(LOW)
    grad_ref[...] = grad
    low_ref[...] = low
    first, second = low[:, :half], low[:, half:]
    ctx1_ref[...] = (nn(first, voa_ref[:, width:]) + nn(second, vob_ref[:, width:])).astype(LOW)
    ctx2_ref[...] = (nn(first, voc_ref[:, width:]) + nn(second, vod_ref[:, width:])).astype(LOW)


def input_kernel(
    qk1_ref, v1_ref, qk2_ref, v2_ref,
    qka_ref, qkb_ref, qkc_ref, qkd_ref, voa_ref, vob_ref, voc_ref, vod_ref,
    full_ref, low_ref,
):
    half = qka_ref.shape[0]
    width = v1_ref.shape[1]
    qk1, v1, qk2, v2 = qk1_ref[...], v1_ref[...], qk2_ref[...], v2_ref[...]
    first = (
        nt(qk1, qka_ref[...]) + nt(v1, voa_ref[:, :width])
        + nt(qk2, qkc_ref[...]) + nt(v2, voc_ref[:, :width])
    )
    second = (
        nt(qk1, qkb_ref[...]) + nt(v1, vob_ref[:, :width])
        + nt(qk2, qkd_ref[...]) + nt(v2, vod_ref[:, :width])
    )
    full_ref[:, :half] = first
    full_ref[:, half:] = second
    low_ref[:, :half] = first.astype(LOW)
    low_ref[:, half:] = second.astype(LOW)


def rope_tables():
    half = HD // 2
    lane = jnp.arange(128) % HD
    freq = jnp.exp(-jnp.log(10000.0) * (lane % half).astype(FULL) / half)
    angle = jnp.arange(L, dtype=FULL)[:, None] * freq[None, :]
    return jnp.cos(angle), jnp.where(lane < half, -1.0, 1.0)[None, :] * jnp.sin(angle)


def adam_update(weight, first, second, grad, ratio, rate, decay):
    clipped = grad * ratio
    first_new = AVERAGING * first + (1.0 - AVERAGING) * clipped
    second_new = AVERAGING * second + (1.0 - AVERAGING) * clipped * clipped
    correction = 1.0 - AVERAGING**ADAM_STEP
    step = first_new / correction / (jnp.sqrt(second_new / correction) + 1e-08)
    return (weight - rate * (step + decay * weight), first_new, second_new)


def tn(rows, grads):
    out = lax.dot_general(rows, grads, (((0,), (0,)), ((), ())), preferred_element_type=FULL)
    return out.astype(LOW)


def per_device(
    layer_input, layer_cotangent,
    attend_weight, attend_first, attend_second,
    output_weight, output_first, output_second,
    gated_weight, gated_first, gated_second,
    down_weight, down_first, down_second,
    norm_gains, gains_first, gains_second,
):
    rows = layer_input.shape[0]
    wide = lax.axis_size("wide")
    block = D // wide
    me = lax.axis_index("wide")
    narrow = lax.axis_index("narrow")
    core = narrow % 2
    cols = attend_weight.shape[2]

    bits = wide_bits()
    near = bits[:-1]
    half = D // 2
    hid = down_weight.shape[0]

    attend_low = attend_weight.astype(LOW)
    att = jnp.concatenate(
        [attend_low[0], attend_low[1], attend_low[2], output_weight.T.astype(LOW)], axis=1
    )
    gu = jnp.concatenate([gated_weight[0], gated_weight[1]], axis=1).astype(LOW)
    down = down_weight.T.astype(LOW)

    order = me ^ jnp.array(block_masks(), jnp.int32)
    source = (order[:, None] * block + jnp.arange(block)[None, :]).reshape(1, D)
    mover = (lax.broadcasted_iota(jnp.int32, (D, D), 0) == source).astype(LOW)

    def whole_sequence(own):
        moved = jnp.dot(own, mover, preferred_element_type=FULL).astype(LOW)
        received = swap(moved, "narrow", 1)
        return jnp.where(
            core == 0,
            jnp.concatenate([moved, received], axis=0),
            jnp.concatenate([received, moved], axis=0),
        )

    def own_rows(value):
        return lax.dynamic_slice_in_dim(value, core * rows, rows, axis=0)

    first = widen(att, near[:1])
    gu = widen(after(gu, first), near[:1])
    att = widen(first, near[1:])
    att_y = swap(att, "wide", 1)
    att_x = swap(att, "narrow", 2)
    gu = widen(after(gu, att), near[1:])
    down = widen(after(down, att), near[:1])
    gains = norm_gains.astype(LOW).astype(FULL)[None]
    gains = widen(after(gains, att), bits)
    gains = gains.transpose(1, 0, 2).reshape(2, 1, D)
    inputs = whole_sequence(layer_input)
    upstream = whole_sequence(layer_cotangent)
    cosine, sine = rope_tables()

    inputs, att, att_y, att_x, gu, down, gains, upstream, cosine, sine = lax.optimization_barrier(
        (inputs, att, att_y, att_x, gu, down, gains, upstream, cosine, sine)
    )
    pair = 2 * cols
    qk_corner = swap(att_y[:, :pair], "narrow", 2)
    vo_corner = swap(att_x[:, pair:], "wide", 1)
    gu_y = swap(gu, "wide", 1)
    gu_x = swap(gu, "narrow", 2)
    down = widen(down, near[1:])
    qk = [[(att, pair, 0), (att_y, pair, 0)], [(att_x, pair, 0), qk_corner]]
    vo = [[(att, pair, 1), (att_y, pair, 1)], [(att_x, pair, 1), vo_corner]]
    saved = [attend_forward(inputs, qk[0], vo[0], cosine, sine)]
    second_in = after(inputs, saved[0][3], down)
    saved.append(attend_forward(second_in, qk[1], vo[1], cosine, sine))
    context = [s[3] for s in saved]

    gu_y, gu_x, context, down = lax.optimization_barrier((gu_y, gu_x, context, down))
    gate_corner = swap(gu_y[:, :hid], "narrow", 2)
    up_corner = swap(gu_x[:, hid:], "wide", 1)
    down_y = swap(down, "wide", 1)
    down_x = swap(down, "narrow", 2)
    gate_w = [[(gu, hid, 0), (gu_y, hid, 0)], [(gu_x, hid, 0), gate_corner]]
    up_w = [[(gu, hid, 1), (gu_y, hid, 1)], [(gu_x, hid, 1), up_corner]]
    (attn_part,) = by_rows(
        project_kernel, "project", 1.3e9, context, vo[0] + vo[1], [(D, LOW)]
    )
    attn_other = swap(attn_part, "narrow", 1)
    flow = [(hid, FULL), (hid, FULL), (hid, LOW)]
    normed_one, inv_one, hidden_low, gate1, up1, act1 = by_rows(
        enter_kernel, "enter", 2e9, [inputs, attn_part, attn_other],
        [gains[0], *gate_w[0], *up_w[0]], [(D, FULL), (1, FULL), (D, LOW)] + flow,
    )
    down_y, down_x, hidden_low = lax.optimization_barrier((down_y, down_x, hidden_low))
    down_corner = swap(down_y, "narrow", 2)
    gate2, up2, act2 = by_rows(
        more_kernel, "more", 2e9, [hidden_low], [*gate_w[1], *up_w[1]], flow
    )
    down_w = [down, down_y, down_x, down_corner]
    (ffn_part,) = by_rows(down_kernel, "down", 2e9, [act1, act2], down_w, [(D, LOW)])
    ffn_other = swap(ffn_part, "narrow", 1)

    (
        layer_output, grad_two, grad_two_low, gg1, ug1, gg2, ug2, mid_part, gain_two_grad,
    ) = by_rows(
        back_kernel, "back", 6e9,
        [normed_one, ffn_part, ffn_other, upstream, gate1, up1, gate2, up2],
        [gains[0], gains[1], *down_w, *gate_w[0], *up_w[0], *gate_w[1], *up_w[1]],
        [(D, LOW), (D, FULL), (D, LOW)] + [(hid, LOW)] * 4 + [(D, LOW)], sums=1,
    )
    mid_other = swap(mid_part, "narrow", 1)
    ha, hb = hidden_low[:, :half], hidden_low[:, half:]
    down_x = swap(tn(grad_two_low, act2), "narrow", 2)
    gate_y1 = swap(tn(hb, gg1), "wide", 1)
    gate_y2 = swap(tn(hb, gg2), "wide", 1)
    up_x = swap(tn(hidden_low, ug2), "narrow", 2)
    down_own = tn(grad_two_low, act1)
    gate_1, gate_2 = tn(ha, gg1), tn(ha, gg2)
    up_own = tn(hidden_low, ug1)
    mid_part, mid_other, down_own, gate_1, gate_2, up_own = lax.optimization_barrier(
        (mid_part, mid_other, down_own, gate_1, gate_2, up_own)
    )
    grad_one, grad_one_low, dctx1, dctx2, gain_one_grad = by_rows(
        leave_kernel, "leave", 2e9, [grad_two, mid_part, mid_other, normed_one, inv_one],
        [gains[0], *vo[0], *vo[1]],
        [(D, FULL), (D, LOW), (context[0].shape[1], LOW), (context[0].shape[1], LOW)], sums=1,
    )

    q, k, v, _, lse = saved[1]
    dqk2, dv2 = attend_backward(q, k, v, lse, dctx2, cosine, sine)
    xa, xb = inputs[:, :half], inputs[:, half:]
    d_out2 = tn(grad_one_low, context[1])
    vo2 = jnp.concatenate([tn(inputs, dv2), d_out2], axis=1)
    vo_x = swap(vo2, "narrow", 2)
    qk_y2 = swap(tn(xb, dqk2), "wide", 1)
    qk_2 = tn(xa, dqk2)
    down_sum = add(down_own, down_x)
    gate_sum1, gate_sum2 = add(gate_1, gate_y1), add(gate_2, gate_y2)
    dctx1, down_sum, gate_sum1, gate_sum2, qk_2 = lax.optimization_barrier(
        (dctx1, down_sum, gate_sum1, gate_sum2, qk_2)
    )
    down_y = swap(down_sum[half:].astype(LOW), "wide", 1)
    gate_x = swap(gate_sum2.astype(LOW), "narrow", 2)
    q, k, v, _, lse = saved[0]
    dqk1, dv1 = attend_backward(q, k, v, lse, dctx1, cosine, sine)
    qk_y1 = swap(tn(xb, dqk1), "wide", 1)
    vo1 = jnp.concatenate([tn(inputs, dv1), tn(grad_one_low, context[0])], axis=1)
    qk_1 = tn(xa, dqk1)

    up_sum = add(up_own, up_x)
    up_y = swap(up_sum[half:].astype(LOW), "wide", 1)
    back = near[::-1]
    down_red = narrow_down(add(down_sum[:half], down_y), back)
    gate_red = narrow_down(add(gate_sum1, gate_x), back)
    vo_sum = add(vo1, vo_x)
    vo_y = swap(vo_sum[half:].astype(LOW), "wide", 1)
    qk_sum = add(qk_1, qk_y1)
    qk_x = swap(add(qk_2, qk_y2).astype(LOW), "narrow", 2)
    up_red = narrow_down(add(up_sum[:half], up_y), back)
    last = jnp.concatenate([add(qk_sum, qk_x), add(vo_sum[:half], vo_y)], axis=1)
    att_red = narrow_down(last, back)

    gain_red = jnp.concatenate([gain_one_grad, gain_two_grad], axis=0).reshape(2, wide, block)
    gain_red = gain_red.transpose(1, 0, 2)
    gain_red = gain_red + swap(gain_red, "narrow", 2)
    for bit in bits[::-1]:
        part = gain_red.shape[0] // 2
        gain_red = gain_red[:part] + swap(gain_red[part:], "wide", bit)
    gain_red = gain_red[0]

    part_full, part_low = by_rows(
        input_kernel, "inputs", 2e9, [dqk1, dv1, dqk2, dv2],
        qk[0] + qk[1] + vo[0] + vo[1], [(D, FULL), (D, LOW)],
    )
    theirs = lax.dynamic_slice_in_dim(part_low, (1 - core) * rows, rows, axis=0)
    input_grad = own_rows(grad_one) + own_rows(part_full) + swap(theirs, "narrow", 1).astype(FULL)
    input_grad = lax.dot_general(
        input_grad, mover.astype(FULL), (((1,), (1,)), ((), ())),
        precision=lax.Precision.HIGHEST, preferred_element_type=FULL,
    )
    layer_output = nt(own_rows(layer_output), mover).astype(LOW)

    square = sum(jnp.sum(g * g) for g in (att_red, gate_red, up_red, down_red))
    square = square + jnp.where(narrow == 0, jnp.sum(gain_red * gain_red), 0.0)
    total = tree_sum(jnp.full((1, 128), square, FULL), "narrow")
    total = tree_sum(total, "wide")[0, 0]
    grad_norm = jnp.sqrt(total)
    all_tokens = rows * wide * lax.axis_size("narrow")
    clip = 0.02 * math.sqrt(all_tokens * (4 * D * D + 3 * D * FF + 2 * D))
    ratio = clip / jnp.maximum(grad_norm, clip)
    attend_red = jnp.stack([att_red[:, k * cols : (k + 1) * cols] for k in range(3)])
    output_red = att_red[:, 3 * cols :].T
    gated_red = jnp.stack([gate_red, up_red])
    new_attend = adam_update(
        attend_weight, attend_first, attend_second, attend_red, ratio, D ** (-0.5), WEIGHT_DECAY
    )
    new_output = adam_update(
        output_weight, output_first, output_second, output_red, ratio,
        max(D // 64, 1) ** (-0.5), WEIGHT_DECAY,
    )
    new_gated = adam_update(
        gated_weight, gated_first, gated_second, gated_red, ratio, D ** (-0.5), WEIGHT_DECAY
    )
    new_down = adam_update(
        down_weight, down_first, down_second, down_red.T, ratio, FF ** (-0.5), WEIGHT_DECAY
    )
    new_gains = adam_update(norm_gains, gains_first, gains_second, gain_red, ratio, 0.4, 0.0)
    return (
        layer_output, input_grad, grad_norm,
        *new_attend, *new_output, *new_gated, *new_down, *new_gains,
    )


def solution(mesh):
    rows = P(("wide", "narrow"), None)
    stacked = P(None, "wide", "narrow")
    turned = P("narrow", "wide")
    gains = P(None, "wide")
    params = (stacked,) * 3 + (turned,) * 3 + (stacked,) * 3 + (turned,) * 3 + (gains,) * 3
    return jax.shard_map(
        per_device,
        mesh=mesh,
        in_specs=(rows, rows) + params,
        out_specs=(rows, rows, P()) + params,
        check_vma=False,
    )
```

```python
import functools
import math

import jax
import jax.numpy as jnp
from jax import lax
from jax.experimental import pallas as pl
from jax.experimental.pallas import tpu as pltpu
from jax.sharding import PartitionSpec as P

D = 768
HD = 64
FF = 2048
L = 1024
ADAM_STEP = 5

EPSILON = 1e-05
WEIGHT_DECAY = 0.1
AVERAGING = 0.5

LOW = jnp.bfloat16
FULL = jnp.float32
QB = 256
MASKED = -1e30


def swap(value, axis, bit):
    size = lax.axis_size(axis)
    return lax.ppermute(value, axis, [(i, i ^ bit) for i in range(size)])


def wide_bits():
    top = lax.axis_size("wide").bit_length() - 1
    return [1 << b for b in range(top - 1, -1, -1)]


def block_masks():
    masks = [0]
    for bit in wide_bits():
        masks = masks + [m ^ bit for m in masks]
    return masks


def after(value, *done):
    return lax.optimization_barrier((value, done))[0]


def widen(held, bits):
    for bit in bits:
        held = jnp.concatenate([held, swap(held, "wide", bit)], axis=0)
    return held


def add(kept, received):
    return kept.astype(FULL) + received.astype(FULL)


def narrow_down(held, bits):
    for bit in bits:
        half = held.shape[0] // 2
        held = add(held[:half], swap(held[half:].astype(LOW), "wide", bit))
    return held


def turn(value, cosine, sine, sign):
    width = value.shape[1]
    lane = lax.broadcasted_iota(jnp.int32, value.shape, 1) % HD
    other = jnp.where(
        lane < HD // 2,
        pltpu.roll(value, width - HD // 2, 1),
        pltpu.roll(value, HD // 2, 1),
    )
    reps = width // 128
    return value * jnp.concatenate([cosine] * reps, axis=1) + sign * other * jnp.concatenate(
        [sine] * reps, axis=1
    )


def nn(a, b):
    return lax.dot_general(a, b, (((1,), (0,)), ((), ())), preferred_element_type=FULL)


def nt(a, b):
    return lax.dot_general(a, b, (((1,), (1,)), ((), ())), preferred_element_type=FULL)


def diagonal(scores):
    key = lax.broadcasted_iota(jnp.int32, scores.shape, 0)
    query = lax.broadcasted_iota(jnp.int32, scores.shape, 1)
    return jnp.where(key <= query, scores, MASKED)


def flip(value):
    return value.astype(FULL).T


def attend_kernel(
    rows_ref, qka_ref, qkb_ref, voa_ref, vob_ref, cos_ref, sin_ref,
    q_ref, k_ref, v_ref, ctx_ref, lse_ref, hold,
):
    heads = q_ref.shape[0]
    width = heads * HD
    half = qka_ref.shape[0]

    def project(i, carry):
        rows = pl.ds(pl.multiple_of(i * QB, QB), QB)
        first, second = rows_ref[rows, :half], rows_ref[rows, half:]
        pair = nn(first, qka_ref[...]) + nn(second, qkb_ref[...])
        pair = turn(pair, cos_ref[rows, :], sin_ref[rows, :], 1.0)
        value = nn(first, voa_ref[:, :width]) + nn(second, vob_ref[:, :width])
        for h in range(heads):
            q_ref[h, rows, :] = (pair[:, h * HD : (h + 1) * HD] * (HD**-0.5)).astype(LOW)
            k_ref[h, rows, :] = pair[:, width + h * HD : width + (h + 1) * HD].astype(LOW)
            v_ref[h, rows, :] = value[:, h * HD : (h + 1) * HD].astype(LOW)
        return carry

    lax.fori_loop(0, L // QB, project, 0)

    def head(h, carry):
        turned = flip(v_ref[h]).astype(LOW)
        for i in range(L // QB):
            lo, hi = i * QB, (i + 1) * QB
            query = q_ref[h, lo:hi, :]
            diag = diagonal(nt(k_ref[h, lo:hi, :], query))
            peak = jnp.max(diag, axis=0, keepdims=True)
            if i:
                body = nt(k_ref[h, :lo, :], query)
                peak = jnp.maximum(peak, jnp.max(body, axis=0, keepdims=True))
            weight = jnp.exp(diag - peak)
            total = jnp.sum(weight, axis=0, keepdims=True)
            out = nn(turned[:, lo:hi], weight.astype(LOW))
            if i:
                weight = jnp.exp(body - peak)
                total = total + jnp.sum(weight, axis=0, keepdims=True)
                out = out + nn(turned[:, :lo], weight.astype(LOW))
            lse_ref[h, :, lo:hi] = peak + jnp.log(total)
            hold[h, lo:hi, :] = (out / total).T.astype(LOW)
        return carry

    lax.fori_loop(0, heads, head, 0)
    for h in range(heads):
        ctx_ref[:, h * HD : (h + 1) * HD] = hold[h]


def whole(array):
    zero = (0,) * array.ndim
    return pl.BlockSpec(array.shape, lambda *_: zero)


def columns(piece):
    if not isinstance(piece, tuple):
        return piece, whole(piece)
    array, width, j = piece
    return array, pl.BlockSpec((array.shape[0], width), lambda *_: (0, j))


def width_of(piece):
    return piece[1] if isinstance(piece, tuple) else piece.shape[1]


def attend_forward(rows, qk, vo, cosine, sine):
    heads = width_of(qk[0]) // 2 // HD
    headed = jax.ShapeDtypeStruct((heads, L, HD), LOW)
    outs = (
        headed, headed, headed,
        jax.ShapeDtypeStruct((L, heads * HD), LOW),
        jax.ShapeDtypeStruct((heads, 1, L), FULL),
    )
    args, specs = zip(*[columns(p) for p in (rows, *qk, *vo, cosine, sine)])
    return pl.pallas_call(
        attend_kernel,
        grid=(1,),
        in_specs=list(specs),
        out_specs=[whole(o) for o in outs],
        out_shape=outs,
        scratch_shapes=[pltpu.VMEM((heads, L, HD), LOW)],
        compiler_params=pltpu.CompilerParams(vmem_limit_bytes=24 << 20),
        cost_estimate=pl.CostEstimate(
            flops=8 * 10**9, bytes_accessed=8 << 20, transcendentals=2 << 20
        ),
        name="attend_forward",
    )(*args)


def attend_back_kernel(
    q_ref, k_ref, v_ref, lse_ref, dctx_ref, cos_ref, sin_ref,
    dqk_ref, dv_ref, dctx, dqk, dk_sum, dv_sum,
):
    heads = q_ref.shape[0]
    width = heads * HD
    for h in range(heads):
        dctx[h] = dctx_ref[:, h * HD : (h + 1) * HD]

    def head(h, carry):
        turned = flip(k_ref[h]).astype(LOW)
        for i in range(L // QB):
            lo, hi = i * QB, (i + 1) * QB
            query, back = q_ref[h, lo:hi, :], dctx[h, lo:hi, :]
            lse = lse_ref[h, :, lo:hi]
            prob = jnp.exp(diagonal(nt(k_ref[h, lo:hi, :], query)) - lse)
            grad = nt(v_ref[h, lo:hi, :], back)
            inner = jnp.sum(prob * grad, axis=0, keepdims=True)
            if i:
                prob_body = jnp.exp(nt(k_ref[h, :lo, :], query) - lse)
                grad_body = nt(v_ref[h, :lo, :], back)
                inner = inner + jnp.sum(prob_body * grad_body, axis=0, keepdims=True)
            score = (prob * (grad - inner)).astype(LOW)
            dv_sum[h, lo:hi, :] = nn(prob.astype(LOW), back)
            dk_sum[h, lo:hi, :] = nn(score, query)
            dquery = nn(turned[:, lo:hi], score)
            if i:
                score = (prob_body * (grad_body - inner)).astype(LOW)
                dv_sum[h, :lo, :] += nn(prob_body.astype(LOW), back)
                dk_sum[h, :lo, :] += nn(score, query)
                dquery = dquery + nn(turned[:, :lo], score)
            dqk[h, lo:hi, :] = (dquery * (HD**-0.5)).T
        return carry

    lax.fori_loop(0, heads, head, 0)

    def finish(i, carry):
        rows = pl.ds(pl.multiple_of(i * QB, QB), QB)
        pair = jnp.concatenate(
            [dqk[h, rows, :] for h in range(heads)] + [dk_sum[h, rows, :] for h in range(heads)],
            axis=1,
        )
        dqk_ref[rows, :] = turn(pair, cos_ref[rows, :], sin_ref[rows, :], -1.0).astype(LOW)
        dv_ref[rows, :] = jnp.concatenate(
            [dv_sum[h, rows, :] for h in range(heads)], axis=1
        ).astype(LOW)
        return carry

    lax.fori_loop(0, L // QB, finish, 0)


def attend_backward(q, k, v, lse, dctx, cosine, sine):
    heads = q.shape[0]
    return pl.pallas_call(
        attend_back_kernel,
        out_shape=(
            jax.ShapeDtypeStruct((L, 2 * heads * HD), LOW),
            jax.ShapeDtypeStruct((L, heads * HD), LOW),
        ),
        scratch_shapes=[
            pltpu.VMEM((heads, L, HD), LOW),
            pltpu.VMEM((heads, L, HD), FULL),
            pltpu.VMEM((heads, L, HD), FULL),
            pltpu.VMEM((heads, L, HD), FULL),
        ],
        compiler_params=pltpu.CompilerParams(vmem_limit_bytes=24 << 20),
        cost_estimate=pl.CostEstimate(
            flops=9 * 10**9, bytes_accessed=8 << 20, transcendentals=2 << 20
        ),
        name="attend_backward",
    )(q, k, v, lse, dctx, cosine, sine)


def held_once(array):
    return pl.BlockSpec(array.shape, lambda i: (0, 0), pipeline_mode=pl.Buffered(1))


def by_rows(kernel, name, flops, row_args, fixed, outs, sums=0, scratch=()):
    specs = [pl.BlockSpec((QB, r.shape[1]), lambda i: (i, 0)) for r in row_args]
    shapes = [jax.ShapeDtypeStruct((L, w), t) for w, t in outs]
    out_specs = [pl.BlockSpec((QB, w), lambda i: (i, 0)) for w, _ in outs]
    shapes += [jax.ShapeDtypeStruct((1, D), FULL)] * sums
    out_specs += [pl.BlockSpec((1, D), lambda i: (0, 0))] * sums
    return pl.pallas_call(
        kernel,
        grid=(L // QB,),
        in_specs=specs + [held_once(f) for f in fixed],
        out_specs=out_specs,
        out_shape=shapes,
        scratch_shapes=list(scratch),
        compiler_params=pltpu.CompilerParams(vmem_limit_bytes=30 << 20),
        cost_estimate=pl.CostEstimate(
            flops=int(flops), bytes_accessed=16 << 20, transcendentals=1 << 20
        ),
        name=name,
    )(*row_args, *fixed)


def rms_scale(residual):
    return lax.rsqrt(jnp.mean(residual * residual, axis=1, keepdims=True) + EPSILON)


def norm_back(scaled, normed, inv):
    return inv * (scaled - normed * jnp.mean(scaled * normed, axis=1, keepdims=True))


def column_sum(sum_ref, value):
    @pl.when(pl.program_id(0) == 0)
    def _():
        sum_ref[...] = jnp.zeros_like(sum_ref)

    sum_ref[...] += jnp.sum(value, axis=0, keepdims=True)


def heads_out(held_ref, refs):
    att_ref, y_ref, x_ref, corner_ref = refs
    width = held_ref.shape[2]

    @pl.when(pl.program_id(0) == 0)
    def _():
        for p, ref in enumerate((att_ref, y_ref, x_ref)):
            held_ref[p] = ref[:, 3 * width :]
        held_ref[3] = corner_ref[:, width:]


def project_kernel(one_ref, two_ref, att_ref, y_ref, x_ref, corner_ref, out_ref, held_ref):
    heads_out(held_ref, (att_ref, y_ref, x_ref, corner_ref))
    half = att_ref.shape[0]
    one, two = one_ref[...], two_ref[...]
    out_ref[:, :half] = (nt(one, held_ref[0]) + nt(two, held_ref[2])).astype(LOW)
    out_ref[:, half:] = (nt(one, held_ref[1]) + nt(two, held_ref[3])).astype(LOW)


def blocks(refs, x, y, kind):
    own_ref, y_ref, x_ref, low_ref, high_ref = refs
    hid = own_ref.shape[1] // 3
    if x and y:
        cut = hid // 2
        if kind == 0:
            return [low_ref[:, :hid]]
        if kind == 1:
            return [low_ref[:, hid:], high_ref[:, :cut]]
        return [high_ref[:, cut:]]
    ref = (x_ref if x else y_ref) if x or y else own_ref
    return [ref[:, kind * hid : (kind + 1) * hid]]


def onto(rows, parts):
    made = [nn(rows, p) for p in parts]
    return made[0] if len(made) == 1 else jnp.concatenate(made, axis=1)


def back_from(grads, parts):
    start, total = 0, 0.0
    for p in parts:
        total = total + nt(grads[:, start : start + p.shape[1]], p)
        start += p.shape[1]
    return total


def gate_up(hidden, refs, x, gate_ref, up_ref, act_ref):
    half = refs[0].shape[0]
    first, second = hidden[:, :half], hidden[:, half:]
    gate = onto(first, blocks(refs, x, 0, 0)) + onto(second, blocks(refs, x, 1, 0))
    up = onto(first, blocks(refs, x, 0, 1)) + onto(second, blocks(refs, x, 1, 1))
    gate_ref[...] = gate
    up_ref[...] = up
    act_ref[...] = (gate * jax.nn.sigmoid(gate) * up).astype(LOW)


def enter_kernel(
    rows_ref, mine_ref, theirs_ref, gain_ref, own_ref, y_ref,
    normed_ref, inv_ref, hidden_ref, gate_ref, up_ref, act_ref,
):
    residual = rows_ref[...].astype(FULL) + add(mine_ref[...], theirs_ref[...])
    inv = rms_scale(residual)
    normed = residual * inv
    hidden = (normed * gain_ref[...]).astype(LOW)
    normed_ref[...] = normed
    inv_ref[...] = inv
    hidden_ref[...] = hidden
    gate_up(hidden, (own_ref, y_ref, None, None, None), 0, gate_ref, up_ref, act_ref)


def rest_kernel(
    hidden_ref, act1_ref, own_ref, y_ref, x_ref, low_ref, high_ref,
    gate_ref, up_ref, act_ref, out_ref,
):
    refs = (own_ref, y_ref, x_ref, low_ref, high_ref)
    half = own_ref.shape[0]
    gate_up(hidden_ref[...], refs, 1, gate_ref, up_ref, act_ref)
    one, two = act1_ref[...], act_ref[...]
    for y in range(2):
        part = back_from(one, blocks(refs, 0, y, 2)) + back_from(two, blocks(refs, 1, y, 2))
        out_ref[:, y * half : (y + 1) * half] = part.astype(LOW)


def back_kernel(
    normed_ref, mine_ref, theirs_ref, up_rows_ref, gate1_ref, up1_ref, gate2_ref, up2_ref,
    gain1_ref, gain2_ref, own_ref, y_ref, x_ref, low_ref, high_ref,
    out_ref, grad_ref, grad_low_ref, gg_ref, ug_ref, mid_ref, sum_ref,
):
    refs = (own_ref, y_ref, x_ref, low_ref, high_ref)
    half, hid = own_ref.shape[0], gate1_ref.shape[1]
    residual = normed_ref[...] * gain1_ref[...] + add(mine_ref[...], theirs_ref[...])
    inv = rms_scale(residual)
    normed = residual * inv
    gain = gain2_ref[...]
    out_ref[...] = (normed * gain).astype(LOW)
    upstream = up_rows_ref[...].astype(FULL)
    column_sum(sum_ref, upstream * normed)
    grad = norm_back(upstream * gain, normed, inv)
    low = grad.astype(LOW)
    grad_ref[...] = grad
    grad_low_ref[...] = low
    first, second = low[:, :half], low[:, half:]
    grads = []
    for x, gate_ref, up_ref in ((0, gate1_ref, up1_ref), (1, gate2_ref, up2_ref)):
        act_grad = onto(first, blocks(refs, x, 0, 2)) + onto(second, blocks(refs, x, 1, 2))
        gate = gate_ref[...]
        sig = jax.nn.sigmoid(gate)
        gg = (act_grad * up_ref[...] * (sig * (1.0 + gate * (1.0 - sig)))).astype(LOW)
        ug = (act_grad * (gate * sig)).astype(LOW)
        gg_ref[:, x * hid : (x + 1) * hid] = gg
        ug_ref[:, x * hid : (x + 1) * hid] = ug
        grads.append((gg, ug))
    for y in range(2):
        total = 0.0
        for x in range(2):
            for kind in range(2):
                total = total + back_from(grads[x][kind], blocks(refs, x, y, kind))
        mid_ref[:, y * half : (y + 1) * half] = total.astype(LOW)


def leave_kernel(
    grad_two_ref, mine_ref, theirs_ref, normed_ref, inv_ref,
    gain_ref, att_ref, y_ref, x_ref, corner_ref,
    grad_ref, low_ref, ctx1_ref, ctx2_ref, sum_ref, held_ref,
):
    heads_out(held_ref, (att_ref, y_ref, x_ref, corner_ref))
    half = att_ref.shape[0]
    hidden_grad = grad_two_ref[...] + add(mine_ref[...], theirs_ref[...])
    normed = normed_ref[...]
    column_sum(sum_ref, hidden_grad * normed)
    grad = norm_back(hidden_grad * gain_ref[...], normed, inv_ref[...])
    low = grad.astype(LOW)
    grad_ref[...] = grad
    low_ref[...] = low
    first, second = low[:, :half], low[:, half:]
    ctx1_ref[...] = (nn(first, held_ref[0]) + nn(second, held_ref[1])).astype(LOW)
    ctx2_ref[...] = (nn(first, held_ref[2]) + nn(second, held_ref[3])).astype(LOW)


def input_kernel(
    qk1_ref, v1_ref, qk2_ref, v2_ref, att_ref, y_ref, x_ref, qk_corner_ref, vo_corner_ref,
    full_ref, low_ref,
):
    half = att_ref.shape[0]
    width = v1_ref.shape[1]
    qk1, v1, qk2, v2 = qk1_ref[...], v1_ref[...], qk2_ref[...], v2_ref[...]
    pair = 2 * width
    first = (
        nt(qk1, att_ref[:, :pair]) + nt(v1, att_ref[:, pair : pair + width])
        + nt(qk2, x_ref[:, :pair]) + nt(v2, x_ref[:, pair : pair + width])
    )
    second = (
        nt(qk1, y_ref[:, :pair]) + nt(v1, y_ref[:, pair : pair + width])
        + nt(qk2, qk_corner_ref[...]) + nt(v2, vo_corner_ref[:, :width])
    )
    full_ref[:, :half] = first
    full_ref[:, half:] = second
    low_ref[:, :half] = first.astype(LOW)
    low_ref[:, half:] = second.astype(LOW)


def rope_tables():
    half = HD // 2
    lane = jnp.arange(128) % HD
    freq = jnp.exp(-jnp.log(10000.0) * (lane % half).astype(FULL) / half)
    angle = jnp.arange(L, dtype=FULL)[:, None] * freq[None, :]
    return jnp.cos(angle), jnp.where(lane < half, -1.0, 1.0)[None, :] * jnp.sin(angle)


def adam_update(weight, first, second, grad, ratio, rate, decay):
    clipped = grad * ratio
    first_new = AVERAGING * first + (1.0 - AVERAGING) * clipped
    second_new = AVERAGING * second + (1.0 - AVERAGING) * clipped * clipped
    correction = 1.0 - AVERAGING**ADAM_STEP
    step = first_new / correction / (jnp.sqrt(second_new / correction) + 1e-08)
    return (weight - rate * (step + decay * weight), first_new, second_new)


def tn(rows, grads):
    out = lax.dot_general(rows, grads, (((0,), (0,)), ((), ())), preferred_element_type=FULL)
    return out.astype(LOW)


def per_device(
    layer_input, layer_cotangent,
    attend_weight, attend_first, attend_second,
    output_weight, output_first, output_second,
    gated_weight, gated_first, gated_second,
    down_weight, down_first, down_second,
    norm_gains, gains_first, gains_second,
):
    rows = layer_input.shape[0]
    wide = lax.axis_size("wide")
    block = D // wide
    me = lax.axis_index("wide")
    narrow = lax.axis_index("narrow")
    core = narrow % 2
    cols = attend_weight.shape[2]

    bits = wide_bits()
    near = bits[:-1]
    half = D // 2
    hid = down_weight.shape[0]

    bits = wide_bits()
    near = bits[:-1]
    half = D // 2
    hid = down_weight.shape[0]
    pair = 2 * cols

    attend_low = attend_weight.astype(LOW)
    att = jnp.concatenate(
        [attend_low[0], attend_low[1], attend_low[2], output_weight.T.astype(LOW)], axis=1
    )
    ffn = jnp.concatenate([gated_weight[0], gated_weight[1], down_weight.T], axis=1).astype(LOW)

    order = me ^ jnp.array(block_masks(), jnp.int32)
    source = (order[:, None] * block + jnp.arange(block)[None, :]).reshape(1, D)
    mover = (lax.broadcasted_iota(jnp.int32, (D, D), 0) == source).astype(LOW)

    def both_halves(mine, theirs):
        return jnp.where(
            core == 0,
            jnp.concatenate([mine, theirs], axis=0),
            jnp.concatenate([theirs, mine], axis=0),
        )

    def own_rows(value):
        return lax.dynamic_slice_in_dim(value, core * rows, rows, axis=0)

    first = widen(att, near[:1])
    gains = widen(norm_gains.astype(LOW).astype(FULL)[None], bits)
    moved_in = jnp.dot(layer_input, mover, preferred_element_type=FULL).astype(LOW)
    moved_up = jnp.dot(layer_cotangent, mover, preferred_element_type=FULL).astype(LOW)
    other_in = swap(moved_in, "narrow", 1)
    other_up = swap(moved_up, "narrow", 1)
    ffn = widen(after(ffn, first), near[:1])
    att = widen(first, near[1:])
    att, other_in, other_up, gains = lax.optimization_barrier((att, other_in, other_up, gains))
    att_y = swap(att, "wide", 1)
    att_x = swap(att, "narrow", 2)
    ffn = widen(after(ffn, att), near[1:])
    gains = gains.transpose(1, 0, 2).reshape(2, 1, D)
    inputs = both_halves(moved_in, other_in)
    upstream = both_halves(moved_up, other_up)
    cosine, sine = rope_tables()

    inputs, att, att_y, att_x, ffn, gains, upstream, cosine, sine = lax.optimization_barrier(
        (inputs, att, att_y, att_x, ffn, gains, upstream, cosine, sine)
    )
    qk_corner = swap(att_y[:, :pair], "narrow", 2)
    vo_corner = swap(att_x[:, pair:], "wide", 1)
    ffn_y = swap(ffn, "wide", 1)
    ffn_x = swap(ffn, "narrow", 2)
    qk = [[(att, pair, 0), (att_y, pair, 0)], [(att_x, pair, 0), qk_corner]]
    vo = [[(att, pair, 1), (att_y, pair, 1)], [(att_x, pair, 1), vo_corner]]
    saved = [attend_forward(inputs, qk[0], vo[0], cosine, sine)]
    second_in = after(inputs, saved[0][3])
    saved.append(attend_forward(second_in, qk[1], vo[1], cosine, sine))
    context = [s[3] for s in saved]

    ffn_y, ffn_x, context = lax.optimization_barrier((ffn_y, ffn_x, context))
    middle = ffn.shape[1] // 2
    ffn_low = swap(ffn_y[:, :middle], "narrow", 2)
    ffn_high = swap(ffn_x[:, middle:], "wide", 1)
    ffn_all = [ffn, ffn_y, ffn_x, ffn_low, ffn_high]
    att_out = [att, att_y, att_x, vo_corner]
    held = [pltpu.VMEM((4, half, cols), LOW)]
    (attn_part,) = by_rows(
        project_kernel, "project", 2e9, context, att_out, [(D, LOW)], scratch=held
    )
    attn_other = swap(attn_part, "narrow", 1)
    flow = [(hid, FULL), (hid, FULL), (hid, LOW)]
    normed_one, inv_one, hidden_low, gate1, up1, act1 = by_rows(
        enter_kernel, "enter", 4e9, [inputs, attn_part, attn_other],
        [gains[0], ffn, ffn_y], [(D, FULL), (1, FULL), (D, LOW)] + flow,
    )
    gate2, up2, act2, ffn_part = by_rows(
        rest_kernel, "rest", 5e9, [hidden_low, act1], ffn_all, flow + [(D, LOW)]
    )
    ffn_other = swap(ffn_part, "narrow", 1)

    layer_output, grad_two, grad_two_low, gg, ug, mid_part, gain_two_grad = by_rows(
        back_kernel, "back", 9e9,
        [normed_one, ffn_part, ffn_other, upstream, gate1, up1, gate2, up2],
        [gains[0], gains[1], *ffn_all],
        [(D, LOW), (D, FULL), (D, LOW), (2 * hid, LOW), (2 * hid, LOW), (D, LOW)], sums=1,
    )
    mid_other = swap(mid_part, "narrow", 1)
    down_x = swap(tn(grad_two_low, act2), "narrow", 2)
    gate_y = swap(tn(hidden_low[:, half:], gg), "wide", 1)
    up_send = tn(hidden_low, ug[:, hid:])
    down_own = tn(grad_two_low, act1)
    gate_own = tn(hidden_low[:, :half], gg)
    mid_part, mid_other, down_own, gate_own, up_send = lax.optimization_barrier(
        (mid_part, mid_other, down_own, gate_own, up_send)
    )
    grad_one, grad_one_low, dctx1, dctx2, gain_one_grad = by_rows(
        leave_kernel, "leave", 4e9, [grad_two, mid_part, mid_other, normed_one, inv_one],
        [gains[0], *att_out], [(D, FULL), (D, LOW), (cols, LOW), (cols, LOW)], sums=1, scratch=held,
    )

    down_x, gate_y, up_send, grad_one_low = lax.optimization_barrier(
        (down_x, gate_y, up_send, grad_one_low)
    )
    up_x = swap(up_send, "narrow", 2)
    down_sum, gate_sum = add(down_own, down_x), add(gate_own, gate_y)
    down_far, gate_far = down_sum[half:].astype(LOW), gate_sum[:, hid:].astype(LOW)
    down_y = swap(down_far, "wide", 1)
    gate_x = swap(gate_far, "narrow", 2)

    q, k, v, _, lse = saved[1]
    dqk2, dv2 = attend_backward(q, k, v, lse, after(dctx2, down_far, gate_far), cosine, sine)
    xa, xb = inputs[:, :half], inputs[:, half:]
    vo_send = jnp.concatenate([tn(inputs, dv2), tn(grad_one_low, context[1])], axis=1)
    vo_x = swap(vo_send, "narrow", 2)
    qk_send2 = tn(xb, dqk2)
    qk_y2 = swap(qk_send2, "wide", 1)
    back = near[::-1]
    early = jnp.concatenate([add(down_sum[:half], down_y), add(gate_sum[:, :hid], gate_x)], axis=1)
    q, k, v, _, lse = saved[0]
    dctx1, early, up_x = lax.optimization_barrier(
        (after(dctx1, vo_send, qk_send2), early, up_x)
    )
    up_sum = add(tn(hidden_low, ug[:, :hid]), up_x)
    up_far = up_sum[half:].astype(LOW)
    up_y = swap(up_far, "wide", 1)
    early_red = narrow_down(early, back)
    dqk1, dv1 = attend_backward(q, k, v, lse, after(dctx1, up_far), cosine, sine)
    qk_send1 = tn(xb, dqk1)
    qk_y1 = swap(qk_send1, "wide", 1)
    dqk1, dv1, qk_send1 = lax.optimization_barrier((dqk1, dv1, qk_send1))
    vo_sum = add(
        jnp.concatenate([tn(inputs, dv1), tn(grad_one_low, context[0])], axis=1), vo_x
    )
    vo_far = vo_sum[half:].astype(LOW)
    vo_y = swap(vo_far, "wide", 1)
    qk_far = add(tn(xa, dqk2), qk_y2).astype(LOW)
    qk_x = swap(qk_far, "narrow", 2)
    qk_sum = add(tn(xa, dqk1), qk_y1)
    part_full, part_low = by_rows(
        input_kernel, "inputs", 4e9, [after(dqk1, vo_far, qk_far), dv1, dqk2, dv2],
        [att, att_y, att_x, qk_corner, vo_corner], [(D, FULL), (D, LOW)],
    )
    up_red = narrow_down(add(up_sum[:half], up_y), back)
    last = jnp.concatenate([add(qk_sum, qk_x), add(vo_sum[:half], vo_y)], axis=1)
    att_red = narrow_down(last, back)

    theirs = lax.dynamic_slice_in_dim(part_low, (1 - core) * rows, rows, axis=0)
    input_grad = own_rows(grad_one) + own_rows(part_full) + swap(theirs, "narrow", 1).astype(FULL)
    input_grad = lax.dot_general(
        input_grad, mover.astype(FULL), (((1,), (1,)), ((), ())),
        precision=lax.Precision.HIGHEST, preferred_element_type=FULL,
    )
    layer_output = nt(own_rows(layer_output), mover).astype(LOW)

    gain_grads = lax.dot_general(
        jnp.concatenate([gain_one_grad, gain_two_grad], axis=0), mover.astype(FULL),
        (((1,), (1,)), ((), ())), precision=lax.Precision.HIGHEST, preferred_element_type=FULL,
    )

    square = jnp.sum(early_red * early_red) + jnp.sum(up_red * up_red)
    square = jnp.full((1, 128), square + jnp.sum(att_red * att_red), FULL)
    square = square + swap(square, "narrow", 1)
    message = jnp.concatenate([gain_grads.reshape(1, 2 * D), square], axis=1)
    message = message + swap(message, "narrow", 2)
    for bit in bits[::-1]:
        message = message + swap(message, "wide", bit)
    gain_sum = message[:, : 2 * D]
    total = message[0, 2 * D] + jnp.sum(gain_sum * gain_sum)
    gain_red = lax.dynamic_index_in_dim(gain_sum.reshape(2, wide, block), me, 1, keepdims=False)
    grad_norm = jnp.sqrt(total)
    all_tokens = rows * wide * lax.axis_size("narrow")
    clip = 0.02 * math.sqrt(all_tokens * (4 * D * D + 3 * D * FF + 2 * D))
    ratio = clip / jnp.maximum(grad_norm, clip)
    attend_red = jnp.stack([att_red[:, k * cols : (k + 1) * cols] for k in range(3)])
    output_red = att_red[:, 3 * cols :].T
    down_red = early_red[:, :hid].T
    gated_red = jnp.stack([early_red[:, hid:], up_red])
    new_attend = adam_update(
        attend_weight, attend_first, attend_second, attend_red, ratio, D ** (-0.5), WEIGHT_DECAY
    )
    new_output = adam_update(
        output_weight, output_first, output_second, output_red, ratio,
        max(D // 64, 1) ** (-0.5), WEIGHT_DECAY,
    )
    new_gated = adam_update(
        gated_weight, gated_first, gated_second, gated_red, ratio, D ** (-0.5), WEIGHT_DECAY
    )
    new_down = adam_update(
        down_weight, down_first, down_second, down_red, ratio, FF ** (-0.5), WEIGHT_DECAY
    )
    new_gains = adam_update(norm_gains, gains_first, gains_second, gain_red, ratio, 0.4, 0.0)
    return (
        layer_output, input_grad, grad_norm,
        *new_attend, *new_output, *new_gated, *new_down, *new_gains,
    )


def solution(mesh):
    rows = P(("wide", "narrow"), None)
    stacked = P(None, "wide", "narrow")
    turned = P("narrow", "wide")
    gains = P(None, "wide")
    params = (stacked,) * 3 + (turned,) * 3 + (stacked,) * 3 + (turned,) * 3 + (gains,) * 3
    return jax.shard_map(
        per_device,
        mesh=mesh,
        in_specs=(rows, rows) + params,
        out_specs=(rows, rows, P()) + params,
        check_vma=False,
    )
```

```python
import functools
import math

import jax
import jax.numpy as jnp
from jax import lax
from jax.experimental import layout
from jax.experimental import pallas as pl
from jax.experimental.pallas import tpu as pltpu
from jax.sharding import PartitionSpec as P

D = 768
HD = 64
FF = 2048
L = 1024
ADAM_STEP = 5

EPSILON = 1e-05
WEIGHT_DECAY = 0.1
AVERAGING = 0.5

LOW = jnp.bfloat16
FULL = jnp.float32
QB = 256
MASKED = -1e30
SMALL = pl.CostEstimate(flops=10**6, bytes_accessed=10**4, transcendentals=0)


def swap(value, axis, bit):
    size = lax.axis_size(axis)
    return lax.ppermute(value, axis, [(i, i ^ bit) for i in range(size)])


def wide_bits():
    top = lax.axis_size("wide").bit_length() - 1
    return [1 << b for b in range(top - 1, -1, -1)]


def block_masks():
    masks = [0]
    for bit in wide_bits():
        masks = masks + [m ^ bit for m in masks]
    return masks


def after(value, *done):
    return lax.optimization_barrier((value, done))[0]


def widen(held, bits):
    for bit in bits:
        held = jnp.concatenate([held, swap(held, "wide", bit)], axis=0)
    return held


def add(kept, received):
    return kept.astype(FULL) + received.astype(FULL)


def narrow_down(held, bits):
    for bit in bits:
        half = held.shape[0] // 2
        held = add(held[:half], swap(held[half:].astype(LOW), "wide", bit))
    return held


def turn(value, cosine, sine, sign):
    width = value.shape[1]
    lane = lax.broadcasted_iota(jnp.int32, value.shape, 1) % HD
    other = jnp.where(
        lane < HD // 2,
        pltpu.roll(value, width - HD // 2, 1),
        pltpu.roll(value, HD // 2, 1),
    )
    reps = width // 128
    return value * jnp.concatenate([cosine] * reps, axis=1) + sign * other * jnp.concatenate(
        [sine] * reps, axis=1
    )


def nn(a, b):
    return lax.dot_general(a, b, (((1,), (0,)), ((), ())), preferred_element_type=FULL)


def nt(a, b):
    return lax.dot_general(a, b, (((1,), (1,)), ((), ())), preferred_element_type=FULL)


def diagonal(scores):
    key = lax.broadcasted_iota(jnp.int32, scores.shape, 0)
    query = lax.broadcasted_iota(jnp.int32, scores.shape, 1)
    return jnp.where(key <= query, scores, MASKED)


def flip(value):
    return value.astype(FULL).T


def attend_kernel(
    rows_ref, qka_ref, qkb_ref, voa_ref, vob_ref, cos_ref, sin_ref,
    q_ref, k_ref, v_ref, ctx_ref, lse_ref, hold,
):
    heads = q_ref.shape[0]
    width = heads * HD
    half = qka_ref.shape[0]

    def project(i, carry):
        rows = pl.ds(pl.multiple_of(i * QB, QB), QB)
        first, second = rows_ref[rows, :half], rows_ref[rows, half:]
        pair = nn(first, qka_ref[...]) + nn(second, qkb_ref[...])
        pair = turn(pair, cos_ref[rows, :], sin_ref[rows, :], 1.0)
        value = nn(first, voa_ref[:, :width]) + nn(second, vob_ref[:, :width])
        for h in range(heads):
            q_ref[h, rows, :] = (pair[:, h * HD : (h + 1) * HD] * (HD**-0.5)).astype(LOW)
            k_ref[h, rows, :] = pair[:, width + h * HD : width + (h + 1) * HD].astype(LOW)
            v_ref[h, rows, :] = value[:, h * HD : (h + 1) * HD].astype(LOW)
        return carry

    lax.fori_loop(0, L // QB, project, 0)

    def head(h, carry):
        turned = flip(v_ref[h]).astype(LOW)
        for i in range(L // QB):
            lo, hi = i * QB, (i + 1) * QB
            query = q_ref[h, lo:hi, :]
            diag = diagonal(nt(k_ref[h, lo:hi, :], query))
            peak = jnp.max(diag, axis=0, keepdims=True)
            if i:
                body = nt(k_ref[h, :lo, :], query)
                peak = jnp.maximum(peak, jnp.max(body, axis=0, keepdims=True))
            weight = jnp.exp(diag - peak)
            total = jnp.sum(weight, axis=0, keepdims=True)
            out = nn(turned[:, lo:hi], weight.astype(LOW))
            if i:
                weight = jnp.exp(body - peak)
                total = total + jnp.sum(weight, axis=0, keepdims=True)
                out = out + nn(turned[:, :lo], weight.astype(LOW))
            lse_ref[h, :, lo:hi] = peak + jnp.log(total)
            hold[h, lo:hi, :] = (out / total).T.astype(LOW)
        return carry

    lax.fori_loop(0, heads, head, 0)
    for h in range(heads):
        ctx_ref[:, h * HD : (h + 1) * HD] = hold[h]


def pinned(array):
    return pltpu.with_memory_space_constraint(array, pltpu.HBM)


def whole(array):
    zero = (0,) * len(array.shape)
    return pl.BlockSpec(array.shape, lambda *_: zero)


def columns(piece):
    if not isinstance(piece, tuple):
        return piece, whole(piece)
    array, width, j = piece
    return array, pl.BlockSpec((array.shape[0], width), lambda *_: (0, j))


def width_of(piece):
    return piece[1] if isinstance(piece, tuple) else piece.shape[1]


def attend_forward(rows, qk, vo, cosine, sine):
    heads = width_of(qk[0]) // 2 // HD
    headed = pltpu.HBM((heads, L, HD), LOW)
    outs = (
        headed, headed, headed,
        jax.ShapeDtypeStruct((L, heads * HD), LOW),
        pltpu.HBM((heads, 1, L), FULL),
    )
    args, specs = zip(*[columns(p) for p in (rows, *qk, *vo, cosine, sine)])
    return pl.pallas_call(
        attend_kernel,
        grid=(1,),
        in_specs=list(specs),
        out_specs=[whole(o) for o in outs],
        out_shape=outs,
        scratch_shapes=[pltpu.VMEM((heads, L, HD), LOW)],
        compiler_params=pltpu.CompilerParams(vmem_limit_bytes=24 << 20),
        cost_estimate=SMALL,
        name="attend_forward",
    )(*args)


def attend_back_kernel(
    q_ref, k_ref, v_ref, lse_ref, dctx_ref, cos_ref, sin_ref,
    dqk_ref, dv_ref, dctx, dqk, dk_sum, dv_sum,
):
    heads = q_ref.shape[0]
    width = heads * HD
    for h in range(heads):
        dctx[h] = dctx_ref[:, h * HD : (h + 1) * HD]

    def head(h, carry):
        turned = flip(k_ref[h]).astype(LOW)
        for i in range(L // QB):
            lo, hi = i * QB, (i + 1) * QB
            query, back = q_ref[h, lo:hi, :], dctx[h, lo:hi, :]
            lse = lse_ref[h, :, lo:hi]
            prob = jnp.exp(diagonal(nt(k_ref[h, lo:hi, :], query)) - lse)
            grad = nt(v_ref[h, lo:hi, :], back)
            inner = jnp.sum(prob * grad, axis=0, keepdims=True)
            if i:
                prob_body = jnp.exp(nt(k_ref[h, :lo, :], query) - lse)
                grad_body = nt(v_ref[h, :lo, :], back)
                inner = inner + jnp.sum(prob_body * grad_body, axis=0, keepdims=True)
            score = (prob * (grad - inner)).astype(LOW)
            dv_sum[h, lo:hi, :] = nn(prob.astype(LOW), back)
            dk_sum[h, lo:hi, :] = nn(score, query)
            dquery = nn(turned[:, lo:hi], score)
            if i:
                score = (prob_body * (grad_body - inner)).astype(LOW)
                dv_sum[h, :lo, :] += nn(prob_body.astype(LOW), back)
                dk_sum[h, :lo, :] += nn(score, query)
                dquery = dquery + nn(turned[:, :lo], score)
            dqk[h, lo:hi, :] = (dquery * (HD**-0.5)).T
        return carry

    lax.fori_loop(0, heads, head, 0)

    def finish(i, carry):
        rows = pl.ds(pl.multiple_of(i * QB, QB), QB)
        pair = jnp.concatenate(
            [dqk[h, rows, :] for h in range(heads)] + [dk_sum[h, rows, :] for h in range(heads)],
            axis=1,
        )
        dqk_ref[rows, :] = turn(pair, cos_ref[rows, :], sin_ref[rows, :], -1.0).astype(LOW)
        dv_ref[rows, :] = jnp.concatenate(
            [dv_sum[h, rows, :] for h in range(heads)], axis=1
        ).astype(LOW)
        return carry

    lax.fori_loop(0, L // QB, finish, 0)


def attend_backward(q, k, v, lse, dctx, cosine, sine):
    heads = q.shape[0]
    return pl.pallas_call(
        attend_back_kernel,
        out_shape=(
            jax.ShapeDtypeStruct((L, 2 * heads * HD), LOW),
            jax.ShapeDtypeStruct((L, heads * HD), LOW),
        ),
        scratch_shapes=[
            pltpu.VMEM((heads, L, HD), LOW),
            pltpu.VMEM((heads, L, HD), FULL),
            pltpu.VMEM((heads, L, HD), FULL),
            pltpu.VMEM((heads, L, HD), FULL),
        ],
        compiler_params=pltpu.CompilerParams(vmem_limit_bytes=24 << 20),
        cost_estimate=SMALL,
        name="attend_backward",
    )(pinned(q), pinned(k), pinned(v), pinned(lse), dctx, cosine, sine)


def held_once(array):
    zero = (0,) * array.ndim
    return pl.BlockSpec(array.shape, lambda *_: zero, pipeline_mode=pl.Buffered(1))


def by_rows(kernel, name, flops, row_args, fixed, outs, sums=0, scratch=()):
    specs = [pl.BlockSpec((QB, r.shape[1]), lambda i: (i, 0)) for r in row_args]
    shapes = [
        (pltpu.HBM if away else jax.ShapeDtypeStruct)((L, w), t) for w, t, away in outs
    ]
    out_specs = [pl.BlockSpec((QB, w), lambda i: (i, 0)) for w, _, _ in outs]
    shapes += [jax.ShapeDtypeStruct((1, D), FULL)] * sums
    out_specs += [pl.BlockSpec((1, D), lambda i: (0, 0))] * sums
    row_args = [pinned(r) if r.dtype == FULL else r for r in row_args]
    return pl.pallas_call(
        kernel,
        grid=(L // QB,),
        in_specs=specs + [held_once(f) for f in fixed],
        out_specs=out_specs,
        out_shape=shapes,
        scratch_shapes=list(scratch),
        compiler_params=pltpu.CompilerParams(vmem_limit_bytes=30 << 20),
        cost_estimate=SMALL,
        name=name,
    )(*row_args, *[pinned(f) for f in fixed])


def rms_scale(residual):
    return lax.rsqrt(jnp.mean(residual * residual, axis=1, keepdims=True) + EPSILON)


def norm_back(scaled, normed, inv):
    return inv * (scaled - normed * jnp.mean(scaled * normed, axis=1, keepdims=True))


def column_sum(sum_ref, value):
    @pl.when(pl.program_id(0) == 0)
    def _():
        sum_ref[...] = jnp.zeros_like(sum_ref)

    sum_ref[...] += jnp.sum(value, axis=0, keepdims=True)


def heads_out(held_ref, refs):
    att_ref, y_ref, x_ref, corner_ref = refs
    width = held_ref.shape[2]

    @pl.when(pl.program_id(0) == 0)
    def _():
        for p, ref in enumerate((att_ref, y_ref, x_ref)):
            held_ref[p] = ref[:, 3 * width :]
        held_ref[3] = corner_ref[:, width:]


def project_kernel(one_ref, two_ref, att_ref, y_ref, x_ref, corner_ref, out_ref, held_ref):
    heads_out(held_ref, (att_ref, y_ref, x_ref, corner_ref))
    half = att_ref.shape[0]
    one, two = one_ref[...], two_ref[...]
    out_ref[:, :half] = (nt(one, held_ref[0]) + nt(two, held_ref[2])).astype(LOW)
    out_ref[:, half:] = (nt(one, held_ref[1]) + nt(two, held_ref[3])).astype(LOW)


def blocks(refs, x, y, kind):
    own_ref, y_ref, x_ref, gate_ref, up_ref, down_ref = refs
    if kind == 2:
        return [down_ref[2 * x + y]]
    if x and y:
        return [(up_ref if kind else gate_ref)[...]]
    ref = (x_ref if x else y_ref) if x or y else own_ref
    hid = ref.shape[1] // 2
    return [ref[:, kind * hid : (kind + 1) * hid]]


def onto(rows, parts):
    made = [nn(rows, p) for p in parts]
    return made[0] if len(made) == 1 else jnp.concatenate(made, axis=1)


def back_from(grads, parts):
    start, total = 0, 0.0
    for p in parts:
        total = total + nt(grads[:, start : start + p.shape[1]], p)
        start += p.shape[1]
    return total


def gate_up(hidden, refs, x, gate_ref, up_ref, act_ref):
    half = refs[0].shape[0]
    first, second = hidden[:, :half], hidden[:, half:]
    gate = onto(first, blocks(refs, x, 0, 0)) + onto(second, blocks(refs, x, 1, 0))
    up = onto(first, blocks(refs, x, 0, 1)) + onto(second, blocks(refs, x, 1, 1))
    gate_ref[...] = gate
    up_ref[...] = up
    act_ref[...] = (gate * jax.nn.sigmoid(gate) * up).astype(LOW)


def enter_kernel(
    rows_ref, mine_ref, theirs_ref, gain_ref, own_ref, y_ref,
    normed_ref, inv_ref, hidden_ref, gate_ref, up_ref, act_ref,
):
    residual = rows_ref[...].astype(FULL) + add(mine_ref[...], theirs_ref[...])
    inv = rms_scale(residual)
    normed = residual * inv
    hidden = (normed * gain_ref[...]).astype(LOW)
    normed_ref[...] = normed
    inv_ref[...] = inv
    hidden_ref[...] = hidden
    gate_up(hidden, (own_ref, y_ref, None, None, None, None), 0, gate_ref, up_ref, act_ref)


def rest_kernel(
    hidden_ref, act1_ref, own_ref, y_ref, x_ref, low_ref, high_ref, down_ref,
    gate_ref, up_ref, act_ref, out_ref,
):
    refs = (own_ref, y_ref, x_ref, low_ref, high_ref, down_ref)
    half = own_ref.shape[0]
    gate_up(hidden_ref[...], refs, 1, gate_ref, up_ref, act_ref)
    one, two = act1_ref[...], act_ref[...]
    for y in range(2):
        part = back_from(one, blocks(refs, 0, y, 2)) + back_from(two, blocks(refs, 1, y, 2))
        out_ref[:, y * half : (y + 1) * half] = part.astype(LOW)


def turn_kernel(
    normed_ref, mine_ref, theirs_ref, up_rows_ref, gain1_ref, gain2_ref,
    out_ref, grad_ref, low_ref, sum_ref,
):
    residual = normed_ref[...] * gain1_ref[...] + add(mine_ref[...], theirs_ref[...])
    inv = rms_scale(residual)
    normed = residual * inv
    gain = gain2_ref[...]
    out_ref[...] = (normed * gain).astype(LOW)
    upstream = up_rows_ref[...].astype(FULL)
    column_sum(sum_ref, upstream * normed)
    grad = norm_back(upstream * gain, normed, inv)
    grad_ref[...] = grad
    low_ref[...] = grad.astype(LOW)


def back_kernel(low_ref, gate1_ref, up1_ref, gate2_ref, up2_ref, down_ref, gg_ref, ug_ref):
    half, hid = down_ref.shape[1], gate1_ref.shape[1]
    first, second = low_ref[:, :half], low_ref[:, half:]
    for x, gate_ref, up_ref in ((0, gate1_ref, up1_ref), (1, gate2_ref, up2_ref)):
        act_grad = nn(first, down_ref[2 * x]) + nn(second, down_ref[2 * x + 1])
        gate = gate_ref[...]
        sig = jax.nn.sigmoid(gate)
        gg = act_grad * up_ref[...] * (sig * (1.0 + gate * (1.0 - sig)))
        gg_ref[:, x * hid : (x + 1) * hid] = gg.astype(LOW)
        ug_ref[:, x * hid : (x + 1) * hid] = (act_grad * (gate * sig)).astype(LOW)


def mid_kernel(gg_ref, ug_ref, own_ref, y_ref, x_ref, low_ref, high_ref, mid_ref):
    refs = (own_ref, y_ref, x_ref, low_ref, high_ref, None)
    half, hid = own_ref.shape[0], gg_ref.shape[1] // 2
    for y in range(2):
        total = 0.0
        for x in range(2):
            for kind, ref in enumerate((gg_ref, ug_ref)):
                total = total + back_from(ref[:, x * hid : (x + 1) * hid], blocks(refs, x, y, kind))
        mid_ref[:, y * half : (y + 1) * half] = total.astype(LOW)


def leave_kernel(
    grad_two_ref, mine_ref, theirs_ref, normed_ref, inv_ref,
    gain_ref, att_ref, y_ref, x_ref, corner_ref,
    grad_ref, low_ref, ctx1_ref, ctx2_ref, sum_ref, held_ref,
):
    heads_out(held_ref, (att_ref, y_ref, x_ref, corner_ref))
    half = att_ref.shape[0]
    hidden_grad = grad_two_ref[...] + add(mine_ref[...], theirs_ref[...])
    normed = normed_ref[...]
    column_sum(sum_ref, hidden_grad * normed)
    grad = norm_back(hidden_grad * gain_ref[...], normed, inv_ref[...])
    low = grad.astype(LOW)
    grad_ref[...] = grad
    low_ref[...] = low
    first, second = low[:, :half], low[:, half:]
    ctx1_ref[...] = (nn(first, held_ref[0]) + nn(second, held_ref[1])).astype(LOW)
    ctx2_ref[...] = (nn(first, held_ref[2]) + nn(second, held_ref[3])).astype(LOW)


def input_kernel(
    qk1_ref, v1_ref, qk2_ref, v2_ref, att_ref, y_ref, x_ref, qk_corner_ref, vo_corner_ref,
    full_ref, low_ref,
):
    half = att_ref.shape[0]
    width = v1_ref.shape[1]
    qk1, v1, qk2, v2 = qk1_ref[...], v1_ref[...], qk2_ref[...], v2_ref[...]
    pair = 2 * width
    first = (
        nt(qk1, att_ref[:, :pair]) + nt(v1, att_ref[:, pair : pair + width])
        + nt(qk2, x_ref[:, :pair]) + nt(v2, x_ref[:, pair : pair + width])
    )
    second = (
        nt(qk1, y_ref[:, :pair]) + nt(v1, y_ref[:, pair : pair + width])
        + nt(qk2, qk_corner_ref[...]) + nt(v2, vo_corner_ref[:, :width])
    )
    full_ref[:, :half] = first
    full_ref[:, half:] = second
    low_ref[:, :half] = first.astype(LOW)
    low_ref[:, half:] = second.astype(LOW)


def heads_grad_kernel(
    rows_ref, grad_ref, qk_ref, v_ref, ctx_ref, qk_near_ref, qk_far_ref, vo_ref
):
    width = v_ref.shape[1]
    rows = flip(rows_ref[...]).astype(LOW)
    qk = nn(rows, qk_ref[...]).astype(LOW)
    vo_ref[:, :width] = nn(rows, v_ref[...]).astype(LOW)
    vo_ref[:, width:] = nn(flip(grad_ref[...]).astype(LOW), ctx_ref[...]).astype(LOW)

    @pl.when(pl.program_id(0) == 0)
    def _():
        qk_near_ref[...] = qk

    @pl.when(pl.program_id(0) == 1)
    def _():
        qk_far_ref[...] = qk


def heads_grad(rows, grad, dqk, dv, context):
    half, pair = D // 2, dqk.shape[1]
    split = pl.BlockSpec((L, half), lambda i: (0, i))
    outs = [jax.ShapeDtypeStruct((half, pair), LOW)] * 2 + [jax.ShapeDtypeStruct((D, pair), LOW)]
    held = [pl.BlockSpec((half, pair), lambda i: (0, 0))] * 2
    return pl.pallas_call(
        heads_grad_kernel,
        grid=(2,),
        in_specs=[split, split] + [held_once(g) for g in (dqk, dv, context)],
        out_specs=held + [pl.BlockSpec((half, pair), lambda i: (i, 0))],
        out_shape=outs,
        compiler_params=pltpu.CompilerParams(vmem_limit_bytes=24 << 20),
        cost_estimate=SMALL,
        name="heads_grad",
    )(rows, grad, dqk, dv, context)


def finish_kernel(core_ref, one_ref, full_ref, out_ref, theirs_ref, mover_ref, grad_ref, low_ref):
    mover = mover_ref[...]
    grad = one_ref[...] + full_ref[...] + theirs_ref[...].astype(FULL)
    total = 0.0
    for _ in range(3):
        part = grad.astype(LOW)
        total = total + nt(part, mover)
        grad = grad - part.astype(FULL)
    grad_ref[...] = total
    low_ref[...] = nt(out_ref[...], mover).astype(LOW)


def finish(core, grad_one, part_full, layer_output, theirs, mover):
    rows = theirs.shape[0]
    steps = rows // QB
    mine = pl.BlockSpec((QB, D), lambda i, c: (c[0] * steps + i, 0))
    plain = pl.BlockSpec((QB, D), lambda i, c: (i, 0))
    return pl.pallas_call(
        finish_kernel,
        grid_spec=pltpu.PrefetchScalarGridSpec(
            num_scalar_prefetch=1,
            grid=(steps,),
            in_specs=[mine, mine, mine, plain, held_once(mover)],
            out_specs=[plain, plain],
        ),
        out_shape=[
            jax.ShapeDtypeStruct((rows, D), FULL), jax.ShapeDtypeStruct((rows, D), LOW)
        ],
        cost_estimate=SMALL,
        name="finish",
    )(core, pinned(grad_one), pinned(part_full), pinned(layer_output), theirs, mover)


def adam_kernel(rates, *refs):
    ratio = refs[0][0, 0]
    att, ffn, down = (r[...] for r in refs[1:4])
    ins, outs = refs[4:16], refs[16:]

    def update(p, at, grad):
        rate, decay = rates[p]
        old = [ref[at] for ref in ins[3 * p : 3 * p + 3]]
        for ref, value in zip(
            outs[3 * p : 3 * p + 3], adam_update(*old, grad, ratio, rate, decay)
        ):
            ref[at] = value

    width, hid = att.shape[1] // 4, ffn.shape[1] // 2
    for k in range(3):
        update(0, k, att[:, k * width : (k + 1) * width])
    update(1, ..., att[:, 3 * width :].T)
    for k in range(2):
        update(2, k, ffn[:, k * hid : (k + 1) * hid])
    update(3, ..., down)


def adam(ratio, rates, grads, params):
    flat = [array for group in params for array in group]
    outs = [jax.ShapeDtypeStruct(w.shape, FULL) for w in flat]
    vmem = pl.BlockSpec(memory_space=pltpu.VMEM)
    made = pl.pallas_call(
        functools.partial(adam_kernel, rates),
        in_specs=[pl.BlockSpec(memory_space=pltpu.SMEM)] + [vmem] * (len(grads) + len(flat)),
        out_specs=[vmem] * len(outs),
        out_shape=outs,
        name="adam",
    )(ratio, *grads, *flat)
    return [made[i : i + 3] for i in range(0, len(made), 3)]


def rope_tables():
    half = HD // 2
    lane = jnp.arange(128) % HD
    freq = jnp.exp(-jnp.log(10000.0) * (lane % half).astype(FULL) / half)
    angle = jnp.arange(L, dtype=FULL)[:, None] * freq[None, :]
    return jnp.cos(angle), jnp.where(lane < half, -1.0, 1.0)[None, :] * jnp.sin(angle)


def adam_update(weight, first, second, grad, ratio, rate, decay):
    clipped = grad * ratio
    first_new = AVERAGING * first + (1.0 - AVERAGING) * clipped
    second_new = AVERAGING * second + (1.0 - AVERAGING) * clipped * clipped
    correction = 1.0 - AVERAGING**ADAM_STEP
    step = first_new / correction / (jnp.sqrt(second_new / correction) + 1e-08)
    return (weight - rate * (step + decay * weight), first_new, second_new)


def tn(rows, grads):
    out = lax.dot_general(rows, grads, (((0,), (0,)), ((), ())), preferred_element_type=FULL)
    return layout.with_layout_constraint(out.astype(LOW), layout.Layout((0, 1)))


def per_device(
    layer_input, layer_cotangent,
    attend_weight, attend_first, attend_second,
    output_weight, output_first, output_second,
    gated_weight, gated_first, gated_second,
    down_weight, down_first, down_second,
    norm_gains, gains_first, gains_second,
):
    rows = layer_input.shape[0]
    wide = lax.axis_size("wide")
    block = D // wide
    me = lax.axis_index("wide")
    narrow = lax.axis_index("narrow")
    core = narrow % 2
    cols = attend_weight.shape[2]

    bits = wide_bits()
    near = bits[:-1]
    half = D // 2
    hid = down_weight.shape[0]

    bits = wide_bits()
    near = bits[:-1]
    half = D // 2
    hid = down_weight.shape[0]
    pair = 2 * cols

    attend_low = attend_weight.astype(LOW)
    att = jnp.concatenate(
        [attend_low[0], attend_low[1], attend_low[2], output_weight.T.astype(LOW)], axis=1
    )
    ffn = jnp.concatenate([gated_weight[0], gated_weight[1]], axis=1).astype(LOW)
    down = down_weight.T.astype(LOW)

    order = me ^ jnp.array(block_masks(), jnp.int32)
    source = (order[:, None] * block + jnp.arange(block)[None, :]).reshape(1, D)
    mover = (lax.broadcasted_iota(jnp.int32, (D, D), 0) == source).astype(LOW)

    def both_halves(mine, theirs):
        return jnp.where(
            core == 0,
            jnp.concatenate([mine, theirs], axis=0),
            jnp.concatenate([theirs, mine], axis=0),
        )

    def own_rows(value):
        return lax.dynamic_slice_in_dim(value, core * rows, rows, axis=0)

    first = widen(att, near[:1])
    first, rows_in, rows_up, down = lax.optimization_barrier(
        (first, layer_input, layer_cotangent, down)
    )
    att = widen(first, near[1:])
    moved_in = jnp.dot(rows_in, mover, preferred_element_type=FULL).astype(LOW)
    moved_up = jnp.dot(rows_up, mover, preferred_element_type=FULL).astype(LOW)
    other_in = swap(moved_in, "narrow", 1)
    other_up = swap(moved_up, "narrow", 1)
    down_y = swap(down, "wide", 1)
    down_x = swap(down, "narrow", 2)
    down = jnp.stack([down, down_y, down_x, swap(down_y, "narrow", 2)])[:, None]
    gains = widen(after(norm_gains, first).astype(LOW).astype(FULL)[None], bits)
    att, down, other_in, other_up = lax.optimization_barrier((att, down, other_in, other_up))
    att_y = swap(att, "wide", 1)
    att_x = swap(att, "narrow", 2)
    ffn = widen(after(ffn, att), near[:1])
    gains = gains.transpose(1, 0, 2).reshape(2, 1, D)
    inputs = both_halves(moved_in, other_in)
    upstream = both_halves(moved_up, other_up)
    cosine, sine = rope_tables()

    inputs, att, att_y, att_x, ffn, gains, upstream, cosine, sine = lax.optimization_barrier(
        (inputs, att, att_y, att_x, ffn, gains, upstream, cosine, sine)
    )
    qk_corner = swap(att_y[:, :pair], "narrow", 2)
    vo_corner = swap(att_x[:, pair:], "wide", 1)
    ffn = widen(ffn, near[1:])
    down = after(down, ffn)
    for bit in near[:1]:
        down = jnp.concatenate([down, swap(down, "wide", bit)], axis=1)
    qk = [[(att, pair, 0), (att_y, pair, 0)], [(att_x, pair, 0), qk_corner]]
    vo = [[(att, pair, 1), (att_y, pair, 1)], [(att_x, pair, 1), vo_corner]]
    saved = [attend_forward(inputs, qk[0], vo[0], cosine, sine)]
    second_in, qk_corner, vo_corner, ffn = lax.optimization_barrier(
        (after(inputs, saved[0][3]), qk_corner, vo_corner, ffn)
    )
    qk[1][1], vo[1][1] = qk_corner, vo_corner
    ffn_y = swap(ffn, "wide", 1)
    ffn_x = swap(ffn, "narrow", 2)
    saved.append(attend_forward(second_in, qk[1], vo[1], cosine, sine))
    context, down = lax.optimization_barrier(([s[3] for s in saved], down))
    att_out = [att, att_y, att_x, vo_corner]
    held = [pltpu.VMEM((4, half, cols), LOW)]
    low_d, full_d = (D, LOW, False), (D, FULL, True)
    (attn_part,) = by_rows(
        project_kernel, "project", 2e9, context, att_out, [low_d], scratch=held
    )
    ffn_y, ffn_x, attn_part = lax.optimization_barrier((ffn_y, ffn_x, attn_part))
    attn_other = swap(attn_part, "narrow", 1)
    for bit in near[1:]:
        down = jnp.concatenate([down, swap(down, "wide", bit)], axis=1)
    down = down.reshape(4, half, hid)
    gate_corner = swap(ffn_y[:, :hid], "narrow", 2)
    up_corner = swap(ffn_x[:, hid:], "wide", 1)
    flow = [(hid, FULL, True), (hid, FULL, True), (hid, LOW, False)]
    normed_one, inv_one, hidden_low, gate1, up1, act1 = by_rows(
        enter_kernel, "enter", 4e9, [inputs, attn_part, attn_other],
        [gains[0], ffn, ffn_y], [full_d, (1, FULL, True), low_d] + flow,
    )
    ffn_all = [ffn, ffn_y, ffn_x, gate_corner, up_corner, down]
    gate2, up2, act2, ffn_part = by_rows(
        rest_kernel, "rest", 5e9, [hidden_low, act1], ffn_all, flow + [low_d]
    )
    ffn_other = swap(ffn_part, "narrow", 1)

    layer_output, grad_two, grad_two_low, gain_two_grad = by_rows(
        turn_kernel, "turn", 3e9, [normed_one, ffn_part, ffn_other, upstream],
        [gains[0], gains[1]], [(D, LOW, True), full_d, low_d], sums=1,
    )
    down_send = tn(grad_two_low, act2)
    down_x = swap(down_send, "narrow", 2)
    wide_flow = (2 * hid, LOW, False)
    gg, ug = by_rows(
        back_kernel, "back", 5e9,
        [after(grad_two_low, down_send), gate1, up1, gate2, up2], [down], [wide_flow, wide_flow],
    )
    gate_send = tn(hidden_low[:, half:], gg)
    up_send = tn(hidden_low, ug[:, hid:])
    gate_y = swap(gate_send, "wide", 1)
    up_x = swap(up_send, "narrow", 2)
    (mid_part,) = by_rows(
        mid_kernel, "mid", 5e9, [after(gg, gate_send, up_send), ug], ffn_all[:5], [low_d]
    )
    mid_other = swap(mid_part, "narrow", 1)
    down_own = tn(grad_two_low, act1)
    gate_own = tn(hidden_low[:, :half], gg)
    up_own = tn(hidden_low, ug[:, :hid])
    mid_part, mid_other, down_own, gate_own, up_own = lax.optimization_barrier(
        (mid_part, mid_other, down_own, gate_own, up_own)
    )
    grad_one, grad_one_low, dctx1, dctx2, gain_one_grad = by_rows(
        leave_kernel, "leave", 4e9, [grad_two, mid_part, mid_other, normed_one, inv_one],
        [gains[0], *att_out], [full_d, low_d, (cols, LOW, False), (cols, LOW, False)],
        sums=1, scratch=held,
    )

    down_x, gate_y, dctx2 = lax.optimization_barrier((down_x, gate_y, dctx2))
    down_sum, gate_sum = add(down_own, down_x), add(gate_own, gate_y)
    down_far, gate_far = down_sum[half:].astype(LOW), gate_sum[:, hid:].astype(LOW)
    down_y = swap(down_far, "wide", 1)
    gate_x = swap(gate_far, "narrow", 2)

    q, k, v, _, lse = saved[1]
    dqk2, dv2 = attend_backward(q, k, v, lse, after(dctx2, down_far, gate_far), cosine, sine)
    qk_near2, qk_send2, vo_send = heads_grad(inputs, grad_one_low, dqk2, dv2, context[1])
    vo_x = swap(vo_send, "narrow", 2)
    qk_y2 = swap(qk_send2, "wide", 1)
    back = near[::-1]
    early = add(down_sum[:half], down_y)
    dctx1, early, up_x = lax.optimization_barrier(
        (after(dctx1, vo_send, qk_send2), early, up_x)
    )
    up_sum = add(up_own, up_x)
    up_far = up_sum[half:].astype(LOW)
    up_y = swap(up_far, "wide", 1)
    early = narrow_down(early, back[:1])
    q, k, v, _, lse = saved[0]
    dqk1, dv1 = attend_backward(q, k, v, lse, after(dctx1, up_far), cosine, sine)
    dqk1, dv1, early, qk_y2, gate_x = lax.optimization_barrier((dqk1, dv1, early, qk_y2, gate_x))
    qk_near1, qk_send1, vo_own = heads_grad(inputs, grad_one_low, dqk1, dv1, context[0])
    qk_y1 = swap(qk_send1, "wide", 1)
    qk_far = add(qk_near2, qk_y2).astype(LOW)
    qk_x = swap(qk_far, "narrow", 2)
    early_red = narrow_down(early, back[1:])
    part_full, part_low = by_rows(
        input_kernel, "inputs", 4e9, [after(dqk1, qk_send1, qk_far), dv1, dqk2, dv2],
        [att, att_y, att_x, qk_corner, vo_corner], [full_d, low_d],
    )
    vo_x, up_y, part_low = lax.optimization_barrier((vo_x, up_y, part_low))
    late = jnp.concatenate([add(gate_sum[:, :hid], gate_x), add(up_sum[:half], up_y)], axis=1)
    late = narrow_down(late, back[:1])
    vo_sum = add(vo_own, vo_x)
    vo_far = vo_sum[half:].astype(LOW)
    vo_y = swap(vo_far, "wide", 1)
    theirs = lax.dynamic_slice_in_dim(part_low, (1 - core) * rows, rows, axis=0)
    theirs = swap(theirs, "narrow", 1)
    qk_sum = add(qk_near1, qk_y1)
    last = jnp.concatenate([add(qk_sum, qk_x), add(vo_sum[:half], vo_y)], axis=1)
    last, early_red, late, part_full = lax.optimization_barrier(
        (last, early_red, late, part_full)
    )
    late_red = narrow_down(late, back[1:])
    last = narrow_down(last, back[:1])
    input_grad, layer_output = finish(
        jnp.full((1,), core, jnp.int32), grad_one, part_full, layer_output, theirs, mover
    )
    gain_grads = lax.dot_general(
        jnp.concatenate([gain_one_grad, gain_two_grad], axis=0), mover.astype(FULL),
        (((1,), (1,)), ((), ())), precision=lax.Precision.HIGHEST, preferred_element_type=FULL,
    )
    early_square = jnp.sum(early_red * early_red) + jnp.sum(late_red * late_red)
    last, input_grad, layer_output, gain_grads, early_square = lax.optimization_barrier(
        (last, input_grad, layer_output, gain_grads, early_square)
    )
    att_red = narrow_down(last, back[1:])

    square = jnp.full((1, 128), early_square + jnp.sum(att_red * att_red), FULL)
    square = square + swap(square, "narrow", 1)
    message = jnp.concatenate([gain_grads.reshape(1, 2 * D), square], axis=1)
    message = message + swap(message, "narrow", 2)
    for bit in bits[::-1]:
        message = message + swap(message, "wide", bit)
    gain_sum = message[:, : 2 * D]
    total = message[0, 2 * D] + jnp.sum(gain_sum * gain_sum)
    gain_red = lax.dynamic_index_in_dim(gain_sum.reshape(2, wide, block), me, 1, keepdims=False)
    grad_norm = jnp.sqrt(total)
    all_tokens = rows * wide * lax.axis_size("narrow")
    clip = 0.02 * math.sqrt(all_tokens * (4 * D * D + 3 * D * FF + 2 * D))
    ratio = clip / jnp.maximum(grad_norm, clip)
    new_attend, new_output, new_gated, new_down = adam(
        jnp.full((1, 1), ratio, FULL),
        (
            (D ** (-0.5), WEIGHT_DECAY),
            (max(D // 64, 1) ** (-0.5), WEIGHT_DECAY),
            (D ** (-0.5), WEIGHT_DECAY),
            (FF ** (-0.5), WEIGHT_DECAY),
        ),
        (att_red, late_red, early_red),
        (
            (attend_weight, attend_first, attend_second),
            (output_weight, output_first, output_second),
            (gated_weight, gated_first, gated_second),
            (down_weight.T, down_first.T, down_second.T),
        ),
    )
    new_down = [value.T for value in new_down]
    new_gains = adam_update(norm_gains, gains_first, gains_second, gain_red, ratio, 0.4, 0.0)
    return (
        layer_output, input_grad, grad_norm,
        *new_attend, *new_output, *new_gated, *new_down, *new_gains,
    )


def solution(mesh):
    rows = P(("wide", "narrow"), None)
    stacked = P(None, "wide", "narrow")
    turned = P("narrow", "wide")
    gains = P(None, "wide")
    params = (stacked,) * 3 + (turned,) * 3 + (stacked,) * 3 + (turned,) * 3 + (gains,) * 3
    return jax.shard_map(
        per_device,
        mesh=mesh,
        in_specs=(rows, rows) + params,
        out_specs=(rows, rows, P()) + params,
        check_vma=False,
    )
```

```python
import functools
import math

import jax
import jax.numpy as jnp
from jax import lax
from jax.experimental import layout
from jax.experimental import pallas as pl
from jax.experimental.pallas import tpu as pltpu
from jax.sharding import PartitionSpec as P

D = 768
HD = 64
FF = 2048
L = 1024
ADAM_STEP = 5

EPSILON = 1e-05
WEIGHT_DECAY = 0.1
AVERAGING = 0.5

LOW = jnp.bfloat16
FULL = jnp.float32
QB = 256
MASKED = -1e30
SMALL = pl.CostEstimate(flops=10**6, bytes_accessed=10**4, transcendentals=0)


def swap(value, axis, bit):
    size = lax.axis_size(axis)
    return lax.ppermute(value, axis, [(i, i ^ bit) for i in range(size)])


def wide_bits():
    top = lax.axis_size("wide").bit_length() - 1
    return [1 << b for b in range(top - 1, -1, -1)]


def block_masks():
    masks = [0]
    for bit in wide_bits():
        masks = masks + [m ^ bit for m in masks]
    return masks


def after(value, *done):
    return lax.optimization_barrier((value, done))[0]


def widen(held, bits):
    for bit in bits:
        held = jnp.concatenate([held, swap(held, "wide", bit)], axis=0)
    return held


def add(kept, received):
    return kept.astype(FULL) + received.astype(FULL)


def narrow_down(held, bits):
    for bit in bits:
        half = held.shape[0] // 2
        held = add(held[:half], swap(held[half:].astype(LOW), "wide", bit))
    return held


def turn(value, cosine, sine, sign):
    width = value.shape[1]
    lane = lax.broadcasted_iota(jnp.int32, value.shape, 1) % HD
    other = jnp.where(
        lane < HD // 2,
        pltpu.roll(value, width - HD // 2, 1),
        pltpu.roll(value, HD // 2, 1),
    )
    reps = width // 128
    return value * jnp.concatenate([cosine] * reps, axis=1) + sign * other * jnp.concatenate(
        [sine] * reps, axis=1
    )


def nn(a, b):
    return lax.dot_general(a, b, (((1,), (0,)), ((), ())), preferred_element_type=FULL)


def nt(a, b):
    return lax.dot_general(a, b, (((1,), (1,)), ((), ())), preferred_element_type=FULL)


def diagonal(scores):
    key = lax.broadcasted_iota(jnp.int32, scores.shape, 0)
    query = lax.broadcasted_iota(jnp.int32, scores.shape, 1)
    return jnp.where(key <= query, scores, MASKED)


def flip(value):
    return value.astype(FULL).T


def attend_kernel(
    rows_ref, qka_ref, qkb_ref, voa_ref, vob_ref, cos_ref, sin_ref,
    q_ref, k_ref, v_ref, ctx_ref, lse_ref, hold, q_all, k_all, v_all,
):
    heads = q_all.shape[0]
    width = heads * HD
    half = qka_ref.shape[0]
    h = pl.program_id(0)

    def project(i, carry):
        rows = pl.ds(pl.multiple_of(i * QB, QB), QB)
        first, second = rows_ref[rows, :half], rows_ref[rows, half:]
        pair = nn(first, qka_ref[...]) + nn(second, qkb_ref[...])
        pair = turn(pair, cos_ref[rows, :], sin_ref[rows, :], 1.0)
        value = nn(first, voa_ref[:, :width]) + nn(second, vob_ref[:, :width])
        for h in range(heads):
            q_all[h, rows, :] = (pair[:, h * HD : (h + 1) * HD] * (HD**-0.5)).astype(LOW)
            k_all[h, rows, :] = pair[:, width + h * HD : width + (h + 1) * HD].astype(LOW)
            v_all[h, rows, :] = value[:, h * HD : (h + 1) * HD].astype(LOW)
        return carry

    @pl.when(h == 0)
    def _():
        lax.fori_loop(0, L // QB, project, 0)

    q_ref[0] = q_all[h]
    k_ref[0] = k_all[h]
    v_ref[0] = v_all[h]
    turned = flip(v_all[h]).astype(LOW)
    for i in range(L // QB):
        lo, hi = i * QB, (i + 1) * QB
        query = q_all[h, lo:hi, :]
        diag = diagonal(nt(k_all[h, lo:hi, :], query))
        peak = jnp.max(diag, axis=0, keepdims=True)
        if i:
            body = nt(k_all[h, :lo, :], query)
            peak = jnp.maximum(peak, jnp.max(body, axis=0, keepdims=True))
        weight = jnp.exp(diag - peak)
        total = jnp.sum(weight, axis=0, keepdims=True)
        out = nn(turned[:, lo:hi], weight.astype(LOW))
        if i:
            weight = jnp.exp(body - peak)
            total = total + jnp.sum(weight, axis=0, keepdims=True)
            out = out + nn(turned[:, :lo], weight.astype(LOW))
        lse_ref[0, :, lo:hi] = peak + jnp.log(total)
        hold[h, lo:hi, :] = (out / total).T.astype(LOW)

    @pl.when(h == heads - 1)
    def _():
        for j in range(heads):
            ctx_ref[:, j * HD : (j + 1) * HD] = hold[j]


def pinned(array):
    return pltpu.with_memory_space_constraint(array, pltpu.HBM)


def whole(array):
    zero = (0,) * len(array.shape)
    return pl.BlockSpec(array.shape, lambda *_: zero)


def by_head(shape):
    return pl.BlockSpec(shape, lambda h: (h, 0, 0))


def columns(piece):
    if not isinstance(piece, tuple):
        return piece, whole(piece)
    array, width, j = piece
    return array, pl.BlockSpec((array.shape[0], width), lambda *_: (0, j))


def width_of(piece):
    return piece[1] if isinstance(piece, tuple) else piece.shape[1]


def attend_forward(rows, qk, vo, cosine, sine):
    heads = width_of(qk[0]) // 2 // HD
    headed = pltpu.HBM((heads, L, HD), LOW)
    outs = (
        headed, headed, headed,
        jax.ShapeDtypeStruct((L, heads * HD), LOW),
        pltpu.HBM((heads, 1, L), FULL),
    )
    args, specs = zip(*[columns(p) for p in (rows, *qk, *vo, cosine, sine)])
    return pl.pallas_call(
        attend_kernel,
        grid=(heads,),
        in_specs=list(specs),
        out_specs=[by_head((1, L, HD))] * 3 + [whole(outs[3]), by_head((1, 1, L))],
        out_shape=outs,
        scratch_shapes=[pltpu.VMEM((heads, L, HD), LOW)] * 4,
        compiler_params=pltpu.CompilerParams(vmem_limit_bytes=24 << 20),
        cost_estimate=SMALL,
        name="attend_forward",
    )(*args)


def attend_back_kernel(
    q_ref, k_ref, v_ref, lse_ref, dctx_ref, cos_ref, sin_ref,
    dqk_ref, dv_ref, dctx, dqk, dk_sum, dv_sum,
):
    heads = dctx.shape[0]
    h = pl.program_id(0)

    @pl.when(h == 0)
    def _():
        for j in range(heads):
            dctx[j] = dctx_ref[:, j * HD : (j + 1) * HD]

    turned = flip(k_ref[0]).astype(LOW)
    for i in range(L // QB):
        lo, hi = i * QB, (i + 1) * QB
        query, back = q_ref[0, lo:hi, :], dctx[h, lo:hi, :]
        lse = lse_ref[0, :, lo:hi]
        prob = jnp.exp(diagonal(nt(k_ref[0, lo:hi, :], query)) - lse)
        grad = nt(v_ref[0, lo:hi, :], back)
        inner = jnp.sum(prob * grad, axis=0, keepdims=True)
        if i:
            prob_body = jnp.exp(nt(k_ref[0, :lo, :], query) - lse)
            grad_body = nt(v_ref[0, :lo, :], back)
            inner = inner + jnp.sum(prob_body * grad_body, axis=0, keepdims=True)
        score = (prob * (grad - inner)).astype(LOW)
        dv_sum[h, lo:hi, :] = nn(prob.astype(LOW), back)
        dk_sum[h, lo:hi, :] = nn(score, query)
        dquery = nn(turned[:, lo:hi], score)
        if i:
            score = (prob_body * (grad_body - inner)).astype(LOW)
            dv_sum[h, :lo, :] += nn(prob_body.astype(LOW), back)
            dk_sum[h, :lo, :] += nn(score, query)
            dquery = dquery + nn(turned[:, :lo], score)
        dqk[h, lo:hi, :] = (dquery * (HD**-0.5)).T

    def finish(i, carry):
        rows = pl.ds(pl.multiple_of(i * QB, QB), QB)
        pair = jnp.concatenate(
            [dqk[j, rows, :] for j in range(heads)] + [dk_sum[j, rows, :] for j in range(heads)],
            axis=1,
        )
        dqk_ref[rows, :] = turn(pair, cos_ref[rows, :], sin_ref[rows, :], -1.0).astype(LOW)
        dv_ref[rows, :] = jnp.concatenate(
            [dv_sum[j, rows, :] for j in range(heads)], axis=1
        ).astype(LOW)
        return carry

    @pl.when(h == heads - 1)
    def _():
        lax.fori_loop(0, L // QB, finish, 0)


def attend_backward(q, k, v, lse, dctx, cosine, sine):
    heads = q.shape[0]
    outs = (
        jax.ShapeDtypeStruct((L, 2 * heads * HD), LOW),
        jax.ShapeDtypeStruct((L, heads * HD), LOW),
    )
    return pl.pallas_call(
        attend_back_kernel,
        grid=(heads,),
        in_specs=[by_head((1, L, HD))] * 3
        + [by_head((1, 1, L)), whole(dctx), whole(cosine), whole(sine)],
        out_specs=[whole(o) for o in outs],
        out_shape=outs,
        scratch_shapes=[pltpu.VMEM((heads, L, HD), LOW)] + [pltpu.VMEM((heads, L, HD), FULL)] * 3,
        compiler_params=pltpu.CompilerParams(vmem_limit_bytes=24 << 20),
        cost_estimate=SMALL,
        name="attend_backward",
    )(pinned(q), pinned(k), pinned(v), pinned(lse), dctx, cosine, sine)


def held_once(array):
    zero = (0,) * array.ndim
    return pl.BlockSpec(array.shape, lambda *_: zero, pipeline_mode=pl.Buffered(1))


def by_rows(kernel, name, flops, row_args, fixed, outs, sums=0, scratch=()):
    specs = [pl.BlockSpec((QB, r.shape[1]), lambda i: (i, 0)) for r in row_args]
    shapes = [
        (pltpu.HBM if away else jax.ShapeDtypeStruct)((L, w), t) for w, t, away in outs
    ]
    out_specs = [pl.BlockSpec((QB, w), lambda i: (i, 0)) for w, _, _ in outs]
    shapes += [jax.ShapeDtypeStruct((1, D), FULL)] * sums
    out_specs += [pl.BlockSpec((1, D), lambda i: (0, 0))] * sums
    row_args = [pinned(r) if r.dtype == FULL else r for r in row_args]
    return pl.pallas_call(
        kernel,
        grid=(L // QB,),
        in_specs=specs + [held_once(f) for f in fixed],
        out_specs=out_specs,
        out_shape=shapes,
        scratch_shapes=list(scratch),
        compiler_params=pltpu.CompilerParams(vmem_limit_bytes=30 << 20),
        cost_estimate=SMALL,
        name=name,
    )(*row_args, *[pinned(f) for f in fixed])


def rms_scale(residual):
    return lax.rsqrt(jnp.mean(residual * residual, axis=1, keepdims=True) + EPSILON)


def norm_back(scaled, normed, inv):
    return inv * (scaled - normed * jnp.mean(scaled * normed, axis=1, keepdims=True))


def column_sum(sum_ref, value):
    @pl.when(pl.program_id(0) == 0)
    def _():
        sum_ref[...] = jnp.zeros_like(sum_ref)

    sum_ref[...] += jnp.sum(value, axis=0, keepdims=True)


def heads_out(held_ref, refs):
    att_ref, y_ref, x_ref, corner_ref = refs
    width = held_ref.shape[2]

    @pl.when(pl.program_id(0) == 0)
    def _():
        for p, ref in enumerate((att_ref, y_ref, x_ref)):
            held_ref[p] = ref[:, 3 * width :]
        held_ref[3] = corner_ref[:, width:]


def project_kernel(one_ref, two_ref, att_ref, y_ref, x_ref, corner_ref, out_ref, held_ref):
    heads_out(held_ref, (att_ref, y_ref, x_ref, corner_ref))
    half = att_ref.shape[0]
    one, two = one_ref[...], two_ref[...]
    out_ref[:, :half] = (nt(one, held_ref[0]) + nt(two, held_ref[2])).astype(LOW)
    out_ref[:, half:] = (nt(one, held_ref[1]) + nt(two, held_ref[3])).astype(LOW)


def blocks(refs, x, y, kind):
    own_ref, y_ref, x_ref, gate_ref, up_ref, down_ref = refs
    if kind == 2:
        return [down_ref[2 * x + y]]
    if x and y:
        return [(up_ref if kind else gate_ref)[...]]
    ref = (x_ref if x else y_ref) if x or y else own_ref
    hid = ref.shape[1] // 2
    return [ref[:, kind * hid : (kind + 1) * hid]]


def onto(rows, parts):
    made = [nn(rows, p) for p in parts]
    return made[0] if len(made) == 1 else jnp.concatenate(made, axis=1)


def back_from(grads, parts):
    start, total = 0, 0.0
    for p in parts:
        total = total + nt(grads[:, start : start + p.shape[1]], p)
        start += p.shape[1]
    return total


def gate_up(hidden, refs, x, gate_ref, up_ref, act_ref):
    half = refs[0].shape[0]
    first, second = hidden[:, :half], hidden[:, half:]
    gate = onto(first, blocks(refs, x, 0, 0)) + onto(second, blocks(refs, x, 1, 0))
    up = onto(first, blocks(refs, x, 0, 1)) + onto(second, blocks(refs, x, 1, 1))
    gate_ref[...] = gate.astype(LOW)
    up_ref[...] = up.astype(LOW)
    act_ref[...] = (gate * jax.nn.sigmoid(gate) * up).astype(LOW)


def enter_kernel(
    rows_ref, mine_ref, theirs_ref, gain_ref, own_ref, y_ref,
    normed_ref, inv_ref, hidden_ref, gate_ref, up_ref, act_ref,
):
    residual = rows_ref[...].astype(FULL) + add(mine_ref[...], theirs_ref[...])
    inv = rms_scale(residual)
    normed = residual * inv
    hidden = (normed * gain_ref[...]).astype(LOW)
    normed_ref[...] = normed.astype(LOW)
    inv_ref[...] = inv
    hidden_ref[...] = hidden
    gate_up(hidden, (own_ref, y_ref, None, None, None, None), 0, gate_ref, up_ref, act_ref)


def rest_kernel(
    hidden_ref, act1_ref, own_ref, y_ref, x_ref, low_ref, high_ref, down_ref,
    gate_ref, up_ref, act_ref, out_ref,
):
    refs = (own_ref, y_ref, x_ref, low_ref, high_ref, down_ref)
    half = own_ref.shape[0]
    gate_up(hidden_ref[...], refs, 1, gate_ref, up_ref, act_ref)
    one, two = act1_ref[...], act_ref[...]
    for y in range(2):
        part = back_from(one, blocks(refs, 0, y, 2)) + back_from(two, blocks(refs, 1, y, 2))
        out_ref[:, y * half : (y + 1) * half] = part.astype(LOW)


def turn_kernel(
    normed_ref, mine_ref, theirs_ref, up_rows_ref, gain1_ref, gain2_ref,
    out_ref, low_ref, sum_ref,
):
    residual = normed_ref[...].astype(FULL) * gain1_ref[...] + add(mine_ref[...], theirs_ref[...])
    inv = rms_scale(residual)
    normed = residual * inv
    gain = gain2_ref[...]
    out_ref[...] = (normed * gain).astype(LOW)
    upstream = up_rows_ref[...].astype(FULL)
    column_sum(sum_ref, upstream * normed)
    low_ref[...] = norm_back(upstream * gain, normed, inv).astype(LOW)


def back_kernel(low_ref, gate1_ref, up1_ref, gate2_ref, up2_ref, down_ref, gg_ref, ug_ref):
    half, hid = down_ref.shape[1], gate1_ref.shape[1]
    first, second = low_ref[:, :half], low_ref[:, half:]
    for x, gate_ref, up_ref in ((0, gate1_ref, up1_ref), (1, gate2_ref, up2_ref)):
        act_grad = nn(first, down_ref[2 * x]) + nn(second, down_ref[2 * x + 1])
        gate, up = gate_ref[...].astype(FULL), up_ref[...].astype(FULL)
        sig = jax.nn.sigmoid(gate)
        gg = act_grad * up * (sig * (1.0 + gate * (1.0 - sig)))
        gg_ref[:, x * hid : (x + 1) * hid] = gg.astype(LOW)
        ug_ref[:, x * hid : (x + 1) * hid] = (act_grad * (gate * sig)).astype(LOW)


def mid_kernel(gg_ref, ug_ref, own_ref, y_ref, x_ref, low_ref, high_ref, mid_ref):
    refs = (own_ref, y_ref, x_ref, low_ref, high_ref, None)
    half, hid = own_ref.shape[0], gg_ref.shape[1] // 2
    for y in range(2):
        total = 0.0
        for x in range(2):
            for kind, ref in enumerate((gg_ref, ug_ref)):
                total = total + back_from(ref[:, x * hid : (x + 1) * hid], blocks(refs, x, y, kind))
        mid_ref[:, y * half : (y + 1) * half] = total.astype(LOW)


def leave_kernel(
    grad_two_ref, mine_ref, theirs_ref, normed_ref, inv_ref,
    gain_ref, att_ref, y_ref, x_ref, corner_ref,
    low_ref, ctx1_ref, ctx2_ref, sum_ref, held_ref,
):
    heads_out(held_ref, (att_ref, y_ref, x_ref, corner_ref))
    half = att_ref.shape[0]
    hidden_grad = grad_two_ref[...].astype(FULL) + add(mine_ref[...], theirs_ref[...])
    normed = normed_ref[...].astype(FULL)
    column_sum(sum_ref, hidden_grad * normed)
    grad = norm_back(hidden_grad * gain_ref[...], normed, inv_ref[...])
    low = grad.astype(LOW)
    low_ref[...] = low
    first, second = low[:, :half], low[:, half:]
    ctx1_ref[...] = (nn(first, held_ref[0]) + nn(second, held_ref[1])).astype(LOW)
    ctx2_ref[...] = (nn(first, held_ref[2]) + nn(second, held_ref[3])).astype(LOW)


def input_kernel(
    qk1_ref, v1_ref, qk2_ref, v2_ref, att_ref, y_ref, x_ref, qk_corner_ref, vo_corner_ref,
    full_ref, low_ref,
):
    half = att_ref.shape[0]
    width = v1_ref.shape[1]
    qk1, v1, qk2, v2 = qk1_ref[...], v1_ref[...], qk2_ref[...], v2_ref[...]
    pair = 2 * width
    first = (
        nt(qk1, att_ref[:, :pair]) + nt(v1, att_ref[:, pair : pair + width])
        + nt(qk2, x_ref[:, :pair]) + nt(v2, x_ref[:, pair : pair + width])
    )
    second = (
        nt(qk1, y_ref[:, :pair]) + nt(v1, y_ref[:, pair : pair + width])
        + nt(qk2, qk_corner_ref[...]) + nt(v2, vo_corner_ref[:, :width])
    )
    full_ref[:, :half] = first
    full_ref[:, half:] = second
    low_ref[:, :half] = first.astype(LOW)
    low_ref[:, half:] = second.astype(LOW)


def heads_grad_kernel(
    rows_ref, grad_ref, qk_ref, v_ref, ctx_ref, qk_near_ref, qk_far_ref, vo_ref
):
    width = v_ref.shape[1]
    rows = flip(rows_ref[...]).astype(LOW)
    qk = nn(rows, qk_ref[...]).astype(LOW)
    vo_ref[:, :width] = nn(rows, v_ref[...]).astype(LOW)
    vo_ref[:, width:] = nn(flip(grad_ref[...]).astype(LOW), ctx_ref[...]).astype(LOW)

    @pl.when(pl.program_id(0) == 0)
    def _():
        qk_near_ref[...] = qk

    @pl.when(pl.program_id(0) == 1)
    def _():
        qk_far_ref[...] = qk


def heads_grad(rows, grad, dqk, dv, context):
    half, pair = D // 2, dqk.shape[1]
    split = pl.BlockSpec((L, half), lambda i: (0, i))
    outs = [jax.ShapeDtypeStruct((half, pair), LOW)] * 2 + [jax.ShapeDtypeStruct((D, pair), LOW)]
    held = [pl.BlockSpec((half, pair), lambda i: (0, 0))] * 2
    return pl.pallas_call(
        heads_grad_kernel,
        grid=(2,),
        in_specs=[split, split] + [held_once(g) for g in (dqk, dv, context)],
        out_specs=held + [pl.BlockSpec((half, pair), lambda i: (i, 0))],
        out_shape=outs,
        compiler_params=pltpu.CompilerParams(vmem_limit_bytes=24 << 20),
        cost_estimate=SMALL,
        name="heads_grad",
    )(rows, grad, dqk, dv, context)


def finish_kernel(core_ref, one_ref, full_ref, out_ref, theirs_ref, mover_ref, grad_ref, low_ref):
    mover = mover_ref[...]
    grad = one_ref[...].astype(FULL) + full_ref[...] + theirs_ref[...].astype(FULL)
    total = 0.0
    for _ in range(3):
        part = grad.astype(LOW)
        total = total + nt(part, mover)
        grad = grad - part.astype(FULL)
    grad_ref[...] = total
    low_ref[...] = nt(out_ref[...], mover).astype(LOW)


def finish(core, grad_one, part_full, layer_output, theirs, mover):
    rows = theirs.shape[0]
    steps = rows // QB
    mine = pl.BlockSpec((QB, D), lambda i, c: (c[0] * steps + i, 0))
    plain = pl.BlockSpec((QB, D), lambda i, c: (i, 0))
    return pl.pallas_call(
        finish_kernel,
        grid_spec=pltpu.PrefetchScalarGridSpec(
            num_scalar_prefetch=1,
            grid=(steps,),
            in_specs=[mine, mine, mine, plain, held_once(mover)],
            out_specs=[plain, plain],
        ),
        out_shape=[
            jax.ShapeDtypeStruct((rows, D), FULL), jax.ShapeDtypeStruct((rows, D), LOW)
        ],
        cost_estimate=SMALL,
        name="finish",
    )(core, grad_one, pinned(part_full), pinned(layer_output), theirs, mover)


def adam_kernel(clip, rates, *refs):
    me = refs[0][0]
    message = refs[1][...] + refs[2][...]
    att, ffn, down = (r[...] for r in refs[3:6])
    ins, norm_ref, outs = refs[6:21], refs[21], refs[22:]
    gain_sum = message[:, : 2 * D]
    total = message[:, 2 * D : 2 * D + 1] + jnp.sum(gain_sum * gain_sum, axis=1, keepdims=True)
    norm = jnp.sqrt(total)
    norm_ref[...] = norm
    ratio = clip / jnp.maximum(norm, clip)

    def update(p, at, grad):
        rate, decay = rates[p]
        old = [ref[at] for ref in ins[3 * p : 3 * p + 3]]
        for ref, value in zip(
            outs[3 * p : 3 * p + 3], adam_update(*old, grad, ratio, rate, decay)
        ):
            ref[at] = value

    width, hid = att.shape[1] // 4, ffn.shape[1] // 2
    for k in range(3):
        update(0, k, att[:, k * width : (k + 1) * width])
    update(1, ..., att[:, 3 * width :].T)
    for k in range(2):
        update(2, k, ffn[:, k * hid : (k + 1) * hid])
    update(3, ..., down)
    block = ins[12].shape[1]
    for k in range(2):
        mine = jnp.zeros((1, block), FULL)
        for j in range(D // block):
            start = k * D + j * block
            mine = jnp.where(me == j, gain_sum[:, start : start + block], mine)
        update(4, pl.ds(k, 1), mine)


def adam(me, clip, rates, grads, params):
    flat = [array for group in params for array in group]
    outs = [jax.ShapeDtypeStruct((1, 1), FULL)]
    outs += [jax.ShapeDtypeStruct(w.shape, FULL) for w in flat]
    vmem = pl.BlockSpec(memory_space=pltpu.VMEM)
    norm, *made = pl.pallas_call(
        functools.partial(adam_kernel, clip, rates),
        in_specs=[pl.BlockSpec(memory_space=pltpu.SMEM)] + [vmem] * (len(grads) + len(flat)),
        out_specs=[vmem] * len(outs),
        out_shape=outs,
        name="adam",
    )(me, *grads, *flat)
    return norm[0, 0], [made[i : i + 3] for i in range(0, len(made), 3)]


def rope_tables():
    half = HD // 2
    lane = jnp.arange(128) % HD
    freq = jnp.exp(-jnp.log(10000.0) * (lane % half).astype(FULL) / half)
    angle = jnp.arange(L, dtype=FULL)[:, None] * freq[None, :]
    return jnp.cos(angle), jnp.where(lane < half, -1.0, 1.0)[None, :] * jnp.sin(angle)


def adam_update(weight, first, second, grad, ratio, rate, decay):
    clipped = grad * ratio
    first_new = AVERAGING * first + (1.0 - AVERAGING) * clipped
    second_new = AVERAGING * second + (1.0 - AVERAGING) * clipped * clipped
    correction = 1.0 - AVERAGING**ADAM_STEP
    step = first_new / correction / (jnp.sqrt(second_new / correction) + 1e-08)
    return (weight - rate * (step + decay * weight), first_new, second_new)


def tn(rows, grads):
    out = lax.dot_general(rows, grads, (((0,), (0,)), ((), ())), preferred_element_type=FULL)
    return layout.with_layout_constraint(out.astype(LOW), layout.Layout((0, 1)))


def per_device(
    layer_input, layer_cotangent,
    attend_weight, attend_first, attend_second,
    output_weight, output_first, output_second,
    gated_weight, gated_first, gated_second,
    down_weight, down_first, down_second,
    norm_gains, gains_first, gains_second,
):
    rows = layer_input.shape[0]
    wide = lax.axis_size("wide")
    block = D // wide
    me = lax.axis_index("wide")
    narrow = lax.axis_index("narrow")
    core = narrow % 2
    cols = attend_weight.shape[2]

    bits = wide_bits()
    near = bits[:-1]
    half = D // 2
    hid = down_weight.shape[0]

    bits = wide_bits()
    near = bits[:-1]
    half = D // 2
    hid = down_weight.shape[0]
    pair = 2 * cols

    attend_low = attend_weight.astype(LOW)
    att = jnp.concatenate(
        [attend_low[0], attend_low[1], attend_low[2], output_weight.T.astype(LOW)], axis=1
    )
    ffn = jnp.concatenate([gated_weight[0], gated_weight[1]], axis=1).astype(LOW)
    down = down_weight.T.astype(LOW)

    order = me ^ jnp.array(block_masks(), jnp.int32)
    source = (order[:, None] * block + jnp.arange(block)[None, :]).reshape(1, D)
    mover = (lax.broadcasted_iota(jnp.int32, (D, D), 0) == source).astype(LOW)

    def both_halves(mine, theirs):
        return jnp.where(
            core == 0,
            jnp.concatenate([mine, theirs], axis=0),
            jnp.concatenate([theirs, mine], axis=0),
        )

    def own_rows(value):
        return lax.dynamic_slice_in_dim(value, core * rows, rows, axis=0)

    first = widen(att, near[:1])
    gains = widen(after(norm_gains, att).astype(LOW).astype(FULL)[None], bits[:1])
    first, down, gains = lax.optimization_barrier((first, down, gains))
    gains = widen(gains, bits[1:-1])
    att = widen(first, near[1:])
    down_y = swap(down, "wide", 1)
    down_x = swap(down, "narrow", 2)
    moved_in = jnp.dot(after(layer_input, first), mover, preferred_element_type=FULL).astype(LOW)
    att, down_y, down_x, gains, moved_in = lax.optimization_barrier(
        (att, down_y, down_x, gains, moved_in)
    )
    att_y = swap(att, "wide", 1)
    att_x = swap(att, "narrow", 2)
    ffn = widen(after(ffn, att), near[:1])
    inputs = both_halves(moved_in, swap(moved_in, "narrow", 1))
    down = jnp.stack([down, down_y, down_x, swap(down_y, "narrow", 2)])[:, None]
    cosine, sine = rope_tables()

    inputs, att, att_y, att_x, ffn, down, cosine, sine = lax.optimization_barrier(
        (inputs, att, att_y, att_x, ffn, down, cosine, sine)
    )
    qk_corner = swap(att_y[:, :pair], "narrow", 2)
    vo_corner = swap(att_x[:, pair:], "wide", 1)
    ffn = widen(ffn, near[1:])
    gains = widen(after(gains, inputs), bits[-1:])
    down = after(down, ffn)
    for bit in near[:1]:
        down = jnp.concatenate([down, swap(down, "wide", bit)], axis=1)
    qk = [[(att, pair, 0), (att_y, pair, 0)], [(att_x, pair, 0), qk_corner]]
    vo = [[(att, pair, 1), (att_y, pair, 1)], [(att_x, pair, 1), vo_corner]]
    saved = [attend_forward(inputs, qk[0], vo[0], cosine, sine)]
    second_in, qk_corner, vo_corner, ffn, gains = lax.optimization_barrier(
        (after(inputs, saved[0][3]), qk_corner, vo_corner, ffn, gains)
    )
    rows_up = after(layer_cotangent, second_in)
    moved_up = jnp.dot(rows_up, mover, preferred_element_type=FULL).astype(LOW)
    upstream = both_halves(moved_up, swap(moved_up, "narrow", 1))
    gains = gains.transpose(1, 0, 2).reshape(2, 1, D)
    qk[1][1], vo[1][1] = qk_corner, vo_corner
    ffn_y = swap(ffn, "wide", 1)
    ffn_x = swap(ffn, "narrow", 2)
    saved.append(attend_forward(second_in, qk[1], vo[1], cosine, sine))
    context = [s[3] for s in saved]
    att_out = [att, att_y, att_x, vo_corner]
    held = [pltpu.VMEM((4, half, cols), LOW)]
    low_d, full_d = (D, LOW, False), (D, FULL, True)
    (attn_part,) = by_rows(
        project_kernel, "project", 2e9, context, att_out, [low_d], scratch=held
    )
    ffn_y, ffn_x, attn_part, down, upstream = lax.optimization_barrier(
        (ffn_y, ffn_x, attn_part, down, upstream)
    )
    attn_other = swap(attn_part, "narrow", 1)
    down_far = [swap(down, "wide", bit) for bit in near[1:2]]
    gate_corner = swap(ffn_y[:, :hid], "narrow", 2)
    up_corner = swap(ffn_x[:, hid:], "wide", 1)
    flow = [(hid, LOW, True), (hid, LOW, True), (hid, LOW, False)]
    normed_one, inv_one, hidden_low, gate1, up1, act1 = by_rows(
        enter_kernel, "enter", 4e9, [inputs, attn_part, attn_other],
        [gains[0], ffn, ffn_y], [(D, LOW, True), (1, FULL, True), low_d] + flow,
    )
    hidden_low, down, down_far = lax.optimization_barrier((hidden_low, down, down_far))
    down = jnp.concatenate([down, *down_far], axis=1)
    for bit in near[2:]:
        down = jnp.concatenate([down, swap(down, "wide", bit)], axis=1)
    down = down.reshape(4, half, hid)
    ffn_all = [ffn, ffn_y, ffn_x, gate_corner, up_corner, down]
    gate2, up2, act2, ffn_part = by_rows(
        rest_kernel, "rest", 5e9, [hidden_low, act1], ffn_all, flow + [low_d]
    )
    ffn_other = swap(ffn_part, "narrow", 1)

    layer_output, grad_two_low, gain_two_grad = by_rows(
        turn_kernel, "turn", 3e9, [normed_one, ffn_part, ffn_other, upstream],
        [gains[0], gains[1]], [(D, LOW, True), low_d], sums=1,
    )
    down_send = tn(grad_two_low, act2)
    down_x = swap(down_send, "narrow", 2)
    wide_flow = (2 * hid, LOW, False)
    gg, ug = by_rows(
        back_kernel, "back", 5e9,
        [after(grad_two_low, down_send), gate1, up1, gate2, up2], [down], [wide_flow, wide_flow],
    )
    gate_send = tn(hidden_low[:, half:], gg)
    up_send = tn(hidden_low, ug[:, hid:])
    gate_y = swap(gate_send, "wide", 1)
    up_x = swap(up_send, "narrow", 2)
    (mid_part,) = by_rows(
        mid_kernel, "mid", 5e9, [after(gg, gate_send, up_send), ug], ffn_all[:5], [low_d]
    )
    mid_other = swap(mid_part, "narrow", 1)
    down_own = tn(grad_two_low, act1)
    gate_own = tn(hidden_low[:, :half], gg)
    up_own = tn(hidden_low, ug[:, :hid])
    mid_part, mid_other, down_own, gate_own, up_own = lax.optimization_barrier(
        (mid_part, mid_other, down_own, gate_own, up_own)
    )
    grad_one_low, dctx1, dctx2, gain_one_grad = by_rows(
        leave_kernel, "leave", 4e9, [grad_two_low, mid_part, mid_other, normed_one, inv_one],
        [gains[0], *att_out], [low_d, (cols, LOW, False), (cols, LOW, False)],
        sums=1, scratch=held,
    )

    down_x, gate_y, dctx2 = lax.optimization_barrier((down_x, gate_y, dctx2))
    down_sum, gate_sum = add(down_own, down_x), add(gate_own, gate_y)
    down_far, gate_far = down_sum[half:].astype(LOW), gate_sum[:, hid:].astype(LOW)
    down_y = swap(down_far, "wide", 1)
    gate_x = swap(gate_far, "narrow", 2)

    q, k, v, _, lse = saved[1]
    dqk2, dv2 = attend_backward(q, k, v, lse, after(dctx2, down_far, gate_far), cosine, sine)
    qk_near2, qk_send2, vo_send = heads_grad(inputs, grad_one_low, dqk2, dv2, context[1])
    vo_x = swap(vo_send, "narrow", 2)
    qk_y2 = swap(qk_send2, "wide", 1)
    back = near[::-1]
    early = add(down_sum[:half], down_y)
    dctx1, early, up_x = lax.optimization_barrier(
        (after(dctx1, vo_send, qk_send2), early, up_x)
    )
    up_sum = add(up_own, up_x)
    up_far = up_sum[half:].astype(LOW)
    up_y = swap(up_far, "wide", 1)
    early = narrow_down(early, back[:1])
    q, k, v, _, lse = saved[0]
    dqk1, dv1 = attend_backward(q, k, v, lse, after(dctx1, up_far), cosine, sine)
    dqk1, dv1, early, qk_y2, gate_x = lax.optimization_barrier((dqk1, dv1, early, qk_y2, gate_x))
    qk_near1, qk_send1, vo_own = heads_grad(inputs, grad_one_low, dqk1, dv1, context[0])
    qk_y1 = swap(qk_send1, "wide", 1)
    qk_far = add(qk_near2, qk_y2).astype(LOW)
    qk_x = swap(qk_far, "narrow", 2)
    early_red = narrow_down(early, back[1:])
    part_full, part_low = by_rows(
        input_kernel, "inputs", 4e9, [dqk1, dv1, dqk2, dv2],
        [att, att_y, att_x, qk_corner, vo_corner], [full_d, low_d],
    )
    late = jnp.concatenate([add(gate_sum[:, :hid], gate_x), add(up_sum[:half], up_y)], axis=1)
    late = narrow_down(late, back[:1])
    vo_sum = add(vo_own, vo_x)
    vo_far = vo_sum[half:].astype(LOW)
    vo_y = swap(vo_far, "wide", 1)
    theirs = lax.dynamic_slice_in_dim(part_low, (1 - core) * rows, rows, axis=0)
    theirs = swap(theirs, "narrow", 1)
    qk_sum = add(qk_near1, qk_y1)
    last = jnp.concatenate([add(qk_sum, qk_x), add(vo_sum[:half], vo_y)], axis=1)
    last, early_red, late, part_full = lax.optimization_barrier(
        (last, early_red, late, part_full)
    )
    late_red = narrow_down(late, back[1:])
    last = narrow_down(last, back[:1])
    gain_grads = lax.dot_general(
        jnp.concatenate([gain_one_grad, gain_two_grad], axis=0), mover.astype(FULL),
        (((1,), (1,)), ((), ())), precision=lax.Precision.HIGHEST, preferred_element_type=FULL,
    )
    early_square = jnp.sum(early_red * early_red) + jnp.sum(late_red * late_red)
    last, gain_grads, early_square = lax.optimization_barrier((last, gain_grads, early_square))
    att_red = narrow_down(last, back[1:])
    input_grad, layer_output = finish(
        jnp.full((1,), core, jnp.int32), grad_one_low, part_full, layer_output,
        after(theirs, att_red), mover,
    )

    square = jnp.full((1, 128), early_square + jnp.sum(att_red * att_red), FULL)
    square = square + swap(square, "narrow", 1)
    message = jnp.concatenate([gain_grads.reshape(1, 2 * D), square], axis=1)
    message = message + swap(message, "narrow", 2)
    for bit in bits[::-1][:-1]:
        message = message + swap(message, "wide", bit)
    received = swap(message, "wide", bits[0])
    all_tokens = rows * wide * lax.axis_size("narrow")
    clip = 0.02 * math.sqrt(all_tokens * (4 * D * D + 3 * D * FF + 2 * D))
    grad_norm, (new_attend, new_output, new_gated, new_down, new_gains) = adam(
        jnp.full((1,), me, jnp.int32),
        clip,
        (
            (D ** (-0.5), WEIGHT_DECAY),
            (max(D // 64, 1) ** (-0.5), WEIGHT_DECAY),
            (D ** (-0.5), WEIGHT_DECAY),
            (FF ** (-0.5), WEIGHT_DECAY),
            (0.4, 0.0),
        ),
        (message, received, att_red, late_red, early_red),
        (
            (attend_weight, attend_first, attend_second),
            (output_weight, output_first, output_second),
            (gated_weight, gated_first, gated_second),
            (down_weight.T, down_first.T, down_second.T),
            (norm_gains, gains_first, gains_second),
        ),
    )
    new_down = [value.T for value in new_down]
    return (
        layer_output, input_grad, grad_norm,
        *new_attend, *new_output, *new_gated, *new_down, *new_gains,
    )


def solution(mesh):
    rows = P(("wide", "narrow"), None)
    stacked = P(None, "wide", "narrow")
    turned = P("narrow", "wide")
    gains = P(None, "wide")
    params = (stacked,) * 3 + (turned,) * 3 + (stacked,) * 3 + (turned,) * 3 + (gains,) * 3
    return jax.shard_map(
        per_device,
        mesh=mesh,
        in_specs=(rows, rows) + params,
        out_specs=(rows, rows, P()) + params,
        check_vma=False,
    )
```

```python
import functools
import math

import jax
import jax.numpy as jnp
from jax import lax
from jax.experimental import layout
from jax.experimental import pallas as pl
from jax.experimental.pallas import tpu as pltpu
from jax.sharding import PartitionSpec as P

D = 768
HD = 64
FF = 2048
L = 1024
ADAM_STEP = 5

EPSILON = 1e-05
WEIGHT_DECAY = 0.1
AVERAGING = 0.5

LOW = jnp.bfloat16
FULL = jnp.float32
QB = 256
MASKED = -1e30
SMALL = pl.CostEstimate(flops=10**6, bytes_accessed=10**4, transcendentals=0)


def swap(value, axis, bit):
    size = lax.axis_size(axis)
    return lax.ppermute(value, axis, [(i, i ^ bit) for i in range(size)])


def wide_bits():
    top = lax.axis_size("wide").bit_length() - 1
    return [1 << b for b in range(top - 1, -1, -1)]


def block_masks():
    masks = [0]
    for bit in wide_bits():
        masks = masks + [m ^ bit for m in masks]
    return masks


def after(value, *done):
    return lax.optimization_barrier((value, done))[0]


def widen(held, bits):
    for bit in bits:
        held = jnp.concatenate([held, swap(held, "wide", bit)], axis=0)
    return held


def add(kept, received):
    return kept.astype(FULL) + received.astype(FULL)


def narrow_down(held, bits):
    for bit in bits:
        half = held.shape[0] // 2
        held = add(held[:half], swap(held[half:].astype(LOW), "wide", bit))
    return held


def turn(value, cosine, sine, sign):
    width = value.shape[1]
    lane = lax.broadcasted_iota(jnp.int32, value.shape, 1) % HD
    other = jnp.where(
        lane < HD // 2,
        pltpu.roll(value, width - HD // 2, 1),
        pltpu.roll(value, HD // 2, 1),
    )
    reps = width // 128
    return value * jnp.concatenate([cosine] * reps, axis=1) + sign * other * jnp.concatenate(
        [sine] * reps, axis=1
    )


def nn(a, b):
    return lax.dot_general(a, b, (((1,), (0,)), ((), ())), preferred_element_type=FULL)


def nt(a, b):
    return lax.dot_general(a, b, (((1,), (1,)), ((), ())), preferred_element_type=FULL)


def diagonal(scores):
    key = lax.broadcasted_iota(jnp.int32, scores.shape, 0)
    query = lax.broadcasted_iota(jnp.int32, scores.shape, 1)
    return jnp.where(key <= query, scores, MASKED)


def flip(value):
    return value.astype(FULL).T


def attend_kernel(
    rows_ref, qka_ref, qkb_ref, voa_ref, vob_ref, cos_ref, sin_ref,
    q_ref, k_ref, v_ref, ctx_ref, lse_ref, hold, q_all, k_all, v_all, weights,
):
    heads = q_all.shape[0]
    width = heads * HD
    half = qka_ref.shape[0]
    h = pl.program_id(0)

    def project(i, carry):
        rows = pl.ds(pl.multiple_of(i * QB, QB), QB)
        made = nn(rows_ref[rows, :], weights[...])
        pair = turn(made[:, : 2 * width], cos_ref[rows, :], sin_ref[rows, :], 1.0)
        for h in range(heads):
            at = h * HD
            q_all[h, rows, :] = (pair[:, at : at + HD] * (HD**-0.5)).astype(LOW)
            k_all[h, rows, :] = pair[:, width + at : width + at + HD].astype(LOW)
            v_all[h, rows, :] = made[:, 2 * width + at : 2 * width + at + HD].astype(LOW)
        return carry

    @pl.when(h == 0)
    def _():
        for start, qk_ref, vo_ref in ((0, qka_ref, voa_ref), (half, qkb_ref, vob_ref)):
            weights[start : start + half, : 2 * width] = qk_ref[...]
            weights[start : start + half, 2 * width :] = vo_ref[:, :width]

    @pl.when(h == 0)
    def _():
        lax.fori_loop(0, L // QB, project, 0)

    q_ref[0] = q_all[h]
    k_ref[0] = k_all[h]
    v_ref[0] = v_all[h]
    turned = flip(v_all[h]).astype(LOW)
    for i in range(L // QB):
        lo, hi = i * QB, (i + 1) * QB
        query = q_all[h, lo:hi, :]
        diag = diagonal(nt(k_all[h, lo:hi, :], query))
        peak = jnp.max(diag, axis=0, keepdims=True)
        if i:
            body = nt(k_all[h, :lo, :], query)
            peak = jnp.maximum(peak, jnp.max(body, axis=0, keepdims=True))
        weight = jnp.exp(diag - peak)
        total = jnp.sum(weight, axis=0, keepdims=True)
        out = nn(turned[:, lo:hi], weight.astype(LOW))
        if i:
            weight = jnp.exp(body - peak)
            total = total + jnp.sum(weight, axis=0, keepdims=True)
            out = out + nn(turned[:, :lo], weight.astype(LOW))
        lse_ref[0, :, lo:hi] = peak + jnp.log(total)
        hold[h, lo:hi, :] = (out / total).T.astype(LOW)

    @pl.when(h == heads - 1)
    def _():
        for j in range(heads):
            ctx_ref[:, j * HD : (j + 1) * HD] = hold[j]


def pinned(array):
    return pltpu.with_memory_space_constraint(array, pltpu.HBM)


def whole(array):
    zero = (0,) * len(array.shape)
    return pl.BlockSpec(array.shape, lambda *_: zero)


def by_head(shape):
    return pl.BlockSpec(shape, lambda h: (h, 0, 0))


def columns(piece, mode=None):
    array, width, j = piece if isinstance(piece, tuple) else (piece, piece.shape[-1], 0)
    lead = (0,) * (array.ndim - 1)
    shape = array.shape[:-1] + (width,)
    return array, pl.BlockSpec(shape, lambda *_: lead + (j,), pipeline_mode=mode)


def width_of(piece):
    return piece[1] if isinstance(piece, tuple) else piece.shape[1]


def attend_forward(rows, qk, vo, cosine, sine):
    heads = width_of(qk[0]) // 2 // HD
    headed = pltpu.HBM((heads, L, HD), LOW)
    outs = (
        headed, headed, headed,
        jax.ShapeDtypeStruct((L, heads * HD), LOW),
        pltpu.HBM((heads, 1, L), FULL),
    )
    args, specs = zip(*[columns(p) for p in (rows, *qk, *vo, cosine, sine)])
    return pl.pallas_call(
        attend_kernel,
        grid=(heads,),
        in_specs=list(specs),
        out_specs=[by_head((1, L, HD))] * 3 + [whole(outs[3]), by_head((1, 1, L))],
        out_shape=outs,
        scratch_shapes=[pltpu.VMEM((heads, L, HD), LOW)] * 4
        + [pltpu.VMEM((D, 3 * heads * HD), LOW)],
        compiler_params=pltpu.CompilerParams(vmem_limit_bytes=24 << 20),
        cost_estimate=SMALL,
        name="attend_forward",
    )(pinned(args[0]), *args[1:])


def attend_back_kernel(
    q_ref, k_ref, v_ref, lse_ref, dctx_ref, cos_ref, sin_ref,
    dqk_ref, dv_ref, dctx, dqk, dk_sum, dv_sum,
):
    heads = dctx.shape[0]
    h = pl.program_id(0)

    @pl.when(h == 0)
    def _():
        for j in range(heads):
            dctx[j] = dctx_ref[:, j * HD : (j + 1) * HD]

    turned = flip(k_ref[0]).astype(LOW)
    for i in range(L // QB):
        lo, hi = i * QB, (i + 1) * QB
        query, back = q_ref[0, lo:hi, :], dctx[h, lo:hi, :]
        lse = lse_ref[0, :, lo:hi]
        prob = jnp.exp(diagonal(nt(k_ref[0, lo:hi, :], query)) - lse)
        grad = nt(v_ref[0, lo:hi, :], back)
        inner = jnp.sum(prob * grad, axis=0, keepdims=True)
        if i:
            prob_body = jnp.exp(nt(k_ref[0, :lo, :], query) - lse)
            grad_body = nt(v_ref[0, :lo, :], back)
            inner = inner + jnp.sum(prob_body * grad_body, axis=0, keepdims=True)
        score = (prob * (grad - inner)).astype(LOW)
        dv_sum[h, lo:hi, :] = nn(prob.astype(LOW), back)
        dk_sum[h, lo:hi, :] = nn(score, query)
        dquery = nn(turned[:, lo:hi], score)
        if i:
            score = (prob_body * (grad_body - inner)).astype(LOW)
            dv_sum[h, :lo, :] += nn(prob_body.astype(LOW), back)
            dk_sum[h, :lo, :] += nn(score, query)
            dquery = dquery + nn(turned[:, :lo], score)
        dqk[h, lo:hi, :] = (dquery * (HD**-0.5)).T

    def finish(i, carry):
        rows = pl.ds(pl.multiple_of(i * QB, QB), QB)
        pair = jnp.concatenate(
            [dqk[j, rows, :] for j in range(heads)] + [dk_sum[j, rows, :] for j in range(heads)],
            axis=1,
        )
        dqk_ref[rows, :] = turn(pair, cos_ref[rows, :], sin_ref[rows, :], -1.0).astype(LOW)
        dv_ref[rows, :] = jnp.concatenate(
            [dv_sum[j, rows, :] for j in range(heads)], axis=1
        ).astype(LOW)
        return carry

    @pl.when(h == heads - 1)
    def _():
        lax.fori_loop(0, L // QB, finish, 0)


def attend_backward(q, k, v, lse, dctx, cosine, sine):
    heads = q.shape[0]
    outs = (
        jax.ShapeDtypeStruct((L, 2 * heads * HD), LOW),
        jax.ShapeDtypeStruct((L, heads * HD), LOW),
    )
    return pl.pallas_call(
        attend_back_kernel,
        grid=(heads,),
        in_specs=[by_head((1, L, HD))] * 3
        + [by_head((1, 1, L)), whole(dctx), whole(cosine), whole(sine)],
        out_specs=[whole(o) for o in outs],
        out_shape=outs,
        scratch_shapes=[pltpu.VMEM((heads, L, HD), LOW)] + [pltpu.VMEM((heads, L, HD), FULL)] * 3,
        compiler_params=pltpu.CompilerParams(vmem_limit_bytes=24 << 20),
        cost_estimate=SMALL,
        name="attend_backward",
    )(pinned(q), pinned(k), pinned(v), pinned(lse), dctx, cosine, sine)


def held_once(array):
    zero = (0,) * array.ndim
    return pl.BlockSpec(array.shape, lambda *_: zero, pipeline_mode=pl.Buffered(1))


def in_top():
    return pl.program_id(0) < pl.num_programs(0) // 2


def halves(step, width):
    steps = L // step // 2
    return [
        pl.BlockSpec((step, width), lambda i: (jnp.minimum(i, steps - 1), 0)),
        pl.BlockSpec((step, width), lambda i: (jnp.maximum(i - steps, 0), 0)),
    ]


def by_rows(kernel, name, row_args, fixed, outs, sums=0, kept=(), scratch=(), step=QB):
    specs, flat = [], []
    for r in row_args:
        if isinstance(r, tuple):
            specs += halves(step, r[0].shape[1])
            flat += r
        else:
            specs.append(pl.BlockSpec((step, r.shape[1]), lambda i: (i, 0)))
            flat.append(r)
    held, held_specs = zip(*[columns(f, pl.Buffered(1)) for f in fixed])
    shapes = [
        (pltpu.HBM if away else jax.ShapeDtypeStruct)((L, w), t) for w, t, away in outs
    ]
    out_specs = [pl.BlockSpec((step, w), lambda i: (i, 0)) for w, _, _ in outs]
    if not outs:
        shapes = [jax.ShapeDtypeStruct((L // 2, D), LOW)] * 2
        out_specs = halves(step, D)
    rows_out = len(shapes)
    shapes += [jax.ShapeDtypeStruct((1, D), FULL)] * sums
    shapes += [pltpu.HBM(shape, LOW) for shape in kept]
    out_specs += [whole(o) for o in shapes[rows_out:]]
    return pl.pallas_call(
        kernel,
        grid=(L // step,),
        in_specs=specs + list(held_specs),
        out_specs=out_specs,
        out_shape=shapes,
        scratch_shapes=list(scratch),
        compiler_params=pltpu.CompilerParams(vmem_limit_bytes=32 << 20),
        cost_estimate=SMALL,
        name=name,
    )(*flat, *[pinned(f) if f.dtype == LOW else f for f in held])


def rms_scale(residual):
    return lax.rsqrt(jnp.mean(residual * residual, axis=1, keepdims=True) + EPSILON)


def norm_back(scaled, normed, inv):
    return inv * (scaled - normed * jnp.mean(scaled * normed, axis=1, keepdims=True))


def column_sum(sum_ref, value):
    @pl.when(pl.program_id(0) == 0)
    def _():
        sum_ref[...] = jnp.zeros_like(sum_ref)

    sum_ref[...] += jnp.sum(value, axis=0, keepdims=True)


def heads_out(held_ref, refs):
    att_ref, y_ref, x_ref, corner_ref = refs
    half, width = att_ref.shape[0], held_ref.shape[2]

    @pl.when(pl.program_id(0) == 0)
    def _():
        held_ref[0, :half] = att_ref[:, 3 * width :]
        held_ref[0, half:] = y_ref[:, 3 * width :]
        held_ref[1, :half] = x_ref[:, 3 * width :]
        held_ref[1, half:] = corner_ref[:, width:]


def project_kernel(one_ref, two_ref, att_ref, y_ref, x_ref, corner_ref, out_ref, held_ref):
    heads_out(held_ref, (att_ref, y_ref, x_ref, corner_ref))
    out_ref[...] = (nt(one_ref[...], held_ref[0]) + nt(two_ref[...], held_ref[1])).astype(LOW)


def gate_up(hidden, weights_ref, gate_ref, up_ref, act_ref):
    hid = gate_ref.shape[1]
    gate = nn(hidden, weights_ref[:, :hid])
    up = nn(hidden, weights_ref[:, hid:])
    gate_ref[...] = gate.astype(LOW)
    up_ref[...] = up.astype(LOW)
    act_ref[...] = (gate * jax.nn.sigmoid(gate) * up).astype(LOW)


def enter_kernel(
    rows_ref, mine_ref, theirs_ref, gain_ref, own_ref, y_ref,
    normed_ref, inv_ref, hidden_ref, gate_ref, up_ref, act_ref, weights_ref,
):
    half = own_ref.shape[0]

    @pl.when(pl.program_id(0) == 0)
    def _():
        weights_ref[:half] = own_ref[...]
        weights_ref[half:] = y_ref[...]

    residual = rows_ref[...].astype(FULL) + add(mine_ref[...], theirs_ref[...])
    inv = rms_scale(residual)
    normed = residual * inv
    hidden = (normed * gain_ref[0]).astype(LOW)
    normed_ref[...] = normed.astype(LOW)
    inv_ref[...] = inv
    hidden_ref[...] = hidden
    gate_up(hidden, weights_ref, gate_ref, up_ref, act_ref)


def rest_kernel(
    hidden_ref, act1_ref, x_ref, gate_corner_ref, up_corner_ref,
    low_own_ref, low_y_ref, low_x_ref, low_corner_ref, high_ref,
    gate_ref, up_ref, act_ref, out_ref, weights_ref, down_ref,
):
    half, hid = x_ref.shape[0], gate_ref.shape[1]
    cut = high_ref.shape[2]

    @pl.when(pl.program_id(0) == 0)
    def _():
        weights_ref[:half] = x_ref[...]
        weights_ref[half:, :hid] = gate_corner_ref[...]
        weights_ref[half:, hid:] = up_corner_ref[...]
        down_ref[0, :half, :cut] = low_own_ref[...]
        down_ref[0, half:, :cut] = low_y_ref[...]
        down_ref[1, :half, :cut] = low_x_ref[...]
        down_ref[1, half:, :cut] = low_corner_ref[...]
        down_ref[:, :, cut:] = high_ref[...]

    gate_up(hidden_ref[...], weights_ref, gate_ref, up_ref, act_ref)
    out_ref[...] = (nt(act1_ref[...], down_ref[0]) + nt(act_ref[...], down_ref[1])).astype(LOW)


def turn_kernel(
    normed_ref, mine_ref, theirs_ref, up_rows_ref, gains_ref,
    out_ref, low_ref, sum_ref,
):
    residual = normed_ref[...].astype(FULL) * gains_ref[0] + add(mine_ref[...], theirs_ref[...])
    inv = rms_scale(residual)
    normed = residual * inv
    gain = gains_ref[1]
    out_ref[...] = (normed * gain).astype(LOW)
    upstream = up_rows_ref[...].astype(FULL)
    column_sum(sum_ref, upstream * normed)
    low_ref[...] = norm_back(upstream * gain, normed, inv).astype(LOW)


def back_kernel(low_ref, gate1_ref, up1_ref, gate2_ref, up2_ref, down_ref, gg_ref, ug_ref):
    hid = gate1_ref.shape[1]
    low = low_ref[...]
    for x, gate_ref, up_ref in ((0, gate1_ref, up1_ref), (1, gate2_ref, up2_ref)):
        act_grad = nn(low, down_ref[x])
        gate, up = gate_ref[...].astype(FULL), up_ref[...].astype(FULL)
        sig = jax.nn.sigmoid(gate)
        gg = act_grad * up * (sig * (1.0 + gate * (1.0 - sig)))
        gg_ref[:, x * hid : (x + 1) * hid] = gg.astype(LOW)
        ug_ref[:, x * hid : (x + 1) * hid] = (act_grad * (gate * sig)).astype(LOW)


def mid_kernel(gg_ref, ug_ref, own_ref, other_ref, top_ref, bottom_ref):
    hid = gg_ref.shape[1] // 2
    total = 0.0
    for x, weights_ref in enumerate((own_ref, other_ref)):
        cols = slice(x * hid, (x + 1) * hid)
        total = total + nt(gg_ref[:, cols], weights_ref[:, :hid])
        total = total + nt(ug_ref[:, cols], weights_ref[:, hid:])
    low = total.astype(LOW)

    @pl.when(in_top())
    def _():
        top_ref[...] = low

    @pl.when(jnp.logical_not(in_top()))
    def _():
        bottom_ref[...] = low


def leave_kernel(
    grad_two_ref, mine_top_ref, mine_bottom_ref, theirs_top_ref, theirs_bottom_ref,
    normed_ref, inv_ref, gains_ref, att_ref, y_ref, x_ref, corner_ref,
    low_ref, ctx1_ref, ctx2_ref, sum_ref, held_ref,
):
    heads_out(held_ref, (att_ref, y_ref, x_ref, corner_ref))
    top = add(mine_top_ref[...], theirs_top_ref[...])
    bottom = add(mine_bottom_ref[...], theirs_bottom_ref[...])
    hidden_grad = grad_two_ref[...].astype(FULL) + jnp.where(in_top(), top, bottom)
    normed = normed_ref[...].astype(FULL)
    column_sum(sum_ref, hidden_grad * normed)
    low = norm_back(hidden_grad * gains_ref[0], normed, inv_ref[...]).astype(LOW)
    low_ref[...] = low
    ctx1_ref[...] = nn(low, held_ref[0]).astype(LOW)
    ctx2_ref[...] = nn(low, held_ref[1]).astype(LOW)


def input_kernel(
    qk1_ref, v1_ref, qk2_ref, v2_ref, att_ref, y_ref, x_ref, qk_corner_ref, vo_corner_ref,
    full_ref, low_ref, held_ref,
):
    half, width = att_ref.shape[0], v1_ref.shape[1]
    pair = 2 * width

    @pl.when(pl.program_id(0) == 0)
    def _():
        held_ref[0, :half] = att_ref[:, : pair + width]
        held_ref[0, half:] = y_ref[:, : pair + width]
        held_ref[1, :half] = x_ref[:, : pair + width]
        held_ref[1, half:, :pair] = qk_corner_ref[...]
        held_ref[1, half:, pair:] = vo_corner_ref[:, :width]

    total = 0.0
    for x, qk_ref, v_ref in ((0, qk1_ref, v1_ref), (1, qk2_ref, v2_ref)):
        total = total + nt(qk_ref[...], held_ref[x, :, :pair])
        total = total + nt(v_ref[...], held_ref[x, :, pair:])
    full_ref[...] = total
    low_ref[...] = total.astype(LOW)


def heads_grad_kernel(
    rows_ref, grad_ref, qk_ref, v_ref, ctx_ref, qk_near_ref, qk_far_ref, vo_ref
):
    width = v_ref.shape[1]
    rows = flip(rows_ref[...]).astype(LOW)
    qk = nn(rows, qk_ref[...]).astype(LOW)
    vo_ref[:, :width] = nn(rows, v_ref[...]).astype(LOW)
    vo_ref[:, width:] = nn(flip(grad_ref[...]).astype(LOW), ctx_ref[...]).astype(LOW)

    @pl.when(pl.program_id(0) == 0)
    def _():
        qk_near_ref[...] = qk

    @pl.when(pl.program_id(0) == 1)
    def _():
        qk_far_ref[...] = qk


def heads_grad(rows, grad, dqk, dv, context):
    half, pair = D // 2, dqk.shape[1]
    split = pl.BlockSpec((L, half), lambda i: (0, i))
    outs = [jax.ShapeDtypeStruct((half, pair), LOW)] * 2 + [jax.ShapeDtypeStruct((D, pair), LOW)]
    held = [pl.BlockSpec((half, pair), lambda i: (0, 0))] * 2
    return pl.pallas_call(
        heads_grad_kernel,
        grid=(2,),
        in_specs=[split, split] + [held_once(g) for g in (dqk, dv, context)],
        out_specs=held + [pl.BlockSpec((half, pair), lambda i: (i, 0))],
        out_shape=outs,
        compiler_params=pltpu.CompilerParams(vmem_limit_bytes=24 << 20),
        cost_estimate=SMALL,
        name="heads_grad",
    )(rows, grad, dqk, dv, context)


def in_order(value, mover):
    total = 0.0
    for _ in range(3):
        part = value.astype(LOW)
        total = total + nt(part, mover)
        value = value - part.astype(FULL)
    return total


def finish_kernel(
    core_ref, one_ref, full_ref, out_ref, theirs_ref, mover_ref, gain_one_ref, gain_two_ref,
    grad_ref, low_ref, first_ref, second_ref,
):
    mover = mover_ref[...]
    grad = one_ref[...].astype(FULL) + full_ref[...] + theirs_ref[...].astype(FULL)
    grad_ref[...] = in_order(grad, mover)
    low_ref[...] = nt(out_ref[...], mover).astype(LOW)

    @pl.when(pl.program_id(0) == 0)
    def _():
        both = jnp.concatenate([gain_one_ref[...], gain_two_ref[...]], axis=0)
        both = in_order(both, mover)
        first_ref[...] = both[:1]
        second_ref[...] = both[1:]


def finish(core, grad_one, part_full, layer_output, theirs, mover, gain_one, gain_two):
    rows = theirs.shape[0]
    block = 128
    steps = rows // block
    mine = pl.BlockSpec((block, D), lambda i, c: (c[0] * steps + i, 0))
    plain = pl.BlockSpec((block, D), lambda i, c: (i, 0))
    return pl.pallas_call(
        finish_kernel,
        grid_spec=pltpu.PrefetchScalarGridSpec(
            num_scalar_prefetch=1,
            grid=(steps,),
            in_specs=[mine, mine, mine, plain, held_once(mover), whole(gain_one), whole(gain_two)],
            out_specs=[plain, plain, whole(gain_one), whole(gain_two)],
        ),
        out_shape=[
            jax.ShapeDtypeStruct((rows, D), FULL), jax.ShapeDtypeStruct((rows, D), LOW)
        ] + [jax.ShapeDtypeStruct((1, D), FULL)] * 2,
        cost_estimate=SMALL,
        name="finish",
    )(
        core, grad_one, pinned(part_full), pinned(layer_output), theirs, mover,
        gain_one, gain_two,
    )


def adam_kernel(clip, rates, *refs):
    me = refs[0][0]
    message = refs[1][...] + refs[2][...]
    att_ref, ffn_ref, down_ref = refs[3:6]
    ins, norm_ref, outs = refs[6:21], refs[21], refs[22:]
    block = ins[12].shape[1]
    gain_sum = message[:, : 2 * D]
    total = message[:, 2 * D : 2 * D + 1] + jnp.sum(gain_sum * gain_sum, axis=1, keepdims=True)
    norm = jnp.sqrt(total)
    norm_ref[...] = norm
    ratio = clip / jnp.maximum(norm, clip)

    def update(p, at, grad):
        rate, decay = rates[p]
        old = [ref[at] for ref in ins[3 * p : 3 * p + 3]]
        for ref, value in zip(
            outs[3 * p : 3 * p + 3], adam_update(*old, grad, ratio, rate, decay)
        ):
            ref[at] = value

    width, hid = att_ref.shape[1] // 4, ffn_ref.shape[1] // 2
    step = 16 if block % 16 == 0 else block

    def some(i, carry):
        rows = pl.ds(pl.multiple_of(i * step, step), step) if step < block else slice(None)
        for k in range(3):
            update(0, (k, rows), att_ref[rows, k * width : (k + 1) * width])
        for k in range(2):
            update(2, (k, rows), ffn_ref[rows, k * hid : (k + 1) * hid])
        update(3, rows, down_ref[rows, :])
        return carry

    if step < block:
        lax.fori_loop(0, block // step, some, 0)
    else:
        some(0, 0)
    update(1, ..., att_ref[:, 3 * width :].T)
    for k in range(2):
        mine = jnp.zeros((1, block), FULL)
        for j in range(D // block):
            start = k * D + j * block
            mine = jnp.where(me == j, gain_sum[:, start : start + block], mine)
        update(4, pl.ds(k, 1), mine)


def adam(me, clip, rates, grads, params):
    flat = [array for group in params for array in group]
    outs = [jax.ShapeDtypeStruct((1, 1), FULL)]
    outs += [jax.ShapeDtypeStruct(w.shape, FULL) for w in flat]
    vmem = pl.BlockSpec(memory_space=pltpu.VMEM)
    norm, *made = pl.pallas_call(
        functools.partial(adam_kernel, clip, rates),
        in_specs=[pl.BlockSpec(memory_space=pltpu.SMEM)] + [vmem] * (len(grads) + len(flat)),
        out_specs=[vmem] * len(outs),
        out_shape=outs,
        name="adam",
    )(me, *grads, *flat)
    return norm[0, 0], [made[i : i + 3] for i in range(0, len(made), 3)]


def rope_tables():
    half = HD // 2
    lane = jnp.arange(128) % HD
    freq = jnp.exp(-jnp.log(10000.0) * (lane % half).astype(FULL) / half)
    angle = jnp.arange(L, dtype=FULL)[:, None] * freq[None, :]
    return jnp.cos(angle), jnp.where(lane < half, -1.0, 1.0)[None, :] * jnp.sin(angle)


def adam_update(weight, first, second, grad, ratio, rate, decay):
    clipped = grad * ratio
    first_new = AVERAGING * first + (1.0 - AVERAGING) * clipped
    second_new = AVERAGING * second + (1.0 - AVERAGING) * clipped * clipped
    correction = 1.0 - AVERAGING**ADAM_STEP
    step = first_new / correction / (jnp.sqrt(second_new / correction) + 1e-08)
    return (weight - rate * (step + decay * weight), first_new, second_new)


def tn(rows, grads):
    out = lax.dot_general(rows, grads, (((0,), (0,)), ((), ())), preferred_element_type=FULL)
    return layout.with_layout_constraint(out.astype(LOW), layout.Layout((0, 1)))


def per_device(
    layer_input, layer_cotangent,
    attend_weight, attend_first, attend_second,
    output_weight, output_first, output_second,
    gated_weight, gated_first, gated_second,
    down_weight, down_first, down_second,
    norm_gains, gains_first, gains_second,
):
    rows = layer_input.shape[0]
    wide = lax.axis_size("wide")
    block = D // wide
    me = lax.axis_index("wide")
    narrow = lax.axis_index("narrow")
    core = narrow % 2
    cols = attend_weight.shape[2]

    bits = wide_bits()
    near = bits[:-1]
    half = D // 2
    hid = down_weight.shape[0]

    bits = wide_bits()
    near = bits[:-1]
    half = D // 2
    hid = down_weight.shape[0]
    pair = 2 * cols

    attend_low = attend_weight.astype(LOW)
    att = jnp.concatenate(
        [attend_low[0], attend_low[1], attend_low[2], output_weight.T.astype(LOW)], axis=1
    )
    cut = hid // 2
    down_t = down_weight.T
    ffn = jnp.concatenate([gated_weight[0], gated_weight[1], down_t[:, :cut]], axis=1).astype(LOW)
    down = down_t[:, cut:].astype(LOW)

    order = me ^ jnp.array(block_masks(), jnp.int32)
    source = (order[:, None] * block + jnp.arange(block)[None, :]).reshape(1, D)
    mover = (lax.broadcasted_iota(jnp.int32, (D, D), 0) == source).astype(LOW)
    mover = lax.optimization_barrier(mover)

    def both_halves(mine, theirs):
        return jnp.where(
            core == 0,
            jnp.concatenate([mine, theirs], axis=0),
            jnp.concatenate([theirs, mine], axis=0),
        )

    def own_rows(value):
        return lax.dynamic_slice_in_dim(value, core * rows, rows, axis=0)

    first = widen(att, near[:1])
    gains = widen(after(norm_gains, att).astype(LOW).astype(FULL)[None], bits[:1])
    first, down, gains = lax.optimization_barrier((first, down, gains))
    gains = widen(gains, bits[1:-1])
    att = widen(first, near[1:])
    down_y = swap(down, "wide", 1)
    down_x = swap(down, "narrow", 2)
    moved_in = jnp.dot(after(layer_input, first), mover, preferred_element_type=FULL).astype(LOW)
    att, down_y, down_x, gains, moved_in = lax.optimization_barrier(
        (att, down_y, down_x, gains, moved_in)
    )
    att_y = swap(att, "wide", 1)
    att_x = swap(att, "narrow", 2)
    ffn = widen(after(ffn, att), near[:1])
    gains = widen(gains, bits[-1:])
    inputs = both_halves(moved_in, swap(moved_in, "narrow", 1))
    cosine, sine = rope_tables()

    inputs, att, att_y, att_x, ffn, gains, cosine, sine = lax.optimization_barrier(
        (inputs, att, att_y, att_x, ffn, gains, cosine, sine)
    )
    gains = gains.transpose(1, 0, 2).reshape(2, 1, D)
    down_corner = swap(down_y, "narrow", 2)
    qk_corner = swap(att_y[:, :pair], "narrow", 2)
    vo_corner = swap(att_x[:, pair:], "wide", 1)
    ffn = widen(ffn, near[1:])
    qk = [[(att, pair, 0), (att_y, pair, 0)], [(att_x, pair, 0), qk_corner]]
    vo = [[(att, pair, 1), (att_y, pair, 1)], [(att_x, pair, 1), vo_corner]]
    saved = [attend_forward(inputs, qk[0], vo[0], cosine, sine)]
    rows_up = after(layer_cotangent, inputs)
    moved_up = jnp.dot(rows_up, mover, preferred_element_type=FULL).astype(LOW)
    second_in, qk_corner, vo_corner, ffn, down_corner, moved_up = lax.optimization_barrier(
        (after(inputs, saved[0][3]), qk_corner, vo_corner, ffn, down_corner, moved_up)
    )
    other_up = swap(moved_up, "narrow", 1)
    down = jnp.stack([down, down_y, down_x, down_corner])[:, None]
    for bit in near[:1]:
        down = jnp.concatenate([down, swap(down, "wide", bit)], axis=1)
    qk[1][1], vo[1][1] = qk_corner, vo_corner
    ffn_y = swap(ffn, "wide", 1)
    ffn_x = swap(ffn, "narrow", 2)
    saved.append(attend_forward(second_in, qk[1], vo[1], cosine, sine))
    context = [s[3] for s in saved]
    att_out = [att, att_y, att_x, vo_corner]
    held = [pltpu.VMEM((2, D, cols), LOW)]
    low_d, full_d = (D, LOW, False), (D, FULL, True)
    (attn_part,) = by_rows(
        project_kernel, "project", context, att_out, [low_d], scratch=held
    )
    ffn_y, ffn_x, attn_part, down = lax.optimization_barrier((ffn_y, ffn_x, attn_part, down))
    attn_other = swap(attn_part, "narrow", 1)
    down_far = [swap(down, "wide", bit) for bit in near[1:2]]
    gate_corner = swap(ffn_y[:, :hid], "narrow", 2)
    up_corner = swap(ffn_x[:, hid:], "wide", 1)
    flow = [(hid, LOW, True), (hid, LOW, True), (hid, LOW, False)]
    normed_one, inv_one, hidden_low, gate1, up1, act1, gu_own = by_rows(
        enter_kernel, "enter", [pinned(inputs), attn_part, attn_other],
        [gains, (ffn, 2 * hid, 0), (ffn_y, 2 * hid, 0)],
        [(D, LOW, True), (1, FULL, True), low_d] + flow, kept=[(D, 2 * hid)],
    )
    hidden_low, down, down_far = lax.optimization_barrier((hidden_low, down, down_far))
    upstream = both_halves(after(moved_up, hidden_low), other_up)
    down = jnp.concatenate([down, *down_far], axis=1)
    for bit in near[2:]:
        down = jnp.concatenate([down, swap(down, "wide", bit)], axis=1)
    down = down.reshape(2, D, hid - cut)
    last_cols = 2 * hid // cut
    gate2, up2, act2, ffn_part, gu_other, down_all = by_rows(
        rest_kernel, "rest", [after(hidden_low, upstream), act1],
        [
            (ffn_x, 2 * hid, 0), gate_corner, (up_corner, hid, 0),
            (ffn, cut, last_cols), (ffn_y, cut, last_cols), (ffn_x, cut, last_cols),
            (up_corner, cut, hid // cut), down,
        ],
        flow + [low_d], kept=[(D, 2 * hid), (2, D, hid)],
    )
    ffn_other = swap(ffn_part, "narrow", 1)

    layer_output, grad_two_low, gain_two_grad = by_rows(
        turn_kernel, "turn", [pinned(normed_one), ffn_part, ffn_other, pinned(upstream)],
        [gains], [(D, LOW, True), low_d], sums=1, step=128,
    )
    down_send = tn(grad_two_low, act2)
    down_x = swap(down_send, "narrow", 2)
    wide_flow = (2 * hid, LOW, False)
    saves = [pinned(r) for r in (gate1, up1, gate2, up2)]
    gg, ug = by_rows(
        back_kernel, "back",
        [after(grad_two_low, down_send), *saves], [down_all], [wide_flow, wide_flow],
    )
    gate_send = tn(hidden_low[:, half:], gg)
    up_send = tn(hidden_low, ug[:, hid:])
    gate_y = swap(gate_send, "wide", 1)
    up_x = swap(up_send, "narrow", 2)
    mid_part = by_rows(
        mid_kernel, "mid", [after(gg, gate_send, up_send), ug], [gu_own, gu_other], []
    )
    mid_other = [swap(part, "narrow", 1) for part in mid_part]
    down_own = tn(grad_two_low, act1)
    gate_own = tn(hidden_low[:, :half], gg)
    up_own = tn(hidden_low, ug[:, :hid])
    mid_part, mid_other, down_own, gate_own, up_own, down_x = lax.optimization_barrier(
        (mid_part, mid_other, down_own, gate_own, up_own, down_x)
    )
    grad_one_low, dctx1, dctx2, gain_one_grad = by_rows(
        leave_kernel, "leave",
        [grad_two_low, tuple(mid_part), tuple(mid_other), pinned(normed_one), pinned(inv_one)],
        [gains, *att_out], [low_d, (cols, LOW, False), (cols, LOW, False)],
        sums=1, scratch=held,
    )

    q, k, v, _, lse = saved[1]
    dqk2, dv2 = attend_backward(q, k, v, lse, dctx2, cosine, sine)
    down_x, gate_y, dqk2, dv2 = lax.optimization_barrier((down_x, gate_y, dqk2, dv2))
    down_sum, gate_sum = add(down_own, down_x), add(gate_own, gate_y)
    down_y = swap(down_sum[half:].astype(LOW), "wide", 1)
    gate_far = gate_sum[:, hid:].astype(LOW)
    gate_x = swap(gate_far, "narrow", 2)
    qk_near2, qk_send2, vo_send = heads_grad(inputs, grad_one_low, after(dqk2, gate_far), dv2, context[1])
    vo_x = swap(vo_send, "narrow", 2)
    qk_y2 = swap(qk_send2, "wide", 1)
    back = near[::-1]
    q, k, v, _, lse = saved[0]
    dqk1, dv1 = attend_backward(q, k, v, lse, after(dctx1, vo_send, qk_send2), cosine, sine)
    dqk1, dv1, up_x, down_y, qk_y2, gate_x = lax.optimization_barrier(
        (dqk1, dv1, up_x, down_y, qk_y2, gate_x)
    )
    early = narrow_down(add(down_sum[:half], down_y), back[:1])
    up_sum = add(up_own, up_x)
    up_y = swap(up_sum[half:].astype(LOW), "wide", 1)
    qk_near1, qk_send1, vo_own = heads_grad(inputs, grad_one_low, dqk1, dv1, context[0])
    qk_y1 = swap(qk_send1, "wide", 1)
    qk_far = add(qk_near2, qk_y2).astype(LOW)
    qk_x = swap(qk_far, "narrow", 2)
    part_full, part_low = by_rows(
        input_kernel, "inputs", [after(dqk1, qk_send1, qk_far, early), dv1, dqk2, dv2],
        [att, att_y, att_x, qk_corner, vo_corner], [full_d, low_d],
        scratch=[pltpu.VMEM((2, D, 3 * cols), LOW)],
    )
    early, part_low = lax.optimization_barrier((early, part_low))
    early_red = narrow_down(early, back[1:])
    late = jnp.concatenate([add(gate_sum[:, :hid], gate_x), add(up_sum[:half], up_y)], axis=1)
    late = narrow_down(late, back[:1])
    vo_sum = add(vo_own, vo_x)
    vo_far = vo_sum[half:].astype(LOW)
    vo_y = swap(vo_far, "wide", 1)
    theirs = lax.dynamic_slice_in_dim(part_low, (1 - core) * rows, rows, axis=0)
    theirs = swap(theirs, "narrow", 1)
    qk_sum = add(qk_near1, qk_y1)
    last = jnp.concatenate([add(qk_sum, qk_x), add(vo_sum[:half], vo_y)], axis=1)
    last, early_red, late, part_full = lax.optimization_barrier(
        (last, early_red, late, part_full)
    )
    late_red = narrow_down(late, back[1:])
    last = narrow_down(last, back[:1])
    early_square = jnp.sum(early_red * early_red) + jnp.sum(late_red * late_red)
    input_grad, layer_output, gain_one_grad, gain_two_grad = finish(
        jnp.full((1,), core, jnp.int32), grad_one_low, part_full, layer_output,
        after(theirs, last), mover, gain_one_grad, gain_two_grad,
    )
    att_red = narrow_down(last, back[1:])
    att_red, early_square, input_grad, layer_output, gain_one_grad, gain_two_grad = (
        lax.optimization_barrier(
            (att_red, early_square, input_grad, layer_output, gain_one_grad, gain_two_grad)
        )
    )

    square = jnp.full((1, 128), early_square + jnp.sum(att_red * att_red), FULL)
    square = square + swap(square, "narrow", 1)
    message = jnp.concatenate([gain_one_grad, gain_two_grad, square], axis=1)
    message = message + swap(message, "narrow", 2)
    for bit in bits[::-1][:-1]:
        message = message + swap(message, "wide", bit)
    received = swap(message, "wide", bits[0])
    all_tokens = rows * wide * lax.axis_size("narrow")
    clip = 0.02 * math.sqrt(all_tokens * (4 * D * D + 3 * D * FF + 2 * D))
    grad_norm, (new_attend, new_output, new_gated, new_down, new_gains) = adam(
        jnp.full((1,), me, jnp.int32),
        clip,
        (
            (D ** (-0.5), WEIGHT_DECAY),
            (max(D // 64, 1) ** (-0.5), WEIGHT_DECAY),
            (D ** (-0.5), WEIGHT_DECAY),
            (FF ** (-0.5), WEIGHT_DECAY),
            (0.4, 0.0),
        ),
        (message, received, att_red, late_red, early_red),
        (
            (attend_weight, attend_first, attend_second),
            (output_weight, output_first, output_second),
            (gated_weight, gated_first, gated_second),
            (down_weight.T, down_first.T, down_second.T),
            (norm_gains, gains_first, gains_second),
        ),
    )
    new_down = [value.T for value in new_down]
    return (
        layer_output, input_grad, grad_norm,
        *new_attend, *new_output, *new_gated, *new_down, *new_gains,
    )


def solution(mesh):
    rows = P(("wide", "narrow"), None)
    stacked = P(None, "wide", "narrow")
    turned = P("narrow", "wide")
    gains = P(None, "wide")
    params = (stacked,) * 3 + (turned,) * 3 + (stacked,) * 3 + (turned,) * 3 + (gains,) * 3
    return jax.shard_map(
        per_device,
        mesh=mesh,
        in_specs=(rows, rows) + params,
        out_specs=(rows, rows, P()) + params,
        check_vma=False,
    )
```

```python
import functools
import math

import jax
import jax.numpy as jnp
from jax import lax
from jax.experimental import layout
from jax.experimental import pallas as pl
from jax.experimental.pallas import tpu as pltpu
from jax.sharding import PartitionSpec as P

D = 768
HD = 64
FF = 2048
L = 1024
ADAM_STEP = 5

EPSILON = 1e-05
WEIGHT_DECAY = 0.1
AVERAGING = 0.5

LOW = jnp.bfloat16
FULL = jnp.float32
QB = 256
MASKED = -1e30
SMALL = pl.CostEstimate(flops=10**6, bytes_accessed=10**4, transcendentals=0)


def swap(value, axis, bit):
    size = lax.axis_size(axis)
    return lax.ppermute(value, axis, [(i, i ^ bit) for i in range(size)])


def wide_bits():
    top = lax.axis_size("wide").bit_length() - 1
    return [1 << b for b in range(top - 1, -1, -1)]


def block_masks():
    masks = [0]
    for bit in wide_bits():
        masks = masks + [m ^ bit for m in masks]
    return masks


def after(value, *done):
    return lax.optimization_barrier((value, done))[0]


def widen(held, bits):
    for bit in bits:
        held = jnp.concatenate([held, swap(held, "wide", bit)], axis=0)
    return held


def add(kept, received):
    return kept.astype(FULL) + received.astype(FULL)


def narrow_down(held, bits):
    for bit in bits:
        half = held.shape[0] // 2
        held = add(held[:half], swap(held[half:].astype(LOW), "wide", bit))
    return held


def turn(value, cosine, sine, sign):
    width = value.shape[1]
    lane = lax.broadcasted_iota(jnp.int32, value.shape, 1) % HD
    other = jnp.where(
        lane < HD // 2,
        pltpu.roll(value, width - HD // 2, 1),
        pltpu.roll(value, HD // 2, 1),
    )
    reps = width // 128
    return value * jnp.concatenate([cosine] * reps, axis=1) + sign * other * jnp.concatenate(
        [sine] * reps, axis=1
    )


def nn(a, b):
    return lax.dot_general(a, b, (((1,), (0,)), ((), ())), preferred_element_type=FULL)


def nt(a, b):
    return lax.dot_general(a, b, (((1,), (1,)), ((), ())), preferred_element_type=FULL)


def diagonal(scores):
    key = lax.broadcasted_iota(jnp.int32, scores.shape, 0)
    query = lax.broadcasted_iota(jnp.int32, scores.shape, 1)
    return jnp.where(key <= query, scores, MASKED)


def flip(value):
    return value.astype(FULL).T


def attend_kernel(
    rows_ref, qka_ref, qkb_ref, voa_ref, vob_ref, cos_ref, sin_ref,
    q_ref, k_ref, v_ref, ctx_ref, lse_ref, hold,
):
    heads = q_ref.shape[0]
    width = heads * HD
    half = qka_ref.shape[0]

    def project(i, carry):
        rows = pl.ds(pl.multiple_of(i * QB, QB), QB)
        first, second = rows_ref[rows, :half], rows_ref[rows, half:]
        pair = nn(first, qka_ref[...]) + nn(second, qkb_ref[...])
        pair = turn(pair, cos_ref[rows, :], sin_ref[rows, :], 1.0)
        value = nn(first, voa_ref[:, :width]) + nn(second, vob_ref[:, :width])
        for h in range(heads):
            q_ref[h, rows, :] = (pair[:, h * HD : (h + 1) * HD] * (HD**-0.5)).astype(LOW)
            k_ref[h, rows, :] = pair[:, width + h * HD : width + (h + 1) * HD].astype(LOW)
            v_ref[h, rows, :] = value[:, h * HD : (h + 1) * HD].astype(LOW)
        return carry

    lax.fori_loop(0, L // QB, project, 0)

    def head(h, carry):
        turned = flip(v_ref[h]).astype(LOW)
        for i in range(L // QB):
            lo, hi = i * QB, (i + 1) * QB
            query = q_ref[h, lo:hi, :]
            diag = diagonal(nt(k_ref[h, lo:hi, :], query))
            peak = jnp.max(diag, axis=0, keepdims=True)
            if i:
                body = nt(k_ref[h, :lo, :], query)
                peak = jnp.maximum(peak, jnp.max(body, axis=0, keepdims=True))
            weight = jnp.exp(diag - peak)
            total = jnp.sum(weight, axis=0, keepdims=True)
            out = nn(turned[:, lo:hi], weight.astype(LOW))
            if i:
                weight = jnp.exp(body - peak)
                total = total + jnp.sum(weight, axis=0, keepdims=True)
                out = out + nn(turned[:, :lo], weight.astype(LOW))
            lse_ref[h, :, lo:hi] = peak + jnp.log(total)
            hold[h, lo:hi, :] = (out / total).T.astype(LOW)
        return carry

    lax.fori_loop(0, heads, head, 0)
    for h in range(heads):
        ctx_ref[:, h * HD : (h + 1) * HD] = hold[h]


def pinned(array):
    return pltpu.with_memory_space_constraint(array, pltpu.HBM)


def whole(array):
    zero = (0,) * len(array.shape)
    return pl.BlockSpec(array.shape, lambda *_: zero)


def by_head(shape):
    return pl.BlockSpec(shape, lambda h: (h, 0, 0))


def columns(piece, mode=None):
    array, width, j = piece if isinstance(piece, tuple) else (piece, piece.shape[-1], 0)
    lead = (0,) * (array.ndim - 1)
    shape = array.shape[:-1] + (width,)
    return array, pl.BlockSpec(shape, lambda *_: lead + (j,), pipeline_mode=mode)


def width_of(piece):
    return piece[1] if isinstance(piece, tuple) else piece.shape[1]


def attend_forward(rows, qk, vo, cosine, sine):
    heads = width_of(qk[0]) // 2 // HD
    headed = pltpu.HBM((heads, L, HD), LOW)
    outs = (
        headed, headed, headed,
        jax.ShapeDtypeStruct((L, heads * HD), LOW),
        pltpu.HBM((heads, 1, L), FULL),
    )
    args, specs = zip(*[columns(p) for p in (rows, *qk, *vo, pinned(cosine), pinned(sine))])
    return pl.pallas_call(
        attend_kernel,
        grid=(1,),
        in_specs=list(specs),
        out_specs=[whole(o) for o in outs],
        out_shape=outs,
        scratch_shapes=[pltpu.VMEM((heads, L, HD), LOW)],
        compiler_params=pltpu.CompilerParams(vmem_limit_bytes=24 << 20),
        cost_estimate=SMALL,
        name="attend_forward",
    )(*args)


def attend_back_kernel(
    q_ref, k_ref, v_ref, lse_ref, dctx_ref, cos_ref, sin_ref,
    dqk_ref, dv_ref, dctx, dqk, dk_sum, dv_sum,
):
    heads = dctx.shape[0]
    h = pl.program_id(0)

    @pl.when(h == 0)
    def _():
        for j in range(heads):
            dctx[j] = dctx_ref[:, j * HD : (j + 1) * HD]

    turned = flip(k_ref[0]).astype(LOW)
    for i in range(L // QB):
        lo, hi = i * QB, (i + 1) * QB
        query, back = q_ref[0, lo:hi, :], dctx[h, lo:hi, :]
        lse = lse_ref[0, :, lo:hi]
        prob = jnp.exp(diagonal(nt(k_ref[0, lo:hi, :], query)) - lse)
        grad = nt(v_ref[0, lo:hi, :], back)
        inner = jnp.sum(prob * grad, axis=0, keepdims=True)
        if i:
            prob_body = jnp.exp(nt(k_ref[0, :lo, :], query) - lse)
            grad_body = nt(v_ref[0, :lo, :], back)
            inner = inner + jnp.sum(prob_body * grad_body, axis=0, keepdims=True)
        score = (prob * (grad - inner)).astype(LOW)
        dv_sum[h, lo:hi, :] = nn(prob.astype(LOW), back)
        dk_sum[h, lo:hi, :] = nn(score, query)
        dquery = nn(turned[:, lo:hi], score)
        if i:
            score = (prob_body * (grad_body - inner)).astype(LOW)
            dv_sum[h, :lo, :] += nn(prob_body.astype(LOW), back)
            dk_sum[h, :lo, :] += nn(score, query)
            dquery = dquery + nn(turned[:, :lo], score)
        dqk[h, lo:hi, :] = (dquery * (HD**-0.5)).T

    def finish(i, carry):
        rows = pl.ds(pl.multiple_of(i * QB, QB), QB)
        pair = jnp.concatenate(
            [dqk[j, rows, :] for j in range(heads)] + [dk_sum[j, rows, :] for j in range(heads)],
            axis=1,
        )
        dqk_ref[rows, :] = turn(pair, cos_ref[rows, :], sin_ref[rows, :], -1.0).astype(LOW)
        dv_ref[rows, :] = jnp.concatenate(
            [dv_sum[j, rows, :] for j in range(heads)], axis=1
        ).astype(LOW)
        return carry

    @pl.when(h == heads - 1)
    def _():
        lax.fori_loop(0, L // QB, finish, 0)


def attend_backward(q, k, v, lse, dctx, cosine, sine):
    heads = q.shape[0]
    outs = (
        jax.ShapeDtypeStruct((L, 2 * heads * HD), LOW),
        jax.ShapeDtypeStruct((L, heads * HD), LOW),
    )
    return pl.pallas_call(
        attend_back_kernel,
        grid=(heads,),
        in_specs=[by_head((1, L, HD))] * 3
        + [by_head((1, 1, L)), whole(dctx), whole(cosine), whole(sine)],
        out_specs=[whole(o) for o in outs],
        out_shape=outs,
        scratch_shapes=[pltpu.VMEM((heads, L, HD), LOW)] + [pltpu.VMEM((heads, L, HD), FULL)] * 3,
        compiler_params=pltpu.CompilerParams(vmem_limit_bytes=24 << 20),
        cost_estimate=SMALL,
        name="attend_backward",
    )(pinned(q), pinned(k), pinned(v), pinned(lse), pinned(dctx), pinned(cosine), pinned(sine))


def held_once(array):
    zero = (0,) * array.ndim
    return pl.BlockSpec(array.shape, lambda *_: zero, pipeline_mode=pl.Buffered(1))


def in_top():
    return pl.program_id(0) < pl.num_programs(0) // 2


def halves(step, width):
    steps = L // step // 2
    return [
        pl.BlockSpec((step, width), lambda i: (jnp.minimum(i, steps - 1), 0)),
        pl.BlockSpec((step, width), lambda i: (jnp.maximum(i - steps, 0), 0)),
    ]


def by_rows(kernel, name, row_args, fixed, outs, sums=0, kept=(), scratch=(), loose=()):
    step = QB
    specs, flat = [], []
    for r in row_args:
        if isinstance(r, tuple):
            specs += halves(step, r[0].shape[1])
            flat += r
        else:
            specs.append(pl.BlockSpec((step, r.shape[1]), lambda i: (i, 0)))
            flat.append(r)
    held, held_specs = zip(*[columns(f, pl.Buffered(1)) for f in fixed])
    shapes = [
        (pltpu.HBM if away else jax.ShapeDtypeStruct)((L, w), t) for w, t, away in outs
    ]
    out_specs = [pl.BlockSpec((step, w), lambda i: (i, 0)) for w, _, _ in outs]
    if not outs:
        shapes = [jax.ShapeDtypeStruct((L // 2, D), LOW)] * 2
        out_specs = halves(step, D)
    rows_out = len(shapes)
    shapes += [jax.ShapeDtypeStruct((1, D), FULL)] * sums
    shapes += [pltpu.HBM(shape, LOW) for shape in kept]
    out_specs += [whole(o) for o in shapes[rows_out:]]
    return pl.pallas_call(
        kernel,
        grid=(L // step,),
        in_specs=specs + list(held_specs),
        out_specs=out_specs,
        out_shape=shapes,
        scratch_shapes=list(scratch),
        compiler_params=pltpu.CompilerParams(vmem_limit_bytes=32 << 20),
        cost_estimate=SMALL,
        name=name,
    )(*flat, *[f if f.dtype == FULL or i in loose else pinned(f) for i, f in enumerate(held)])


def rms_scale(residual):
    return lax.rsqrt(jnp.mean(residual * residual, axis=1, keepdims=True) + EPSILON)


def norm_back(scaled, normed, inv):
    return inv * (scaled - normed * jnp.mean(scaled * normed, axis=1, keepdims=True))


def column_sum(sum_ref, value):
    @pl.when(pl.program_id(0) == 0)
    def _():
        sum_ref[...] = jnp.zeros_like(sum_ref)

    sum_ref[...] += jnp.sum(value, axis=0, keepdims=True)


def heads_out(held_ref, refs):
    att_ref, y_ref, x_ref, corner_ref = refs
    half, width = att_ref.shape[0], held_ref.shape[2]

    @pl.when(pl.program_id(0) == 0)
    def _():
        held_ref[0, :half] = att_ref[:, 3 * width :]
        held_ref[0, half:] = y_ref[:, 3 * width :]
        held_ref[1, :half] = x_ref[:, 3 * width :]
        held_ref[1, half:] = corner_ref[:, width:]


def project_kernel(one_ref, two_ref, att_ref, y_ref, x_ref, corner_ref, out_ref, held_ref):
    heads_out(held_ref, (att_ref, y_ref, x_ref, corner_ref))
    out_ref[...] = (nt(one_ref[...], held_ref[0]) + nt(two_ref[...], held_ref[1])).astype(LOW)


def gate_up(hidden, weights_ref, gate_ref, up_ref, act_ref):
    hid = gate_ref.shape[1]
    gate = nn(hidden, weights_ref[:, :hid])
    up = nn(hidden, weights_ref[:, hid:])
    gate_ref[...] = gate.astype(LOW)
    up_ref[...] = up.astype(LOW)
    act_ref[...] = (gate * jax.nn.sigmoid(gate) * up).astype(LOW)


def enter_kernel(
    rows_ref, mine_ref, theirs_ref, gain_ref, own_ref, y_ref,
    normed_ref, inv_ref, hidden_ref, gate_ref, up_ref, act_ref, weights_ref,
):
    half = own_ref.shape[0]

    @pl.when(pl.program_id(0) == 0)
    def _():
        weights_ref[:half] = own_ref[...]
        weights_ref[half:] = y_ref[...]

    residual = rows_ref[...].astype(FULL) + add(mine_ref[...], theirs_ref[...])
    inv = rms_scale(residual)
    normed = residual * inv
    hidden = (normed * gain_ref[0]).astype(LOW)
    normed_ref[...] = normed.astype(LOW)
    inv_ref[...] = inv
    hidden_ref[...] = hidden
    gate_up(hidden, weights_ref, gate_ref, up_ref, act_ref)


def rest_kernel(
    hidden_ref, act1_ref, x_ref, gate_corner_ref, up_corner_ref,
    low_own_ref, low_y_ref, low_x_ref, low_corner_ref, high_ref,
    gate_ref, up_ref, act_ref, out_ref, weights_ref, down_ref,
):
    half, hid = x_ref.shape[0], gate_ref.shape[1]
    cut = high_ref.shape[2]

    @pl.when(pl.program_id(0) == 0)
    def _():
        weights_ref[:half] = x_ref[...]
        weights_ref[half:, :hid] = gate_corner_ref[...]
        weights_ref[half:, hid:] = up_corner_ref[...]
        down_ref[0, :half, :cut] = low_own_ref[...]
        down_ref[0, half:, :cut] = low_y_ref[...]
        down_ref[1, :half, :cut] = low_x_ref[...]
        down_ref[1, half:, :cut] = low_corner_ref[...]
        down_ref[:, :, cut:] = high_ref[...]

    gate_up(hidden_ref[...], weights_ref, gate_ref, up_ref, act_ref)
    out_ref[...] = (nt(act1_ref[...], down_ref[0]) + nt(act_ref[...], down_ref[1])).astype(LOW)


def turn_kernel(
    normed_ref, mine_ref, theirs_ref, up_rows_ref, gains_ref,
    out_ref, low_ref, sum_ref,
):
    residual = normed_ref[...].astype(FULL) * gains_ref[0] + add(mine_ref[...], theirs_ref[...])
    inv = rms_scale(residual)
    normed = residual * inv
    gain = gains_ref[1]
    out_ref[...] = (normed * gain).astype(LOW)
    upstream = up_rows_ref[...].astype(FULL)
    column_sum(sum_ref, upstream * normed)
    low_ref[...] = norm_back(upstream * gain, normed, inv).astype(LOW)


def back_kernel(low_ref, gate1_ref, up1_ref, gate2_ref, up2_ref, down_ref, gg_ref, ug_ref):
    hid = gate1_ref.shape[1]
    low = low_ref[...]
    for x, gate_ref, up_ref in ((0, gate1_ref, up1_ref), (1, gate2_ref, up2_ref)):
        act_grad = nn(low, down_ref[x])
        gate, up = gate_ref[...].astype(FULL), up_ref[...].astype(FULL)
        sig = jax.nn.sigmoid(gate)
        gg = act_grad * up * (sig * (1.0 + gate * (1.0 - sig)))
        gg_ref[:, x * hid : (x + 1) * hid] = gg.astype(LOW)
        ug_ref[:, x * hid : (x + 1) * hid] = (act_grad * (gate * sig)).astype(LOW)


def mid_kernel(gg_ref, ug_ref, own_ref, other_ref, top_ref, bottom_ref):
    hid = gg_ref.shape[1] // 2
    total = 0.0
    for x, weights_ref in enumerate((own_ref, other_ref)):
        cols = slice(x * hid, (x + 1) * hid)
        total = total + nt(gg_ref[:, cols], weights_ref[:, :hid])
        total = total + nt(ug_ref[:, cols], weights_ref[:, hid:])
    low = total.astype(LOW)

    @pl.when(in_top())
    def _():
        top_ref[...] = low

    @pl.when(jnp.logical_not(in_top()))
    def _():
        bottom_ref[...] = low


def leave_kernel(
    grad_two_ref, mine_top_ref, mine_bottom_ref, theirs_top_ref, theirs_bottom_ref,
    normed_ref, inv_ref, gains_ref, att_ref, y_ref, x_ref, corner_ref,
    low_ref, ctx1_ref, ctx2_ref, sum_ref, held_ref,
):
    heads_out(held_ref, (att_ref, y_ref, x_ref, corner_ref))
    top = add(mine_top_ref[...], theirs_top_ref[...])
    bottom = add(mine_bottom_ref[...], theirs_bottom_ref[...])
    hidden_grad = grad_two_ref[...].astype(FULL) + jnp.where(in_top(), top, bottom)
    normed = normed_ref[...].astype(FULL)
    column_sum(sum_ref, hidden_grad * normed)
    low = norm_back(hidden_grad * gains_ref[0], normed, inv_ref[...]).astype(LOW)
    low_ref[...] = low
    ctx1_ref[...] = nn(low, held_ref[0]).astype(LOW)
    ctx2_ref[...] = nn(low, held_ref[1]).astype(LOW)


def input_kernel(
    qk1_ref, v1_ref, qk2_ref, v2_ref, att_ref, y_ref, x_ref, qk_corner_ref, vo_corner_ref,
    full_ref, low_ref, held_ref,
):
    half, width = att_ref.shape[0], v1_ref.shape[1]
    pair = 2 * width

    @pl.when(pl.program_id(0) == 0)
    def _():
        held_ref[0, :half] = att_ref[:, : pair + width]
        held_ref[0, half:] = y_ref[:, : pair + width]
        held_ref[1, :half] = x_ref[:, : pair + width]
        held_ref[1, half:, :pair] = qk_corner_ref[...]
        held_ref[1, half:, pair:] = vo_corner_ref[:, :width]

    total = 0.0
    for x, qk_ref, v_ref in ((0, qk1_ref, v1_ref), (1, qk2_ref, v2_ref)):
        total = total + nt(qk_ref[...], held_ref[x, :, :pair])
        total = total + nt(v_ref[...], held_ref[x, :, pair:])
    full_ref[...] = total
    low_ref[...] = total.astype(LOW)


def heads_grad_kernel(
    rows_ref, grad_ref, qk_ref, v_ref, ctx_ref, qk_near_ref, qk_far_ref, vo_ref
):
    width = v_ref.shape[1]
    rows = flip(rows_ref[...]).astype(LOW)
    qk = nn(rows, qk_ref[...]).astype(LOW)
    vo_ref[:, :width] = nn(rows, v_ref[...]).astype(LOW)
    vo_ref[:, width:] = nn(flip(grad_ref[...]).astype(LOW), ctx_ref[...]).astype(LOW)

    @pl.when(pl.program_id(0) == 0)
    def _():
        qk_near_ref[...] = qk

    @pl.when(pl.program_id(0) == 1)
    def _():
        qk_far_ref[...] = qk


def heads_grad(rows, grad, dqk, dv, context):
    half, pair = D // 2, dqk.shape[1]
    split = pl.BlockSpec((L, half), lambda i: (0, i))
    outs = [pltpu.HBM((half, pair), LOW)] * 2 + [pltpu.HBM((D, pair), LOW)]
    held = [pl.BlockSpec((half, pair), lambda i: (0, 0))] * 2
    return pl.pallas_call(
        heads_grad_kernel,
        grid=(2,),
        in_specs=[split, split] + [held_once(g) for g in (dqk, dv, context)],
        out_specs=held + [pl.BlockSpec((half, pair), lambda i: (i, 0))],
        out_shape=outs,
        compiler_params=pltpu.CompilerParams(vmem_limit_bytes=24 << 20),
        cost_estimate=SMALL,
        name="heads_grad",
    )(rows, grad, dqk, dv, context)


def in_order(value, mover):
    total = 0.0
    for _ in range(2):
        part = value.astype(LOW)
        total = total + nt(part, mover)
        value = value - part.astype(FULL)
    return total


def finish_kernel(
    core_ref, one_ref, full_ref, out_ref, theirs_ref, mover_ref, *refs
):
    grad_ref, low_ref = refs[-2:]
    mover = mover_ref[...]
    grad = one_ref[...].astype(FULL) + full_ref[...] + theirs_ref[...].astype(FULL)
    grad_ref[...] = in_order(grad, mover)
    low_ref[...] = nt(out_ref[...], mover).astype(LOW)


def finish(part, done, core, grad_one, part_full, layer_output, theirs, mover):
    rows = theirs.shape[0]
    steps = rows // QB
    mine = pl.BlockSpec((QB, D), lambda i, c: (c[0] * steps + part, 0))
    plain = pl.BlockSpec((QB, D), lambda i, c: (part, 0))
    return pl.pallas_call(
        finish_kernel,
        grid_spec=pltpu.PrefetchScalarGridSpec(
            num_scalar_prefetch=1,
            grid=(1,),
            in_specs=[mine, mine, mine, plain, held_once(mover)]
            + [pl.BlockSpec(memory_space=pl.ANY)] * len(done),
            out_specs=[plain, plain],
        ),
        out_shape=[
            jax.ShapeDtypeStruct((rows, D), FULL), jax.ShapeDtypeStruct((rows, D), LOW)
        ],
        input_output_aliases={6 + i: i for i in range(len(done))},
        cost_estimate=pl.CostEstimate(
            flops=4 * 10**9, bytes_accessed=8 << 20, transcendentals=0
        ),
        name="finish",
    )(core, grad_one, pinned(part_full), pinned(layer_output), theirs, mover, *done)


def adam_kernel(clip, rates, *refs):
    me = refs[0][0]
    message = refs[1][...] + refs[2][...]
    att_ref, ffn_ref, down_ref = refs[3:6]
    ins, norm_ref, outs = refs[6:21], refs[21], refs[22:]
    block = ins[12].shape[1]
    gain_sum = message[:, : 2 * D]
    total = message[:, 2 * D : 2 * D + 1] + jnp.sum(gain_sum * gain_sum, axis=1, keepdims=True)
    norm = jnp.sqrt(total)
    norm_ref[...] = norm
    ratio = clip / jnp.maximum(norm, clip)

    def update(p, at, grad):
        rate, decay = rates[p]
        old = [ref[at] for ref in ins[3 * p : 3 * p + 3]]
        for ref, value in zip(
            outs[3 * p : 3 * p + 3], adam_update(*old, grad, ratio, rate, decay)
        ):
            ref[at] = value

    width, hid = att_ref.shape[1] // 4, ffn_ref.shape[1] // 2
    step = 16 if block % 16 == 0 else block

    def some(i, carry):
        rows = pl.ds(pl.multiple_of(i * step, step), step) if step < block else slice(None)
        for k in range(3):
            update(0, (k, rows), att_ref[rows, k * width : (k + 1) * width])
        for k in range(2):
            update(2, (k, rows), ffn_ref[rows, k * hid : (k + 1) * hid])
        update(3, rows, down_ref[rows, :])
        return carry

    if step < block:
        lax.fori_loop(0, block // step, some, 0)
    else:
        some(0, 0)
    update(1, ..., att_ref[:, 3 * width :].T)
    for k in range(2):
        mine = jnp.zeros((1, block), FULL)
        for j in range(D // block):
            start = k * D + j * block
            mine = jnp.where(me == j, gain_sum[:, start : start + block], mine)
        update(4, pl.ds(k, 1), mine)


def adam(me, clip, rates, grads, params):
    flat = [array for group in params for array in group]
    outs = [jax.ShapeDtypeStruct((1, 1), FULL)]
    outs += [jax.ShapeDtypeStruct(w.shape, FULL) for w in flat]
    vmem = pl.BlockSpec(memory_space=pltpu.VMEM)
    norm, *made = pl.pallas_call(
        functools.partial(adam_kernel, clip, rates),
        in_specs=[pl.BlockSpec(memory_space=pltpu.SMEM)] + [vmem] * (len(grads) + len(flat)),
        out_specs=[vmem] * len(outs),
        out_shape=outs,
        name="adam",
    )(me, *grads, *[pltpu.with_memory_space_constraint(f, pltpu.VMEM) for f in flat])
    return norm[0, 0], [made[i : i + 3] for i in range(0, len(made), 3)]


def rope_tables():
    half = HD // 2
    lane = jnp.arange(128) % HD
    freq = jnp.exp(-jnp.log(10000.0) * (lane % half).astype(FULL) / half)
    angle = jnp.arange(L, dtype=FULL)[:, None] * freq[None, :]
    return jnp.cos(angle), jnp.where(lane < half, -1.0, 1.0)[None, :] * jnp.sin(angle)


def adam_update(weight, first, second, grad, ratio, rate, decay):
    clipped = grad * ratio
    first_new = AVERAGING * first + (1.0 - AVERAGING) * clipped
    second_new = AVERAGING * second + (1.0 - AVERAGING) * clipped * clipped
    correction = 1.0 - AVERAGING**ADAM_STEP
    step = first_new / correction / (jnp.sqrt(second_new / correction) + 1e-08)
    return (weight - rate * (step + decay * weight), first_new, second_new)


def tn(rows, grads):
    out = lax.dot_general(rows, grads, (((0,), (0,)), ((), ())), preferred_element_type=FULL)
    return layout.with_layout_constraint(out.astype(LOW), layout.Layout((0, 1)))


def per_device(
    layer_input, layer_cotangent,
    attend_weight, attend_first, attend_second,
    output_weight, output_first, output_second,
    gated_weight, gated_first, gated_second,
    down_weight, down_first, down_second,
    norm_gains, gains_first, gains_second,
):
    rows = layer_input.shape[0]
    wide = lax.axis_size("wide")
    block = D // wide
    me = lax.axis_index("wide")
    narrow = lax.axis_index("narrow")
    core = narrow % 2
    cols = attend_weight.shape[2]

    bits = wide_bits()
    near = bits[:-1]
    half = D // 2
    hid = down_weight.shape[0]

    bits = wide_bits()
    near = bits[:-1]
    half = D // 2
    hid = down_weight.shape[0]
    pair = 2 * cols

    attend_low = attend_weight.astype(LOW)
    att = jnp.concatenate(
        [attend_low[0], attend_low[1], attend_low[2], output_weight.T.astype(LOW)], axis=1
    )
    cut = hid // 2
    down_t = down_weight.T
    ffn = jnp.concatenate([gated_weight[0], gated_weight[1], down_t[:, :cut]], axis=1).astype(LOW)
    down = down_t[:, cut:].astype(LOW)

    order = me ^ jnp.array(block_masks(), jnp.int32)
    source = (order[:, None] * block + jnp.arange(block)[None, :]).reshape(1, D)
    mover = (lax.broadcasted_iota(jnp.int32, (D, D), 0) == source).astype(LOW)
    mover = lax.optimization_barrier(mover)

    def both_halves(mine, theirs):
        first = core == 0
        return jnp.concatenate(
            [jnp.where(first, mine, theirs), jnp.where(first, theirs, mine)], axis=0
        )

    def own_rows(value):
        return lax.dynamic_slice_in_dim(value, core * rows, rows, axis=0)

    first = widen(att, near[:1])
    gains = widen(after(norm_gains, att).astype(LOW).astype(FULL)[None], bits[:1])
    first, down, gains = lax.optimization_barrier((first, down, gains))
    gains = widen(gains, bits[1:-1])
    att = widen(first, near[1:])
    down_y = swap(down, "wide", 1)
    down_x = swap(down, "narrow", 2)
    moved_in = jnp.dot(after(layer_input, first), mover, preferred_element_type=FULL).astype(LOW)
    att, down_y, down_x, gains, moved_in = lax.optimization_barrier(
        (att, down_y, down_x, gains, moved_in)
    )
    att_y = swap(att, "wide", 1)
    att_x = swap(att, "narrow", 2)
    ffn = widen(after(ffn, att), near[:1])
    gains = widen(gains, bits[-1:])
    inputs = both_halves(moved_in, swap(moved_in, "narrow", 1))
    cosine, sine = rope_tables()
    rows_up = after(layer_cotangent, moved_in)
    moved_up = jnp.dot(rows_up, mover, preferred_element_type=FULL).astype(LOW)

    inputs, att, att_y, att_x, ffn, gains, cosine, sine, moved_up = lax.optimization_barrier(
        (inputs, att, att_y, att_x, ffn, gains, cosine, sine, moved_up)
    )
    gains = gains.transpose(1, 0, 2).reshape(2, 1, D)
    down_corner = swap(down_y, "narrow", 2)
    qk_corner = swap(att_y[:, :pair], "narrow", 2)
    vo_corner = swap(att_x[:, pair:], "wide", 1)
    ffn = widen(ffn, near[1:])
    qk = [[(att, pair, 0), (att_y, pair, 0)], [(att_x, pair, 0), qk_corner]]
    vo = [[(att, pair, 1), (att_y, pair, 1)], [(att_x, pair, 1), vo_corner]]
    saved = [attend_forward(inputs, qk[0], vo[0], cosine, sine)]
    second_in, qk_corner, vo_corner, ffn, down_corner, moved_up = lax.optimization_barrier(
        (after(inputs, saved[0][3]), qk_corner, vo_corner, ffn, down_corner, moved_up)
    )
    other_up = swap(moved_up, "narrow", 1)
    down = jnp.stack([down, down_y, down_x, down_corner])[:, None]
    for bit in near[:1]:
        down = jnp.concatenate([down, swap(down, "wide", bit)], axis=1)
    qk[1][1], vo[1][1] = qk_corner, vo_corner
    ffn_y = swap(ffn, "wide", 1)
    ffn_x = swap(ffn, "narrow", 2)
    saved.append(attend_forward(second_in, qk[1], vo[1], cosine, sine))
    context = [s[3] for s in saved]
    att_out = [att, att_y, att_x, vo_corner]
    held = [pltpu.VMEM((2, D, cols), LOW)]
    low_d, full_d = (D, LOW, False), (D, FULL, True)
    (attn_part,) = by_rows(
        project_kernel, "project", context, att_out, [low_d], scratch=held
    )
    ffn_y, ffn_x, attn_part, down = lax.optimization_barrier((ffn_y, ffn_x, attn_part, down))
    attn_other = swap(attn_part, "narrow", 1)
    down_far = [swap(down, "wide", bit) for bit in near[1:2]]
    gate_corner = swap(ffn_y[:, :hid], "narrow", 2)
    up_corner = swap(ffn_x[:, hid:], "wide", 1)
    flow = [(hid, LOW, True), (hid, LOW, True), (hid, LOW, False)]
    normed_one, inv_one, hidden_low, gate1, up1, act1, gu_own = by_rows(
        enter_kernel, "enter", [pinned(inputs), attn_part, attn_other],
        [gains, (ffn, 2 * hid, 0), (ffn_y, 2 * hid, 0)],
        [(D, LOW, True), (1, FULL, True), low_d] + flow, kept=[(D, 2 * hid)],
    )
    hidden_low, down, down_far = lax.optimization_barrier((hidden_low, down, down_far))
    upstream = both_halves(after(moved_up, hidden_low), other_up)
    down = jnp.concatenate([down, *down_far], axis=1)
    for bit in near[2:]:
        down = jnp.concatenate([down, swap(down, "wide", bit)], axis=1)
    down = down.reshape(2, D, hid - cut)
    last_cols = 2 * hid // cut
    gate2, up2, act2, ffn_part, gu_other, down_all = by_rows(
        rest_kernel, "rest", [after(hidden_low, upstream), act1],
        [
            (ffn_x, 2 * hid, 0), gate_corner, (up_corner, hid, 0),
            (ffn, cut, last_cols), (ffn_y, cut, last_cols), (ffn_x, cut, last_cols),
            (up_corner, cut, hid // cut), down,
        ],
        flow + [low_d], kept=[(D, 2 * hid), (2, D, hid)], loose=(1, 2, 6),
    )
    ffn_other = swap(ffn_part, "narrow", 1)

    layer_output, grad_two_low, gain_two_grad = by_rows(
        turn_kernel, "turn", [pinned(normed_one), ffn_part, ffn_other, pinned(upstream)],
        [gains], [(D, LOW, True), low_d], sums=1,
    )
    down_send = tn(grad_two_low, act2)
    down_x = swap(down_send, "narrow", 2)
    wide_flow = (2 * hid, LOW, False)
    saves = [pinned(r) for r in (gate1, up1, gate2, up2)]
    gg, ug = by_rows(
        back_kernel, "back",
        [after(grad_two_low, down_send), *saves], [down_all], [wide_flow, wide_flow],
    )
    gate_send = tn(hidden_low[:, half:], gg)
    up_send = tn(hidden_low, ug[:, hid:])
    gate_y = swap(gate_send, "wide", 1)
    up_x = swap(up_send, "narrow", 2)
    mid_part = by_rows(
        mid_kernel, "mid", [after(gg, gate_send, up_send), ug], [gu_own, gu_other], []
    )
    mid_other = [swap(part, "narrow", 1) for part in mid_part]
    down_own = tn(grad_two_low, act1)
    gate_own = tn(hidden_low[:, :half], gg)
    up_own = tn(hidden_low, ug[:, :hid])
    mid_part, mid_other, down_own, gate_own, up_own, down_x = lax.optimization_barrier(
        (mid_part, mid_other, down_own, gate_own, up_own, down_x)
    )
    grad_one_low, dctx1, dctx2, gain_one_grad = by_rows(
        leave_kernel, "leave",
        [grad_two_low, tuple(mid_part), tuple(mid_other), pinned(normed_one), pinned(inv_one)],
        [gains, *att_out], [low_d, (cols, LOW, True), (cols, LOW, True)],
        sums=1, scratch=held,
    )

    q, k, v, _, lse = saved[1]
    dqk2, dv2 = attend_backward(q, k, v, lse, dctx2, cosine, sine)
    down_x, gate_y, dqk2, dv2 = lax.optimization_barrier((down_x, gate_y, dqk2, dv2))
    down_sum, gate_sum = add(down_own, down_x), add(gate_own, gate_y)
    down_y = swap(down_sum[half:].astype(LOW), "wide", 1)
    gate_far = gate_sum[:, hid:].astype(LOW)
    gate_x = swap(gate_far, "narrow", 2)
    qk_near2, qk_send2, vo_send = heads_grad(inputs, grad_one_low, after(dqk2, gate_far), dv2, context[1])
    vo_x = swap(vo_send, "narrow", 2)
    qk_y2 = swap(qk_send2, "wide", 1)
    back = near[::-1]
    q, k, v, _, lse = saved[0]
    dqk1, dv1 = attend_backward(q, k, v, lse, after(dctx1, vo_send, qk_send2), cosine, sine)
    dqk1, dv1, up_x, down_y, qk_y2, gate_x = lax.optimization_barrier(
        (dqk1, dv1, up_x, down_y, qk_y2, gate_x)
    )
    early = narrow_down(add(down_sum[:half], down_y), back[:1])
    up_sum = add(up_own, up_x)
    up_y = swap(up_sum[half:].astype(LOW), "wide", 1)
    qk_near1, qk_send1, vo_own = heads_grad(inputs, grad_one_low, dqk1, dv1, context[0])
    qk_y1 = swap(qk_send1, "wide", 1)
    qk_far = add(qk_near2, qk_y2).astype(LOW)
    qk_x = swap(qk_far, "narrow", 2)
    vo_sum = add(vo_own, vo_x)
    vo_far = vo_sum[half:].astype(LOW)
    vo_y = swap(vo_far, "wide", 1)
    late = jnp.concatenate([add(gate_sum[:, :hid], gate_x), add(up_sum[:half], up_y)], axis=1)
    early_red = narrow_down(early, back[1:])
    dqk1, vo_sum, late, early_red = lax.optimization_barrier((dqk1, vo_sum, late, early_red))
    part_full, part_low = by_rows(
        input_kernel, "inputs", [dqk1, dv1, dqk2, dv2],
        [att, att_y, att_x, qk_corner, vo_corner], [full_d, low_d],
        scratch=[pltpu.VMEM((2, D, 3 * cols), LOW)],
    )
    late = narrow_down(late, back[:1])
    theirs = lax.dynamic_slice_in_dim(part_low, (1 - core) * rows, rows, axis=0)
    theirs = swap(theirs, "narrow", 1)
    qk_sum = add(qk_near1, qk_y1)
    last = jnp.concatenate([add(qk_sum, qk_x), add(vo_sum[:half], vo_y)], axis=1)
    gain_grads = lax.dot_general(
        jnp.concatenate([gain_one_grad, gain_two_grad], axis=0), mover.astype(FULL),
        (((1,), (1,)), ((), ())), precision=lax.Precision.HIGHEST, preferred_element_type=FULL,
    )
    last, early_red, late, gain_grads = lax.optimization_barrier(
        (last, early_red, late, gain_grads)
    )
    last = narrow_down(last, back[:1])
    late_red = narrow_down(late, back[1:])
    early_square = jnp.sum(early_red * early_red) + jnp.sum(late_red * late_red)
    att_red = narrow_down(last, back[1:])

    square = jnp.full((1, 128), early_square + jnp.sum(att_red * att_red), FULL)
    square = square + swap(square, "narrow", 1)
    message = jnp.concatenate([gain_grads.reshape(1, 2 * D), square], axis=1)
    message = message + swap(message, "narrow", 2)
    which, done = jnp.full((1,), core, jnp.int32), ()
    theirs = after(theirs, message)
    for part in range(rows // QB):
        done = finish(part, done, which, grad_one_low, part_full, layer_output, theirs, mover)
    input_grad, layer_output = done
    for bit in bits[::-1][:-1]:
        message = message + swap(message, "wide", bit)
    received = swap(message, "wide", bits[0])
    all_tokens = rows * wide * lax.axis_size("narrow")
    clip = 0.02 * math.sqrt(all_tokens * (4 * D * D + 3 * D * FF + 2 * D))
    grad_norm, (new_attend, new_output, new_gated, new_down, new_gains) = adam(
        jnp.full((1,), me, jnp.int32),
        clip,
        (
            (D ** (-0.5), WEIGHT_DECAY),
            (max(D // 64, 1) ** (-0.5), WEIGHT_DECAY),
            (D ** (-0.5), WEIGHT_DECAY),
            (FF ** (-0.5), WEIGHT_DECAY),
            (0.4, 0.0),
        ),
        (message, received, att_red, late_red, early_red),
        (
            (attend_weight, attend_first, attend_second),
            (output_weight, output_first, output_second),
            (gated_weight, gated_first, gated_second),
            (down_weight.T, down_first.T, down_second.T),
            (norm_gains, gains_first, gains_second),
        ),
    )
    new_down = [value.T for value in new_down]
    return (
        layer_output, input_grad, grad_norm,
        *new_attend, *new_output, *new_gated, *new_down, *new_gains,
    )


def solution(mesh):
    rows = P(("wide", "narrow"), None)
    stacked = P(None, "wide", "narrow")
    turned = P("narrow", "wide")
    gains = P(None, "wide")
    params = (stacked,) * 3 + (turned,) * 3 + (stacked,) * 3 + (turned,) * 3 + (gains,) * 3
    return jax.shard_map(
        per_device,
        mesh=mesh,
        in_specs=(rows, rows) + params,
        out_specs=(rows, rows, P()) + params,
        check_vma=False,
    )
```

```python
import functools
import math

import jax
import jax.numpy as jnp
from jax import lax
from jax.experimental import layout
from jax.experimental import pallas as pl
from jax.experimental.pallas import tpu as pltpu
from jax.sharding import PartitionSpec as P

D = 768
HD = 64
FF = 2048
L = 1024
ADAM_STEP = 5

EPSILON = 1e-05
WEIGHT_DECAY = 0.1
AVERAGING = 0.5

LOW = jnp.bfloat16
FULL = jnp.float32
QB = 256
MASKED = -1e30
SMALL = pl.CostEstimate(flops=10**6, bytes_accessed=10**4, transcendentals=0)


def swap(value, axis, bit):
    size = lax.axis_size(axis)
    return lax.ppermute(value, axis, [(i, i ^ bit) for i in range(size)])


def wide_bits():
    top = lax.axis_size("wide").bit_length() - 1
    return [1 << b for b in range(top - 1, -1, -1)]


def block_masks():
    masks = [0]
    for bit in wide_bits():
        masks = masks + [m ^ bit for m in masks]
    return masks


def after(value, *done):
    return lax.optimization_barrier((value, done))[0]


def widen(held, bits):
    for bit in bits:
        held = jnp.concatenate([held, swap(held, "wide", bit)], axis=0)
    return held


def add(kept, received):
    return kept.astype(FULL) + received.astype(FULL)


def narrow_down(held, bits):
    for bit in bits:
        half = held.shape[0] // 2
        held = add(held[:half], swap(held[half:].astype(LOW), "wide", bit))
    return held


def turn(value, cosine, sine, sign):
    width = value.shape[1]
    lane = lax.broadcasted_iota(jnp.int32, value.shape, 1) % HD
    other = jnp.where(
        lane < HD // 2,
        pltpu.roll(value, width - HD // 2, 1),
        pltpu.roll(value, HD // 2, 1),
    )
    reps = width // 128
    return value * jnp.concatenate([cosine] * reps, axis=1) + sign * other * jnp.concatenate(
        [sine] * reps, axis=1
    )


def nn(a, b):
    return lax.dot_general(a, b, (((1,), (0,)), ((), ())), preferred_element_type=FULL)


def nt(a, b):
    return lax.dot_general(a, b, (((1,), (1,)), ((), ())), preferred_element_type=FULL)


def diagonal(scores):
    key = lax.broadcasted_iota(jnp.int32, scores.shape, 0)
    query = lax.broadcasted_iota(jnp.int32, scores.shape, 1)
    return jnp.where(key <= query, scores, MASKED)


def flip(value):
    return value.astype(FULL).T


def attend_kernel(
    rows_ref, qka_ref, qkb_ref, voa_ref, vob_ref, cos_ref, sin_ref,
    q_ref, k_ref, v_ref, ctx_ref, lse_ref, hold,
):
    heads = q_ref.shape[0]
    width = heads * HD
    half = qka_ref.shape[0]

    def project(i, carry):
        rows = pl.ds(pl.multiple_of(i * QB, QB), QB)
        first, second = rows_ref[rows, :half], rows_ref[rows, half:]
        pair = nn(first, qka_ref[...]) + nn(second, qkb_ref[...])
        pair = turn(pair, cos_ref[rows, :], sin_ref[rows, :], 1.0)
        value = nn(first, voa_ref[:, :width]) + nn(second, vob_ref[:, :width])
        for h in range(heads):
            q_ref[h, rows, :] = (pair[:, h * HD : (h + 1) * HD] * (HD**-0.5)).astype(LOW)
            k_ref[h, rows, :] = pair[:, width + h * HD : width + (h + 1) * HD].astype(LOW)
            v_ref[h, rows, :] = value[:, h * HD : (h + 1) * HD].astype(LOW)
        return carry

    lax.fori_loop(0, L // QB, project, 0)

    def head(h, carry):
        turned = flip(v_ref[h]).astype(LOW)
        for i in range(L // QB):
            lo, hi = i * QB, (i + 1) * QB
            query = q_ref[h, lo:hi, :]
            diag = diagonal(nt(k_ref[h, lo:hi, :], query))
            peak = jnp.max(diag, axis=0, keepdims=True)
            if i:
                body = nt(k_ref[h, :lo, :], query)
                peak = jnp.maximum(peak, jnp.max(body, axis=0, keepdims=True))
            weight = jnp.exp(diag - peak)
            total = jnp.sum(weight, axis=0, keepdims=True)
            out = nn(turned[:, lo:hi], weight.astype(LOW))
            if i:
                weight = jnp.exp(body - peak)
                total = total + jnp.sum(weight, axis=0, keepdims=True)
                out = out + nn(turned[:, :lo], weight.astype(LOW))
            lse_ref[h, :, lo:hi] = peak + jnp.log(total)
            hold[h, lo:hi, :] = (out / total).T.astype(LOW)
        return carry

    lax.fori_loop(0, heads, head, 0)
    for h in range(heads):
        ctx_ref[:, h * HD : (h + 1) * HD] = hold[h]


def pinned(array):
    return pltpu.with_memory_space_constraint(array, pltpu.HBM)


def whole(array):
    zero = (0,) * len(array.shape)
    return pl.BlockSpec(array.shape, lambda *_: zero)


def by_head(shape):
    return pl.BlockSpec(shape, lambda h: (h, 0, 0))


def columns(piece, mode=None):
    array, width, j = piece if isinstance(piece, tuple) else (piece, piece.shape[-1], 0)
    lead = (0,) * (array.ndim - 1)
    shape = array.shape[:-1] + (width,)
    return array, pl.BlockSpec(shape, lambda *_: lead + (j,), pipeline_mode=mode)


def width_of(piece):
    return piece[1] if isinstance(piece, tuple) else piece.shape[1]


def attend_forward(rows, qk, vo, cosine, sine):
    heads = width_of(qk[0]) // 2 // HD
    headed = pltpu.HBM((heads, L, HD), LOW)
    outs = (
        headed, headed, headed,
        pltpu.HBM((L, heads * HD), LOW),
        pltpu.HBM((heads, 1, L), FULL),
    )
    args, specs = zip(*[columns(p) for p in (rows, *qk, *vo, cosine, sine)])
    return pl.pallas_call(
        attend_kernel,
        grid=(1,),
        in_specs=list(specs),
        out_specs=[whole(o) for o in outs],
        out_shape=outs,
        scratch_shapes=[pltpu.VMEM((heads, L, HD), LOW)],
        compiler_params=pltpu.CompilerParams(vmem_limit_bytes=24 << 20),
        cost_estimate=SMALL,
        name="attend_forward",
    )(*[pinned(a) for a in args])


def attend_back_kernel(
    q_ref, k_ref, v_ref, lse_ref, dctx_ref, cos_ref, sin_ref,
    dqk_ref, dv_ref, dctx, dqk, dk_sum, dv_sum,
):
    heads = dctx.shape[0]
    h = pl.program_id(0)

    @pl.when(h == 0)
    def _():
        for j in range(heads):
            dctx[j] = dctx_ref[:, j * HD : (j + 1) * HD]

    turned = flip(k_ref[0]).astype(LOW)
    for i in range(L // QB):
        lo, hi = i * QB, (i + 1) * QB
        query, back = q_ref[0, lo:hi, :], dctx[h, lo:hi, :]
        lse = lse_ref[0, :, lo:hi]
        prob = jnp.exp(diagonal(nt(k_ref[0, lo:hi, :], query)) - lse)
        grad = nt(v_ref[0, lo:hi, :], back)
        inner = jnp.sum(prob * grad, axis=0, keepdims=True)
        if i:
            prob_body = jnp.exp(nt(k_ref[0, :lo, :], query) - lse)
            grad_body = nt(v_ref[0, :lo, :], back)
            inner = inner + jnp.sum(prob_body * grad_body, axis=0, keepdims=True)
        score = (prob * (grad - inner)).astype(LOW)
        dv_sum[h, lo:hi, :] = nn(prob.astype(LOW), back)
        dk_sum[h, lo:hi, :] = nn(score, query)
        dquery = nn(turned[:, lo:hi], score)
        if i:
            score = (prob_body * (grad_body - inner)).astype(LOW)
            dv_sum[h, :lo, :] += nn(prob_body.astype(LOW), back)
            dk_sum[h, :lo, :] += nn(score, query)
            dquery = dquery + nn(turned[:, :lo], score)
        dqk[h, lo:hi, :] = (dquery * (HD**-0.5)).T

    def finish(i, carry):
        rows = pl.ds(pl.multiple_of(i * QB, QB), QB)
        pair = jnp.concatenate(
            [dqk[j, rows, :] for j in range(heads)] + [dk_sum[j, rows, :] for j in range(heads)],
            axis=1,
        )
        dqk_ref[rows, :] = turn(pair, cos_ref[rows, :], sin_ref[rows, :], -1.0).astype(LOW)
        dv_ref[rows, :] = jnp.concatenate(
            [dv_sum[j, rows, :] for j in range(heads)], axis=1
        ).astype(LOW)
        return carry

    @pl.when(h == heads - 1)
    def _():
        lax.fori_loop(0, L // QB, finish, 0)


def attend_backward(q, k, v, lse, dctx, cosine, sine):
    heads = q.shape[0]
    outs = (
        jax.ShapeDtypeStruct((L, 2 * heads * HD), LOW),
        jax.ShapeDtypeStruct((L, heads * HD), LOW),
    )
    return pl.pallas_call(
        attend_back_kernel,
        grid=(heads,),
        in_specs=[by_head((1, L, HD))] * 3
        + [by_head((1, 1, L)), whole(dctx), whole(cosine), whole(sine)],
        out_specs=[whole(o) for o in outs],
        out_shape=outs,
        scratch_shapes=[pltpu.VMEM((heads, L, HD), LOW)] + [pltpu.VMEM((heads, L, HD), FULL)] * 3,
        compiler_params=pltpu.CompilerParams(vmem_limit_bytes=24 << 20),
        cost_estimate=SMALL,
        name="attend_backward",
    )(pinned(q), pinned(k), pinned(v), pinned(lse), pinned(dctx), pinned(cosine), pinned(sine))


def held_once(array):
    zero = (0,) * array.ndim
    return pl.BlockSpec(array.shape, lambda *_: zero, pipeline_mode=pl.Buffered(1))


def in_top():
    return pl.program_id(0) < pl.num_programs(0) // 2


def halves(step, width):
    steps = L // step // 2
    return [
        pl.BlockSpec((step, width), lambda i: (jnp.minimum(i, steps - 1), 0)),
        pl.BlockSpec((step, width), lambda i: (jnp.maximum(i - steps, 0), 0)),
    ]


def by_rows(kernel, name, row_args, fixed, outs, sums=0, kept=(), scratch=(), loose=(), step=QB):
    specs, flat = [], []
    for r in row_args:
        if isinstance(r, tuple):
            specs += halves(step, r[0].shape[1])
            flat += r
        else:
            specs.append(pl.BlockSpec((step, r.shape[1]), lambda i: (i, 0)))
            flat.append(r)
    held, held_specs = zip(*[columns(f, pl.Buffered(1)) for f in fixed])
    shapes = [
        (pltpu.HBM if away else jax.ShapeDtypeStruct)((L, w), t) for w, t, away in outs
    ]
    out_specs = [pl.BlockSpec((step, w), lambda i: (i, 0)) for w, _, _ in outs]
    if not outs:
        shapes = [jax.ShapeDtypeStruct((L // 2, D), LOW)] * 2
        out_specs = halves(step, D)
    rows_out = len(shapes)
    shapes += [jax.ShapeDtypeStruct((1, D), FULL)] * sums
    shapes += [pltpu.HBM(shape, LOW) for shape in kept]
    out_specs += [whole(o) for o in shapes[rows_out:]]
    return pl.pallas_call(
        kernel,
        grid=(L // step,),
        in_specs=specs + list(held_specs),
        out_specs=out_specs,
        out_shape=shapes,
        scratch_shapes=list(scratch),
        compiler_params=pltpu.CompilerParams(vmem_limit_bytes=32 << 20),
        cost_estimate=SMALL,
        name=name,
    )(*flat, *[f if f.dtype == FULL or i in loose else pinned(f) for i, f in enumerate(held)])


def rms_scale(residual):
    return lax.rsqrt(jnp.mean(residual * residual, axis=1, keepdims=True) + EPSILON)


def norm_back(scaled, normed, inv):
    return inv * (scaled - normed * jnp.mean(scaled * normed, axis=1, keepdims=True))


def column_sum(sum_ref, value):
    @pl.when(pl.program_id(0) == 0)
    def _():
        sum_ref[...] = jnp.zeros_like(sum_ref)

    sum_ref[...] += jnp.sum(value, axis=0, keepdims=True)


def heads_out(held_ref, refs):
    att_ref, y_ref, x_ref, corner_ref = refs
    half, width = att_ref.shape[0], held_ref.shape[2]

    @pl.when(pl.program_id(0) == 0)
    def _():
        held_ref[0, :half] = att_ref[:, 3 * width :]
        held_ref[0, half:] = y_ref[:, 3 * width :]
        held_ref[1, :half] = x_ref[:, 3 * width :]
        held_ref[1, half:] = corner_ref[:, 3 * width :]


def project_kernel(one_ref, two_ref, att_ref, y_ref, x_ref, corner_ref, out_ref, held_ref):
    heads_out(held_ref, (att_ref, y_ref, x_ref, corner_ref))
    out_ref[...] = (nt(one_ref[...], held_ref[0]) + nt(two_ref[...], held_ref[1])).astype(LOW)


def gate_up(hidden, weights_ref, gate_ref, up_ref, act_ref):
    hid = gate_ref.shape[1]
    gate = nn(hidden, weights_ref[:, :hid])
    up = nn(hidden, weights_ref[:, hid:])
    gate_ref[...] = gate.astype(LOW)
    up_ref[...] = up.astype(LOW)
    act_ref[...] = (gate * jax.nn.sigmoid(gate) * up).astype(LOW)


def enter_kernel(
    rows_ref, mine_ref, theirs_ref, gain_ref, own_ref, y_ref,
    normed_ref, inv_ref, hidden_ref, gate_ref, up_ref, act_ref, weights_ref,
):
    half = own_ref.shape[0]

    @pl.when(pl.program_id(0) == 0)
    def _():
        weights_ref[:half] = own_ref[...]
        weights_ref[half:] = y_ref[...]

    residual = rows_ref[...].astype(FULL) + add(mine_ref[...], theirs_ref[...])
    inv = rms_scale(residual)
    normed = residual * inv
    hidden = (normed * gain_ref[0]).astype(LOW)
    normed_ref[...] = normed.astype(LOW)
    inv_ref[...] = inv
    hidden_ref[...] = hidden
    gate_up(hidden, weights_ref, gate_ref, up_ref, act_ref)


def rest_kernel(
    hidden_ref, act1_ref, x_ref, gate_corner_ref, up_corner_ref,
    low_own_ref, low_y_ref, low_x_ref, low_corner_ref, high_ref,
    gate_ref, up_ref, act_ref, out_ref, weights_ref, down_ref,
):
    half, hid = x_ref.shape[0], gate_ref.shape[1]
    cut = high_ref.shape[2]

    @pl.when(pl.program_id(0) == 0)
    def _():
        weights_ref[:half] = x_ref[...]
        weights_ref[half:, :hid] = gate_corner_ref[...]
        weights_ref[half:, hid:] = up_corner_ref[...]
        down_ref[0, :half, :cut] = low_own_ref[...]
        down_ref[0, half:, :cut] = low_y_ref[...]
        down_ref[1, :half, :cut] = low_x_ref[...]
        down_ref[1, half:, :cut] = low_corner_ref[...]
        down_ref[:, :, cut:] = high_ref[...]

    gate_up(hidden_ref[...], weights_ref, gate_ref, up_ref, act_ref)
    out_ref[...] = (nt(act1_ref[...], down_ref[0]) + nt(act_ref[...], down_ref[1])).astype(LOW)


def turn_kernel(
    normed_ref, mine_ref, theirs_ref, up_rows_ref, gains_ref,
    out_ref, low_ref, sum_ref,
):
    residual = normed_ref[...].astype(FULL) * gains_ref[0] + add(mine_ref[...], theirs_ref[...])
    inv = rms_scale(residual)
    normed = residual * inv
    gain = gains_ref[1]
    out_ref[...] = (normed * gain).astype(LOW)
    upstream = up_rows_ref[...].astype(FULL)
    column_sum(sum_ref, upstream * normed)
    low_ref[...] = norm_back(upstream * gain, normed, inv).astype(LOW)


def back_kernel(low_ref, gate1_ref, up1_ref, gate2_ref, up2_ref, down_ref, gg_ref, ug_ref):
    hid = gate1_ref.shape[1]
    low = low_ref[...]
    for x, gate_ref, up_ref in ((0, gate1_ref, up1_ref), (1, gate2_ref, up2_ref)):
        act_grad = nn(low, down_ref[x])
        gate, up = gate_ref[...].astype(FULL), up_ref[...].astype(FULL)
        sig = jax.nn.sigmoid(gate)
        gg = act_grad * up * (sig * (1.0 + gate * (1.0 - sig)))
        gg_ref[:, x * hid : (x + 1) * hid] = gg.astype(LOW)
        ug_ref[:, x * hid : (x + 1) * hid] = (act_grad * (gate * sig)).astype(LOW)


def mid_kernel(gg_ref, ug_ref, own_ref, other_ref, top_ref, bottom_ref):
    hid = gg_ref.shape[1] // 2
    total = 0.0
    for x, weights_ref in enumerate((own_ref, other_ref)):
        cols = slice(x * hid, (x + 1) * hid)
        total = total + nt(gg_ref[:, cols], weights_ref[:, :hid])
        total = total + nt(ug_ref[:, cols], weights_ref[:, hid:])
    low = total.astype(LOW)

    @pl.when(in_top())
    def _():
        top_ref[...] = low

    @pl.when(jnp.logical_not(in_top()))
    def _():
        bottom_ref[...] = low


def leave_kernel(
    grad_two_ref, mine_top_ref, mine_bottom_ref, theirs_top_ref, theirs_bottom_ref,
    normed_ref, inv_ref, gains_ref, att_ref, y_ref, x_ref, corner_ref,
    low_ref, ctx1_ref, ctx2_ref, sum_ref, held_ref,
):
    heads_out(held_ref, (att_ref, y_ref, x_ref, corner_ref))
    top = add(mine_top_ref[...], theirs_top_ref[...])
    bottom = add(mine_bottom_ref[...], theirs_bottom_ref[...])
    hidden_grad = grad_two_ref[...].astype(FULL) + jnp.where(in_top(), top, bottom)
    normed = normed_ref[...].astype(FULL)
    column_sum(sum_ref, hidden_grad * normed)
    low = norm_back(hidden_grad * gains_ref[0], normed, inv_ref[...]).astype(LOW)
    low_ref[...] = low
    ctx1_ref[...] = nn(low, held_ref[0]).astype(LOW)
    ctx2_ref[...] = nn(low, held_ref[1]).astype(LOW)


def input_kernel(
    qk1_ref, v1_ref, qk2_ref, v2_ref, att_ref, y_ref, x_ref, corner_ref,
    full_ref, low_ref, held_ref,
):
    half, width = att_ref.shape[0], v1_ref.shape[1]
    pair = 2 * width

    @pl.when(pl.program_id(0) == 0)
    def _():
        held_ref[0, :half] = att_ref[:, : pair + width]
        held_ref[0, half:] = y_ref[:, : pair + width]
        held_ref[1, :half] = x_ref[:, : pair + width]
        held_ref[1, half:] = corner_ref[:, : pair + width]

    total = 0.0
    for x, qk_ref, v_ref in ((0, qk1_ref, v1_ref), (1, qk2_ref, v2_ref)):
        total = total + nt(qk_ref[...], held_ref[x, :, :pair])
        total = total + nt(v_ref[...], held_ref[x, :, pair:])
    full_ref[...] = total
    low_ref[...] = total.astype(LOW)


def heads_grad_kernel(rows_ref, grad_ref, qk_ref, v_ref, ctx_ref, out_ref, vo_ref):
    width = v_ref.shape[1]
    rows = flip(rows_ref[...]).astype(LOW)
    out_ref[...] = nn(rows, qk_ref[...]).astype(LOW)
    vo_ref[:, :width] = nn(rows, v_ref[...]).astype(LOW)
    vo_ref[:, width:] = nn(flip(grad_ref[...]).astype(LOW), ctx_ref[...]).astype(LOW)


def heads_grad(rows, grad, dqk, dv, context):
    half, pair = D // 2, dqk.shape[1]
    split = pl.BlockSpec((L, 256), lambda i: (0, i))
    qk, vo = pl.pallas_call(
        heads_grad_kernel,
        grid=(D // 256,),
        in_specs=[split, split] + [held_once(g) for g in (dqk, dv, context)],
        out_specs=[pl.BlockSpec((256, pair), lambda i: (i, 0))] * 2,
        out_shape=[pltpu.HBM((D, pair), LOW)] * 2,
        compiler_params=pltpu.CompilerParams(vmem_limit_bytes=24 << 20),
        cost_estimate=SMALL,
        name="heads_grad",
    )(rows, grad, dqk, dv, context)
    return qk[:half], qk[half:], vo


def in_order(value, mover):
    total = 0.0
    for _ in range(2):
        part = value.astype(LOW)
        total = total + nt(part, mover)
        value = value - part.astype(FULL)
    return total


def finish_kernel(
    core_ref, one_ref, full_ref, out_ref, theirs_ref, mover_ref, *refs
):
    grad_ref, low_ref = refs[-2:]
    mover = mover_ref[...]
    grad = one_ref[...].astype(FULL) + full_ref[...] + theirs_ref[...].astype(FULL)
    grad_ref[...] = in_order(grad, mover)
    low_ref[...] = nt(out_ref[...], mover).astype(LOW)


def finish(part, done, core, grad_one, part_full, layer_output, theirs, mover):
    rows = theirs.shape[0]
    steps = rows // QB
    mine = pl.BlockSpec((QB, D), lambda i, c: (c[0] * steps + part, 0))
    plain = pl.BlockSpec((QB, D), lambda i, c: (part, 0))
    return pl.pallas_call(
        finish_kernel,
        grid_spec=pltpu.PrefetchScalarGridSpec(
            num_scalar_prefetch=1,
            grid=(1,),
            in_specs=[mine, mine, mine, plain, held_once(mover)]
            + [pl.BlockSpec(memory_space=pl.ANY)] * len(done),
            out_specs=[plain, plain],
        ),
        out_shape=[
            jax.ShapeDtypeStruct((rows, D), FULL), jax.ShapeDtypeStruct((rows, D), LOW)
        ],
        input_output_aliases={6 + i: i for i in range(len(done))},
        cost_estimate=pl.CostEstimate(
            flops=4 * 10**9, bytes_accessed=8 << 20, transcendentals=0
        ),
        name="finish",
    )(core, grad_one, pinned(part_full), pinned(layer_output), theirs, mover, *done)


def adam_kernel(clip, rates, *refs):
    me = refs[0][0]
    message = refs[1][...] + refs[2][...]
    att_ref, ffn_ref, down_ref = refs[3:6]
    ins, norm_ref, outs = refs[6:21], refs[21], refs[22:]
    block = ins[12].shape[1]
    gain_sum = message[:, : 2 * D]
    total = message[:, 2 * D : 2 * D + 1] + jnp.sum(gain_sum * gain_sum, axis=1, keepdims=True)
    norm = jnp.sqrt(total)
    norm_ref[...] = norm
    ratio = clip / jnp.maximum(norm, clip)

    def update(p, at, grad):
        rate, decay = rates[p]
        old = [ref[at] for ref in ins[3 * p : 3 * p + 3]]
        for ref, value in zip(
            outs[3 * p : 3 * p + 3], adam_update(*old, grad, ratio, rate, decay)
        ):
            ref[at] = value

    width, hid = att_ref.shape[1] // 4, ffn_ref.shape[1] // 2
    step = 32 if block % 32 == 0 else block

    def some(i, carry):
        rows = pl.ds(pl.multiple_of(i * step, step), step) if step < block else slice(None)
        for k in range(3):
            update(0, (k, rows), att_ref[rows, k * width : (k + 1) * width])
        for k in range(2):
            update(2, (k, rows), ffn_ref[rows, k * hid : (k + 1) * hid])
        update(3, rows, down_ref[rows, :])
        return carry

    if step < block:
        lax.fori_loop(0, block // step, some, 0)
    else:
        some(0, 0)
    update(1, ..., att_ref[:, 3 * width :].T)
    for k in range(2):
        mine = jnp.zeros((1, block), FULL)
        for j in range(D // block):
            start = k * D + j * block
            mine = jnp.where(me == j, gain_sum[:, start : start + block], mine)
        update(4, pl.ds(k, 1), mine)


def adam(me, clip, rates, grads, params):
    flat = [array for group in params for array in group]
    outs = [jax.ShapeDtypeStruct((1, 1), FULL)]
    outs += [jax.ShapeDtypeStruct(w.shape, FULL) for w in flat]
    vmem = pl.BlockSpec(memory_space=pltpu.VMEM)
    norm, *made = pl.pallas_call(
        functools.partial(adam_kernel, clip, rates),
        in_specs=[pl.BlockSpec(memory_space=pltpu.SMEM)] + [vmem] * (len(grads) + len(flat)),
        out_specs=[vmem] * len(outs),
        out_shape=outs,
        name="adam",
    )(me, *grads, *[pltpu.with_memory_space_constraint(f, pltpu.VMEM) for f in flat])
    return norm[0, 0], [made[i : i + 3] for i in range(0, len(made), 3)]


def rope_tables(place):
    half = HD // 2
    lane = jnp.arange(128) % HD
    freq = jnp.exp(-jnp.log(10000.0) * (lane % half).astype(FULL) / half)
    angle = place[:, None] * freq[None, :]
    return jnp.cos(angle), jnp.where(lane < half, -1.0, 1.0)[None, :] * jnp.sin(angle)


def adam_update(weight, first, second, grad, ratio, rate, decay):
    clipped = grad * ratio
    first_new = AVERAGING * first + (1.0 - AVERAGING) * clipped
    second_new = AVERAGING * second + (1.0 - AVERAGING) * clipped * clipped
    correction = 1.0 - AVERAGING**ADAM_STEP
    step = first_new / correction / (jnp.sqrt(second_new / correction) + 1e-08)
    return (weight - rate * (step + decay * weight), first_new, second_new)


def tn(rows, grads):
    out = lax.dot_general(rows, grads, (((0,), (0,)), ((), ())), preferred_element_type=FULL)
    return layout.with_layout_constraint(out.astype(LOW), layout.Layout((0, 1)))


def per_device(
    layer_input, layer_cotangent,
    attend_weight, attend_first, attend_second,
    output_weight, output_first, output_second,
    gated_weight, gated_first, gated_second,
    down_weight, down_first, down_second,
    norm_gains, gains_first, gains_second,
):
    rows = layer_input.shape[0]
    wide = lax.axis_size("wide")
    block = D // wide
    me = lax.axis_index("wide")
    narrow = lax.axis_index("narrow")
    core = narrow % 2
    cols = attend_weight.shape[2]

    bits = wide_bits()
    near = bits[:-1]
    half = D // 2
    hid = down_weight.shape[0]

    bits = wide_bits()
    near = bits[:-1]
    half = D // 2
    hid = down_weight.shape[0]
    pair = 2 * cols

    attend_low = attend_weight.astype(LOW)
    att = jnp.concatenate(
        [attend_low[0], attend_low[1], attend_low[2], output_weight.T.astype(LOW)], axis=1
    )
    cut = hid // 2
    down_t = down_weight.T
    ffn = jnp.concatenate([gated_weight[0], gated_weight[1], down_t[:, :cut]], axis=1).astype(LOW)
    down = down_t[:, cut:].astype(LOW)

    order = me ^ jnp.array(block_masks(), jnp.int32)
    source = (order[:, None] * block + jnp.arange(block)[None, :]).reshape(1, D)
    mover = (lax.broadcasted_iota(jnp.int32, (D, D), 0) == source).astype(LOW)
    mover = lax.optimization_barrier(mover)

    def both_halves(mine, theirs):
        first = core == 0
        return jnp.concatenate(
            [jnp.where(first, mine, theirs), jnp.where(first, theirs, mine)], axis=0
        )

    def own_rows(value):
        return lax.dynamic_slice_in_dim(value, core * rows, rows, axis=0)

    first = widen(att, near[:1])
    gains = widen(after(norm_gains, att).astype(LOW).astype(FULL)[None], bits[:1])
    first, down, gains = lax.optimization_barrier((first, down, gains))
    gains = widen(gains, bits[1:-1])
    att = widen(first, near[1:])
    down_y = swap(down, "wide", 1)
    down_x = swap(down, "narrow", 2)
    both = jnp.concatenate([layer_input, layer_cotangent], axis=0)
    moved = jnp.dot(both, mover, preferred_element_type=FULL).astype(LOW)
    place = jnp.arange(L, dtype=FULL)
    att, down_y, down_x, gains, moved, place = lax.optimization_barrier(
        (att, down_y, down_x, gains, moved, place)
    )
    att_y = swap(att, "wide", 1)
    att_x = swap(att, "narrow", 2)
    ffn = widen(after(ffn, att), near[:1])
    gains = widen(gains, bits[-1:])
    inputs = both_halves(moved[:rows], swap(moved[:rows], "narrow", 1))
    moved_up = moved[rows:]
    cosine, sine = rope_tables(place)
    inputs, att, att_y, att_x, ffn, gains, cosine, sine = lax.optimization_barrier(
        (inputs, att, att_y, att_x, ffn, gains, cosine, sine)
    )
    gains = gains.transpose(1, 0, 2).reshape(2, 1, D)
    down_corner = swap(down_y, "narrow", 2)
    qk_corner = swap(att_y[:, :pair], "narrow", 2)
    vo_corner = swap(att_x[:, pair:], "wide", 1)
    ffn = widen(ffn, near[1:])
    qk = [[(att, pair, 0), (att_y, pair, 0)], [(att_x, pair, 0), qk_corner]]
    vo = [[(att, pair, 1), (att_y, pair, 1)], [(att_x, pair, 1), vo_corner]]
    saved = [attend_forward(inputs, qk[0], vo[0], cosine, sine)]
    second_in, qk_corner, vo_corner, ffn, down_corner = lax.optimization_barrier(
        (after(inputs, saved[0][3]), qk_corner, vo_corner, ffn, down_corner)
    )
    other_up = swap(after(moved_up, second_in), "narrow", 1)
    down = jnp.stack([down, down_y, down_x, down_corner])[:, None]
    for bit in near[:1]:
        down = jnp.concatenate([down, swap(down, "wide", bit)], axis=1)
    corner = jnp.concatenate([qk_corner, vo_corner], axis=1)
    qk[1][1], vo[1][1] = (corner, pair, 0), (corner, pair, 1)
    ffn_y = swap(ffn, "wide", 1)
    ffn_x = swap(ffn, "narrow", 2)
    saved.append(attend_forward(second_in, qk[1], vo[1], cosine, sine))
    context = [s[3] for s in saved]
    att_out = [att, att_y, att_x, corner]
    held = [pltpu.VMEM((2, D, cols), LOW)]
    low_d, full_d = (D, LOW, False), (D, FULL, True)
    (attn_part,) = by_rows(
        project_kernel, "project", context, att_out, [low_d], scratch=held
    )
    ffn_y, ffn_x, attn_part, down = lax.optimization_barrier((ffn_y, ffn_x, attn_part, down))
    attn_other = swap(attn_part, "narrow", 1)
    down_far = [swap(down, "wide", bit) for bit in near[1:2]]
    gate_corner = swap(ffn_y[:, :hid], "narrow", 2)
    up_corner = swap(ffn_x[:, hid:], "wide", 1)
    flow = [(hid, LOW, True), (hid, LOW, True), (hid, LOW, False)]
    normed_one, inv_one, hidden_low, gate1, up1, act1, gu_own = by_rows(
        enter_kernel, "enter", [pinned(inputs), attn_part, attn_other],
        [gains, (ffn, 2 * hid, 0), (ffn_y, 2 * hid, 0)],
        [(D, LOW, True), (1, FULL, True), low_d] + flow, kept=[(D, 2 * hid)],
    )
    hidden_low, down, down_far = lax.optimization_barrier((hidden_low, down, down_far))
    moved_up, other_up, hidden_low = lax.optimization_barrier((moved_up, other_up, hidden_low))
    upstream = both_halves(moved_up, other_up)
    down = jnp.concatenate([down, *down_far], axis=1)
    for bit in near[2:]:
        down = jnp.concatenate([down, swap(down, "wide", bit)], axis=1)
    down = down.reshape(2, D, hid - cut)
    last_cols = 2 * hid // cut
    gate2, up2, act2, ffn_part, gu_other, down_all = by_rows(
        rest_kernel, "rest", [after(hidden_low, upstream), act1],
        [
            (ffn_x, 2 * hid, 0), gate_corner, (up_corner, hid, 0),
            (ffn, cut, last_cols), (ffn_y, cut, last_cols), (ffn_x, cut, last_cols),
            (up_corner, cut, hid // cut), down,
        ],
        flow + [low_d], kept=[(D, 2 * hid), (2, D, hid)], loose=(1, 2, 6),
    )
    ffn_other = swap(ffn_part, "narrow", 1)

    layer_output, grad_two_low, gain_two_grad = by_rows(
        turn_kernel, "turn", [pinned(normed_one), ffn_part, ffn_other, pinned(upstream)],
        [gains], [(D, LOW, True), low_d], sums=1,
    )
    down_send = tn(grad_two_low, act2)
    down_x = swap(down_send, "narrow", 2)
    wide_flow = (2 * hid, LOW, False)
    saves = [pinned(r) for r in (gate1, up1, gate2, up2)]
    gg, ug = by_rows(
        back_kernel, "back",
        [after(grad_two_low, down_send), *saves], [down_all], [wide_flow, wide_flow],
    )
    gate_send = tn(hidden_low[:, half:], gg)
    up_send = tn(hidden_low[:, half:], ug)
    gate_y = swap(gate_send, "wide", 1)
    up_y = swap(up_send, "wide", 1)
    mid_part = by_rows(
        mid_kernel, "mid", [after(gg, gate_send, up_send), ug], [gu_own, gu_other], []
    )
    mid_other = [swap(part, "narrow", 1) for part in mid_part]
    down_own = tn(grad_two_low, act1)
    gate_own = tn(hidden_low[:, :half], gg)
    up_own = tn(hidden_low[:, :half], ug)
    mid_part, mid_other, down_own, gate_own, up_own, down_x = lax.optimization_barrier(
        (mid_part, mid_other, down_own, gate_own, up_own, down_x)
    )
    grad_one_low, dctx1, dctx2, gain_one_grad = by_rows(
        leave_kernel, "leave",
        [grad_two_low, tuple(mid_part), tuple(mid_other), pinned(normed_one), pinned(inv_one)],
        [gains, *att_out], [low_d, (cols, LOW, True), (cols, LOW, True)],
        sums=1, scratch=held,
    )

    q, k, v, _, lse = saved[1]
    dqk2, dv2 = attend_backward(q, k, v, lse, dctx2, cosine, sine)
    down_x, gate_y, dqk2, dv2 = lax.optimization_barrier((down_x, gate_y, dqk2, dv2))
    down_sum, gate_sum = add(down_own, down_x), add(gate_own, gate_y)
    down_y = swap(down_sum[half:].astype(LOW), "wide", 1)
    gate_far = gate_sum[:, hid:].astype(LOW)
    gate_x = swap(gate_far, "narrow", 2)
    qk_near2, qk_send2, vo_send = heads_grad(inputs, grad_one_low, after(dqk2, gate_far), dv2, context[1])
    vo_x = swap(vo_send, "narrow", 2)
    qk_y2 = swap(qk_send2, "wide", 1)
    back = near[::-1]
    q, k, v, _, lse = saved[0]
    dqk1, dv1 = attend_backward(q, k, v, lse, after(dctx1, vo_send, qk_send2), cosine, sine)
    dqk1, dv1, up_y, down_y, qk_y2, gate_x = lax.optimization_barrier(
        (dqk1, dv1, up_y, down_y, qk_y2, gate_x)
    )
    early = narrow_down(add(down_sum[:half], down_y), back[:1])
    up_sum = add(up_own, up_y)
    up_x = swap(up_sum[:, hid:].astype(LOW), "narrow", 2)
    qk_near1, qk_send1, vo_own = heads_grad(inputs, grad_one_low, dqk1, dv1, context[0])
    qk_y1 = swap(qk_send1, "wide", 1)
    qk_far = add(qk_near2, qk_y2).astype(LOW)
    qk_x = swap(qk_far, "narrow", 2)
    vo_sum = add(vo_own, vo_x)
    vo_far = vo_sum[half:].astype(LOW)
    vo_y = swap(vo_far, "wide", 1)
    late = jnp.concatenate([add(gate_sum[:, :hid], gate_x), add(up_sum[:, :hid], up_x)], axis=1)
    early_red = narrow_down(early, back[1:])
    dqk1, vo_sum = lax.optimization_barrier((dqk1, vo_sum))
    part_full, part_low = by_rows(
        input_kernel, "inputs", [dqk1, dv1, dqk2, dv2],
        att_out, [full_d, low_d], step=128,
        scratch=[pltpu.VMEM((2, D, 3 * cols), LOW)],
    )
    late = narrow_down(late, back[:1])
    theirs = lax.dynamic_slice_in_dim(part_low, (1 - core) * rows, rows, axis=0)
    theirs = swap(theirs, "narrow", 1)
    qk_sum = add(qk_near1, qk_y1)
    last = jnp.concatenate([add(qk_sum, qk_x), add(vo_sum[:half], vo_y)], axis=1)
    gain_grads = jnp.concatenate([gain_one_grad, gain_two_grad], axis=0)
    gain_low = gain_grads.astype(LOW)
    gain_rest = (gain_grads - gain_low.astype(FULL)).astype(LOW)
    gain_grads = nt(jnp.concatenate([gain_low, gain_rest], axis=0), mover)
    gain_grads = gain_grads[:2] + gain_grads[2:]
    last, early_red, late, gain_grads, part_full = lax.optimization_barrier(
        (last, early_red, late, gain_grads, part_full)
    )
    last = narrow_down(last, back[:1])
    late_red = narrow_down(late, back[1:])
    early_square = jnp.sum(early_red * early_red) + jnp.sum(late_red * late_red)
    att_red = narrow_down(last, back[1:])

    square = jnp.full((1, 128), early_square + jnp.sum(att_red * att_red), FULL)
    square = square + swap(square, "narrow", 1)
    message = jnp.concatenate([gain_grads.reshape(1, 2 * D), square], axis=1)
    message = message + swap(message, "narrow", 2)
    which, done = jnp.full((1,), core, jnp.int32), ()
    theirs = after(theirs, message)
    for part in range(rows // QB):
        done = finish(part, done, which, grad_one_low, part_full, layer_output, theirs, mover)
    input_grad, layer_output = done
    for bit in bits[::-1][:-1]:
        message = message + swap(message, "wide", bit)
    received = swap(message, "wide", bits[0])
    all_tokens = rows * wide * lax.axis_size("narrow")
    clip = 0.02 * math.sqrt(all_tokens * (4 * D * D + 3 * D * FF + 2 * D))
    grad_norm, (new_attend, new_output, new_gated, new_down, new_gains) = adam(
        jnp.full((1,), me, jnp.int32),
        clip,
        (
            (D ** (-0.5), WEIGHT_DECAY),
            (max(D // 64, 1) ** (-0.5), WEIGHT_DECAY),
            (D ** (-0.5), WEIGHT_DECAY),
            (FF ** (-0.5), WEIGHT_DECAY),
            (0.4, 0.0),
        ),
        (message, received, att_red, late_red, early_red),
        (
            (attend_weight, attend_first, attend_second),
            (output_weight, output_first, output_second),
            (gated_weight, gated_first, gated_second),
            (down_weight.T, down_first.T, down_second.T),
            (norm_gains, gains_first, gains_second),
        ),
    )
    new_down = [value.T for value in new_down]
    return (
        layer_output, input_grad, grad_norm,
        *new_attend, *new_output, *new_gated, *new_down, *new_gains,
    )


def solution(mesh):
    rows = P(("wide", "narrow"), None)
    stacked = P(None, "wide", "narrow")
    turned = P("narrow", "wide")
    gains = P(None, "wide")
    params = (stacked,) * 3 + (turned,) * 3 + (stacked,) * 3 + (turned,) * 3 + (gains,) * 3
    return jax.shard_map(
        per_device,
        mesh=mesh,
        in_specs=(rows, rows) + params,
        out_specs=(rows, rows, P()) + params,
        check_vma=False,
    )
```

```python
import functools
import math

import jax
import jax.numpy as jnp
from jax import lax
from jax.experimental import layout
from jax.experimental import pallas as pl
from jax.experimental.pallas import tpu as pltpu
from jax.sharding import PartitionSpec as P

D = 768
HD = 64
FF = 2048
L = 1024
ADAM_STEP = 5

EPSILON = 1e-05
WEIGHT_DECAY = 0.1
AVERAGING = 0.5

LOW = jnp.bfloat16
FULL = jnp.float32
QB = 256
MASKED = -1e30
SMALL = pl.CostEstimate(flops=10**6, bytes_accessed=10**4, transcendentals=0)


def swap(value, axis, bit):
    size = lax.axis_size(axis)
    return lax.ppermute(value, axis, [(i, i ^ bit) for i in range(size)])


def wide_bits():
    top = lax.axis_size("wide").bit_length() - 1
    return [1 << b for b in range(top - 1, -1, -1)]


def block_masks():
    masks = [0]
    for bit in wide_bits():
        masks = masks + [m ^ bit for m in masks]
    return masks


def after(value, *done):
    return lax.optimization_barrier((value, done))[0]


def widen(held, bits):
    for bit in bits:
        held = jnp.concatenate([held, swap(held, "wide", bit)], axis=0)
    return held


def add(kept, received):
    return kept.astype(FULL) + received.astype(FULL)


def narrow_down(held, bits):
    for bit in bits:
        half = held.shape[0] // 2
        held = add(held[:half], swap(held[half:].astype(LOW), "wide", bit))
    return held


def turn(value, cosine, sine, sign):
    width = value.shape[1]
    lane = lax.broadcasted_iota(jnp.int32, value.shape, 1) % HD
    other = jnp.where(
        lane < HD // 2,
        pltpu.roll(value, width - HD // 2, 1),
        pltpu.roll(value, HD // 2, 1),
    )
    reps = width // 128
    return value * jnp.concatenate([cosine] * reps, axis=1) + sign * other * jnp.concatenate(
        [sine] * reps, axis=1
    )


def nn(a, b):
    return lax.dot_general(a, b, (((1,), (0,)), ((), ())), preferred_element_type=FULL)


def nt(a, b):
    return lax.dot_general(a, b, (((1,), (1,)), ((), ())), preferred_element_type=FULL)


def diagonal(scores):
    key = lax.broadcasted_iota(jnp.int32, scores.shape, 0)
    query = lax.broadcasted_iota(jnp.int32, scores.shape, 1)
    return jnp.where(key <= query, scores, MASKED)


def flip(value):
    return value.astype(FULL).T


def attend_kernel(
    rows_ref, qka_ref, qkb_ref, voa_ref, vob_ref, cos_ref, sin_ref,
    q_ref, k_ref, v_ref, ctx_ref, lse_ref, hold,
):
    heads = q_ref.shape[0]
    width = heads * HD
    half = qka_ref.shape[0]

    def project(i, carry):
        rows = pl.ds(pl.multiple_of(i * QB, QB), QB)
        first, second = rows_ref[rows, :half], rows_ref[rows, half:]
        pair = nn(first, qka_ref[...]) + nn(second, qkb_ref[...])
        pair = turn(pair, cos_ref[rows, :], sin_ref[rows, :], 1.0)
        value = nn(first, voa_ref[:, :width]) + nn(second, vob_ref[:, :width])
        for h in range(heads):
            q_ref[h, rows, :] = (pair[:, h * HD : (h + 1) * HD] * (HD**-0.5)).astype(LOW)
            k_ref[h, rows, :] = pair[:, width + h * HD : width + (h + 1) * HD].astype(LOW)
            v_ref[h, rows, :] = value[:, h * HD : (h + 1) * HD].astype(LOW)
        return carry

    lax.fori_loop(0, L // QB, project, 0)

    def head(h, carry):
        turned = flip(v_ref[h]).astype(LOW)
        for i in range(L // QB):
            lo, hi = i * QB, (i + 1) * QB
            query = q_ref[h, lo:hi, :]
            diag = diagonal(nt(k_ref[h, lo:hi, :], query))
            peak = jnp.max(diag, axis=0, keepdims=True)
            if i:
                body = nt(k_ref[h, :lo, :], query)
                peak = jnp.maximum(peak, jnp.max(body, axis=0, keepdims=True))
            weight = jnp.exp(diag - peak)
            total = jnp.sum(weight, axis=0, keepdims=True)
            out = nn(turned[:, lo:hi], weight.astype(LOW))
            if i:
                weight = jnp.exp(body - peak)
                total = total + jnp.sum(weight, axis=0, keepdims=True)
                out = out + nn(turned[:, :lo], weight.astype(LOW))
            lse_ref[h, :, lo:hi] = peak + jnp.log(total)
            hold[h, lo:hi, :] = (out / total).T.astype(LOW)
        return carry

    lax.fori_loop(0, heads, head, 0)
    for h in range(heads):
        ctx_ref[:, h * HD : (h + 1) * HD] = hold[h]


def pinned(array):
    return pltpu.with_memory_space_constraint(array, pltpu.HBM)


def whole(array):
    zero = (0,) * len(array.shape)
    return pl.BlockSpec(array.shape, lambda *_: zero)


def by_head(shape):
    return pl.BlockSpec(shape, lambda h: (h, 0, 0))


def columns(piece, mode=None):
    array, width, j = piece if isinstance(piece, tuple) else (piece, piece.shape[-1], 0)
    lead = (0,) * (array.ndim - 1)
    shape = array.shape[:-1] + (width,)
    return array, pl.BlockSpec(shape, lambda *_: lead + (j,), pipeline_mode=mode)


def width_of(piece):
    return piece[1] if isinstance(piece, tuple) else piece.shape[1]


def attend_forward(rows, qk, vo, cosine, sine):
    heads = width_of(qk[0]) // 2 // HD
    headed = pltpu.HBM((heads, L, HD), LOW)
    outs = (
        headed, headed, headed,
        jax.ShapeDtypeStruct((L, heads * HD), LOW),
        pltpu.HBM((heads, 1, L), FULL),
    )
    args, specs = zip(*[columns(p) for p in (rows, *qk, *vo, cosine, sine)])
    return pl.pallas_call(
        attend_kernel,
        grid=(1,),
        in_specs=list(specs),
        out_specs=[whole(o) for o in outs],
        out_shape=outs,
        scratch_shapes=[pltpu.VMEM((heads, L, HD), LOW)],
        compiler_params=pltpu.CompilerParams(vmem_limit_bytes=24 << 20),
        cost_estimate=SMALL,
        name="attend_forward",
    )(*args)


def attend_back_kernel(
    q_ref, k_ref, v_ref, lse_ref, dctx_ref, cos_ref, sin_ref,
    dqk_ref, dv_ref, dctx, dqk, dk_sum, dv_sum,
):
    heads = dctx.shape[0]
    h = pl.program_id(0)

    @pl.when(h == 0)
    def _():
        for j in range(heads):
            dctx[j] = dctx_ref[:, j * HD : (j + 1) * HD]

    turned = flip(k_ref[0]).astype(LOW)
    for i in range(L // QB):
        lo, hi = i * QB, (i + 1) * QB
        query, back = q_ref[0, lo:hi, :], dctx[h, lo:hi, :]
        lse = lse_ref[0, :, lo:hi]
        prob = jnp.exp(diagonal(nt(k_ref[0, lo:hi, :], query)) - lse)
        grad = nt(v_ref[0, lo:hi, :], back)
        inner = jnp.sum(prob * grad, axis=0, keepdims=True)
        if i:
            prob_body = jnp.exp(nt(k_ref[0, :lo, :], query) - lse)
            grad_body = nt(v_ref[0, :lo, :], back)
            inner = inner + jnp.sum(prob_body * grad_body, axis=0, keepdims=True)
        score = (prob * (grad - inner)).astype(LOW)
        dv_sum[h, lo:hi, :] = nn(prob.astype(LOW), back)
        dk_sum[h, lo:hi, :] = nn(score, query)
        dquery = nn(turned[:, lo:hi], score)
        if i:
            score = (prob_body * (grad_body - inner)).astype(LOW)
            dv_sum[h, :lo, :] += nn(prob_body.astype(LOW), back)
            dk_sum[h, :lo, :] += nn(score, query)
            dquery = dquery + nn(turned[:, :lo], score)
        dqk[h, lo:hi, :] = (dquery * (HD**-0.5)).T

    def finish(i, carry):
        rows = pl.ds(pl.multiple_of(i * QB, QB), QB)
        pair = jnp.concatenate(
            [dqk[j, rows, :] for j in range(heads)] + [dk_sum[j, rows, :] for j in range(heads)],
            axis=1,
        )
        dqk_ref[rows, :] = turn(pair, cos_ref[rows, :], sin_ref[rows, :], -1.0).astype(LOW)
        dv_ref[rows, :] = jnp.concatenate(
            [dv_sum[j, rows, :] for j in range(heads)], axis=1
        ).astype(LOW)
        return carry

    @pl.when(h == heads - 1)
    def _():
        lax.fori_loop(0, L // QB, finish, 0)


def attend_backward(q, k, v, lse, dctx, cosine, sine):
    heads = q.shape[0]
    outs = (
        jax.ShapeDtypeStruct((L, 2 * heads * HD), LOW),
        jax.ShapeDtypeStruct((L, heads * HD), LOW),
    )
    return pl.pallas_call(
        attend_back_kernel,
        grid=(heads,),
        in_specs=[by_head((1, L, HD))] * 3
        + [by_head((1, 1, L)), whole(dctx), whole(cosine), whole(sine)],
        out_specs=[whole(o) for o in outs],
        out_shape=outs,
        scratch_shapes=[pltpu.VMEM((heads, L, HD), LOW)] + [pltpu.VMEM((heads, L, HD), FULL)] * 3,
        compiler_params=pltpu.CompilerParams(vmem_limit_bytes=24 << 20),
        cost_estimate=SMALL,
        name="attend_backward",
    )(pinned(q), pinned(k), pinned(v), pinned(lse), pinned(dctx), pinned(cosine), pinned(sine))


def held_once(array):
    zero = (0,) * array.ndim
    return pl.BlockSpec(array.shape, lambda *_: zero, pipeline_mode=pl.Buffered(1))


def in_top():
    return pl.program_id(0) < pl.num_programs(0) // 2


def halves(step, width):
    steps = L // step // 2
    return [
        pl.BlockSpec((step, width), lambda i: (jnp.minimum(i, steps - 1), 0)),
        pl.BlockSpec((step, width), lambda i: (jnp.maximum(i - steps, 0), 0)),
    ]


def by_rows(kernel, name, row_args, fixed, outs, sums=0, kept=(), scratch=(), loose=(), step=QB):
    specs, flat = [], []
    for r in row_args:
        if isinstance(r, tuple):
            specs += halves(step, r[0].shape[1])
            flat += r
        else:
            specs.append(pl.BlockSpec((step, r.shape[1]), lambda i: (i, 0)))
            flat.append(r)
    held, held_specs = zip(*[columns(f, pl.Buffered(1)) for f in fixed])
    shapes = [
        (pltpu.HBM if away else jax.ShapeDtypeStruct)((L, w), t) for w, t, away in outs
    ]
    out_specs = [pl.BlockSpec((step, w), lambda i: (i, 0)) for w, _, _ in outs]
    if not outs:
        shapes = [jax.ShapeDtypeStruct((L // 2, D), LOW)] * 2
        out_specs = halves(step, D)
    rows_out = len(shapes)
    shapes += [jax.ShapeDtypeStruct((1, D), FULL)] * sums
    shapes += [pltpu.HBM(shape, LOW) for shape in kept]
    out_specs += [whole(o) for o in shapes[rows_out:]]
    return pl.pallas_call(
        kernel,
        grid=(L // step,),
        in_specs=specs + list(held_specs),
        out_specs=out_specs,
        out_shape=shapes,
        scratch_shapes=list(scratch),
        compiler_params=pltpu.CompilerParams(vmem_limit_bytes=32 << 20),
        cost_estimate=SMALL,
        name=name,
    )(*flat, *[f if f.dtype == FULL or i in loose else pinned(f) for i, f in enumerate(held)])


def rms_scale(residual):
    return lax.rsqrt(jnp.mean(residual * residual, axis=1, keepdims=True) + EPSILON)


def norm_back(scaled, normed, inv):
    return inv * (scaled - normed * jnp.mean(scaled * normed, axis=1, keepdims=True))


def column_sum(sum_ref, value):
    @pl.when(pl.program_id(0) == 0)
    def _():
        sum_ref[...] = jnp.zeros_like(sum_ref)

    sum_ref[...] += jnp.sum(value, axis=0, keepdims=True)


def heads_out(held_ref, refs):
    att_ref, y_ref, x_ref, corner_ref = refs
    half, width = att_ref.shape[0], held_ref.shape[2]

    @pl.when(pl.program_id(0) == 0)
    def _():
        held_ref[0, :half] = att_ref[:, 3 * width :]
        held_ref[0, half:] = y_ref[:, 3 * width :]
        held_ref[1, :half] = x_ref[:, 3 * width :]
        held_ref[1, half:] = corner_ref[:, width:]


def project_kernel(one_ref, two_ref, att_ref, y_ref, x_ref, corner_ref, out_ref, held_ref):
    heads_out(held_ref, (att_ref, y_ref, x_ref, corner_ref))
    out_ref[...] = (nt(one_ref[...], held_ref[0]) + nt(two_ref[...], held_ref[1])).astype(LOW)


def gate_up(hidden, weights_ref, gate_ref, up_ref, act_ref):
    hid = gate_ref.shape[1]
    gate = nn(hidden, weights_ref[:, :hid])
    up = nn(hidden, weights_ref[:, hid:])
    gate_ref[...] = gate.astype(LOW)
    up_ref[...] = up.astype(LOW)
    act_ref[...] = (gate * jax.nn.sigmoid(gate) * up).astype(LOW)


def enter_kernel(
    rows_ref, mine_ref, theirs_ref, gain_ref, own_ref, y_ref,
    normed_ref, inv_ref, hidden_ref, gate_ref, up_ref, act_ref, weights_ref,
):
    half = own_ref.shape[0]

    @pl.when(pl.program_id(0) == 0)
    def _():
        weights_ref[:half] = own_ref[...]
        weights_ref[half:] = y_ref[...]

    residual = rows_ref[...].astype(FULL) + add(mine_ref[...], theirs_ref[...])
    inv = rms_scale(residual)
    normed = residual * inv
    hidden = (normed * gain_ref[0]).astype(LOW)
    normed_ref[...] = normed.astype(LOW)
    inv_ref[...] = inv
    hidden_ref[...] = hidden
    gate_up(hidden, weights_ref, gate_ref, up_ref, act_ref)


def rest_kernel(
    hidden_ref, act1_ref, x_ref, gate_corner_ref, up_corner_ref,
    low_own_ref, low_y_ref, low_x_ref, low_corner_ref, high_ref,
    gate_ref, up_ref, act_ref, out_ref, weights_ref, down_ref,
):
    half, hid = x_ref.shape[0], gate_ref.shape[1]
    cut = high_ref.shape[2]

    @pl.when(pl.program_id(0) == 0)
    def _():
        weights_ref[:half] = x_ref[...]
        weights_ref[half:, :hid] = gate_corner_ref[...]
        weights_ref[half:, hid:] = up_corner_ref[...]
        down_ref[0, :half, :cut] = low_own_ref[...]
        down_ref[0, half:, :cut] = low_y_ref[...]
        down_ref[1, :half, :cut] = low_x_ref[...]
        down_ref[1, half:, :cut] = low_corner_ref[...]
        down_ref[:, :, cut:] = high_ref[...]

    gate_up(hidden_ref[...], weights_ref, gate_ref, up_ref, act_ref)
    out_ref[...] = (nt(act1_ref[...], down_ref[0]) + nt(act_ref[...], down_ref[1])).astype(LOW)


def turn_kernel(
    normed_ref, mine_ref, theirs_ref, up_rows_ref, gains_ref,
    out_ref, low_ref, sum_ref,
):
    residual = normed_ref[...].astype(FULL) * gains_ref[0] + add(mine_ref[...], theirs_ref[...])
    inv = rms_scale(residual)
    normed = residual * inv
    gain = gains_ref[1]
    out_ref[...] = (normed * gain).astype(LOW)
    upstream = up_rows_ref[...].astype(FULL)
    column_sum(sum_ref, upstream * normed)
    low_ref[...] = norm_back(upstream * gain, normed, inv).astype(LOW)


def back_kernel(low_ref, gate1_ref, up1_ref, gate2_ref, up2_ref, down_ref, gg_ref, ug_ref):
    hid = gate1_ref.shape[1]
    low = low_ref[...]
    for x, gate_ref, up_ref in ((0, gate1_ref, up1_ref), (1, gate2_ref, up2_ref)):
        act_grad = nn(low, down_ref[x])
        gate, up = gate_ref[...].astype(FULL), up_ref[...].astype(FULL)
        sig = jax.nn.sigmoid(gate)
        gg = act_grad * up * (sig * (1.0 + gate * (1.0 - sig)))
        gg_ref[:, x * hid : (x + 1) * hid] = gg.astype(LOW)
        ug_ref[:, x * hid : (x + 1) * hid] = (act_grad * (gate * sig)).astype(LOW)


def mid_kernel(gg_ref, ug_ref, own_ref, other_ref, top_ref, bottom_ref):
    hid = gg_ref.shape[1] // 2
    total = 0.0
    for x, weights_ref in enumerate((own_ref, other_ref)):
        cols = slice(x * hid, (x + 1) * hid)
        total = total + nt(gg_ref[:, cols], weights_ref[:, :hid])
        total = total + nt(ug_ref[:, cols], weights_ref[:, hid:])
    low = total.astype(LOW)

    @pl.when(in_top())
    def _():
        top_ref[...] = low

    @pl.when(jnp.logical_not(in_top()))
    def _():
        bottom_ref[...] = low


def leave_kernel(
    grad_two_ref, mine_top_ref, mine_bottom_ref, theirs_top_ref, theirs_bottom_ref,
    normed_ref, inv_ref, gains_ref, att_ref, y_ref, x_ref, corner_ref,
    low_ref, ctx1_ref, ctx2_ref, sum_ref, held_ref, mid_ref,
):
    heads_out(held_ref, (att_ref, y_ref, x_ref, corner_ref))

    @pl.when(in_top())
    def _():
        mid_ref[...] = add(mine_top_ref[...], theirs_top_ref[...])

    @pl.when(jnp.logical_not(in_top()))
    def _():
        mid_ref[...] = add(mine_bottom_ref[...], theirs_bottom_ref[...])

    hidden_grad = grad_two_ref[...].astype(FULL) + mid_ref[...]
    normed = normed_ref[...].astype(FULL)
    column_sum(sum_ref, hidden_grad * normed)
    low = norm_back(hidden_grad * gains_ref[0], normed, inv_ref[...]).astype(LOW)
    low_ref[...] = low
    ctx1_ref[...] = nn(low, held_ref[0]).astype(LOW)
    ctx2_ref[...] = nn(low, held_ref[1]).astype(LOW)


def input_kernel(
    qk1_ref, v1_ref, qk2_ref, v2_ref, att_ref, y_ref, x_ref, qk_corner_ref, vo_corner_ref,
    full_ref, low_ref, held_ref,
):
    half, width = att_ref.shape[0], v1_ref.shape[1]
    pair = 2 * width

    @pl.when(pl.program_id(0) == 0)
    def _():
        held_ref[0, :half] = att_ref[:, : pair + width]
        held_ref[0, half:] = y_ref[:, : pair + width]
        held_ref[1, :half] = x_ref[:, : pair + width]
        held_ref[1, half:, :pair] = qk_corner_ref[...]
        held_ref[1, half:, pair:] = vo_corner_ref[:, :width]

    total = 0.0
    for x, qk_ref, v_ref in ((0, qk1_ref, v1_ref), (1, qk2_ref, v2_ref)):
        total = total + nt(qk_ref[...], held_ref[x, :, :pair])
        total = total + nt(v_ref[...], held_ref[x, :, pair:])
    full_ref[...] = total
    low_ref[...] = total.astype(LOW)


def heads_grad_kernel(rows_ref, grad_ref, qk_ref, v_ref, ctx_ref, out_ref, vo_ref):
    width = v_ref.shape[1]
    rows = flip(rows_ref[...]).astype(LOW)
    out_ref[...] = nn(rows, qk_ref[...]).astype(LOW)
    vo_ref[:, :width] = nn(rows, v_ref[...]).astype(LOW)
    vo_ref[:, width:] = nn(flip(grad_ref[...]).astype(LOW), ctx_ref[...]).astype(LOW)


def heads_grad(rows, grad, dqk, dv, context):
    half, pair = D // 2, dqk.shape[1]
    split = pl.BlockSpec((L, 256), lambda i: (0, i))
    qk, vo = pl.pallas_call(
        heads_grad_kernel,
        grid=(D // 256,),
        in_specs=[split, split] + [held_once(g) for g in (dqk, dv, context)],
        out_specs=[pl.BlockSpec((256, pair), lambda i: (i, 0))] * 2,
        out_shape=[pltpu.HBM((D, pair), LOW)] * 2,
        compiler_params=pltpu.CompilerParams(vmem_limit_bytes=24 << 20),
        cost_estimate=SMALL,
        name="heads_grad",
    )(rows, grad, dqk, dv, context)
    return qk[:half], qk[half:], vo


def in_order(value, mover):
    total = 0.0
    for _ in range(2):
        part = value.astype(LOW)
        total = total + nt(part, mover)
        value = value - part.astype(FULL)
    return total


def finish_kernel(
    core_ref, one_ref, full_ref, out_ref, theirs_ref, mover_ref, *refs
):
    grad_ref, low_ref = refs[-2:]
    mover = mover_ref[...]
    grad = one_ref[...].astype(FULL) + full_ref[...] + theirs_ref[...].astype(FULL)
    grad_ref[...] = in_order(grad, mover)
    low_ref[...] = nt(out_ref[...], mover).astype(LOW)


def finish(part, done, core, grad_one, part_full, layer_output, theirs, mover):
    rows = theirs.shape[0]
    steps = rows // QB
    mine = pl.BlockSpec((QB, D), lambda i, c: (c[0] * steps + part, 0))
    plain = pl.BlockSpec((QB, D), lambda i, c: (part, 0))
    return pl.pallas_call(
        finish_kernel,
        grid_spec=pltpu.PrefetchScalarGridSpec(
            num_scalar_prefetch=1,
            grid=(1,),
            in_specs=[mine, mine, mine, plain, held_once(mover)]
            + [pl.BlockSpec(memory_space=pl.ANY)] * len(done),
            out_specs=[plain, plain],
        ),
        out_shape=[
            jax.ShapeDtypeStruct((rows, D), FULL), jax.ShapeDtypeStruct((rows, D), LOW)
        ],
        input_output_aliases={6 + i: i for i in range(len(done))},
        cost_estimate=pl.CostEstimate(
            flops=4 * 10**9, bytes_accessed=8 << 20, transcendentals=0
        ),
        name="finish",
    )(core, grad_one, pinned(part_full), pinned(layer_output), theirs, mover, *done)


def last_kernel(kept_ref, received_ref, square_ref, sum_ref, total_ref):
    value = kept_ref[...] + received_ref[...].astype(FULL)
    sum_ref[...] = value
    total = jnp.sum(jnp.sum(value * value, axis=0, keepdims=True), axis=1, keepdims=True)
    total_ref[...] = square_ref[...] + total


def last_sum(kept, received, square):
    vmem = pl.BlockSpec(memory_space=pltpu.VMEM)
    return pl.pallas_call(
        last_kernel,
        in_specs=[vmem] * 3,
        out_specs=[vmem] * 2,
        out_shape=[jax.ShapeDtypeStruct(kept.shape, FULL), jax.ShapeDtypeStruct((1, 128), FULL)],
        name="last_sum",
    )(kept, received, square)


def adam_kernel(clip, rates, *refs):
    me = refs[0][0]
    message = refs[1][...] + refs[2][...]
    att_ref, ffn_ref, down_ref = refs[3:6]
    ins, norm_ref, outs = refs[6:21], refs[21], refs[22:]
    block = ins[12].shape[1]
    gain_sum = message[:, : 2 * D]
    total = message[:, 2 * D : 2 * D + 1] + jnp.sum(gain_sum * gain_sum, axis=1, keepdims=True)
    norm = jnp.sqrt(total)
    norm_ref[...] = norm
    ratio = clip / jnp.maximum(norm, clip)

    def update(p, at, grad):
        rate, decay = rates[p]
        old = [ref[at] for ref in ins[3 * p : 3 * p + 3]]
        for ref, value in zip(
            outs[3 * p : 3 * p + 3], adam_update(*old, grad, ratio, rate, decay)
        ):
            ref[at] = value

    width, hid = att_ref.shape[1] // 4, ffn_ref.shape[1] // 2
    step = 16 if block % 16 == 0 else block

    def some(i, carry):
        rows = pl.ds(pl.multiple_of(i * step, step), step) if step < block else slice(None)
        for k in range(3):
            update(0, (k, rows), att_ref[rows, k * width : (k + 1) * width])
        for k in range(2):
            update(2, (k, rows), ffn_ref[rows, k * hid : (k + 1) * hid])
        update(3, rows, down_ref[rows, :])
        return carry

    if step < block:
        lax.fori_loop(0, block // step, some, 0)
    else:
        some(0, 0)
    update(1, ..., att_ref[:, 3 * width :].T)
    for k in range(2):
        mine = jnp.zeros((1, block), FULL)
        for j in range(D // block):
            start = k * D + j * block
            mine = jnp.where(me == j, gain_sum[:, start : start + block], mine)
        update(4, pl.ds(k, 1), mine)


def adam(me, clip, rates, grads, params):
    flat = [array for group in params for array in group]
    outs = [jax.ShapeDtypeStruct((1, 1), FULL)]
    outs += [jax.ShapeDtypeStruct(w.shape, FULL) for w in flat]
    vmem = pl.BlockSpec(memory_space=pltpu.VMEM)
    norm, *made = pl.pallas_call(
        functools.partial(adam_kernel, clip, rates),
        in_specs=[pl.BlockSpec(memory_space=pltpu.SMEM)] + [vmem] * (len(grads) + len(flat)),
        out_specs=[vmem] * len(outs),
        out_shape=outs,
        name="adam",
    )(me, *grads, *[pltpu.with_memory_space_constraint(f, pltpu.VMEM) for f in flat])
    return norm[0, 0], [made[i : i + 3] for i in range(0, len(made), 3)]


def rope_tables(place):
    half, low = HD // 2, place.shape[0] // 2
    lane = jnp.arange(128) % HD
    freq = jnp.exp(-jnp.log(10000.0) * (lane % half).astype(FULL) / half)
    angle = place[:, None] * freq[None, :]
    cosine, sine = jnp.cos(angle), jnp.sin(angle)
    c1, s1 = cosine[:low, None], sine[:low, None]
    c2, s2 = cosine[None, low:], sine[None, low:]
    sign = jnp.where(lane < half, -1.0, 1.0)[None, None, :]
    both = c1 * c2 - s1 * s2, sign * (s1 * c2 + c1 * s2)
    return [table.reshape(L, 128) for table in both]


def adam_update(weight, first, second, grad, ratio, rate, decay):
    clipped = grad * ratio
    first_new = AVERAGING * first + (1.0 - AVERAGING) * clipped
    second_new = AVERAGING * second + (1.0 - AVERAGING) * clipped * clipped
    correction = 1.0 - AVERAGING**ADAM_STEP
    step = first_new / correction / (jnp.sqrt(second_new / correction) + 1e-08)
    return (weight - rate * (step + decay * weight), first_new, second_new)


def tn(rows, grads):
    out = lax.dot_general(rows, grads, (((0,), (0,)), ((), ())), preferred_element_type=FULL)
    return layout.with_layout_constraint(out.astype(LOW), layout.Layout((0, 1)))


def per_device(
    layer_input, layer_cotangent,
    attend_weight, attend_first, attend_second,
    output_weight, output_first, output_second,
    gated_weight, gated_first, gated_second,
    down_weight, down_first, down_second,
    norm_gains, gains_first, gains_second,
):
    rows = layer_input.shape[0]
    wide = lax.axis_size("wide")
    block = D // wide
    me = lax.axis_index("wide")
    narrow = lax.axis_index("narrow")
    core = narrow % 2
    cols = attend_weight.shape[2]

    bits = wide_bits()
    near = bits[:-1]
    half = D // 2
    hid = down_weight.shape[0]

    bits = wide_bits()
    near = bits[:-1]
    half = D // 2
    hid = down_weight.shape[0]
    pair = 2 * cols

    attend_low = attend_weight.astype(LOW)
    att = jnp.concatenate(
        [attend_low[0], attend_low[1], attend_low[2], output_weight.T.astype(LOW)], axis=1
    )
    cut = hid // 2
    down_t = down_weight.T
    ffn = jnp.concatenate([gated_weight[0], gated_weight[1], down_t[:, :cut]], axis=1).astype(LOW)
    down = down_t[:, cut:].astype(LOW)

    order = me ^ jnp.array(block_masks(), jnp.int32)
    source = (order[:, None] * block + jnp.arange(block)[None, :]).reshape(1, D)
    mover = (lax.broadcasted_iota(jnp.int32, (D, D), 0) == source).astype(LOW)
    mover = lax.optimization_barrier(mover)

    def both_halves(mine, theirs):
        first = core == 0
        return jnp.concatenate(
            [jnp.where(first, mine, theirs), jnp.where(first, theirs, mine)], axis=0
        )

    def own_rows(value):
        return lax.dynamic_slice_in_dim(value, core * rows, rows, axis=0)

    first = widen(att, near[:1])
    gains = widen(after(norm_gains, att).astype(LOW).astype(FULL)[None], bits[:1])
    first, down, gains = lax.optimization_barrier((first, down, gains))
    gains = widen(gains, bits[1:-1])
    att = widen(first, near[1:])
    down_y = swap(down, "wide", 1)
    down_x = swap(down, "narrow", 2)
    both = jnp.concatenate([layer_input, layer_cotangent], axis=0)
    moved = jnp.dot(both, mover, preferred_element_type=FULL).astype(LOW)
    place = jnp.arange(32, dtype=FULL)
    place = jnp.concatenate([32.0 * place, place])
    att, down_y, down_x, gains, moved, place = lax.optimization_barrier(
        (att, down_y, down_x, gains, moved, place)
    )
    att_y = swap(att, "wide", 1)
    att_x = swap(att, "narrow", 2)
    ffn = widen(after(ffn, att), near[:1])
    inputs = both_halves(moved[:rows], swap(moved[:rows], "narrow", 1))
    inputs, gains = lax.optimization_barrier((inputs, gains))
    gains = widen(gains, bits[-1:])
    moved_up = moved[rows:]
    cosine, sine = rope_tables(place)
    inputs, att, att_y, att_x, ffn, gains, cosine, sine = lax.optimization_barrier(
        (inputs, att, att_y, att_x, ffn, gains, cosine, sine)
    )
    gains = gains.transpose(1, 0, 2).reshape(2, 1, D)
    down_corner = swap(down_y, "narrow", 2)
    qk_corner = swap(att_y[:, :pair], "narrow", 2)
    vo_corner = swap(att_x[:, pair:], "wide", 1)
    ffn = widen(ffn, near[1:])
    qk = [[(att, pair, 0), (att_y, pair, 0)], [(att_x, pair, 0), qk_corner]]
    vo = [[(att, pair, 1), (att_y, pair, 1)], [(att_x, pair, 1), vo_corner]]
    saved = [attend_forward(inputs, qk[0], vo[0], cosine, sine)]
    second_in, qk_corner, vo_corner, ffn, down_corner = lax.optimization_barrier(
        (after(inputs, saved[0][3]), qk_corner, vo_corner, ffn, down_corner)
    )
    other_up = swap(after(moved_up, second_in), "narrow", 1)
    down = jnp.stack([down, down_y, down_x, down_corner])[:, None]
    for bit in near[:1]:
        down = jnp.concatenate([down, swap(down, "wide", bit)], axis=1)
    qk[1][1], vo[1][1] = qk_corner, vo_corner
    ffn_y = swap(ffn, "wide", 1)
    ffn_x = swap(ffn, "narrow", 2)
    saved.append(attend_forward(second_in, qk[1], vo[1], cosine, sine))
    context = [s[3] for s in saved]
    att_out = [att, att_y, att_x, vo_corner]
    held = [pltpu.VMEM((2, D, cols), LOW)]
    low_d, full_d = (D, LOW, False), (D, FULL, True)
    (attn_part,) = by_rows(
        project_kernel, "project", context, att_out, [low_d], scratch=held
    )
    ffn_y, ffn_x, attn_part, down = lax.optimization_barrier((ffn_y, ffn_x, attn_part, down))
    attn_other = swap(attn_part, "narrow", 1)
    down_far = [swap(down, "wide", bit) for bit in near[1:2]]
    gate_corner = swap(ffn_y[:, :hid], "narrow", 2)
    up_corner = swap(ffn_x[:, hid:], "wide", 1)
    flow = [(hid, LOW, True), (hid, LOW, True), (hid, LOW, False)]
    normed_one, inv_one, hidden_low, gate1, up1, act1, gu_own = by_rows(
        enter_kernel, "enter", [pinned(inputs), attn_part, attn_other],
        [gains, (ffn, 2 * hid, 0), (ffn_y, 2 * hid, 0)],
        [(D, LOW, True), (1, FULL, True), low_d] + flow, kept=[(D, 2 * hid)],
    )
    hidden_low, down, down_far = lax.optimization_barrier((hidden_low, down, down_far))
    moved_up, other_up, hidden_low = lax.optimization_barrier((moved_up, other_up, hidden_low))
    upstream = both_halves(moved_up, other_up)
    down = jnp.concatenate([down, *down_far], axis=1)
    for bit in near[2:]:
        down = jnp.concatenate([down, swap(down, "wide", bit)], axis=1)
    down = down.reshape(2, D, hid - cut)
    last_cols = 2 * hid // cut
    gate2, up2, act2, ffn_part, gu_other, down_all = by_rows(
        rest_kernel, "rest", [after(hidden_low, upstream), act1],
        [
            (ffn_x, 2 * hid, 0), gate_corner, (up_corner, hid, 0),
            (ffn, cut, last_cols), (ffn_y, cut, last_cols), (ffn_x, cut, last_cols),
            (up_corner, cut, hid // cut), down,
        ],
        flow + [low_d], kept=[(D, 2 * hid), (2, D, hid)], loose=(1, 2, 6),
    )
    ffn_other = swap(ffn_part, "narrow", 1)

    layer_output, grad_two_low, gain_two_grad = by_rows(
        turn_kernel, "turn", [pinned(normed_one), ffn_part, ffn_other, pinned(upstream)],
        [gains], [(D, LOW, True), low_d], sums=1,
    )
    down_send = tn(grad_two_low, act2)
    down_x = swap(down_send, "narrow", 2)
    wide_flow = (2 * hid, LOW, False)
    saves = [pinned(r) for r in (gate1, up1, gate2, up2)]
    gg, ug = by_rows(
        back_kernel, "back",
        [after(grad_two_low, down_send), *saves], [down_all], [wide_flow, wide_flow],
    )
    gate_send = tn(hidden_low[:, half:], gg)
    up_send = tn(hidden_low[:, half:], ug)
    gate_y = swap(gate_send, "wide", 1)
    up_y = swap(up_send, "wide", 1)
    mid_part = by_rows(
        mid_kernel, "mid", [after(gg, gate_send, up_send), ug], [gu_own, gu_other], []
    )
    mid_other = [swap(part, "narrow", 1) for part in mid_part]
    down_own = tn(grad_two_low, act1)
    gate_own = tn(hidden_low[:, :half], gg)
    up_own = tn(hidden_low[:, :half], ug)
    mid_part, mid_other, down_own, gate_own, up_own, down_x = lax.optimization_barrier(
        (mid_part, mid_other, down_own, gate_own, up_own, down_x)
    )
    grad_one_low, dctx1, dctx2, gain_one_grad = by_rows(
        leave_kernel, "leave",
        [grad_two_low, tuple(mid_part), tuple(mid_other), pinned(normed_one), pinned(inv_one)],
        [gains, *att_out], [low_d, (cols, LOW, True), (cols, LOW, True)],
        sums=1, scratch=held + [pltpu.VMEM((QB, D), FULL)],
    )

    q, k, v, _, lse = saved[1]
    dqk2, dv2 = attend_backward(q, k, v, lse, dctx2, cosine, sine)
    down_x, gate_y, dqk2, dv2 = lax.optimization_barrier((down_x, gate_y, dqk2, dv2))
    down_sum, gate_sum = add(down_own, down_x), add(gate_own, gate_y)
    down_y = swap(down_sum[half:].astype(LOW), "wide", 1)
    gate_far = gate_sum[:, hid:].astype(LOW)
    gate_x = swap(gate_far, "narrow", 2)
    qk_near2, qk_send2, vo_send = heads_grad(inputs, grad_one_low, after(dqk2, gate_far), dv2, context[1])
    vo_x = swap(vo_send, "narrow", 2)
    qk_y2 = swap(qk_send2, "wide", 1)
    back = near[::-1]
    q, k, v, _, lse = saved[0]
    dqk1, dv1 = attend_backward(q, k, v, lse, after(dctx1, vo_send, qk_send2), cosine, sine)
    dqk1, dv1, up_y, down_y, qk_y2, gate_x = lax.optimization_barrier(
        (dqk1, dv1, up_y, down_y, qk_y2, gate_x)
    )
    early = narrow_down(add(down_sum[:half], down_y), back[:1])
    up_sum = add(up_own, up_y)
    up_x = swap(up_sum[:, hid:].astype(LOW), "narrow", 2)
    qk_near1, qk_send1, vo_own = heads_grad(inputs, grad_one_low, dqk1, dv1, context[0])
    qk_y1 = swap(qk_send1, "wide", 1)
    qk_far = add(qk_near2, qk_y2).astype(LOW)
    qk_x = swap(qk_far, "narrow", 2)
    vo_sum = add(vo_own, vo_x)
    vo_far = vo_sum[half:].astype(LOW)
    vo_y = swap(vo_far, "wide", 1)
    late = jnp.concatenate([add(gate_sum[:, :hid], gate_x), add(up_sum[:, :hid], up_x)], axis=1)
    early_red = narrow_down(early, back[1:])
    dqk1, vo_sum, late = lax.optimization_barrier((dqk1, vo_sum, late))
    part_full, part_low = by_rows(
        input_kernel, "inputs", [dqk1, dv1, dqk2, dv2],
        [att, att_y, att_x, qk_corner, vo_corner], [full_d, low_d], step=128,
        scratch=[pltpu.VMEM((2, D, 3 * cols), LOW)],
    )
    late = narrow_down(late, back[:1])
    theirs = lax.dynamic_slice_in_dim(part_low, (1 - core) * rows, rows, axis=0)
    theirs = swap(theirs, "narrow", 1)
    qk_sum = add(qk_near1, qk_y1)
    last = jnp.concatenate([add(qk_sum, qk_x), add(vo_sum[:half], vo_y)], axis=1)
    gain_grads = jnp.concatenate([gain_one_grad, gain_two_grad], axis=0)
    gain_low = gain_grads.astype(LOW)
    gain_rest = (gain_grads - gain_low.astype(FULL)).astype(LOW)
    gain_grads = nt(jnp.concatenate([gain_low, gain_rest], axis=0), mover)
    gain_grads = gain_grads[:2] + gain_grads[2:]
    last, early_red, late, gain_grads, part_full = lax.optimization_barrier(
        (last, early_red, late, gain_grads, part_full)
    )
    last = narrow_down(last, back[:1])
    late_red = narrow_down(late, back[1:])
    early_square = jnp.sum(early_red * early_red) + jnp.sum(late_red * late_red)
    last = narrow_down(last, back[1:-1])
    att_red, square = last_sum(
        last[:block], swap(last[block:].astype(LOW), "wide", back[-1]),
        jnp.full((1, 128), early_square, FULL),
    )

    square = square + swap(square, "narrow", 1)
    message = jnp.concatenate([gain_grads.reshape(1, 2 * D), square], axis=1)
    message = message + swap(message, "narrow", 2)
    which, done = jnp.full((1,), core, jnp.int32), ()
    theirs = after(theirs, message)
    for part in range(rows // QB):
        done = finish(part, done, which, grad_one_low, part_full, layer_output, theirs, mover)
    input_grad, layer_output = done
    for bit in bits[::-1][:-1]:
        message = message + swap(message, "wide", bit)
    received = swap(message, "wide", bits[0])
    all_tokens = rows * wide * lax.axis_size("narrow")
    clip = 0.02 * math.sqrt(all_tokens * (4 * D * D + 3 * D * FF + 2 * D))
    grad_norm, (new_attend, new_output, new_gated, new_down, new_gains) = adam(
        jnp.full((1,), me, jnp.int32),
        clip,
        (
            (D ** (-0.5), WEIGHT_DECAY),
            (max(D // 64, 1) ** (-0.5), WEIGHT_DECAY),
            (D ** (-0.5), WEIGHT_DECAY),
            (FF ** (-0.5), WEIGHT_DECAY),
            (0.4, 0.0),
        ),
        (message, received, att_red, late_red, early_red),
        (
            (attend_weight, attend_first, attend_second),
            (output_weight, output_first, output_second),
            (gated_weight, gated_first, gated_second),
            (down_weight.T, down_first.T, down_second.T),
            (norm_gains, gains_first, gains_second),
        ),
    )
    new_down = [value.T for value in new_down]
    return (
        layer_output, input_grad, grad_norm,
        *new_attend, *new_output, *new_gated, *new_down, *new_gains,
    )


def solution(mesh):
    rows = P(("wide", "narrow"), None)
    stacked = P(None, "wide", "narrow")
    turned = P("narrow", "wide")
    gains = P(None, "wide")
    params = (stacked,) * 3 + (turned,) * 3 + (stacked,) * 3 + (turned,) * 3 + (gains,) * 3
    return jax.shard_map(
        per_device,
        mesh=mesh,
        in_specs=(rows, rows) + params,
        out_specs=(rows, rows, P()) + params,
        check_vma=False,
    )
```

```python
import functools
import math

import jax
import jax.numpy as jnp
from jax import lax
from jax.experimental import layout
from jax.experimental import pallas as pl
from jax.experimental.pallas import tpu as pltpu
from jax.sharding import PartitionSpec as P

D = 768
HD = 64
FF = 2048
L = 1024
ADAM_STEP = 5

EPSILON = 1e-05
WEIGHT_DECAY = 0.1
AVERAGING = 0.5

LOW = jnp.bfloat16
FULL = jnp.float32
QB = 256
MASKED = -1e30
SMALL = pl.CostEstimate(flops=10**6, bytes_accessed=10**4, transcendentals=0)


def swap(value, axis, bit):
    size = lax.axis_size(axis)
    return lax.ppermute(value, axis, [(i, i ^ bit) for i in range(size)])


def wide_bits():
    top = lax.axis_size("wide").bit_length() - 1
    return [1 << b for b in range(top - 1, -1, -1)]


def block_masks():
    masks = [0]
    for bit in wide_bits():
        masks = masks + [m ^ bit for m in masks]
    return masks


def after(value, *done):
    return lax.optimization_barrier((value, done))[0]


def widen(held, bits):
    for bit in bits:
        held = jnp.concatenate([held, swap(held, "wide", bit)], axis=0)
    return held


def add(kept, received):
    return kept.astype(FULL) + received.astype(FULL)


def narrow_down(held, bits):
    for bit in bits:
        half = held.shape[0] // 2
        held = add(held[:half], swap(held[half:].astype(LOW), "wide", bit))
    return held


def turn(value, cosine, sine, sign):
    width = value.shape[1]
    lane = lax.broadcasted_iota(jnp.int32, value.shape, 1) % HD
    other = jnp.where(
        lane < HD // 2,
        pltpu.roll(value, width - HD // 2, 1),
        pltpu.roll(value, HD // 2, 1),
    )
    reps = width // 128
    return value * jnp.concatenate([cosine] * reps, axis=1) + sign * other * jnp.concatenate(
        [sine] * reps, axis=1
    )


def nn(a, b):
    return lax.dot_general(a, b, (((1,), (0,)), ((), ())), preferred_element_type=FULL)


def nt(a, b):
    return lax.dot_general(a, b, (((1,), (1,)), ((), ())), preferred_element_type=FULL)


def diagonal(scores):
    key = lax.broadcasted_iota(jnp.int32, scores.shape, 0)
    query = lax.broadcasted_iota(jnp.int32, scores.shape, 1)
    return jnp.where(key <= query, scores, MASKED)


def flip(value):
    return value.astype(FULL).T


def attend_kernel(
    rows_ref, qka_ref, qkb_ref, voa_ref, vob_ref, cos_ref, sin_ref,
    q_ref, k_ref, v_ref, ctx_ref, lse_ref, hold,
):
    heads = q_ref.shape[0]
    width = heads * HD
    half = qka_ref.shape[0]

    def project(i, carry):
        rows = pl.ds(pl.multiple_of(i * QB, QB), QB)
        first, second = rows_ref[rows, :half], rows_ref[rows, half:]
        pair = nn(first, qka_ref[...]) + nn(second, qkb_ref[...])
        pair = turn(pair, cos_ref[rows, :], sin_ref[rows, :], 1.0)
        value = nn(first, voa_ref[:, :width]) + nn(second, vob_ref[:, :width])
        for h in range(heads):
            q_ref[h, rows, :] = (pair[:, h * HD : (h + 1) * HD] * (HD**-0.5)).astype(LOW)
            k_ref[h, rows, :] = pair[:, width + h * HD : width + (h + 1) * HD].astype(LOW)
            v_ref[h, rows, :] = value[:, h * HD : (h + 1) * HD].astype(LOW)
        return carry

    lax.fori_loop(0, L // QB, project, 0)

    def head(h, carry):
        turned = flip(v_ref[h]).astype(LOW)
        for i in range(L // QB):
            lo, hi = i * QB, (i + 1) * QB
            query = q_ref[h, lo:hi, :]
            diag = diagonal(nt(k_ref[h, lo:hi, :], query))
            peak = jnp.max(diag, axis=0, keepdims=True)
            if i:
                body = nt(k_ref[h, :lo, :], query)
                peak = jnp.maximum(peak, jnp.max(body, axis=0, keepdims=True))
            weight = jnp.exp(diag - peak)
            total = jnp.sum(weight, axis=0, keepdims=True)
            out = nn(turned[:, lo:hi], weight.astype(LOW))
            if i:
                weight = jnp.exp(body - peak)
                total = total + jnp.sum(weight, axis=0, keepdims=True)
                out = out + nn(turned[:, :lo], weight.astype(LOW))
            lse_ref[h, :, lo:hi] = peak + jnp.log(total)
            hold[h, lo:hi, :] = (out / total).T.astype(LOW)
        return carry

    lax.fori_loop(0, heads, head, 0)
    for h in range(heads):
        ctx_ref[:, h * HD : (h + 1) * HD] = hold[h]


def pinned(array):
    return pltpu.with_memory_space_constraint(array, pltpu.HBM)


def whole(array):
    zero = (0,) * len(array.shape)
    return pl.BlockSpec(array.shape, lambda *_: zero)


def by_head(shape):
    return pl.BlockSpec(shape, lambda h: (h, 0, 0))


def columns(piece, mode=None):
    array, width, j = piece if isinstance(piece, tuple) else (piece, piece.shape[-1], 0)
    lead = (0,) * (array.ndim - 1)
    shape = array.shape[:-1] + (width,)
    return array, pl.BlockSpec(shape, lambda *_: lead + (j,), pipeline_mode=mode)


def width_of(piece):
    return piece[1] if isinstance(piece, tuple) else piece.shape[1]


def attend_forward(rows, qk, vo, cosine, sine):
    heads = width_of(qk[0]) // 2 // HD
    headed = pltpu.HBM((heads, L, HD), LOW)
    outs = (
        headed, headed, headed,
        jax.ShapeDtypeStruct((L, heads * HD), LOW),
        pltpu.HBM((heads, 1, L), FULL),
    )
    args, specs = zip(*[columns(p) for p in (rows, *qk, *vo, cosine, sine)])
    return pl.pallas_call(
        attend_kernel,
        grid=(1,),
        in_specs=list(specs),
        out_specs=[whole(o) for o in outs],
        out_shape=outs,
        scratch_shapes=[pltpu.VMEM((heads, L, HD), LOW)],
        compiler_params=pltpu.CompilerParams(vmem_limit_bytes=24 << 20),
        cost_estimate=SMALL,
        name="attend_forward",
    )(*args)


def attend_back_kernel(
    q_ref, k_ref, v_ref, lse_ref, dctx_ref, cos_ref, sin_ref,
    dqk_ref, dv_ref, dctx, dqk, dk_sum, dv_sum,
):
    heads = dctx.shape[0]
    h = pl.program_id(0)

    @pl.when(h == 0)
    def _():
        for j in range(heads):
            dctx[j] = dctx_ref[:, j * HD : (j + 1) * HD]

    turned = flip(k_ref[0]).astype(LOW)
    for i in range(L // QB):
        lo, hi = i * QB, (i + 1) * QB
        query, back = q_ref[0, lo:hi, :], dctx[h, lo:hi, :]
        lse = lse_ref[0, :, lo:hi]
        prob = jnp.exp(diagonal(nt(k_ref[0, lo:hi, :], query)) - lse)
        grad = nt(v_ref[0, lo:hi, :], back)
        inner = jnp.sum(prob * grad, axis=0, keepdims=True)
        if i:
            prob_body = jnp.exp(nt(k_ref[0, :lo, :], query) - lse)
            grad_body = nt(v_ref[0, :lo, :], back)
            inner = inner + jnp.sum(prob_body * grad_body, axis=0, keepdims=True)
        score = (prob * (grad - inner)).astype(LOW)
        dv_sum[h, lo:hi, :] = nn(prob.astype(LOW), back)
        dk_sum[h, lo:hi, :] = nn(score, query)
        dquery = nn(turned[:, lo:hi], score)
        if i:
            score = (prob_body * (grad_body - inner)).astype(LOW)
            dv_sum[h, :lo, :] += nn(prob_body.astype(LOW), back)
            dk_sum[h, :lo, :] += nn(score, query)
            dquery = dquery + nn(turned[:, :lo], score)
        dqk[h, lo:hi, :] = (dquery * (HD**-0.5)).T

    def finish(i, carry):
        rows = pl.ds(pl.multiple_of(i * QB, QB), QB)
        pair = jnp.concatenate(
            [dqk[j, rows, :] for j in range(heads)] + [dk_sum[j, rows, :] for j in range(heads)],
            axis=1,
        )
        dqk_ref[rows, :] = turn(pair, cos_ref[rows, :], sin_ref[rows, :], -1.0).astype(LOW)
        dv_ref[rows, :] = jnp.concatenate(
            [dv_sum[j, rows, :] for j in range(heads)], axis=1
        ).astype(LOW)
        return carry

    @pl.when(h == heads - 1)
    def _():
        lax.fori_loop(0, L // QB, finish, 0)


def attend_backward(q, k, v, lse, dctx, cosine, sine):
    heads = q.shape[0]
    outs = (
        jax.ShapeDtypeStruct((L, 2 * heads * HD), LOW),
        jax.ShapeDtypeStruct((L, heads * HD), LOW),
    )
    return pl.pallas_call(
        attend_back_kernel,
        grid=(heads,),
        in_specs=[by_head((1, L, HD))] * 3
        + [by_head((1, 1, L)), whole(dctx), whole(cosine), whole(sine)],
        out_specs=[whole(o) for o in outs],
        out_shape=outs,
        scratch_shapes=[pltpu.VMEM((heads, L, HD), LOW)] + [pltpu.VMEM((heads, L, HD), FULL)] * 3,
        compiler_params=pltpu.CompilerParams(vmem_limit_bytes=24 << 20),
        cost_estimate=SMALL,
        name="attend_backward",
    )(pinned(q), pinned(k), pinned(v), pinned(lse), pinned(dctx), pinned(cosine), pinned(sine))


def held_once(array):
    zero = (0,) * array.ndim
    return pl.BlockSpec(array.shape, lambda *_: zero, pipeline_mode=pl.Buffered(1))


def in_top():
    return pl.program_id(0) < pl.num_programs(0) // 2


def halves(step, width):
    steps = L // step // 2
    return [
        pl.BlockSpec((step, width), lambda i: (jnp.minimum(i, steps - 1), 0)),
        pl.BlockSpec((step, width), lambda i: (jnp.maximum(i - steps, 0), 0)),
    ]


def by_rows(kernel, name, row_args, fixed, outs, sums=0, kept=(), scratch=(), loose=(), step=QB):
    specs, flat = [], []
    for r in row_args:
        if isinstance(r, tuple):
            specs += halves(step, r[0].shape[1])
            flat += r
        else:
            specs.append(pl.BlockSpec((step, r.shape[1]), lambda i: (i, 0)))
            flat.append(r)
    held, held_specs = zip(*[columns(f, pl.Buffered(1)) for f in fixed])
    shapes = [
        (pltpu.HBM if away else jax.ShapeDtypeStruct)((L, w), t) for w, t, away in outs
    ]
    out_specs = [pl.BlockSpec((step, w), lambda i: (i, 0)) for w, _, _ in outs]
    if not outs:
        shapes = [jax.ShapeDtypeStruct((L // 2, D), LOW)] * 2
        out_specs = halves(step, D)
    rows_out = len(shapes)
    shapes += [jax.ShapeDtypeStruct((1, D), FULL)] * sums
    shapes += [pltpu.HBM(shape, LOW) for shape in kept]
    out_specs += [whole(o) for o in shapes[rows_out:]]
    return pl.pallas_call(
        kernel,
        grid=(L // step,),
        in_specs=specs + list(held_specs),
        out_specs=out_specs,
        out_shape=shapes,
        scratch_shapes=list(scratch),
        compiler_params=pltpu.CompilerParams(vmem_limit_bytes=32 << 20),
        cost_estimate=SMALL,
        name=name,
    )(*flat, *[f if f.dtype == FULL or i in loose else pinned(f) for i, f in enumerate(held)])


def rms_scale(residual):
    return lax.rsqrt(jnp.mean(residual * residual, axis=1, keepdims=True) + EPSILON)


def norm_back(scaled, normed, inv):
    return inv * (scaled - normed * jnp.mean(scaled * normed, axis=1, keepdims=True))


def column_sum(sum_ref, value):
    @pl.when(pl.program_id(0) == 0)
    def _():
        sum_ref[...] = jnp.zeros_like(sum_ref)

    sum_ref[...] += jnp.sum(value, axis=0, keepdims=True)


def heads_out(held_ref, refs):
    att_ref, y_ref, x_ref, corner_ref = refs
    half, width = att_ref.shape[0], held_ref.shape[2]

    @pl.when(pl.program_id(0) == 0)
    def _():
        held_ref[0, :half] = att_ref[:, 3 * width :]
        held_ref[0, half:] = y_ref[:, 3 * width :]
        held_ref[1, :half] = x_ref[:, 3 * width :]
        held_ref[1, half:] = corner_ref[:, width:]


def project_kernel(one_ref, two_ref, att_ref, y_ref, x_ref, corner_ref, out_ref, held_ref):
    heads_out(held_ref, (att_ref, y_ref, x_ref, corner_ref))
    out_ref[...] = (nt(one_ref[...], held_ref[0]) + nt(two_ref[...], held_ref[1])).astype(LOW)


def gate_up(hidden, weights_ref, gate_ref, up_ref, act_ref):
    hid = gate_ref.shape[1]
    gate = nn(hidden, weights_ref[:, :hid])
    up = nn(hidden, weights_ref[:, hid:])
    gate_ref[...] = gate.astype(LOW)
    up_ref[...] = up.astype(LOW)
    act_ref[...] = (gate * jax.nn.sigmoid(gate) * up).astype(LOW)


def enter_kernel(
    rows_ref, mine_ref, theirs_ref, gain_ref, own_ref, y_ref,
    normed_ref, inv_ref, hidden_ref, gate_ref, up_ref, act_ref, weights_ref,
):
    half = own_ref.shape[0]

    @pl.when(pl.program_id(0) == 0)
    def _():
        weights_ref[:half] = own_ref[...]
        weights_ref[half:] = y_ref[...]

    residual = rows_ref[...].astype(FULL) + add(mine_ref[...], theirs_ref[...])
    inv = rms_scale(residual)
    normed = residual * inv
    hidden = (normed * gain_ref[0]).astype(LOW)
    normed_ref[...] = normed.astype(LOW)
    inv_ref[...] = inv
    hidden_ref[...] = hidden
    gate_up(hidden, weights_ref, gate_ref, up_ref, act_ref)


def rest_kernel(
    hidden_ref, act1_ref, x_ref, gate_corner_ref, up_corner_ref,
    low_own_ref, low_y_ref, low_x_ref, low_corner_ref, high_ref,
    gate_ref, up_ref, act_ref, out_ref, weights_ref, down_ref,
):
    half, hid = x_ref.shape[0], gate_ref.shape[1]
    cut = high_ref.shape[2]

    @pl.when(pl.program_id(0) == 0)
    def _():
        weights_ref[:half] = x_ref[...]
        weights_ref[half:, :hid] = gate_corner_ref[...]
        weights_ref[half:, hid:] = up_corner_ref[...]
        down_ref[0, :half, :cut] = low_own_ref[...]
        down_ref[0, half:, :cut] = low_y_ref[...]
        down_ref[1, :half, :cut] = low_x_ref[...]
        down_ref[1, half:, :cut] = low_corner_ref[...]
        down_ref[:, :, cut:] = high_ref[...]

    gate_up(hidden_ref[...], weights_ref, gate_ref, up_ref, act_ref)
    out_ref[...] = (nt(act1_ref[...], down_ref[0]) + nt(act_ref[...], down_ref[1])).astype(LOW)


def turn_kernel(
    normed_ref, mine_ref, theirs_ref, up_rows_ref, gains_ref,
    out_ref, low_ref, sum_ref,
):
    residual = normed_ref[...].astype(FULL) * gains_ref[0] + add(mine_ref[...], theirs_ref[...])
    inv = rms_scale(residual)
    normed = residual * inv
    gain = gains_ref[1]
    out_ref[...] = (normed * gain).astype(LOW)
    upstream = up_rows_ref[...].astype(FULL)
    column_sum(sum_ref, upstream * normed)
    low_ref[...] = norm_back(upstream * gain, normed, inv).astype(LOW)


def back_kernel(low_ref, gate1_ref, up1_ref, gate2_ref, up2_ref, down_ref, gg_ref, ug_ref):
    hid = gate1_ref.shape[1]
    low = low_ref[...]
    for x, gate_ref, up_ref in ((0, gate1_ref, up1_ref), (1, gate2_ref, up2_ref)):
        act_grad = nn(low, down_ref[x])
        gate, up = gate_ref[...].astype(FULL), up_ref[...].astype(FULL)
        sig = jax.nn.sigmoid(gate)
        gg = act_grad * up * (sig * (1.0 + gate * (1.0 - sig)))
        gg_ref[:, x * hid : (x + 1) * hid] = gg.astype(LOW)
        ug_ref[:, x * hid : (x + 1) * hid] = (act_grad * (gate * sig)).astype(LOW)


def mid_kernel(gg_ref, ug_ref, own_ref, other_ref, top_ref, bottom_ref):
    hid = gg_ref.shape[1] // 2
    total = 0.0
    for x, weights_ref in enumerate((own_ref, other_ref)):
        cols = slice(x * hid, (x + 1) * hid)
        total = total + nt(gg_ref[:, cols], weights_ref[:, :hid])
        total = total + nt(ug_ref[:, cols], weights_ref[:, hid:])
    low = total.astype(LOW)

    @pl.when(in_top())
    def _():
        top_ref[...] = low

    @pl.when(jnp.logical_not(in_top()))
    def _():
        bottom_ref[...] = low


def leave_kernel(
    grad_two_ref, mine_top_ref, mine_bottom_ref, theirs_top_ref, theirs_bottom_ref,
    normed_ref, inv_ref, gains_ref, att_ref, y_ref, x_ref, corner_ref,
    low_ref, ctx1_ref, ctx2_ref, sum_ref, held_ref, mid_ref,
):
    heads_out(held_ref, (att_ref, y_ref, x_ref, corner_ref))

    @pl.when(in_top())
    def _():
        mid_ref[...] = add(mine_top_ref[...], theirs_top_ref[...])

    @pl.when(jnp.logical_not(in_top()))
    def _():
        mid_ref[...] = add(mine_bottom_ref[...], theirs_bottom_ref[...])

    hidden_grad = grad_two_ref[...].astype(FULL) + mid_ref[...]
    normed = normed_ref[...].astype(FULL)
    column_sum(sum_ref, hidden_grad * normed)
    low = norm_back(hidden_grad * gains_ref[0], normed, inv_ref[...]).astype(LOW)
    low_ref[...] = low
    ctx1_ref[...] = nn(low, held_ref[0]).astype(LOW)
    ctx2_ref[...] = nn(low, held_ref[1]).astype(LOW)


def input_kernel(
    qk1_ref, v1_ref, qk2_ref, v2_ref, att_ref, y_ref, x_ref, qk_corner_ref, vo_corner_ref,
    full_ref, low_ref, held_ref,
):
    half, width = att_ref.shape[0], v1_ref.shape[1]
    pair = 2 * width

    @pl.when(pl.program_id(0) == 0)
    def _():
        held_ref[0, :half] = att_ref[:, : pair + width]
        held_ref[0, half:] = y_ref[:, : pair + width]
        held_ref[1, :half] = x_ref[:, : pair + width]
        held_ref[1, half:, :pair] = qk_corner_ref[...]
        held_ref[1, half:, pair:] = vo_corner_ref[:, :width]

    total = 0.0
    for x, qk_ref, v_ref in ((0, qk1_ref, v1_ref), (1, qk2_ref, v2_ref)):
        total = total + nt(qk_ref[...], held_ref[x, :, :pair])
        total = total + nt(v_ref[...], held_ref[x, :, pair:])
    full_ref[...] = total
    low_ref[...] = total.astype(LOW)


def heads_grad_kernel(
    rows_ref, grad_ref, qk_ref, v_ref, ctx_ref, near_ref, far_ref, vo_ref
):
    width = v_ref.shape[1]
    rows = flip(rows_ref[...]).astype(LOW)
    qk = nn(rows, qk_ref[...]).astype(LOW)
    step, half = qk.shape[0], near_ref.shape[0]
    for i in range(D // step):

        @pl.when(pl.program_id(0) == i)
        def _(start=i * step):
            near = max(min(half - start, step), 0)
            if near:
                near_ref[start : start + near] = qk[:near]
            if near < step:
                far_ref[start + near - half : start + step - half] = qk[near:]

    vo_ref[:, :width] = nn(rows, v_ref[...]).astype(LOW)
    vo_ref[:, width:] = nn(flip(grad_ref[...]).astype(LOW), ctx_ref[...]).astype(LOW)


def heads_grad(rows, grad, dqk, dv, context):
    half, pair = D // 2, dqk.shape[1]
    split = pl.BlockSpec((L, 256), lambda i: (0, i))
    held = pl.BlockSpec((half, pair), lambda i: (0, 0))
    return pl.pallas_call(
        heads_grad_kernel,
        grid=(D // 256,),
        in_specs=[split, split] + [held_once(g) for g in (dqk, dv, context)],
        out_specs=[held, held, pl.BlockSpec((256, pair), lambda i: (i, 0))],
        out_shape=[pltpu.HBM((half, pair), LOW)] * 2 + [pltpu.HBM((D, pair), LOW)],
        compiler_params=pltpu.CompilerParams(vmem_limit_bytes=24 << 20),
        cost_estimate=SMALL,
        name="heads_grad",
    )(rows, grad, dqk, dv, context)


def in_order(value, mover):
    total = 0.0
    for _ in range(2):
        part = value.astype(LOW)
        total = total + nt(part, mover)
        value = value - part.astype(FULL)
    return total


def finish_kernel(
    core_ref, one_ref, full_ref, out_ref, theirs_ref, mover_ref, grad_ref, low_ref
):
    mover = mover_ref[...]
    grad = one_ref[...].astype(FULL) + full_ref[...] + theirs_ref[...].astype(FULL)
    grad_ref[...] = in_order(grad, mover)
    low_ref[...] = nt(out_ref[...], mover).astype(LOW)


def finish(core, grad_one, part_full, layer_output, theirs, mover):
    rows = theirs.shape[0]
    steps = rows // QB
    mine = pl.BlockSpec((QB, D), lambda i, c: (c[0] * steps + i, 0))
    plain = pl.BlockSpec((QB, D), lambda i, c: (i, 0))
    return pl.pallas_call(
        finish_kernel,
        grid_spec=pltpu.PrefetchScalarGridSpec(
            num_scalar_prefetch=1,
            grid=(steps,),
            in_specs=[mine, mine, mine, plain, held_once(mover)],
            out_specs=[plain, plain],
        ),
        out_shape=[
            jax.ShapeDtypeStruct((rows, D), FULL), jax.ShapeDtypeStruct((rows, D), LOW)
        ],
        cost_estimate=SMALL,
        name="finish",
    )(core, grad_one, pinned(part_full), pinned(layer_output), theirs, mover)


def last_kernel(kept_ref, received_ref, square_ref, sum_ref, total_ref):
    value = kept_ref[...] + received_ref[...].astype(FULL)
    sum_ref[...] = value
    total = jnp.sum(jnp.sum(value * value, axis=0, keepdims=True), axis=1, keepdims=True)
    total_ref[...] = square_ref[...] + total


def last_sum(kept, received, square):
    vmem = pl.BlockSpec(memory_space=pltpu.VMEM)
    return pl.pallas_call(
        last_kernel,
        in_specs=[vmem] * 3,
        out_specs=[vmem] * 2,
        out_shape=[jax.ShapeDtypeStruct(kept.shape, FULL), jax.ShapeDtypeStruct((1, 128), FULL)],
        name="last_sum",
    )(kept, received, square)


def adam_kernel(clip, rates, *refs):
    me = refs[0][0]
    message = refs[1][...] + refs[2][...]
    att_ref, ffn_ref, down_ref = refs[3:6]
    ins, norm_ref, outs = refs[6:21], refs[21], refs[22:]
    block = ins[12].shape[1]
    gain_sum = message[:, : 2 * D]
    total = message[:, 2 * D : 2 * D + 1] + jnp.sum(gain_sum * gain_sum, axis=1, keepdims=True)
    norm = jnp.sqrt(total)
    norm_ref[...] = norm
    ratio = clip / jnp.maximum(norm, clip)

    def update(p, at, grad):
        rate, decay = rates[p]
        old = [ref[at] for ref in ins[3 * p : 3 * p + 3]]
        for ref, value in zip(
            outs[3 * p : 3 * p + 3], adam_update(*old, grad, ratio, rate, decay)
        ):
            ref[at] = value

    width, hid = att_ref.shape[1] // 4, ffn_ref.shape[1] // 2
    step = 16 if block % 16 == 0 else block

    def some(i, carry):
        rows = pl.ds(pl.multiple_of(i * step, step), step) if step < block else slice(None)
        for k in range(3):
            update(0, (k, rows), att_ref[rows, k * width : (k + 1) * width])
        for k in range(2):
            update(2, (k, rows), ffn_ref[rows, k * hid : (k + 1) * hid])
        update(3, rows, down_ref[rows, :])
        return carry

    if step < block:
        lax.fori_loop(0, block // step, some, 0)
    else:
        some(0, 0)
    update(1, ..., att_ref[:, 3 * width :].T)
    for k in range(2):
        mine = jnp.zeros((1, block), FULL)
        for j in range(D // block):
            start = k * D + j * block
            mine = jnp.where(me == j, gain_sum[:, start : start + block], mine)
        update(4, pl.ds(k, 1), mine)


def adam(me, clip, rates, grads, params):
    flat = [array for group in params for array in group]
    outs = [jax.ShapeDtypeStruct((1, 1), FULL)]
    outs += [jax.ShapeDtypeStruct(w.shape, FULL) for w in flat]
    vmem = pl.BlockSpec(memory_space=pltpu.VMEM)
    norm, *made = pl.pallas_call(
        functools.partial(adam_kernel, clip, rates),
        in_specs=[pl.BlockSpec(memory_space=pltpu.SMEM)] + [vmem] * (len(grads) + len(flat)),
        out_specs=[vmem] * len(outs),
        out_shape=outs,
        name="adam",
    )(me, *grads, *[pltpu.with_memory_space_constraint(f, pltpu.VMEM) for f in flat])
    return norm[0, 0], [made[i : i + 3] for i in range(0, len(made), 3)]


def rope_tables(place):
    half, low = HD // 2, place.shape[0] // 2
    lane = jnp.arange(128) % HD
    freq = jnp.exp(-jnp.log(10000.0) * (lane % half).astype(FULL) / half)
    angle = place[:, None] * freq[None, :]
    cosine, sine = jnp.cos(angle), jnp.sin(angle)
    c1, s1 = cosine[:low, None], sine[:low, None]
    c2, s2 = cosine[None, low:], sine[None, low:]
    sign = jnp.where(lane < half, -1.0, 1.0)[None, None, :]
    both = c1 * c2 - s1 * s2, sign * (s1 * c2 + c1 * s2)
    return [table.reshape(L, 128) for table in both]


def adam_update(weight, first, second, grad, ratio, rate, decay):
    clipped = grad * ratio
    first_new = AVERAGING * first + (1.0 - AVERAGING) * clipped
    second_new = AVERAGING * second + (1.0 - AVERAGING) * clipped * clipped
    correction = 1.0 - AVERAGING**ADAM_STEP
    step = first_new / correction / (jnp.sqrt(second_new / correction) + 1e-08)
    return (weight - rate * (step + decay * weight), first_new, second_new)


def tn(rows, grads):
    out = lax.dot_general(rows, grads, (((0,), (0,)), ((), ())), preferred_element_type=FULL)
    return layout.with_layout_constraint(out.astype(LOW), layout.Layout((0, 1)))


def per_device(
    layer_input, layer_cotangent,
    attend_weight, attend_first, attend_second,
    output_weight, output_first, output_second,
    gated_weight, gated_first, gated_second,
    down_weight, down_first, down_second,
    norm_gains, gains_first, gains_second,
):
    rows = layer_input.shape[0]
    wide = lax.axis_size("wide")
    block = D // wide
    me = lax.axis_index("wide")
    narrow = lax.axis_index("narrow")
    core = narrow % 2
    cols = attend_weight.shape[2]

    bits = wide_bits()
    near = bits[:-1]
    half = D // 2
    hid = down_weight.shape[0]

    bits = wide_bits()
    near = bits[:-1]
    half = D // 2
    hid = down_weight.shape[0]
    pair = 2 * cols

    attend_low = attend_weight.astype(LOW)
    att = jnp.concatenate(
        [attend_low[0], attend_low[1], attend_low[2], output_weight.T.astype(LOW)], axis=1
    )
    cut = hid // 2
    down_t = down_weight.T
    ffn = jnp.concatenate([gated_weight[0], gated_weight[1], down_t[:, :cut]], axis=1).astype(LOW)
    down = down_t[:, cut:].astype(LOW)

    order = me ^ jnp.array(block_masks(), jnp.int32)
    source = (order[:, None] * block + jnp.arange(block)[None, :]).reshape(1, D)
    mover = (lax.broadcasted_iota(jnp.int32, (D, D), 0) == source).astype(LOW)
    mover = lax.optimization_barrier(mover)

    def both_halves(mine, theirs):
        first = core == 0
        return jnp.concatenate(
            [jnp.where(first, mine, theirs), jnp.where(first, theirs, mine)], axis=0
        )

    def own_rows(value):
        return lax.dynamic_slice_in_dim(value, core * rows, rows, axis=0)

    first = widen(att, near[:1])
    gains = widen(after(norm_gains, att).astype(LOW).astype(FULL)[None], bits[:1])
    first, down, gains = lax.optimization_barrier((first, down, gains))
    gains = widen(gains, bits[1:-1])
    att = widen(first, near[1:])
    down_y = swap(down, "wide", 1)
    down_x = swap(down, "narrow", 2)
    both = jnp.concatenate([layer_input, layer_cotangent], axis=0)
    moved = jnp.dot(both, mover, preferred_element_type=FULL).astype(LOW)
    place = jnp.arange(32, dtype=FULL)
    place = jnp.concatenate([32.0 * place, place])
    att, down_y, down_x, gains, moved, place = lax.optimization_barrier(
        (att, down_y, down_x, gains, moved, place)
    )
    att_y = swap(att, "wide", 1)
    att_x = swap(att, "narrow", 2)
    ffn = widen(after(ffn, att), near[:1])
    inputs = both_halves(moved[:rows], swap(moved[:rows], "narrow", 1))
    inputs, gains = lax.optimization_barrier((inputs, gains))
    gains = widen(gains, bits[-1:])
    moved_up = moved[rows:]
    cosine, sine = rope_tables(place)
    inputs, att, att_y, att_x, ffn, gains, cosine, sine = lax.optimization_barrier(
        (inputs, att, att_y, att_x, ffn, gains, cosine, sine)
    )
    gains = gains.transpose(1, 0, 2).reshape(2, 1, D)
    down_corner = swap(down_y, "narrow", 2)
    qk_corner = swap(att_y[:, :pair], "narrow", 2)
    vo_corner = swap(att_x[:, pair:], "wide", 1)
    ffn = widen(ffn, near[1:])
    qk = [[(att, pair, 0), (att_y, pair, 0)], [(att_x, pair, 0), qk_corner]]
    vo = [[(att, pair, 1), (att_y, pair, 1)], [(att_x, pair, 1), vo_corner]]
    saved = [attend_forward(inputs, qk[0], vo[0], cosine, sine)]
    second_in, qk_corner, vo_corner, ffn, down_corner = lax.optimization_barrier(
        (after(inputs, saved[0][3]), qk_corner, vo_corner, ffn, down_corner)
    )
    other_up = swap(after(moved_up, second_in), "narrow", 1)
    down = jnp.stack([down, down_y, down_x, down_corner])[:, None]
    for bit in near[:1]:
        down = jnp.concatenate([down, swap(down, "wide", bit)], axis=1)
    qk[1][1], vo[1][1] = qk_corner, vo_corner
    ffn_y = swap(ffn, "wide", 1)
    ffn_x = swap(ffn, "narrow", 2)
    saved.append(attend_forward(second_in, qk[1], vo[1], cosine, sine))
    context = [s[3] for s in saved]
    att_out = [att, att_y, att_x, vo_corner]
    held = [pltpu.VMEM((2, D, cols), LOW)]
    low_d, full_d = (D, LOW, False), (D, FULL, True)
    (attn_part,) = by_rows(
        project_kernel, "project", context, att_out, [low_d], scratch=held
    )
    ffn_y, ffn_x, attn_part, down = lax.optimization_barrier((ffn_y, ffn_x, attn_part, down))
    attn_other = swap(attn_part, "narrow", 1)
    down_far = [swap(down, "wide", bit) for bit in near[1:2]]
    gate_corner = swap(ffn_y[:, :hid], "narrow", 2)
    up_corner = swap(ffn_x[:, hid:], "wide", 1)
    flow = [(hid, LOW, True), (hid, LOW, True), (hid, LOW, False)]
    normed_one, inv_one, hidden_low, gate1, up1, act1, gu_own = by_rows(
        enter_kernel, "enter", [pinned(inputs), attn_part, attn_other],
        [gains, (ffn, 2 * hid, 0), (ffn_y, 2 * hid, 0)],
        [(D, LOW, True), (1, FULL, True), low_d] + flow, kept=[(D, 2 * hid)],
    )
    hidden_low, down, down_far = lax.optimization_barrier((hidden_low, down, down_far))
    moved_up, other_up, hidden_low = lax.optimization_barrier((moved_up, other_up, hidden_low))
    upstream = both_halves(moved_up, other_up)
    down = jnp.concatenate([down, *down_far], axis=1)
    for bit in near[2:]:
        down = jnp.concatenate([down, swap(down, "wide", bit)], axis=1)
    down = down.reshape(2, D, hid - cut)
    last_cols = 2 * hid // cut
    gate2, up2, act2, ffn_part, gu_other, down_all = by_rows(
        rest_kernel, "rest", [after(hidden_low, upstream), act1],
        [
            (ffn_x, 2 * hid, 0), gate_corner, (up_corner, hid, 0),
            (ffn, cut, last_cols), (ffn_y, cut, last_cols), (ffn_x, cut, last_cols),
            (up_corner, cut, hid // cut), down,
        ],
        flow + [low_d], kept=[(D, 2 * hid), (2, D, hid)], loose=(1, 2, 6),
    )
    ffn_other = swap(ffn_part, "narrow", 1)

    layer_output, grad_two_low, gain_two_grad = by_rows(
        turn_kernel, "turn", [pinned(normed_one), ffn_part, ffn_other, pinned(upstream)],
        [gains], [(D, LOW, True), low_d], sums=1,
    )
    down_send = tn(grad_two_low, act2)
    down_x = swap(down_send, "narrow", 2)
    wide_flow = (2 * hid, LOW, False)
    saves = [pinned(r) for r in (gate1, up1, gate2, up2)]
    gg, ug = by_rows(
        back_kernel, "back",
        [after(grad_two_low, down_send), *saves], [down_all], [wide_flow, wide_flow],
    )
    gate_send = tn(hidden_low[:, half:], gg)
    up_send = tn(hidden_low[:, half:], ug)
    gate_y = swap(gate_send, "wide", 1)
    up_y = swap(up_send, "wide", 1)
    mid_part = by_rows(
        mid_kernel, "mid", [after(gg, gate_send, up_send), ug], [gu_own, gu_other], []
    )
    mid_other = [swap(part, "narrow", 1) for part in mid_part]
    down_own = tn(grad_two_low, act1)
    gate_own = tn(hidden_low[:, :half], gg)
    up_own = tn(hidden_low[:, :half], ug)
    mid_part, mid_other, down_own, gate_own, up_own, down_x = lax.optimization_barrier(
        (mid_part, mid_other, down_own, gate_own, up_own, down_x)
    )
    grad_one_low, dctx1, dctx2, gain_one_grad = by_rows(
        leave_kernel, "leave",
        [grad_two_low, tuple(mid_part), tuple(mid_other), pinned(normed_one), pinned(inv_one)],
        [gains, *att_out], [low_d, (cols, LOW, True), (cols, LOW, True)],
        sums=1, scratch=held + [pltpu.VMEM((QB, D), FULL)],
    )

    q, k, v, _, lse = saved[1]
    dqk2, dv2 = attend_backward(q, k, v, lse, dctx2, cosine, sine)
    down_x, gate_y, dqk2, dv2 = lax.optimization_barrier((down_x, gate_y, dqk2, dv2))
    down_sum, gate_sum = add(down_own, down_x), add(gate_own, gate_y)
    down_y = swap(down_sum[half:].astype(LOW), "wide", 1)
    gate_far = gate_sum[:, hid:].astype(LOW)
    gate_x = swap(gate_far, "narrow", 2)
    qk_near2, qk_send2, vo_send = heads_grad(inputs, grad_one_low, after(dqk2, gate_far), dv2, context[1])
    qk_y2 = swap(qk_send2, "wide", 1)
    back = near[::-1]
    q, k, v, _, lse = saved[0]
    up_y, vo_done = lax.optimization_barrier((up_y, vo_send))
    up_sum = add(up_own, up_y)
    up_far = up_sum[:, hid:].astype(LOW)
    dctx1, up_far, vo_done = lax.optimization_barrier((dctx1, up_far, vo_done))
    up_x = swap(up_far, "narrow", 2)
    vo_x = swap(vo_done, "narrow", 2)
    dqk1, dv1 = attend_backward(q, k, v, lse, dctx1, cosine, sine)
    dqk1, dv1, down_y, qk_y2, gate_x = lax.optimization_barrier(
        (dqk1, dv1, down_y, qk_y2, gate_x)
    )
    early = narrow_down(add(down_sum[:half], down_y), back[:1])
    qk_near1, qk_send1, vo_own = heads_grad(inputs, grad_one_low, dqk1, dv1, context[0])
    qk_y1 = swap(qk_send1, "wide", 1)
    qk_far = add(qk_near2, qk_y2).astype(LOW)
    qk_x = swap(qk_far, "narrow", 2)
    vo_sum = add(vo_own, vo_x)
    vo_far = vo_sum[half:].astype(LOW)
    vo_y = swap(vo_far, "wide", 1)
    early_red = narrow_down(early, back[1:])
    late = jnp.concatenate([add(gate_sum[:, :hid], gate_x), add(up_sum[:, :hid], up_x)], axis=1)
    dqk1, vo_sum, late = lax.optimization_barrier((dqk1, vo_sum, late))
    late = narrow_down(late, back[:1])
    part_full, part_low = by_rows(
        input_kernel, "inputs", [dqk1, dv1, dqk2, dv2],
        [att, att_y, att_x, qk_corner, vo_corner], [full_d, low_d],
        scratch=[pltpu.VMEM((2, D, 3 * cols), LOW)],
    )
    theirs = lax.dynamic_slice_in_dim(part_low, (1 - core) * rows, rows, axis=0)
    theirs = swap(theirs, "narrow", 1)
    qk_sum = add(qk_near1, qk_y1)
    last = jnp.concatenate([add(qk_sum, qk_x), add(vo_sum[:half], vo_y)], axis=1)
    gain_grads = jnp.concatenate([gain_one_grad, gain_two_grad], axis=0)
    gain_low = gain_grads.astype(LOW)
    gain_rest = (gain_grads - gain_low.astype(FULL)).astype(LOW)
    gain_grads = nt(jnp.concatenate([gain_low, gain_rest], axis=0), mover)
    gain_grads = gain_grads[:2] + gain_grads[2:]
    last, early_red, late, gain_grads = lax.optimization_barrier(
        (last, early_red, late, gain_grads)
    )
    last = narrow_down(last, back[:1])
    late_red = narrow_down(late, back[1:])
    early_square = jnp.sum(early_red * early_red) + jnp.sum(late_red * late_red)
    last = narrow_down(last, back[1:-1])
    received = swap(last[block:].astype(LOW), "wide", back[-1])
    input_grad, layer_output = finish(
        jnp.full((1,), core, jnp.int32), grad_one_low, part_full, layer_output, theirs, mover
    )
    received, early_square, input_grad, layer_output = lax.optimization_barrier(
        (received, early_square, input_grad, layer_output)
    )
    att_red, square = last_sum(last[:block], received, jnp.full((1, 128), early_square, FULL))

    square = square + swap(square, "narrow", 1)
    message = jnp.concatenate([gain_grads.reshape(1, 2 * D), square], axis=1)
    message = message + swap(message, "narrow", 2)
    for bit in bits[::-1][:-1]:
        message = message + swap(message, "wide", bit)
    received = swap(message, "wide", bits[0])
    all_tokens = rows * wide * lax.axis_size("narrow")
    clip = 0.02 * math.sqrt(all_tokens * (4 * D * D + 3 * D * FF + 2 * D))
    grad_norm, (new_attend, new_output, new_gated, new_down, new_gains) = adam(
        jnp.full((1,), me, jnp.int32),
        clip,
        (
            (D ** (-0.5), WEIGHT_DECAY),
            (max(D // 64, 1) ** (-0.5), WEIGHT_DECAY),
            (D ** (-0.5), WEIGHT_DECAY),
            (FF ** (-0.5), WEIGHT_DECAY),
            (0.4, 0.0),
        ),
        (message, received, att_red, late_red, early_red),
        (
            (attend_weight, attend_first, attend_second),
            (output_weight, output_first, output_second),
            (gated_weight, gated_first, gated_second),
            (down_weight.T, down_first.T, down_second.T),
            (norm_gains, gains_first, gains_second),
        ),
    )
    new_down = [value.T for value in new_down]
    return (
        layer_output, input_grad, grad_norm,
        *new_attend, *new_output, *new_gated, *new_down, *new_gains,
    )


def solution(mesh):
    rows = P(("wide", "narrow"), None)
    stacked = P(None, "wide", "narrow")
    turned = P("narrow", "wide")
    gains = P(None, "wide")
    params = (stacked,) * 3 + (turned,) * 3 + (stacked,) * 3 + (turned,) * 3 + (gains,) * 3
    return jax.shard_map(
        per_device,
        mesh=mesh,
        in_specs=(rows, rows) + params,
        out_specs=(rows, rows, P()) + params,
        check_vma=False,
    )
```

```python
import functools
import math

import jax
import jax.numpy as jnp
from jax import lax
from jax.experimental import layout
from jax.experimental import pallas as pl
from jax.experimental.pallas import tpu as pltpu
from jax.sharding import PartitionSpec as P

D = 768
HD = 64
FF = 2048
L = 1024
ADAM_STEP = 5

EPSILON = 1e-05
WEIGHT_DECAY = 0.1
AVERAGING = 0.5

LOW = jnp.bfloat16
FULL = jnp.float32
QB = 256
MASKED = -1e30
SMALL = pl.CostEstimate(flops=10**6, bytes_accessed=10**4, transcendentals=0)


def swap(value, axis, bit):
    size = lax.axis_size(axis)
    return lax.ppermute(value, axis, [(i, i ^ bit) for i in range(size)])


def wide_bits():
    top = lax.axis_size("wide").bit_length() - 1
    return [1 << b for b in range(top - 1, -1, -1)]


def block_masks():
    masks = [0]
    for bit in wide_bits():
        masks = masks + [m ^ bit for m in masks]
    return masks


def after(value, *done):
    return lax.optimization_barrier((value, done))[0]


def widen(held, bits):
    for bit in bits:
        held = jnp.concatenate([held, swap(held, "wide", bit)], axis=0)
    return held


def add(kept, received):
    return kept.astype(FULL) + received.astype(FULL)


def narrow_down(held, bits):
    for bit in bits:
        half = held.shape[0] // 2
        held = add(held[:half], swap(held[half:].astype(LOW), "wide", bit))
    return held


def turn(value, cosine, sine, sign):
    width = value.shape[1]
    lane = lax.broadcasted_iota(jnp.int32, value.shape, 1) % HD
    other = jnp.where(
        lane < HD // 2,
        pltpu.roll(value, width - HD // 2, 1),
        pltpu.roll(value, HD // 2, 1),
    )
    reps = width // 128
    return value * jnp.concatenate([cosine] * reps, axis=1) + sign * other * jnp.concatenate(
        [sine] * reps, axis=1
    )


def nn(a, b):
    return lax.dot_general(a, b, (((1,), (0,)), ((), ())), preferred_element_type=FULL)


def nt(a, b):
    return lax.dot_general(a, b, (((1,), (1,)), ((), ())), preferred_element_type=FULL)


def diagonal(scores):
    key = lax.broadcasted_iota(jnp.int32, scores.shape, 0)
    query = lax.broadcasted_iota(jnp.int32, scores.shape, 1)
    return jnp.where(key <= query, scores, MASKED)


def flip(value):
    return value.astype(FULL).T


def attend_kernel(
    rows_ref, qka_ref, qkb_ref, voa_ref, vob_ref, cos_ref, sin_ref,
    q_ref, k_ref, v_ref, ctx_ref, lse_ref, hold,
):
    heads = q_ref.shape[0]
    width = heads * HD
    half = qka_ref.shape[0]

    def project(i, carry):
        rows = pl.ds(pl.multiple_of(i * QB, QB), QB)
        first, second = rows_ref[rows, :half], rows_ref[rows, half:]
        pair = nn(first, qka_ref[...]) + nn(second, qkb_ref[...])
        pair = turn(pair, cos_ref[rows, :], sin_ref[rows, :], 1.0)
        value = nn(first, voa_ref[:, :width]) + nn(second, vob_ref[:, :width])
        for h in range(heads):
            q_ref[h, rows, :] = (pair[:, h * HD : (h + 1) * HD] * (HD**-0.5)).astype(LOW)
            k_ref[h, rows, :] = pair[:, width + h * HD : width + (h + 1) * HD].astype(LOW)
            v_ref[h, rows, :] = value[:, h * HD : (h + 1) * HD].astype(LOW)
        return carry

    lax.fori_loop(0, L // QB, project, 0)

    def head(h, carry):
        turned = flip(v_ref[h]).astype(LOW)
        for i in range(L // QB):
            lo, hi = i * QB, (i + 1) * QB
            query = q_ref[h, lo:hi, :]
            diag = diagonal(nt(k_ref[h, lo:hi, :], query))
            peak = jnp.max(diag, axis=0, keepdims=True)
            if i:
                body = nt(k_ref[h, :lo, :], query)
                peak = jnp.maximum(peak, jnp.max(body, axis=0, keepdims=True))
            weight = jnp.exp(diag - peak)
            total = jnp.sum(weight, axis=0, keepdims=True)
            out = nn(turned[:, lo:hi], weight.astype(LOW))
            if i:
                weight = jnp.exp(body - peak)
                total = total + jnp.sum(weight, axis=0, keepdims=True)
                out = out + nn(turned[:, :lo], weight.astype(LOW))
            lse_ref[h, :, lo:hi] = peak + jnp.log(total)
            hold[h, lo:hi, :] = (out / total).T.astype(LOW)
        return carry

    lax.fori_loop(0, heads, head, 0)
    for h in range(heads):
        ctx_ref[:, h * HD : (h + 1) * HD] = hold[h]


def pinned(array):
    return pltpu.with_memory_space_constraint(array, pltpu.HBM)


def whole(array):
    zero = (0,) * len(array.shape)
    return pl.BlockSpec(array.shape, lambda *_: zero)


def by_head(shape):
    return pl.BlockSpec(shape, lambda h: (h, 0, 0))


def columns(piece, mode=None):
    array, width, j = piece if isinstance(piece, tuple) else (piece, piece.shape[-1], 0)
    lead = (0,) * (array.ndim - 1)
    shape = array.shape[:-1] + (width,)
    return array, pl.BlockSpec(shape, lambda *_: lead + (j,), pipeline_mode=mode)


def width_of(piece):
    return piece[1] if isinstance(piece, tuple) else piece.shape[1]


def attend_forward(rows, qk, vo, cosine, sine):
    heads = width_of(qk[0]) // 2 // HD
    headed = pltpu.HBM((heads, L, HD), LOW)
    outs = (
        headed, headed, headed,
        jax.ShapeDtypeStruct((L, heads * HD), LOW),
        pltpu.HBM((heads, 1, L), FULL),
    )
    args, specs = zip(*[columns(p) for p in (rows, *qk, *vo, cosine, sine)])
    return pl.pallas_call(
        attend_kernel,
        grid=(1,),
        in_specs=list(specs),
        out_specs=[whole(o) for o in outs],
        out_shape=outs,
        scratch_shapes=[pltpu.VMEM((heads, L, HD), LOW)],
        compiler_params=pltpu.CompilerParams(vmem_limit_bytes=24 << 20),
        cost_estimate=SMALL,
        name="attend_forward",
    )(*args)


def attend_back_kernel(
    q_ref, k_ref, v_ref, lse_ref, dctx_ref, cos_ref, sin_ref,
    dqk_ref, dv_ref, dctx, dqk, dk_sum, dv_sum,
):
    heads = dctx.shape[0]
    h = pl.program_id(0)

    @pl.when(h == 0)
    def _():
        for j in range(heads):
            dctx[j] = dctx_ref[:, j * HD : (j + 1) * HD]

    turned = flip(k_ref[0]).astype(LOW)
    for i in range(L // QB):
        lo, hi = i * QB, (i + 1) * QB
        query, back = q_ref[0, lo:hi, :], dctx[h, lo:hi, :]
        lse = lse_ref[0, :, lo:hi]
        prob = jnp.exp(diagonal(nt(k_ref[0, lo:hi, :], query)) - lse)
        grad = nt(v_ref[0, lo:hi, :], back)
        inner = jnp.sum(prob * grad, axis=0, keepdims=True)
        if i:
            prob_body = jnp.exp(nt(k_ref[0, :lo, :], query) - lse)
            grad_body = nt(v_ref[0, :lo, :], back)
            inner = inner + jnp.sum(prob_body * grad_body, axis=0, keepdims=True)
        score = (prob * (grad - inner)).astype(LOW)
        dv_sum[h, lo:hi, :] = nn(prob.astype(LOW), back)
        dk_sum[h, lo:hi, :] = nn(score, query)
        dquery = nn(turned[:, lo:hi], score)
        if i:
            score = (prob_body * (grad_body - inner)).astype(LOW)
            dv_sum[h, :lo, :] += nn(prob_body.astype(LOW), back)
            dk_sum[h, :lo, :] += nn(score, query)
            dquery = dquery + nn(turned[:, :lo], score)
        dqk[h, lo:hi, :] = (dquery * (HD**-0.5)).T

    def finish(i, carry):
        rows = pl.ds(pl.multiple_of(i * QB, QB), QB)
        pair = jnp.concatenate(
            [dqk[j, rows, :] for j in range(heads)] + [dk_sum[j, rows, :] for j in range(heads)],
            axis=1,
        )
        dqk_ref[rows, :] = turn(pair, cos_ref[rows, :], sin_ref[rows, :], -1.0).astype(LOW)
        dv_ref[rows, :] = jnp.concatenate(
            [dv_sum[j, rows, :] for j in range(heads)], axis=1
        ).astype(LOW)
        return carry

    @pl.when(h == heads - 1)
    def _():
        lax.fori_loop(0, L // QB, finish, 0)


def attend_backward(q, k, v, lse, dctx, cosine, sine):
    heads = q.shape[0]
    outs = (
        jax.ShapeDtypeStruct((L, 2 * heads * HD), LOW),
        jax.ShapeDtypeStruct((L, heads * HD), LOW),
    )
    return pl.pallas_call(
        attend_back_kernel,
        grid=(heads,),
        in_specs=[by_head((1, L, HD))] * 3
        + [by_head((1, 1, L)), whole(dctx), whole(cosine), whole(sine)],
        out_specs=[whole(o) for o in outs],
        out_shape=outs,
        scratch_shapes=[pltpu.VMEM((heads, L, HD), LOW)] + [pltpu.VMEM((heads, L, HD), FULL)] * 3,
        compiler_params=pltpu.CompilerParams(vmem_limit_bytes=24 << 20),
        cost_estimate=SMALL,
        name="attend_backward",
    )(pinned(q), pinned(k), pinned(v), pinned(lse), pinned(dctx), pinned(cosine), pinned(sine))


def held_once(array):
    zero = (0,) * array.ndim
    return pl.BlockSpec(array.shape, lambda *_: zero, pipeline_mode=pl.Buffered(1))


def in_top():
    return pl.program_id(0) < pl.num_programs(0) // 2


def halves(step, width):
    steps = L // step // 2
    return [
        pl.BlockSpec((step, width), lambda i: (jnp.minimum(i, steps - 1), 0)),
        pl.BlockSpec((step, width), lambda i: (jnp.maximum(i - steps, 0), 0)),
    ]


def by_rows(kernel, name, row_args, fixed, outs, sums=0, kept=(), scratch=(), loose=(), step=QB):
    specs, flat = [], []
    for r in row_args:
        if isinstance(r, tuple):
            specs += halves(step, r[0].shape[1])
            flat += r
        else:
            specs.append(pl.BlockSpec((step, r.shape[1]), lambda i: (i, 0)))
            flat.append(r)
    held, held_specs = zip(*[columns(f, pl.Buffered(1)) for f in fixed])
    shapes = [
        (pltpu.HBM if away else jax.ShapeDtypeStruct)((L, w), t) for w, t, away in outs
    ]
    out_specs = [pl.BlockSpec((step, w), lambda i: (i, 0)) for w, _, _ in outs]
    if not outs:
        shapes = [jax.ShapeDtypeStruct((L // 2, D), LOW)] * 2
        out_specs = halves(step, D)
    rows_out = len(shapes)
    shapes += [jax.ShapeDtypeStruct((1, D), FULL)] * sums
    shapes += [pltpu.HBM(shape, LOW) for shape in kept]
    out_specs += [whole(o) for o in shapes[rows_out:]]
    return pl.pallas_call(
        kernel,
        grid=(L // step,),
        in_specs=specs + list(held_specs),
        out_specs=out_specs,
        out_shape=shapes,
        scratch_shapes=list(scratch),
        compiler_params=pltpu.CompilerParams(vmem_limit_bytes=32 << 20),
        cost_estimate=SMALL,
        name=name,
    )(*flat, *[f if f.dtype == FULL or i in loose else pinned(f) for i, f in enumerate(held)])


def rms_scale(residual):
    return lax.rsqrt(jnp.mean(residual * residual, axis=1, keepdims=True) + EPSILON)


def norm_back(scaled, normed, inv):
    return inv * (scaled - normed * jnp.mean(scaled * normed, axis=1, keepdims=True))


def column_sum(sum_ref, value):
    @pl.when(pl.program_id(0) == 0)
    def _():
        sum_ref[...] = jnp.zeros_like(sum_ref)

    sum_ref[...] += jnp.sum(value, axis=0, keepdims=True)


def heads_out(held_ref, refs):
    att_ref, y_ref, x_ref, corner_ref = refs
    half, width = att_ref.shape[0], held_ref.shape[2]

    @pl.when(pl.program_id(0) == 0)
    def _():
        held_ref[0, :half] = att_ref[:, 3 * width :]
        held_ref[0, half:] = y_ref[:, 3 * width :]
        held_ref[1, :half] = x_ref[:, 3 * width :]
        held_ref[1, half:] = corner_ref[:, width:]


def project_kernel(one_ref, two_ref, att_ref, y_ref, x_ref, corner_ref, out_ref, held_ref):
    heads_out(held_ref, (att_ref, y_ref, x_ref, corner_ref))
    out_ref[...] = (nt(one_ref[...], held_ref[0]) + nt(two_ref[...], held_ref[1])).astype(LOW)


def gate_up(hidden, weights_ref, gate_ref, up_ref, act_ref):
    hid = gate_ref.shape[1]
    gate = nn(hidden, weights_ref[:, :hid])
    up = nn(hidden, weights_ref[:, hid:])
    gate_ref[...] = gate.astype(LOW)
    up_ref[...] = up.astype(LOW)
    act_ref[...] = (gate * jax.nn.sigmoid(gate) * up).astype(LOW)


def enter_kernel(
    rows_ref, mine_ref, theirs_ref, gain_ref, own_ref, y_ref,
    normed_ref, inv_ref, hidden_ref, gate_ref, up_ref, act_ref, weights_ref,
):
    half = own_ref.shape[0]

    @pl.when(pl.program_id(0) == 0)
    def _():
        weights_ref[:half] = own_ref[...]
        weights_ref[half:] = y_ref[...]

    residual = rows_ref[...].astype(FULL) + add(mine_ref[...], theirs_ref[...])
    inv = rms_scale(residual)
    normed = residual * inv
    hidden = (normed * gain_ref[0]).astype(LOW)
    normed_ref[...] = normed.astype(LOW)
    inv_ref[...] = inv
    hidden_ref[...] = hidden
    gate_up(hidden, weights_ref, gate_ref, up_ref, act_ref)


def rest_kernel(
    hidden_ref, act1_ref, x_ref, gate_corner_ref, up_corner_ref,
    low_own_ref, low_y_ref, low_x_ref, low_corner_ref, high_ref,
    gate_ref, up_ref, act_ref, out_ref, weights_ref, down_ref,
):
    half, hid = x_ref.shape[0], gate_ref.shape[1]
    cut = high_ref.shape[2]

    @pl.when(pl.program_id(0) == 0)
    def _():
        weights_ref[:half] = x_ref[...]
        weights_ref[half:, :hid] = gate_corner_ref[...]
        weights_ref[half:, hid:] = up_corner_ref[...]
        down_ref[0, :half, :cut] = low_own_ref[...]
        down_ref[0, half:, :cut] = low_y_ref[...]
        down_ref[1, :half, :cut] = low_x_ref[...]
        down_ref[1, half:, :cut] = low_corner_ref[...]
        down_ref[:, :, cut:] = high_ref[...]

    gate_up(hidden_ref[...], weights_ref, gate_ref, up_ref, act_ref)
    out_ref[...] = (nt(act1_ref[...], down_ref[0]) + nt(act_ref[...], down_ref[1])).astype(LOW)


def turn_kernel(
    normed_ref, mine_ref, theirs_ref, up_rows_ref, gains_ref,
    out_ref, low_ref, sum_ref,
):
    residual = normed_ref[...].astype(FULL) * gains_ref[0] + add(mine_ref[...], theirs_ref[...])
    inv = rms_scale(residual)
    normed = residual * inv
    gain = gains_ref[1]
    out_ref[...] = (normed * gain).astype(LOW)
    upstream = up_rows_ref[...].astype(FULL)
    column_sum(sum_ref, upstream * normed)
    low_ref[...] = norm_back(upstream * gain, normed, inv).astype(LOW)


def back_kernel(low_ref, gate1_ref, up1_ref, gate2_ref, up2_ref, down_ref, gg_ref, ug_ref):
    hid = gate1_ref.shape[1]
    low = low_ref[...]
    for x, gate_ref, up_ref in ((0, gate1_ref, up1_ref), (1, gate2_ref, up2_ref)):
        act_grad = nn(low, down_ref[x])
        gate, up = gate_ref[...].astype(FULL), up_ref[...].astype(FULL)
        sig = jax.nn.sigmoid(gate)
        gg = act_grad * up * (sig * (1.0 + gate * (1.0 - sig)))
        gg_ref[:, x * hid : (x + 1) * hid] = gg.astype(LOW)
        ug_ref[:, x * hid : (x + 1) * hid] = (act_grad * (gate * sig)).astype(LOW)


def mid_kernel(gg_ref, ug_ref, own_ref, other_ref, top_ref, bottom_ref):
    hid = gg_ref.shape[1] // 2
    total = 0.0
    for x, weights_ref in enumerate((own_ref, other_ref)):
        cols = slice(x * hid, (x + 1) * hid)
        total = total + nt(gg_ref[:, cols], weights_ref[:, :hid])
        total = total + nt(ug_ref[:, cols], weights_ref[:, hid:])
    low = total.astype(LOW)

    @pl.when(in_top())
    def _():
        top_ref[...] = low

    @pl.when(jnp.logical_not(in_top()))
    def _():
        bottom_ref[...] = low


def leave_kernel(
    grad_two_ref, mine_top_ref, mine_bottom_ref, theirs_top_ref, theirs_bottom_ref,
    normed_ref, inv_ref, gains_ref, att_ref, y_ref, x_ref, corner_ref,
    low_ref, ctx1_ref, ctx2_ref, sum_ref, held_ref, mid_ref,
):
    heads_out(held_ref, (att_ref, y_ref, x_ref, corner_ref))

    @pl.when(in_top())
    def _():
        mid_ref[...] = add(mine_top_ref[...], theirs_top_ref[...])

    @pl.when(jnp.logical_not(in_top()))
    def _():
        mid_ref[...] = add(mine_bottom_ref[...], theirs_bottom_ref[...])

    hidden_grad = grad_two_ref[...].astype(FULL) + mid_ref[...]
    normed = normed_ref[...].astype(FULL)
    column_sum(sum_ref, hidden_grad * normed)
    low = norm_back(hidden_grad * gains_ref[0], normed, inv_ref[...]).astype(LOW)
    low_ref[...] = low
    ctx1_ref[...] = nn(low, held_ref[0]).astype(LOW)
    ctx2_ref[...] = nn(low, held_ref[1]).astype(LOW)


def input_kernel(
    qk1_ref, v1_ref, qk2_ref, v2_ref, att_ref, y_ref, x_ref, qk_corner_ref, vo_corner_ref,
    full_ref, low_ref, held_ref,
):
    half, width = att_ref.shape[0], v1_ref.shape[1]
    pair = 2 * width

    @pl.when(pl.program_id(0) == 0)
    def _():
        held_ref[0, :half] = att_ref[:, : pair + width]
        held_ref[0, half:] = y_ref[:, : pair + width]
        held_ref[1, :half] = x_ref[:, : pair + width]
        held_ref[1, half:, :pair] = qk_corner_ref[...]
        held_ref[1, half:, pair:] = vo_corner_ref[:, :width]

    total = 0.0
    for x, qk_ref, v_ref in ((0, qk1_ref, v1_ref), (1, qk2_ref, v2_ref)):
        total = total + nt(qk_ref[...], held_ref[x, :, :pair])
        total = total + nt(v_ref[...], held_ref[x, :, pair:])
    full_ref[...] = total
    low_ref[...] = total.astype(LOW)


def heads_grad_kernel(
    rows_ref, grad_ref, qk_ref, v_ref, ctx_ref, near_ref, far_ref, vo_ref
):
    width = v_ref.shape[1]
    rows = flip(rows_ref[...]).astype(LOW)
    qk = nn(rows, qk_ref[...]).astype(LOW)
    step, half = qk.shape[0], near_ref.shape[0]
    for i in range(D // step):

        @pl.when(pl.program_id(0) == i)
        def _(start=i * step):
            near = max(min(half - start, step), 0)
            if near:
                near_ref[start : start + near] = qk[:near]
            if near < step:
                far_ref[start + near - half : start + step - half] = qk[near:]

    vo_ref[:, :width] = nn(rows, v_ref[...]).astype(LOW)
    vo_ref[:, width:] = nn(flip(grad_ref[...]).astype(LOW), ctx_ref[...]).astype(LOW)


def heads_grad(rows, grad, dqk, dv, context):
    half, pair = D // 2, dqk.shape[1]
    split = pl.BlockSpec((L, 256), lambda i: (0, i))
    held = pl.BlockSpec((half, pair), lambda i: (0, 0))
    return pl.pallas_call(
        heads_grad_kernel,
        grid=(D // 256,),
        in_specs=[split, split] + [held_once(g) for g in (dqk, dv, context)],
        out_specs=[held, held, pl.BlockSpec((256, pair), lambda i: (i, 0))],
        out_shape=[pltpu.HBM((half, pair), LOW)] * 2 + [pltpu.HBM((D, pair), LOW)],
        compiler_params=pltpu.CompilerParams(vmem_limit_bytes=24 << 20),
        cost_estimate=SMALL,
        name="heads_grad",
    )(rows, grad, dqk, dv, context)


def in_order(value, mover):
    total = 0.0
    for _ in range(2):
        part = value.astype(LOW)
        total = total + nt(part, mover)
        value = value - part.astype(FULL)
    return total


def finish_kernel(
    core_ref, one_ref, full_ref, out_ref, theirs_ref, mover_ref, grad_ref, low_ref
):
    mover = mover_ref[...]
    grad = one_ref[...].astype(FULL) + full_ref[...] + theirs_ref[...].astype(FULL)
    grad_ref[...] = in_order(grad, mover)
    low_ref[...] = nt(out_ref[...], mover).astype(LOW)


def finish(core, grad_one, part_full, layer_output, theirs, mover):
    rows = theirs.shape[0]
    steps = rows // QB
    mine = pl.BlockSpec((QB, D), lambda i, c: (c[0] * steps + i, 0))
    plain = pl.BlockSpec((QB, D), lambda i, c: (i, 0))
    return pl.pallas_call(
        finish_kernel,
        grid_spec=pltpu.PrefetchScalarGridSpec(
            num_scalar_prefetch=1,
            grid=(steps,),
            in_specs=[mine, mine, mine, plain, held_once(mover)],
            out_specs=[plain, plain],
        ),
        out_shape=[
            jax.ShapeDtypeStruct((rows, D), FULL), jax.ShapeDtypeStruct((rows, D), LOW)
        ],
        cost_estimate=SMALL,
        name="finish",
    )(core, grad_one, pinned(part_full), pinned(layer_output), theirs, mover)


def last_kernel(
    kept_ref, received_ref, late_ref, late_received_ref, early_ref, sum_ref, late_sum_ref, total_ref
):
    def squares(value):
        return jnp.sum(jnp.sum(value * value, axis=0, keepdims=True), axis=1, keepdims=True)

    value = kept_ref[...] + received_ref[...].astype(FULL)
    late = late_ref[...] + late_received_ref[...].astype(FULL)
    sum_ref[...] = value
    late_sum_ref[...] = late
    total = squares(value) + squares(late) + squares(early_ref[...])
    total_ref[...] = jnp.broadcast_to(total, total_ref.shape)


def last_sums(kept, received, late, late_received, early):
    vmem = pl.BlockSpec(memory_space=pltpu.VMEM)
    return pl.pallas_call(
        last_kernel,
        in_specs=[vmem] * 5,
        out_specs=[vmem] * 3,
        out_shape=[jax.ShapeDtypeStruct(a.shape, FULL) for a in (kept, late)]
        + [jax.ShapeDtypeStruct((1, 128), FULL)],
        name="last_sums",
    )(kept, received, late, late_received, early)


def adam_kernel(clip, rates, *refs):
    me = refs[0][0]
    message = refs[1][...] + refs[2][...]
    att_ref, ffn_ref, down_ref = refs[3:6]
    ins, norm_ref, outs = refs[6:21], refs[21], refs[22:]
    block = ins[12].shape[1]
    gain_sum = message[:, : 2 * D]
    total = message[:, 2 * D : 2 * D + 1] + jnp.sum(gain_sum * gain_sum, axis=1, keepdims=True)
    norm = jnp.sqrt(total)
    norm_ref[...] = norm
    ratio = clip / jnp.maximum(norm, clip)

    def update(p, at, grad):
        rate, decay = rates[p]
        old = [ref[at] for ref in ins[3 * p : 3 * p + 3]]
        for ref, value in zip(
            outs[3 * p : 3 * p + 3], adam_update(*old, grad, ratio, rate, decay)
        ):
            ref[at] = value

    width, hid = att_ref.shape[1] // 4, ffn_ref.shape[1] // 2
    step = 16 if block % 16 == 0 else block

    def some(i, carry):
        rows = pl.ds(pl.multiple_of(i * step, step), step) if step < block else slice(None)
        for k in range(3):
            update(0, (k, rows), att_ref[rows, k * width : (k + 1) * width])
        for k in range(2):
            update(2, (k, rows), ffn_ref[rows, k * hid : (k + 1) * hid])
        update(3, rows, down_ref[rows, :])
        return carry

    if step < block:
        lax.fori_loop(0, block // step, some, 0)
    else:
        some(0, 0)
    update(1, ..., att_ref[:, 3 * width :].T)
    for k in range(2):
        mine = jnp.zeros((1, block), FULL)
        for j in range(D // block):
            start = k * D + j * block
            mine = jnp.where(me == j, gain_sum[:, start : start + block], mine)
        update(4, pl.ds(k, 1), mine)


def adam(me, clip, rates, grads, params):
    flat = [array for group in params for array in group]
    outs = [jax.ShapeDtypeStruct((1, 1), FULL)]
    outs += [jax.ShapeDtypeStruct(w.shape, FULL) for w in flat]
    vmem = pl.BlockSpec(memory_space=pltpu.VMEM)
    norm, *made = pl.pallas_call(
        functools.partial(adam_kernel, clip, rates),
        in_specs=[pl.BlockSpec(memory_space=pltpu.SMEM)] + [vmem] * (len(grads) + len(flat)),
        out_specs=[vmem] * len(outs),
        out_shape=outs,
        name="adam",
    )(me, *grads, *[pltpu.with_memory_space_constraint(f, pltpu.VMEM) for f in flat])
    return norm[0, 0], [made[i : i + 3] for i in range(0, len(made), 3)]


def rope_tables(place):
    half, low = HD // 2, place.shape[0] // 2
    lane = jnp.arange(128) % HD
    freq = jnp.exp(-jnp.log(10000.0) * (lane % half).astype(FULL) / half)
    angle = place[:, None] * freq[None, :]
    cosine, sine = jnp.cos(angle), jnp.sin(angle)
    c1, s1 = cosine[:low, None], sine[:low, None]
    c2, s2 = cosine[None, low:], sine[None, low:]
    sign = jnp.where(lane < half, -1.0, 1.0)[None, None, :]
    both = c1 * c2 - s1 * s2, sign * (s1 * c2 + c1 * s2)
    return [table.reshape(L, 128) for table in both]


def adam_update(weight, first, second, grad, ratio, rate, decay):
    clipped = grad * ratio
    first_new = AVERAGING * first + (1.0 - AVERAGING) * clipped
    second_new = AVERAGING * second + (1.0 - AVERAGING) * clipped * clipped
    correction = 1.0 - AVERAGING**ADAM_STEP
    step = first_new / correction / (jnp.sqrt(second_new / correction) + 1e-08)
    return (weight - rate * (step + decay * weight), first_new, second_new)


def tn(rows, grads):
    out = lax.dot_general(rows, grads, (((0,), (0,)), ((), ())), preferred_element_type=FULL)
    return layout.with_layout_constraint(out.astype(LOW), layout.Layout((0, 1)))


def per_device(
    layer_input, layer_cotangent,
    attend_weight, attend_first, attend_second,
    output_weight, output_first, output_second,
    gated_weight, gated_first, gated_second,
    down_weight, down_first, down_second,
    norm_gains, gains_first, gains_second,
):
    rows = layer_input.shape[0]
    wide = lax.axis_size("wide")
    block = D // wide
    me = lax.axis_index("wide")
    narrow = lax.axis_index("narrow")
    core = narrow % 2
    cols = attend_weight.shape[2]

    bits = wide_bits()
    near = bits[:-1]
    half = D // 2
    hid = down_weight.shape[0]

    bits = wide_bits()
    near = bits[:-1]
    half = D // 2
    hid = down_weight.shape[0]
    pair = 2 * cols

    attend_low = attend_weight.astype(LOW)
    att = jnp.concatenate(
        [attend_low[0], attend_low[1], attend_low[2], output_weight.T.astype(LOW)], axis=1
    )
    cut = hid // 2
    down_t = down_weight.T
    ffn = jnp.concatenate([gated_weight[0], gated_weight[1], down_t[:, :cut]], axis=1).astype(LOW)
    down = down_t[:, cut:].astype(LOW)

    order = me ^ jnp.array(block_masks(), jnp.int32)
    source = (order[:, None] * block + jnp.arange(block)[None, :]).reshape(1, D)
    mover = (lax.broadcasted_iota(jnp.int32, (D, D), 0) == source).astype(LOW)
    mover = lax.optimization_barrier(mover)

    def both_halves(mine, theirs):
        first = core == 0
        return jnp.concatenate(
            [jnp.where(first, mine, theirs), jnp.where(first, theirs, mine)], axis=0
        )

    def own_rows(value):
        return lax.dynamic_slice_in_dim(value, core * rows, rows, axis=0)

    first = widen(att, near[:1])
    gains = widen(after(norm_gains, att).astype(LOW).astype(FULL)[None], bits[:1])
    first, down, gains = lax.optimization_barrier((first, down, gains))
    gains = widen(gains, bits[1:-1])
    att = widen(first, near[1:])
    down_y = swap(down, "wide", 1)
    down_x = swap(down, "narrow", 2)
    both = jnp.concatenate([layer_input, layer_cotangent], axis=0)
    moved = jnp.dot(both, mover, preferred_element_type=FULL).astype(LOW)
    place = jnp.arange(32, dtype=FULL)
    place = jnp.concatenate([32.0 * place, place])
    att, down_y, down_x, gains, moved, place = lax.optimization_barrier(
        (att, down_y, down_x, gains, moved, place)
    )
    att_y = swap(att, "wide", 1)
    att_x = swap(att, "narrow", 2)
    ffn = widen(after(ffn, att), near[:1])
    inputs = both_halves(moved[:rows], swap(moved[:rows], "narrow", 1))
    inputs, gains = lax.optimization_barrier((inputs, gains))
    gains = widen(gains, bits[-1:])
    moved_up = moved[rows:]
    cosine, sine = rope_tables(place)
    inputs, att, att_y, att_x, ffn, gains, cosine, sine = lax.optimization_barrier(
        (inputs, att, att_y, att_x, ffn, gains, cosine, sine)
    )
    gains = gains.transpose(1, 0, 2).reshape(2, 1, D)
    down_corner = swap(down_y, "narrow", 2)
    qk_corner = swap(att_y[:, :pair], "narrow", 2)
    vo_corner = swap(att_x[:, pair:], "wide", 1)
    ffn = widen(ffn, near[1:])
    qk = [[(att, pair, 0), (att_y, pair, 0)], [(att_x, pair, 0), qk_corner]]
    vo = [[(att, pair, 1), (att_y, pair, 1)], [(att_x, pair, 1), vo_corner]]
    saved = [attend_forward(inputs, qk[0], vo[0], cosine, sine)]
    second_in, qk_corner, vo_corner, ffn, down_corner = lax.optimization_barrier(
        (after(inputs, saved[0][3]), qk_corner, vo_corner, ffn, down_corner)
    )
    other_up = swap(after(moved_up, second_in), "narrow", 1)
    down = jnp.stack([down, down_y, down_x, down_corner])[:, None]
    for bit in near[:1]:
        down = jnp.concatenate([down, swap(down, "wide", bit)], axis=1)
    qk[1][1], vo[1][1] = qk_corner, vo_corner
    ffn_y = swap(ffn, "wide", 1)
    ffn_x = swap(ffn, "narrow", 2)
    saved.append(attend_forward(second_in, qk[1], vo[1], cosine, sine))
    context = [s[3] for s in saved]
    att_out = [att, att_y, att_x, vo_corner]
    held = [pltpu.VMEM((2, D, cols), LOW)]
    low_d, full_d = (D, LOW, False), (D, FULL, True)
    (attn_part,) = by_rows(
        project_kernel, "project", context, att_out, [low_d], scratch=held
    )
    ffn_y, ffn_x, attn_part, down = lax.optimization_barrier((ffn_y, ffn_x, attn_part, down))
    attn_other = swap(attn_part, "narrow", 1)
    down_far = [swap(down, "wide", bit) for bit in near[1:2]]
    gate_corner = swap(ffn_y[:, :hid], "narrow", 2)
    up_corner = swap(ffn_x[:, hid:], "wide", 1)
    flow = [(hid, LOW, True), (hid, LOW, True), (hid, LOW, False)]
    normed_one, inv_one, hidden_low, gate1, up1, act1, gu_own = by_rows(
        enter_kernel, "enter", [pinned(inputs), attn_part, pinned(attn_other)],
        [gains, (ffn, 2 * hid, 0), (ffn_y, 2 * hid, 0)],
        [(D, LOW, True), (1, FULL, True), low_d] + flow, kept=[(D, 2 * hid)],
    )
    hidden_low, down, down_far = lax.optimization_barrier((hidden_low, down, down_far))
    moved_up, other_up, hidden_low = lax.optimization_barrier((moved_up, other_up, hidden_low))
    upstream = both_halves(moved_up, other_up)
    down = jnp.concatenate([down, *down_far], axis=1)
    for bit in near[2:]:
        down = jnp.concatenate([down, swap(down, "wide", bit)], axis=1)
    down = down.reshape(2, D, hid - cut)
    last_cols = 2 * hid // cut
    gate2, up2, act2, ffn_part, gu_other, down_all = by_rows(
        rest_kernel, "rest", [after(hidden_low, upstream), act1],
        [
            (ffn_x, 2 * hid, 0), gate_corner, (up_corner, hid, 0),
            (ffn, cut, last_cols), (ffn_y, cut, last_cols), (ffn_x, cut, last_cols),
            (up_corner, cut, hid // cut), down,
        ],
        flow + [low_d], kept=[(D, 2 * hid), (2, D, hid)], loose=(1, 2, 6),
    )
    ffn_other = swap(ffn_part, "narrow", 1)

    layer_output, grad_two_low, gain_two_grad = by_rows(
        turn_kernel, "turn", [pinned(normed_one), ffn_part, ffn_other, pinned(upstream)],
        [gains], [(D, LOW, True), low_d], sums=1,
    )
    down_send = tn(grad_two_low, act2)
    down_x = swap(down_send, "narrow", 2)
    wide_flow = (2 * hid, LOW, False)
    saves = [pinned(r) for r in (gate1, up1, gate2, up2)]
    gg, ug = by_rows(
        back_kernel, "back",
        [after(grad_two_low, down_send), *saves], [down_all], [wide_flow, wide_flow],
    )
    gate_send = tn(hidden_low[:, half:], gg)
    up_send = tn(hidden_low[:, half:], ug)
    gate_y = swap(gate_send, "wide", 1)
    up_y = swap(up_send, "wide", 1)
    mid_part = by_rows(
        mid_kernel, "mid", [after(gg, gate_send, up_send), ug], [gu_own, gu_other], []
    )
    mid_other = [swap(part, "narrow", 1) for part in mid_part]
    down_own = tn(grad_two_low, act1)
    gate_own = tn(hidden_low[:, :half], gg)
    up_own = tn(hidden_low[:, :half], ug)
    mid_part, mid_other, down_own, gate_own, up_own, down_x = lax.optimization_barrier(
        (mid_part, mid_other, down_own, gate_own, up_own, down_x)
    )
    grad_one_low, dctx1, dctx2, gain_one_grad = by_rows(
        leave_kernel, "leave",
        [grad_two_low, tuple(mid_part), tuple(mid_other), pinned(normed_one), pinned(inv_one)],
        [gains, *att_out], [low_d, (cols, LOW, True), (cols, LOW, True)],
        sums=1, scratch=held + [pltpu.VMEM((QB, D), FULL)],
    )

    q, k, v, _, lse = saved[1]
    dqk2, dv2 = attend_backward(q, k, v, lse, dctx2, cosine, sine)
    down_x, gate_y, dqk2, dv2 = lax.optimization_barrier((down_x, gate_y, dqk2, dv2))
    down_sum, gate_sum = add(down_own, down_x), add(gate_own, gate_y)
    down_y = swap(down_sum[half:].astype(LOW), "wide", 1)
    gate_far = gate_sum[:, hid:].astype(LOW)
    gate_x = swap(gate_far, "narrow", 2)
    qk_near2, qk_send2, vo_send = heads_grad(inputs, grad_one_low, after(dqk2, gate_far), dv2, context[1])
    qk_y2 = swap(qk_send2, "wide", 1)
    back = near[::-1]
    q, k, v, _, lse = saved[0]
    up_y, vo_done = lax.optimization_barrier((up_y, vo_send))
    up_sum = add(up_own, up_y)
    up_far = up_sum[:, hid:].astype(LOW)
    dctx1, up_far, vo_done = lax.optimization_barrier((dctx1, up_far, vo_done))
    up_x = swap(up_far, "narrow", 2)
    vo_x = swap(vo_done, "narrow", 2)
    dqk1, dv1 = attend_backward(q, k, v, lse, dctx1, cosine, sine)
    dqk1, dv1, down_y, qk_y2, gate_x = lax.optimization_barrier(
        (dqk1, dv1, down_y, qk_y2, gate_x)
    )
    early = narrow_down(add(down_sum[:half], down_y), back[:1])
    qk_near1, qk_send1, vo_own = heads_grad(inputs, grad_one_low, dqk1, dv1, context[0])
    qk_y1 = swap(qk_send1, "wide", 1)
    qk_far = add(qk_near2, qk_y2).astype(LOW)
    qk_x = swap(qk_far, "narrow", 2)
    vo_sum = add(vo_own, vo_x)
    vo_far = vo_sum[half:].astype(LOW)
    vo_y = swap(vo_far, "wide", 1)
    late = jnp.concatenate([add(gate_sum[:, :hid], gate_x), add(up_sum[:, :hid], up_x)], axis=1)
    dqk1, vo_sum, late, early = lax.optimization_barrier((dqk1, vo_sum, late, early))
    early_red = narrow_down(early, back[1:])
    late = narrow_down(late, back[:1])
    part_full, part_low = by_rows(
        input_kernel, "inputs", [dqk1, dv1, dqk2, dv2],
        [att, att_y, att_x, qk_corner, vo_corner], [full_d, low_d],
        scratch=[pltpu.VMEM((2, D, 3 * cols), LOW)],
    )
    qk_sum = add(qk_near1, qk_y1)
    last = jnp.concatenate([add(qk_sum, qk_x), add(vo_sum[:half], vo_y)], axis=1)
    gain_grads = jnp.concatenate([gain_one_grad, gain_two_grad], axis=0)
    gain_low = gain_grads.astype(LOW)
    gain_rest = (gain_grads - gain_low.astype(FULL)).astype(LOW)
    gain_grads = nt(jnp.concatenate([gain_low, gain_rest], axis=0), mover)
    gain_grads = gain_grads[:2] + gain_grads[2:]
    last, early_red, late, gain_grads, part_low = lax.optimization_barrier(
        (last, early_red, late, gain_grads, part_low)
    )
    theirs = lax.dynamic_slice_in_dim(part_low, (1 - core) * rows, rows, axis=0)
    theirs = swap(theirs, "narrow", 1)
    last = narrow_down(last, back[:1])
    late = narrow_down(late, back[1:-1])
    late_received = swap(late[block:].astype(LOW), "wide", back[-1])
    last = narrow_down(last, back[1:-1])
    received = swap(last[block:].astype(LOW), "wide", back[-1])
    input_grad, layer_output = finish(
        jnp.full((1,), core, jnp.int32), grad_one_low, part_full, layer_output, theirs, mover
    )
    received, input_grad, layer_output = lax.optimization_barrier(
        (received, input_grad, layer_output)
    )
    att_red, late_red, square = last_sums(
        last[:block], received, late[:block], late_received, early_red
    )

    square = square + swap(square, "narrow", 1)
    message = jnp.concatenate([gain_grads.reshape(1, 2 * D), square], axis=1)
    message = message + swap(message, "narrow", 2)
    for bit in bits[::-1][:-1]:
        message = message + swap(message, "wide", bit)
    received = swap(message, "wide", bits[0])
    all_tokens = rows * wide * lax.axis_size("narrow")
    clip = 0.02 * math.sqrt(all_tokens * (4 * D * D + 3 * D * FF + 2 * D))
    grad_norm, (new_attend, new_output, new_gated, new_down, new_gains) = adam(
        jnp.full((1,), me, jnp.int32),
        clip,
        (
            (D ** (-0.5), WEIGHT_DECAY),
            (max(D // 64, 1) ** (-0.5), WEIGHT_DECAY),
            (D ** (-0.5), WEIGHT_DECAY),
            (FF ** (-0.5), WEIGHT_DECAY),
            (0.4, 0.0),
        ),
        (message, received, att_red, late_red, early_red),
        (
            (attend_weight, attend_first, attend_second),
            (output_weight, output_first, output_second),
            (gated_weight, gated_first, gated_second),
            (down_weight.T, down_first.T, down_second.T),
            (norm_gains, gains_first, gains_second),
        ),
    )
    new_down = [value.T for value in new_down]
    return (
        layer_output, input_grad, grad_norm,
        *new_attend, *new_output, *new_gated, *new_down, *new_gains,
    )


def solution(mesh):
    rows = P(("wide", "narrow"), None)
    stacked = P(None, "wide", "narrow")
    turned = P("narrow", "wide")
    gains = P(None, "wide")
    params = (stacked,) * 3 + (turned,) * 3 + (stacked,) * 3 + (turned,) * 3 + (gains,) * 3
    return jax.shard_map(
        per_device,
        mesh=mesh,
        in_specs=(rows, rows) + params,
        out_specs=(rows, rows, P()) + params,
        check_vma=False,
    )
```

```python
import functools
import math

import jax
import jax.numpy as jnp
from jax import lax
from jax.experimental import layout
from jax.experimental import pallas as pl
from jax.experimental.pallas import tpu as pltpu
from jax.sharding import PartitionSpec as P

D = 768
HD = 64
FF = 2048
L = 1024
ADAM_STEP = 5

EPSILON = 1e-05
WEIGHT_DECAY = 0.1
AVERAGING = 0.5

LOW = jnp.bfloat16
FULL = jnp.float32
QB = 256
MASKED = -1e30
SMALL = pl.CostEstimate(flops=10**6, bytes_accessed=10**4, transcendentals=0)


def swap(value, axis, bit):
    size = lax.axis_size(axis)
    return lax.ppermute(value, axis, [(i, i ^ bit) for i in range(size)])


def wide_bits():
    top = lax.axis_size("wide").bit_length() - 1
    return [1 << b for b in range(top - 1, -1, -1)]


def block_masks():
    masks = [0]
    for bit in wide_bits():
        masks = masks + [m ^ bit for m in masks]
    return masks


def after(value, *done):
    return lax.optimization_barrier((value, done))[0]


def widen(held, bits):
    for bit in bits:
        held = jnp.concatenate([held, swap(held, "wide", bit)], axis=0)
    return held


def add(kept, received):
    return kept.astype(FULL) + received.astype(FULL)


def narrow_down(held, bits):
    for bit in bits:
        half = held.shape[0] // 2
        held = add(held[:half], swap(held[half:].astype(LOW), "wide", bit))
    return held


def turn(value, cosine, sine, sign):
    width = value.shape[1]
    lane = lax.broadcasted_iota(jnp.int32, value.shape, 1) % HD
    other = jnp.where(
        lane < HD // 2,
        pltpu.roll(value, width - HD // 2, 1),
        pltpu.roll(value, HD // 2, 1),
    )
    reps = width // 128
    return value * jnp.concatenate([cosine] * reps, axis=1) + sign * other * jnp.concatenate(
        [sine] * reps, axis=1
    )


def nn(a, b):
    return lax.dot_general(a, b, (((1,), (0,)), ((), ())), preferred_element_type=FULL)


def nt(a, b):
    return lax.dot_general(a, b, (((1,), (1,)), ((), ())), preferred_element_type=FULL)


def diagonal(scores):
    key = lax.broadcasted_iota(jnp.int32, scores.shape, 0)
    query = lax.broadcasted_iota(jnp.int32, scores.shape, 1)
    return jnp.where(key <= query, scores, MASKED)


def flip(value):
    return value.astype(FULL).T


def attend_kernel(
    rows_ref, qka_ref, qkb_ref, voa_ref, vob_ref, cos_ref, sin_ref,
    q_ref, k_ref, v_ref, ctx_ref, lse_ref, hold,
):
    heads = q_ref.shape[0]
    width = heads * HD
    half = qka_ref.shape[0]

    def project(i, carry):
        rows = pl.ds(pl.multiple_of(i * QB, QB), QB)
        first, second = rows_ref[rows, :half], rows_ref[rows, half:]
        pair = nn(first, qka_ref[...]) + nn(second, qkb_ref[...])
        pair = turn(pair, cos_ref[rows, :], sin_ref[rows, :], 1.0)
        value = nn(first, voa_ref[:, :width]) + nn(second, vob_ref[:, :width])
        for h in range(heads):
            q_ref[h, rows, :] = (pair[:, h * HD : (h + 1) * HD] * (HD**-0.5)).astype(LOW)
            k_ref[h, rows, :] = pair[:, width + h * HD : width + (h + 1) * HD].astype(LOW)
            v_ref[h, rows, :] = value[:, h * HD : (h + 1) * HD].astype(LOW)
        return carry

    lax.fori_loop(0, L // QB, project, 0)

    def head(h, carry):
        turned = flip(v_ref[h]).astype(LOW)
        for i in range(L // QB):
            lo, hi = i * QB, (i + 1) * QB
            query = q_ref[h, lo:hi, :]
            diag = diagonal(nt(k_ref[h, lo:hi, :], query))
            peak = jnp.max(diag, axis=0, keepdims=True)
            if i:
                body = nt(k_ref[h, :lo, :], query)
                peak = jnp.maximum(peak, jnp.max(body, axis=0, keepdims=True))
            weight = jnp.exp(diag - peak)
            total = jnp.sum(weight, axis=0, keepdims=True)
            out = nn(turned[:, lo:hi], weight.astype(LOW))
            if i:
                weight = jnp.exp(body - peak)
                total = total + jnp.sum(weight, axis=0, keepdims=True)
                out = out + nn(turned[:, :lo], weight.astype(LOW))
            lse_ref[h, :, lo:hi] = peak + jnp.log(total)
            hold[h, lo:hi, :] = (out / total).T.astype(LOW)
        return carry

    lax.fori_loop(0, heads, head, 0)
    for h in range(heads):
        ctx_ref[:, h * HD : (h + 1) * HD] = hold[h]


def pinned(array):
    return pltpu.with_memory_space_constraint(array, pltpu.HBM)


def near_core(array):
    return pltpu.with_memory_space_constraint(array, pltpu.VMEM)


def whole(array):
    zero = (0,) * len(array.shape)
    return pl.BlockSpec(array.shape, lambda *_: zero)


def by_head(shape):
    return pl.BlockSpec(shape, lambda h: (h, 0, 0))


def columns(piece, mode=None):
    array, width, j = piece if isinstance(piece, tuple) else (piece, piece.shape[-1], 0)
    lead = (0,) * (array.ndim - 1)
    shape = array.shape[:-1] + (width,)
    return array, pl.BlockSpec(shape, lambda *_: lead + (j,), pipeline_mode=mode)


def width_of(piece):
    return piece[1] if isinstance(piece, tuple) else piece.shape[1]


def attend_forward(rows, qk, vo, cosine, sine):
    heads = width_of(qk[0]) // 2 // HD
    headed = pltpu.HBM((heads, L, HD), LOW)
    outs = (
        headed, headed, headed,
        jax.ShapeDtypeStruct((L, heads * HD), LOW),
        pltpu.HBM((heads, 1, L), FULL),
    )
    args, specs = zip(*[columns(p) for p in (rows, *qk, *vo, cosine, sine)])
    return pl.pallas_call(
        attend_kernel,
        grid=(1,),
        in_specs=list(specs),
        out_specs=[whole(o) for o in outs],
        out_shape=outs,
        scratch_shapes=[pltpu.VMEM((heads, L, HD), LOW)],
        compiler_params=pltpu.CompilerParams(vmem_limit_bytes=24 << 20),
        cost_estimate=SMALL,
        name="attend_forward",
    )(*args)


def attend_back_kernel(
    q_ref, k_ref, v_ref, lse_ref, dctx_ref, cos_ref, sin_ref,
    dqk_ref, dv_ref, dctx, dqk, dk_sum, dv_sum,
):
    heads = dctx.shape[0]
    h = pl.program_id(0)

    @pl.when(h == 0)
    def _():
        for j in range(heads):
            dctx[j] = dctx_ref[:, j * HD : (j + 1) * HD]

    turned = flip(k_ref[0]).astype(LOW)
    for i in range(L // QB):
        lo, hi = i * QB, (i + 1) * QB
        query, back = q_ref[0, lo:hi, :], dctx[h, lo:hi, :]
        lse = lse_ref[0, :, lo:hi]
        prob = jnp.exp(diagonal(nt(k_ref[0, lo:hi, :], query)) - lse)
        grad = nt(v_ref[0, lo:hi, :], back)
        inner = jnp.sum(prob * grad, axis=0, keepdims=True)
        if i:
            prob_body = jnp.exp(nt(k_ref[0, :lo, :], query) - lse)
            grad_body = nt(v_ref[0, :lo, :], back)
            inner = inner + jnp.sum(prob_body * grad_body, axis=0, keepdims=True)
        score = (prob * (grad - inner)).astype(LOW)
        dv_sum[h, lo:hi, :] = nn(prob.astype(LOW), back)
        dk_sum[h, lo:hi, :] = nn(score, query)
        dquery = nn(turned[:, lo:hi], score)
        if i:
            score = (prob_body * (grad_body - inner)).astype(LOW)
            dv_sum[h, :lo, :] += nn(prob_body.astype(LOW), back)
            dk_sum[h, :lo, :] += nn(score, query)
            dquery = dquery + nn(turned[:, :lo], score)
        dqk[h, lo:hi, :] = (dquery * (HD**-0.5)).T

    def finish(i, carry):
        rows = pl.ds(pl.multiple_of(i * QB, QB), QB)
        pair = jnp.concatenate(
            [dqk[j, rows, :] for j in range(heads)] + [dk_sum[j, rows, :] for j in range(heads)],
            axis=1,
        )
        dqk_ref[rows, :] = turn(pair, cos_ref[rows, :], sin_ref[rows, :], -1.0).astype(LOW)
        dv_ref[rows, :] = jnp.concatenate(
            [dv_sum[j, rows, :] for j in range(heads)], axis=1
        ).astype(LOW)
        return carry

    @pl.when(h == heads - 1)
    def _():
        lax.fori_loop(0, L // QB, finish, 0)


def attend_backward(q, k, v, lse, dctx, cosine, sine):
    heads = q.shape[0]
    outs = (
        jax.ShapeDtypeStruct((L, 2 * heads * HD), LOW),
        jax.ShapeDtypeStruct((L, heads * HD), LOW),
    )
    return pl.pallas_call(
        attend_back_kernel,
        grid=(heads,),
        in_specs=[by_head((1, L, HD))] * 3
        + [by_head((1, 1, L)), whole(dctx), whole(cosine), whole(sine)],
        out_specs=[whole(o) for o in outs],
        out_shape=outs,
        scratch_shapes=[pltpu.VMEM((heads, L, HD), LOW)] + [pltpu.VMEM((heads, L, HD), FULL)] * 3,
        compiler_params=pltpu.CompilerParams(vmem_limit_bytes=24 << 20),
        cost_estimate=SMALL,
        name="attend_backward",
    )(pinned(q), pinned(k), pinned(v), pinned(lse), pinned(dctx), pinned(cosine), pinned(sine))


def held_once(array):
    zero = (0,) * array.ndim
    return pl.BlockSpec(array.shape, lambda *_: zero, pipeline_mode=pl.Buffered(1))


def in_top():
    return pl.program_id(0) < pl.num_programs(0) // 2


def halves(step, width):
    steps = L // step // 2
    return [
        pl.BlockSpec((step, width), lambda i: (jnp.minimum(i, steps - 1), 0)),
        pl.BlockSpec((step, width), lambda i: (jnp.maximum(i - steps, 0), 0)),
    ]


def by_rows(kernel, name, row_args, fixed, outs, sums=0, kept=(), scratch=(), loose=(), step=QB):
    specs, flat = [], []
    for r in row_args:
        if isinstance(r, tuple):
            specs += halves(step, r[0].shape[1])
            flat += r
        else:
            specs.append(pl.BlockSpec((step, r.shape[1]), lambda i: (i, 0)))
            flat.append(r)
    held, held_specs = zip(*[columns(f, pl.Buffered(1)) for f in fixed])
    shapes = [
        (pltpu.HBM if away else jax.ShapeDtypeStruct)((L, w), t) for w, t, away in outs
    ]
    out_specs = [pl.BlockSpec((step, w), lambda i: (i, 0)) for w, _, _ in outs]
    if not outs:
        shapes = [jax.ShapeDtypeStruct((L // 2, D), LOW)] * 2
        out_specs = halves(step, D)
    rows_out = len(shapes)
    shapes += [jax.ShapeDtypeStruct((1, D), FULL)] * sums
    shapes += [pltpu.HBM(shape, LOW) for shape in kept]
    out_specs += [whole(o) for o in shapes[rows_out:]]
    return pl.pallas_call(
        kernel,
        grid=(L // step,),
        in_specs=specs + list(held_specs),
        out_specs=out_specs,
        out_shape=shapes,
        scratch_shapes=list(scratch),
        compiler_params=pltpu.CompilerParams(vmem_limit_bytes=32 << 20),
        cost_estimate=SMALL,
        name=name,
    )(*flat, *[f if f.dtype == FULL or i in loose else pinned(f) for i, f in enumerate(held)])


def rms_scale(residual):
    return lax.rsqrt(jnp.mean(residual * residual, axis=1, keepdims=True) + EPSILON)


def norm_back(scaled, normed, inv):
    return inv * (scaled - normed * jnp.mean(scaled * normed, axis=1, keepdims=True))


def column_sum(sum_ref, value):
    @pl.when(pl.program_id(0) == 0)
    def _():
        sum_ref[...] = jnp.zeros_like(sum_ref)

    sum_ref[...] += jnp.sum(value, axis=0, keepdims=True)


def heads_out(held_ref, refs):
    att_ref, y_ref, x_ref, corner_ref = refs
    half, width = att_ref.shape[0], held_ref.shape[2]

    @pl.when(pl.program_id(0) == 0)
    def _():
        held_ref[0, :half] = att_ref[:, 3 * width :]
        held_ref[0, half:] = y_ref[:, 3 * width :]
        held_ref[1, :half] = x_ref[:, 3 * width :]
        held_ref[1, half:] = corner_ref[:, width:]


def project_kernel(one_ref, two_ref, att_ref, y_ref, x_ref, corner_ref, out_ref, held_ref):
    heads_out(held_ref, (att_ref, y_ref, x_ref, corner_ref))
    out_ref[...] = (nt(one_ref[...], held_ref[0]) + nt(two_ref[...], held_ref[1])).astype(LOW)


def gate_up(hidden, weights_ref, gate_ref, up_ref, act_ref):
    hid = gate_ref.shape[1]
    gate = nn(hidden, weights_ref[:, :hid])
    up = nn(hidden, weights_ref[:, hid:])
    gate_ref[...] = gate.astype(LOW)
    up_ref[...] = up.astype(LOW)
    act_ref[...] = (gate * jax.nn.sigmoid(gate) * up).astype(LOW)


def enter_kernel(
    rows_ref, mine_ref, theirs_ref, gain_ref, own_ref, y_ref,
    normed_ref, inv_ref, hidden_ref, gate_ref, up_ref, act_ref, weights_ref,
):
    half = own_ref.shape[0]

    @pl.when(pl.program_id(0) == 0)
    def _():
        weights_ref[:half] = own_ref[...]
        weights_ref[half:] = y_ref[...]

    residual = rows_ref[...].astype(FULL) + add(mine_ref[...], theirs_ref[...])
    inv = rms_scale(residual)
    normed = residual * inv
    hidden = (normed * gain_ref[0]).astype(LOW)
    normed_ref[...] = normed.astype(LOW)
    inv_ref[...] = inv
    hidden_ref[...] = hidden
    gate_up(hidden, weights_ref, gate_ref, up_ref, act_ref)


def rest_kernel(
    hidden_ref, act1_ref, x_ref, gate_corner_ref, up_corner_ref,
    low_own_ref, low_y_ref, low_x_ref, low_corner_ref, high_ref,
    gate_ref, up_ref, act_ref, out_ref, weights_ref, down_ref,
):
    half, hid = x_ref.shape[0], gate_ref.shape[1]
    cut = high_ref.shape[2]

    @pl.when(pl.program_id(0) == 0)
    def _():
        weights_ref[:half] = x_ref[...]
        weights_ref[half:, :hid] = gate_corner_ref[...]
        weights_ref[half:, hid:] = up_corner_ref[...]
        down_ref[0, :half, :cut] = low_own_ref[...]
        down_ref[0, half:, :cut] = low_y_ref[...]
        down_ref[1, :half, :cut] = low_x_ref[...]
        down_ref[1, half:, :cut] = low_corner_ref[...]
        down_ref[:, :, cut:] = high_ref[...]

    gate_up(hidden_ref[...], weights_ref, gate_ref, up_ref, act_ref)
    out_ref[...] = (nt(act1_ref[...], down_ref[0]) + nt(act_ref[...], down_ref[1])).astype(LOW)


def turn_kernel(
    normed_ref, mine_ref, theirs_ref, up_rows_ref, gains_ref,
    out_ref, low_ref, sum_ref,
):
    residual = normed_ref[...].astype(FULL) * gains_ref[0] + add(mine_ref[...], theirs_ref[...])
    inv = rms_scale(residual)
    normed = residual * inv
    gain = gains_ref[1]
    out_ref[...] = (normed * gain).astype(LOW)
    upstream = up_rows_ref[...].astype(FULL)
    column_sum(sum_ref, upstream * normed)
    low_ref[...] = norm_back(upstream * gain, normed, inv).astype(LOW)


def back_kernel(low_ref, gate1_ref, up1_ref, gate2_ref, up2_ref, down_ref, gg_ref, ug_ref):
    hid = gate1_ref.shape[1]
    low = low_ref[...]
    for x, gate_ref, up_ref in ((0, gate1_ref, up1_ref), (1, gate2_ref, up2_ref)):
        act_grad = nn(low, down_ref[x])
        gate, up = gate_ref[...].astype(FULL), up_ref[...].astype(FULL)
        sig = jax.nn.sigmoid(gate)
        gg = act_grad * up * (sig * (1.0 + gate * (1.0 - sig)))
        gg_ref[:, x * hid : (x + 1) * hid] = gg.astype(LOW)
        ug_ref[:, x * hid : (x + 1) * hid] = (act_grad * (gate * sig)).astype(LOW)


def mid_kernel(gg_ref, ug_ref, own_ref, other_ref, top_ref, bottom_ref):
    hid = gg_ref.shape[1] // 2
    total = 0.0
    for x, weights_ref in enumerate((own_ref, other_ref)):
        cols = slice(x * hid, (x + 1) * hid)
        total = total + nt(gg_ref[:, cols], weights_ref[:, :hid])
        total = total + nt(ug_ref[:, cols], weights_ref[:, hid:])
    low = total.astype(LOW)

    @pl.when(in_top())
    def _():
        top_ref[...] = low

    @pl.when(jnp.logical_not(in_top()))
    def _():
        bottom_ref[...] = low


def leave_kernel(
    grad_two_ref, mine_top_ref, mine_bottom_ref, theirs_top_ref, theirs_bottom_ref,
    normed_ref, inv_ref, gains_ref, att_ref, y_ref, x_ref, corner_ref,
    low_ref, ctx1_ref, ctx2_ref, sum_ref, held_ref, mid_ref,
):
    heads_out(held_ref, (att_ref, y_ref, x_ref, corner_ref))

    @pl.when(in_top())
    def _():
        mid_ref[...] = add(mine_top_ref[...], theirs_top_ref[...])

    @pl.when(jnp.logical_not(in_top()))
    def _():
        mid_ref[...] = add(mine_bottom_ref[...], theirs_bottom_ref[...])

    hidden_grad = grad_two_ref[...].astype(FULL) + mid_ref[...]
    normed = normed_ref[...].astype(FULL)
    column_sum(sum_ref, hidden_grad * normed)
    low = norm_back(hidden_grad * gains_ref[0], normed, inv_ref[...]).astype(LOW)
    low_ref[...] = low
    ctx1_ref[...] = nn(low, held_ref[0]).astype(LOW)
    ctx2_ref[...] = nn(low, held_ref[1]).astype(LOW)


def input_kernel(
    qk1_ref, v1_ref, qk2_ref, v2_ref, att_ref, y_ref, x_ref, qk_corner_ref, vo_corner_ref,
    full_ref, low_ref, held_ref,
):
    half, width = att_ref.shape[0], v1_ref.shape[1]
    pair = 2 * width

    @pl.when(pl.program_id(0) == 0)
    def _():
        held_ref[0, :half] = att_ref[:, : pair + width]
        held_ref[0, half:] = y_ref[:, : pair + width]
        held_ref[1, :half] = x_ref[:, : pair + width]
        held_ref[1, half:, :pair] = qk_corner_ref[...]
        held_ref[1, half:, pair:] = vo_corner_ref[:, :width]

    total = 0.0
    for x, qk_ref, v_ref in ((0, qk1_ref, v1_ref), (1, qk2_ref, v2_ref)):
        total = total + nt(qk_ref[...], held_ref[x, :, :pair])
        total = total + nt(v_ref[...], held_ref[x, :, pair:])
    full_ref[...] = total
    low_ref[...] = total.astype(LOW)


def heads_grad_kernel(
    rows_ref, grad_ref, qk_ref, v_ref, ctx_ref, near_ref, far_ref, vo_ref
):
    width = v_ref.shape[1]
    rows = flip(rows_ref[...]).astype(LOW)
    qk = nn(rows, qk_ref[...]).astype(LOW)
    step, half = qk.shape[0], near_ref.shape[0]
    for i in range(D // step):

        @pl.when(pl.program_id(0) == i)
        def _(start=i * step):
            near = max(min(half - start, step), 0)
            if near:
                near_ref[start : start + near] = qk[:near]
            if near < step:
                far_ref[start + near - half : start + step - half] = qk[near:]

    vo_ref[:, :width] = nn(rows, v_ref[...]).astype(LOW)
    vo_ref[:, width:] = nn(flip(grad_ref[...]).astype(LOW), ctx_ref[...]).astype(LOW)


def heads_grad(rows, grad, dqk, dv, context):
    half, pair = D // 2, dqk.shape[1]
    split = pl.BlockSpec((L, 256), lambda i: (0, i))
    held = pl.BlockSpec((half, pair), lambda i: (0, 0))
    return pl.pallas_call(
        heads_grad_kernel,
        grid=(D // 256,),
        in_specs=[split, split] + [held_once(g) for g in (dqk, dv, context)],
        out_specs=[held, held, pl.BlockSpec((256, pair), lambda i: (i, 0))],
        out_shape=[pltpu.HBM((half, pair), LOW)] * 2 + [pltpu.HBM((D, pair), LOW)],
        compiler_params=pltpu.CompilerParams(vmem_limit_bytes=24 << 20),
        cost_estimate=SMALL,
        name="heads_grad",
    )(rows, grad, dqk, dv, context)


def in_order(value, mover):
    total = 0.0
    for _ in range(2):
        part = value.astype(LOW)
        total = total + nt(part, mover)
        value = value - part.astype(FULL)
    return total


def finish_kernel(
    core_ref, one_ref, full_ref, out_ref, theirs_ref, mover_ref, grad_ref, low_ref
):
    mover = mover_ref[...]
    grad = one_ref[...].astype(FULL) + full_ref[...] + theirs_ref[...].astype(FULL)
    grad_ref[...] = in_order(grad, mover)
    low_ref[...] = nt(out_ref[...], mover).astype(LOW)


def finish(core, grad_one, part_full, layer_output, theirs, mover):
    rows = theirs.shape[0]
    steps = rows // QB
    mine = pl.BlockSpec((QB, D), lambda i, c: (c[0] * steps + i, 0))
    plain = pl.BlockSpec((QB, D), lambda i, c: (i, 0))
    return pl.pallas_call(
        finish_kernel,
        grid_spec=pltpu.PrefetchScalarGridSpec(
            num_scalar_prefetch=1,
            grid=(steps,),
            in_specs=[mine, mine, mine, plain, held_once(mover)],
            out_specs=[plain, plain],
        ),
        out_shape=[
            jax.ShapeDtypeStruct((rows, D), FULL), jax.ShapeDtypeStruct((rows, D), LOW)
        ],
        cost_estimate=SMALL,
        name="finish",
    )(core, grad_one, pinned(part_full), pinned(layer_output), pinned(theirs), mover)


def last_kernel(
    kept_ref, received_ref, late_ref, late_received_ref, early_ref, sum_ref, late_sum_ref, total_ref
):
    def squares(value):
        return jnp.sum(jnp.sum(value * value, axis=0, keepdims=True), axis=1, keepdims=True)

    block = received_ref.shape[0]
    value = kept_ref[:block] + received_ref[...].astype(FULL)
    late = late_ref[:block] + late_received_ref[...].astype(FULL)
    sum_ref[...] = value
    late_sum_ref[...] = late
    total = squares(value) + squares(late) + squares(early_ref[...])
    total_ref[...] = jnp.broadcast_to(total, total_ref.shape)


def last_sums(kept, received, late, late_received, early):
    vmem = pl.BlockSpec(memory_space=pltpu.VMEM)
    return pl.pallas_call(
        last_kernel,
        in_specs=[vmem] * 5,
        out_specs=[vmem] * 3,
        out_shape=[jax.ShapeDtypeStruct(a.shape, FULL) for a in (received, late_received)]
        + [jax.ShapeDtypeStruct((1, 128), FULL)],
        name="last_sums",
    )(kept, near_core(received), late, near_core(late_received), early)


def adam_kernel(clip, rates, *refs):
    me = refs[0][0]
    message = refs[1][...] + refs[2][...]
    att_ref, ffn_ref, down_ref = refs[3:6]
    ins, norm_ref, outs = refs[6:21], refs[21], refs[22:]
    block = ins[12].shape[1]
    gain_sum = message[:, : 2 * D]
    total = message[:, 2 * D : 2 * D + 1] + jnp.sum(gain_sum * gain_sum, axis=1, keepdims=True)
    norm = jnp.sqrt(total)
    norm_ref[...] = norm
    ratio = clip / jnp.maximum(norm, clip)

    def update(p, at, grad):
        rate, decay = rates[p]
        old = [ref[at] for ref in ins[3 * p : 3 * p + 3]]
        for ref, value in zip(
            outs[3 * p : 3 * p + 3], adam_update(*old, grad, ratio, rate, decay)
        ):
            ref[at] = value

    width, hid = att_ref.shape[1] // 4, ffn_ref.shape[1] // 2
    step = 16 if block % 16 == 0 else block

    def some(i, carry):
        rows = pl.ds(pl.multiple_of(i * step, step), step) if step < block else slice(None)
        for k in range(3):
            update(0, (k, rows), att_ref[rows, k * width : (k + 1) * width])
        for k in range(2):
            update(2, (k, rows), ffn_ref[rows, k * hid : (k + 1) * hid])
        update(3, rows, down_ref[rows, :])
        return carry

    if step < block:
        lax.fori_loop(0, block // step, some, 0)
    else:
        some(0, 0)
    update(1, ..., att_ref[:, 3 * width :].T)
    for k in range(2):
        mine = jnp.zeros((1, block), FULL)
        for j in range(D // block):
            start = k * D + j * block
            mine = jnp.where(me == j, gain_sum[:, start : start + block], mine)
        update(4, pl.ds(k, 1), mine)


def adam(me, clip, rates, grads, params):
    flat = [array for group in params for array in group]
    outs = [jax.ShapeDtypeStruct((1, 1), FULL)]
    outs += [jax.ShapeDtypeStruct(w.shape, FULL) for w in flat]
    vmem = pl.BlockSpec(memory_space=pltpu.VMEM)
    norm, *made = pl.pallas_call(
        functools.partial(adam_kernel, clip, rates),
        in_specs=[pl.BlockSpec(memory_space=pltpu.SMEM)] + [vmem] * (len(grads) + len(flat)),
        out_specs=[vmem] * len(outs),
        out_shape=outs,
        name="adam",
    )(me, *grads, *[pltpu.with_memory_space_constraint(f, pltpu.VMEM) for f in flat])
    return norm[0, 0], [made[i : i + 3] for i in range(0, len(made), 3)]


def rope_tables(place):
    half, low = HD // 2, place.shape[0] // 2
    lane = jnp.arange(128) % HD
    freq = jnp.exp(-jnp.log(10000.0) * (lane % half).astype(FULL) / half)
    angle = place[:, None] * freq[None, :]
    cosine, sine = jnp.cos(angle), jnp.sin(angle)
    c1, s1 = cosine[:low, None], sine[:low, None]
    c2, s2 = cosine[None, low:], sine[None, low:]
    sign = jnp.where(lane < half, -1.0, 1.0)[None, None, :]
    both = c1 * c2 - s1 * s2, sign * (s1 * c2 + c1 * s2)
    return [table.reshape(L, 128) for table in both]


def adam_update(weight, first, second, grad, ratio, rate, decay):
    clipped = grad * ratio
    first_new = AVERAGING * first + (1.0 - AVERAGING) * clipped
    second_new = AVERAGING * second + (1.0 - AVERAGING) * clipped * clipped
    correction = 1.0 - AVERAGING**ADAM_STEP
    step = first_new / correction / (jnp.sqrt(second_new / correction) + 1e-08)
    return (weight - rate * (step + decay * weight), first_new, second_new)


def tn(rows, grads):
    out = lax.dot_general(rows, grads, (((0,), (0,)), ((), ())), preferred_element_type=FULL)
    return layout.with_layout_constraint(out.astype(LOW), layout.Layout((0, 1)))


def per_device(
    layer_input, layer_cotangent,
    attend_weight, attend_first, attend_second,
    output_weight, output_first, output_second,
    gated_weight, gated_first, gated_second,
    down_weight, down_first, down_second,
    norm_gains, gains_first, gains_second,
):
    rows = layer_input.shape[0]
    wide = lax.axis_size("wide")
    block = D // wide
    me = lax.axis_index("wide")
    narrow = lax.axis_index("narrow")
    core = narrow % 2
    cols = attend_weight.shape[2]

    bits = wide_bits()
    near = bits[:-1]
    half = D // 2
    hid = down_weight.shape[0]

    bits = wide_bits()
    near = bits[:-1]
    half = D // 2
    hid = down_weight.shape[0]
    pair = 2 * cols

    attend_low = attend_weight.astype(LOW)
    att = jnp.concatenate(
        [attend_low[0], attend_low[1], attend_low[2], output_weight.T.astype(LOW)], axis=1
    )
    cut = hid // 2
    down_t = down_weight.T
    ffn = jnp.concatenate([gated_weight[0], gated_weight[1], down_t[:, :cut]], axis=1).astype(LOW)
    down = down_t[:, cut:].astype(LOW)

    order = me ^ jnp.array(block_masks(), jnp.int32)
    source = (order[:, None] * block + jnp.arange(block)[None, :]).reshape(1, D)
    mover = (lax.broadcasted_iota(jnp.int32, (D, D), 0) == source).astype(LOW)
    mover = lax.optimization_barrier(mover)

    def both_halves(mine, theirs):
        first = core == 0
        return jnp.concatenate(
            [jnp.where(first, mine, theirs), jnp.where(first, theirs, mine)], axis=0
        )

    def own_rows(value):
        return lax.dynamic_slice_in_dim(value, core * rows, rows, axis=0)

    first = widen(att, near[:1])
    gains = widen(after(norm_gains, att).astype(LOW).astype(FULL)[None], bits[:1])
    first, down, gains = lax.optimization_barrier((first, down, gains))
    gains = widen(gains, bits[1:-1])
    att = widen(first, near[1:])
    down_y = swap(down, "wide", 1)
    down_x = swap(down, "narrow", 2)
    both = jnp.concatenate([layer_input, layer_cotangent], axis=0)
    moved = jnp.dot(both, mover, preferred_element_type=FULL).astype(LOW)
    place = jnp.arange(32, dtype=FULL)
    place = jnp.concatenate([32.0 * place, place])
    att, down_y, down_x, gains, moved, place = lax.optimization_barrier(
        (att, down_y, down_x, gains, moved, place)
    )
    att_y = swap(att, "wide", 1)
    att_x = swap(att, "narrow", 2)
    ffn = widen(after(ffn, att), near[:1])
    inputs = both_halves(moved[:rows], swap(moved[:rows], "narrow", 1))
    inputs, gains = lax.optimization_barrier((inputs, gains))
    gains = widen(gains, bits[-1:])
    moved_up = moved[rows:]
    cosine, sine = rope_tables(place)
    inputs, att, att_y, att_x, ffn, gains, cosine, sine = lax.optimization_barrier(
        (inputs, att, att_y, att_x, ffn, gains, cosine, sine)
    )
    gains = gains.transpose(1, 0, 2).reshape(2, 1, D)
    down_corner = swap(down_y, "narrow", 2)
    qk_corner = swap(att_y[:, :pair], "narrow", 2)
    vo_corner = swap(att_x[:, pair:], "wide", 1)
    ffn = widen(ffn, near[1:])
    qk = [[(att, pair, 0), (att_y, pair, 0)], [(att_x, pair, 0), qk_corner]]
    vo = [[(att, pair, 1), (att_y, pair, 1)], [(att_x, pair, 1), vo_corner]]
    saved = [attend_forward(inputs, qk[0], vo[0], cosine, sine)]
    second_in, qk_corner, vo_corner, ffn, down_corner = lax.optimization_barrier(
        (after(inputs, saved[0][3]), qk_corner, vo_corner, ffn, down_corner)
    )
    other_up = swap(after(moved_up, second_in), "narrow", 1)
    down = jnp.stack([down, down_y, down_x, down_corner])[:, None]
    for bit in near[:1]:
        down = jnp.concatenate([down, swap(down, "wide", bit)], axis=1)
    qk[1][1], vo[1][1] = qk_corner, vo_corner
    ffn_y = swap(ffn, "wide", 1)
    ffn_x = swap(ffn, "narrow", 2)
    saved.append(attend_forward(second_in, qk[1], vo[1], cosine, sine))
    context = [s[3] for s in saved]
    att_out = [att, att_y, att_x, vo_corner]
    held = [pltpu.VMEM((2, D, cols), LOW)]
    low_d, full_d = (D, LOW, False), (D, FULL, True)
    (attn_part,) = by_rows(
        project_kernel, "project", context, att_out, [low_d], scratch=held
    )
    ffn_y, ffn_x, attn_part, down = lax.optimization_barrier((ffn_y, ffn_x, attn_part, down))
    attn_other = swap(attn_part, "narrow", 1)
    down_far = [swap(down, "wide", bit) for bit in near[1:2]]
    gate_corner = swap(ffn_y[:, :hid], "narrow", 2)
    up_corner = swap(ffn_x[:, hid:], "wide", 1)
    flow = [(hid, LOW, True), (hid, LOW, True), (hid, LOW, False)]
    normed_one, inv_one, hidden_low, gate1, up1, act1, gu_own = by_rows(
        enter_kernel, "enter", [pinned(inputs), attn_part, pinned(attn_other)],
        [gains, (ffn, 2 * hid, 0), (ffn_y, 2 * hid, 0)],
        [(D, LOW, True), (1, FULL, True), low_d] + flow, kept=[(D, 2 * hid)],
    )
    hidden_low, down, down_far = lax.optimization_barrier((hidden_low, down, down_far))
    moved_up, other_up, hidden_low = lax.optimization_barrier((moved_up, other_up, hidden_low))
    upstream = both_halves(moved_up, other_up)
    down = jnp.concatenate([down, *down_far], axis=1)
    for bit in near[2:]:
        down = jnp.concatenate([down, swap(down, "wide", bit)], axis=1)
    down = down.reshape(2, D, hid - cut)
    last_cols = 2 * hid // cut
    gate2, up2, act2, ffn_part, gu_other, down_all = by_rows(
        rest_kernel, "rest", [after(hidden_low, upstream), act1],
        [
            (ffn_x, 2 * hid, 0), gate_corner, (up_corner, hid, 0),
            (ffn, cut, last_cols), (ffn_y, cut, last_cols), (ffn_x, cut, last_cols),
            (up_corner, cut, hid // cut), down,
        ],
        flow + [low_d], kept=[(D, 2 * hid), (2, D, hid)], loose=(1, 2, 6),
    )
    ffn_other = swap(ffn_part, "narrow", 1)

    layer_output, grad_two_low, gain_two_grad = by_rows(
        turn_kernel, "turn", [pinned(normed_one), ffn_part, ffn_other, pinned(upstream)],
        [gains], [(D, LOW, True), low_d], sums=1,
    )
    down_send = tn(grad_two_low, act2)
    down_x = swap(down_send, "narrow", 2)
    wide_flow = (2 * hid, LOW, False)
    saves = [pinned(r) for r in (gate1, up1, gate2, up2)]
    gg, ug = by_rows(
        back_kernel, "back",
        [after(grad_two_low, down_send), *saves], [down_all], [wide_flow, wide_flow],
    )
    gate_send = tn(hidden_low[:, half:], gg)
    up_send = tn(hidden_low[:, half:], ug)
    gate_y = swap(gate_send, "wide", 1)
    up_y = swap(up_send, "wide", 1)
    mid_part = by_rows(
        mid_kernel, "mid", [after(gg, gate_send, up_send), ug], [gu_own, gu_other], []
    )
    mid_other = [swap(part, "narrow", 1) for part in mid_part]
    down_own = tn(grad_two_low, act1)
    gate_own = tn(hidden_low[:, :half], gg)
    up_own = tn(hidden_low[:, :half], ug)
    mid_part, mid_other, down_own, gate_own, up_own, down_x = lax.optimization_barrier(
        (mid_part, mid_other, down_own, gate_own, up_own, down_x)
    )
    grad_one_low, dctx1, dctx2, gain_one_grad = by_rows(
        leave_kernel, "leave",
        [grad_two_low, tuple(mid_part), tuple(mid_other), pinned(normed_one), pinned(inv_one)],
        [gains, *att_out], [low_d, (cols, LOW, True), (cols, LOW, True)],
        sums=1, scratch=held + [pltpu.VMEM((QB, D), FULL)],
    )

    q, k, v, _, lse = saved[1]
    dqk2, dv2 = attend_backward(q, k, v, lse, dctx2, cosine, sine)
    down_x, gate_y, dqk2, dv2 = lax.optimization_barrier((down_x, gate_y, dqk2, dv2))
    down_sum, gate_sum = add(down_own, down_x), add(gate_own, gate_y)
    down_y = swap(down_sum[half:].astype(LOW), "wide", 1)
    gate_far = gate_sum[:, hid:].astype(LOW)
    gate_x = swap(gate_far, "narrow", 2)
    qk_near2, qk_send2, vo_send = heads_grad(inputs, grad_one_low, after(dqk2, gate_far), dv2, context[1])
    qk_y2 = swap(qk_send2, "wide", 1)
    back = near[::-1]
    q, k, v, _, lse = saved[0]
    up_y, vo_done = lax.optimization_barrier((up_y, vo_send))
    up_sum = add(up_own, up_y)
    up_far = up_sum[:, hid:].astype(LOW)
    dctx1, up_far, vo_done = lax.optimization_barrier((dctx1, up_far, vo_done))
    up_x = swap(up_far, "narrow", 2)
    vo_x = swap(vo_done, "narrow", 2)
    dqk1, dv1 = attend_backward(q, k, v, lse, dctx1, cosine, sine)
    dqk1, dv1, down_y, qk_y2, gate_x = lax.optimization_barrier(
        (dqk1, dv1, down_y, qk_y2, gate_x)
    )
    early = narrow_down(add(down_sum[:half], down_y), back[:1])
    qk_near1, qk_send1, vo_own = heads_grad(inputs, grad_one_low, dqk1, dv1, context[0])
    qk_y1 = swap(qk_send1, "wide", 1)
    qk_far = add(qk_near2, qk_y2).astype(LOW)
    qk_x = swap(qk_far, "narrow", 2)
    vo_sum = add(vo_own, vo_x)
    vo_far = vo_sum[half:].astype(LOW)
    vo_y = swap(vo_far, "wide", 1)
    late = jnp.concatenate([add(gate_sum[:, :hid], gate_x), add(up_sum[:, :hid], up_x)], axis=1)
    dqk1, vo_sum, late, early = lax.optimization_barrier((dqk1, vo_sum, late, early))
    early_red = narrow_down(early, back[1:])
    late = narrow_down(late, back[:1])
    part_full, part_low = by_rows(
        input_kernel, "inputs", [dqk1, dv1, dqk2, dv2],
        [att, att_y, att_x, qk_corner, vo_corner], [full_d, low_d],
        scratch=[pltpu.VMEM((2, D, 3 * cols), LOW)],
    )
    qk_sum = add(qk_near1, qk_y1)
    last = jnp.concatenate([add(qk_sum, qk_x), add(vo_sum[:half], vo_y)], axis=1)
    gain_grads = jnp.concatenate([gain_one_grad, gain_two_grad], axis=0)
    gain_low = gain_grads.astype(LOW)
    gain_rest = (gain_grads - gain_low.astype(FULL)).astype(LOW)
    gain_grads = nt(jnp.concatenate([gain_low, gain_rest], axis=0), mover)
    gain_grads = gain_grads[:2] + gain_grads[2:]
    last, early_red, late, gain_grads, part_low = lax.optimization_barrier(
        (last, early_red, late, gain_grads, part_low)
    )
    theirs = lax.dynamic_slice_in_dim(part_low, (1 - core) * rows, rows, axis=0)
    theirs = swap(theirs, "narrow", 1)
    last = narrow_down(last, back[:1])
    late = narrow_down(late, back[1:-1])
    late_received = swap(late[block:].astype(LOW), "wide", back[-1])
    last = narrow_down(last, back[1:-1])
    received = swap(last[block:].astype(LOW), "wide", back[-1])
    input_grad, layer_output = finish(
        jnp.full((1,), core, jnp.int32), grad_one_low, part_full, layer_output, theirs, mover
    )
    received, input_grad, layer_output = lax.optimization_barrier(
        (received, input_grad, layer_output)
    )
    att_red, late_red, square = last_sums(
        last, received, late, late_received, early_red
    )

    square = square + swap(square, "narrow", 1)
    message = jnp.concatenate([gain_grads.reshape(1, 2 * D), square], axis=1)
    message = message + swap(message, "narrow", 2)
    for bit in bits[::-1][:-1]:
        message = message + swap(message, "wide", bit)
    received = swap(message, "wide", bits[0])
    all_tokens = rows * wide * lax.axis_size("narrow")
    clip = 0.02 * math.sqrt(all_tokens * (4 * D * D + 3 * D * FF + 2 * D))
    grad_norm, (new_attend, new_output, new_gated, new_down, new_gains) = adam(
        jnp.full((1,), me, jnp.int32),
        clip,
        (
            (D ** (-0.5), WEIGHT_DECAY),
            (max(D // 64, 1) ** (-0.5), WEIGHT_DECAY),
            (D ** (-0.5), WEIGHT_DECAY),
            (FF ** (-0.5), WEIGHT_DECAY),
            (0.4, 0.0),
        ),
        (message, near_core(received), att_red, late_red, early_red),
        (
            (attend_weight, attend_first, attend_second),
            (output_weight, output_first, output_second),
            (gated_weight, gated_first, gated_second),
            (down_weight.T, down_first.T, down_second.T),
            (norm_gains, gains_first, gains_second),
        ),
    )
    new_down = [value.T for value in new_down]
    return (
        layer_output, input_grad, grad_norm,
        *new_attend, *new_output, *new_gated, *new_down, *new_gains,
    )


def solution(mesh):
    rows = P(("wide", "narrow"), None)
    stacked = P(None, "wide", "narrow")
    turned = P("narrow", "wide")
    gains = P(None, "wide")
    params = (stacked,) * 3 + (turned,) * 3 + (stacked,) * 3 + (turned,) * 3 + (gains,) * 3
    return jax.shard_map(
        per_device,
        mesh=mesh,
        in_specs=(rows, rows) + params,
        out_specs=(rows, rows, P()) + params,
        check_vma=False,
    )
```
